32 devices in a mesh: shard: 4 (over y, core), ctx: 4 (over z), tp: 2 (over x).
Axes of the slice: x: 2, y: 2, z: 4, core: 2. Of those that a mesh axis runs over, the one named last changes fastest.
Arguments:
- tokens: bfloat16 [8, 1024, 768], P('shard', 'ctx'), may hold values from -4 to 4
- lengths: int32 [8], P('shard'), may hold values from 256 to 1024, as said below
- w_qkv: float32 [768, 3, 768], P(('shard', 'ctx'), None, 'tp'), may hold values from -0.21875 to 0.21875
- b_qv: float32 [2, 768], P(None, 'tp'), may hold values from -3 to 3
- w_out: float32 [768, 768], P('tp', ('shard', 'ctx')), may hold values from -0.625 to 0.625
- w_gu: float32 [768, 2, 3072], P(('shard', 'ctx'), None, 'tp'), may hold values from -0.21875 to 0.21875
- w_down: float32 [3072, 768], P('tp', ('shard', 'ctx')), may hold values from -0.109375 to 0.109375
- vectors: float32 [6, 768], replicated, may hold values from 0.25 to 1.75
- cotangent: bfloat16 [8, 1024, 768], P('shard', 'ctx'), may hold values from -6 to 6
Outputs:
- output: bfloat16 [8, 1024, 768], P('shard', 'ctx')
- input_grad: float32 [8, 1024, 768], P('shard', 'ctx')
- grad_qkv: float32 [768, 3, 768], P(('shard', 'ctx'), None, 'tp')
- grad_bqv: float32 [2, 768], P(None, 'tp')
- grad_out: float32 [768, 768], P('tp', ('shard', 'ctx'))
- grad_gu: float32 [768, 2, 3072], P(('shard', 'ctx'), None, 'tp')
- grad_down: float32 [3072, 768], P('tp', ('shard', 'ctx'))
- grad_vectors: float32 [6, 768], replicated
The draws below stay inside these ranges and needn't reach their ends.
Inputs may be any that keep to these rules, and one draw needn't show every extreme that they name: `lengths`: sequence 0 has all 1024 slots valid and sequence 1 has 256.
All inputs are finite; a program needn't handle non-finite values.
Results may differ from the reference program's by a relative error of at most 0.018.
Values may be sent and summed in bfloat16 or wider, within the bound.
No kernel may reach another device: no remote copies, remote signals or barrier semaphores. Data moves between devices by JAX's collectives and lax.ppermute only.
A program may use at most 128 MiB of HBM per device.

```python
import jax
import jax.numpy as jnp
from jax import lax

D = 768
H = 12
HD = 64
FF = 3072
SLOTS = 256
LEN = 1024
SEQS = 8
N_CTX = 4


def draw_tokens(key, part):
    values = jax.random.truncated_normal(key, -4.0, 4.0, (SEQS, LEN, D), jnp.float32)
    return values.astype(jnp.bfloat16)


def draw_lengths(key, part):
    values = jax.random.randint(key, (SEQS,), LEN // 4, LEN + 1, dtype=jnp.int32)
    values = values.at[0].set(LEN)
    return values.at[1].set(LEN // 4)


def steps_of(stream_key, dims, pieces, least, high):
    level, own = 1.0, jax.random.fold_in(stream_key, 6)
    for position, blocks in pieces:
        heights = jnp.exp(jax.random.uniform(jax.random.fold_in(own, position), (blocks,), jnp.float32, least / len(pieces), high / len(pieces)))
        level = level * jnp.repeat(heights, dims[position] // blocks).reshape([-1 if axis == position else 1 for axis in range(len(dims))])
    return level


def noise(rng, extent, scale, bound, pieces=(), held_as=jnp.bfloat16):
    values = scale * jax.random.normal(rng, extent, jnp.float32)
    if pieces:
        values = values * steps_of(rng, extent, pieces, -0.22, 0.18)
    return jnp.clip(values, -bound, bound).astype(held_as)


def setup_inputs(seed: int = 0) -> dict:
    key_of = jax.random.split(jax.random.key(seed), 10)
    tokens = draw_tokens(jax.random.fold_in(key_of[9], 71), 0)
    lengths = draw_lengths(jax.random.fold_in(key_of[9], 71), 0)
    w_qkv = noise(key_of[2], (D, 3, D), D ** -0.5, 0.21875, ((0, 16), (2, 2)), jnp.float32)
    b_qv = noise(key_of[3], (2, D), 0.5, 3.0, ((1, 2),), jnp.float32)
    w_out = noise(key_of[4], (D, D), (D // 8) ** -0.5, 0.625, ((0, 2), (1, 16)), jnp.float32)
    w_gu = noise(key_of[5], (D, 2, FF), D ** -0.5, 0.21875, ((0, 16), (2, 2)), jnp.float32)
    w_down = noise(key_of[6], (FF, D), FF ** -0.5, 0.109375, ((0, 2), (1, 16)), jnp.float32)
    vectors = jnp.clip(1.0 + 0.15 * jax.random.normal(key_of[7], (6, D), jnp.float32), 0.25, 1.75)
    cotangent = noise(key_of[8], (SEQS, LEN, D), 1.0, 6.0, ((0, 4), (1, 4)))
    return dict(tokens=tokens, lengths=lengths, w_qkv=w_qkv, b_qv=b_qv, w_out=w_out, w_gu=w_gu, w_down=w_down, vectors=vectors, cotangent=cotangent)


@jax.custom_vjp
def low(v):
    return lax.optimization_barrier(v.astype(jnp.bfloat16)).astype(jnp.float32)

@jax.custom_vjp
def low_back(v):
    return v

def low_keep(v):
    return (low(v), None)

def low_pass(kept, grad):
    return (grad,)

def back_keep(v):
    return (v, None)

def back_low(kept, grad):
    return (low(grad),)
low.defvjp(low_keep, low_pass)
low_back.defvjp(back_keep, back_low)
highest = lax.Precision.HIGHEST
negative = -1e+30
epsilon = 1e-12

def head_slopes():
    power = 2 ** (H.bit_length() - 1)
    heads_index = jnp.arange(H, dtype=jnp.int32)
    early = -8.0 * (heads_index + 1).astype(jnp.float32) / power
    later = -4.0 * (2 * (heads_index - power) + 1).astype(jnp.float32) / power
    return jnp.exp2(jnp.where(heads_index < power, early, later))

def layer_norm(values, gain, shift):
    centred = values - lax.optimization_barrier(jnp.mean(values, axis=-1, keepdims=True))
    spread = lax.optimization_barrier(jnp.mean(centred * centred, axis=-1, keepdims=True))
    return centred * lax.rsqrt(spread + epsilon) * gain + shift

def forward(sequence_in, length, w_qkv, b_qv, w_out, w_gu, w_down, vectors):
    proj_weight = low(w_qkv)
    out_weight = low(w_out)
    glu_weight = low(w_gu)
    down_weight = low(w_down)
    projected = jnp.einsum('td,dcm->tcm', sequence_in, proj_weight, precision=highest)
    queries = low_back(low(projected[:, 0] + b_qv[0])).reshape(LEN, H, HD)
    keys_all = low_back(low(projected[:, 1])).reshape(LEN, H, HD)
    values_all = low_back(low(projected[:, 2] + b_qv[1])).reshape(LEN, H, HD)
    slot_ids = jnp.arange(LEN, dtype=jnp.int32)
    places = slot_ids % SLOTS * N_CTX + slot_ids // SLOTS
    live_slots = places < length
    live_float = live_slots.astype(jnp.float32)
    slopes = head_slopes()
    block_rows = min(512, LEN)

    def attend(block_item):
        query_block, query_place, query_live = block_item
        scores = jnp.einsum('qhe,khe->hqk', query_block, keys_all, precision=highest) * 0.125
        distance = jnp.abs(query_place[:, None] - places[None, :]).astype(jnp.float32)
        scores = low_back(scores - slopes[:, None, None] * distance[None])
        scores = jnp.where(live_slots[None, None, :], scores, negative)
        expo = jnp.exp(scores)
        totals = lax.optimization_barrier(jnp.sum(expo, axis=-1)) + (1.0 - query_live)[None, :]
        weighted = low_back(jnp.einsum('hqk,khe->qhe', low(expo), values_all, precision=highest))
        return weighted / jnp.transpose(totals)[:, :, None]
    blocks_count = LEN // block_rows
    heads_out = lax.map(jax.checkpoint(attend), (queries.reshape(blocks_count, block_rows, H, HD), places.reshape(blocks_count, block_rows), live_float.reshape(blocks_count, block_rows)))
    mixed = low_back(low(heads_out.reshape(LEN, D)))
    attn = low_back(jnp.dot(mixed, out_weight, precision=highest) + vectors[4])
    hidden = layer_norm(sequence_in + attn, vectors[0], vectors[1])
    gated = jnp.einsum('td,dcf->tcf', low(hidden), glu_weight, precision=highest)
    gate_input = low_back(gated[:, 0])
    upper = low_back(gated[:, 1])
    activated = low(jax.nn.gelu(gate_input, approximate=False) * upper)
    ffn = low_back(jnp.dot(activated, down_weight, precision=highest) + vectors[5])
    return layer_norm(hidden + ffn, vectors[2], vectors[3]) * live_float[:, None]

def reference(tokens, lengths, w_qkv, b_qv, w_out, w_gu, w_down, vectors, cotangent):
    params = (w_qkv, b_qv, w_out, w_gu, w_down, vectors)

    def per_sequence(totals, seq_item):
        sequence_in, grad_in, length = seq_item

        def run_layer(tokens_in, first, second, third, fourth, fifth, sixth):
            return forward(tokens_in, length, first, second, third, fourth, fifth, sixth)
        result, pull = jax.vjp(run_layer, sequence_in, w_qkv, b_qv, w_out, w_gu, w_down, vectors)
        grads = pull(grad_in)
        totals = jax.tree.map(jnp.add, totals, tuple(grads[1:]))
        return (totals, (result.astype(jnp.bfloat16), grads[0]))
    start_totals = tuple((jnp.zeros_like(param) for param in params))
    totals, (output, input_grad) = lax.scan(per_sequence, start_totals, (tokens.astype(jnp.float32), cotangent.astype(jnp.float32), lengths))
    return (output, input_grad, totals[0], totals[1], totals[2], totals[3], totals[4], totals[5])
```

```python
import functools
import math

import jax
import jax.numpy as jnp
import numpy as np
from jax import lax
from jax.experimental import pallas as pl
from jax.experimental.pallas import tpu as pltpu
from jax.sharding import PartitionSpec as P

H = 12
HD = 64
LOG2E = math.log2(math.e)
FAR = 1e30
TILE = 64
BLOCK = 384

epsilon = 1e-12
f32 = jnp.float32
bf16 = jnp.bfloat16
VMEM = pl.BlockSpec(memory_space=pltpu.VMEM)
SMEM = pl.BlockSpec(memory_space=pltpu.SMEM)


def slope_table():
    power = 2 ** (H.bit_length() - 1)
    heads = np.arange(H)
    early = -8.0 * (heads + 1) / power
    later = -4.0 * (2 * (heads - power) + 1) / power
    return np.exp2(np.where(heads < power, early, later)).astype(np.float32)


def dot_nn(a, b):
    return jnp.dot(a, b, preferred_element_type=f32)


def dot_nt(a, b):
    return lax.dot_general(a, b, (((1,), (1,)), ((), ())), preferred_element_type=f32)


def params(*semantics):
    return pltpu.CompilerParams(
        dimension_semantics=semantics or None, vmem_limit_bytes=56 * 1024 * 1024
    )


def cost(flops, nbytes, exps=0):
    return pl.CostEstimate(flops=int(flops), bytes_accessed=int(nbytes), transcendentals=int(exps))


def shape(dims, dtype):
    return jax.ShapeDtypeStruct(dims, dtype)


def xor_pairs(axis, distance):
    return [(i, i ^ distance) for i in range(lax.axis_size(axis))]


def swap(value, axis, distance):
    return lax.ppermute(value, axis, xor_pairs(axis, distance))


def live_mask(lens, rank, n_ctx, seqs, slots):
    slot = lax.broadcasted_iota(jnp.int32, (slots, 1), 0)
    place = slot * n_ctx + rank
    return jnp.concatenate(
        [jnp.where(place < lens[s], 1.0, 0.0).astype(f32) for s in range(seqs)], axis=0
    )


def normalise(z):
    centred = z - jnp.mean(z, axis=-1, keepdims=True)
    spread = jnp.mean(centred * centred, axis=-1, keepdims=True)
    scale = lax.rsqrt(spread + epsilon)
    return centred * scale, scale


def normalise_back(grad_hat, hat, scale):
    inner = jnp.mean(grad_hat * hat, axis=-1, keepdims=True)
    return scale * (grad_hat - jnp.mean(grad_hat, axis=-1, keepdims=True) - hat * inner)


def project_kernel(n, seqs, heads, ids, tok, bias, *refs):
    pieces = refs[: 4 * n]
    sends = refs[4 * n : 5 * n]
    whole = refs[5 * n]
    stage = refs[5 * n + 1]
    y, c, z = ids[0], ids[1], ids[2]
    rows = pieces[0].shape[0]
    for k in range(4 * n):
        ky, kc, kz = k // (2 * n), k // n % 2, k % n
        index = ((y ^ ky) * 2 + (c ^ kc)) * n + (z ^ kz)
        whole[pl.ds(pl.multiple_of(index * rows, rows), rows), :] = pieces[k][...]
    slots = sends[0].shape[1]
    width = heads * HD
    per = seqs * heads // n
    for s in range(seqs):
        acc = dot_nn(tok[s * slots : (s + 1) * slots, :], whole[...]) + bias[...]
        turned = acc.astype(bf16).T
        for h in range(heads):
            i = s * heads + h
            at = ((i % n) * per + i // n) * 3
            for part in range(3):
                first = part * width + h * HD
                stage[(at + part) * HD : (at + part + 1) * HD, :] = turned[first : first + HD, :]
    size = per * 3 * HD
    for d in range(n):
        sends[d][...] = stage[pl.ds(pl.multiple_of((z ^ d) * size, size), size), :]


def project(ids, tok, bias, pieces, n, seqs, heads):
    slots = tok.shape[0] // seqs
    size = seqs * heads // n * 3 * HD
    model, wide = tok.shape[1], bias.shape[1]
    return pl.pallas_call(
        functools.partial(project_kernel, n, seqs, heads),
        out_shape=[shape((size, slots), bf16)] * n + [shape((model, wide), bf16)],
        in_specs=[SMEM] + [VMEM] * (2 + len(pieces)),
        out_specs=[VMEM] * (n + 1),
        scratch_shapes=[pltpu.VMEM((size * n, slots), bf16)],
        compiler_params=params(),
        cost_estimate=cost(2 * tok.shape[0] * model * wide, 6e6),
        name="project",
    )(ids, tok, bias, *pieces)


def pair_scalars(n, heads, ids, lens, slopes):
    j = pl.program_id(0)
    z, t = ids[2], ids[3]
    i = z + n * j
    s = i // heads
    h = i - s * heads
    return z, lens[s], slopes[t * heads + h] * LOG2E


def query_place(n, slots, z, d):
    lane = lax.broadcasted_iota(jnp.int32, (1, slots), 1)
    return lane * n + (z ^ d)


def key_place(n, z, tile, length, slope):
    row = lax.broadcasted_iota(jnp.int32, (TILE, 1), 0)
    places = []
    for d in range(n):
        place = (tile * TILE + row) * n + (z ^ d)
        places.append(jnp.where(place < length, place.astype(f32) * slope, FAR))
    return jnp.concatenate(places, axis=0)


def gather_rows(ref, tile, n):
    rows = pl.ds(pl.multiple_of(tile * TILE, TILE), TILE)
    return jnp.concatenate([ref[d, rows, :] for d in range(n)], axis=0)


def attend_kernel(n, heads, ids, lens, slopes, *refs):
    inputs = refs[:n]
    outs = refs[n : 2 * n]
    att_ref, den_ref = refs[2 * n], refs[2 * n + 1]
    k_s, v_s, acc, den = refs[2 * n + 2 :]
    slots = inputs[0].shape[1]
    z, length, slope = pair_scalars(n, heads, ids, lens, slopes)
    for d in range(n):
        k_s[d] = inputs[d][HD : 2 * HD, :].T
        v_s[d] = inputs[d][2 * HD : 3 * HD, :].T
    acc[...] = jnp.zeros_like(acc)
    den[...] = jnp.zeros_like(den)

    def tile_step(tile, unused):
        keys = gather_rows(k_s, tile, n)
        values = gather_rows(v_s, tile, n).T
        places = key_place(n, z, tile, length, slope)
        for d in range(n):
            cols = slice(d * slots, (d + 1) * slots)
            there = query_place(n, slots, z, d).astype(f32) * slope
            scores = dot_nn(keys, inputs[d][0:HD, :]) * (0.125 * LOG2E)
            e = jnp.exp2(scores - jnp.abs(there - places))
            den[:, cols] += jnp.sum(e, axis=0, keepdims=True)
            acc[:, cols] += dot_nn(values, e.astype(bf16))
        return unused

    step = TILE * n
    lax.fori_loop(0, (length + step - 1) // step, tile_step, 0)
    for d in range(n):
        cols = slice(d * slots, (d + 1) * slots)
        padded = jnp.where(query_place(n, slots, z, d) < length, 0.0, 1.0)
        total = den[:, cols] + padded
        att = acc[:, cols] / total
        att_ref[:, cols] = att
        den_ref[0, :, cols] = total
        outs[d][...] = att.astype(bf16)


def attend(ids, lens, slopes, blocks, n, heads, per):
    slots = blocks[0].shape[1]
    every = n * slots
    return pl.pallas_call(
        functools.partial(attend_kernel, n, heads),
        grid=(per,),
        out_shape=[shape((per * HD, slots), bf16)] * n
        + [shape((per * HD, every), f32), shape((per, 1, every), f32)],
        in_specs=[SMEM] * 3 + [pl.BlockSpec((3 * HD, slots), lambda j: (j, 0))] * n,
        out_specs=[pl.BlockSpec((HD, slots), lambda j: (j, 0))] * n
        + [
            pl.BlockSpec((HD, every), lambda j: (j, 0)),
            pl.BlockSpec((1, 1, every), lambda j: (j, 0, 0)),
        ],
        scratch_shapes=[
            pltpu.VMEM((n, slots, HD), bf16),
            pltpu.VMEM((n, slots, HD), bf16),
            pltpu.VMEM((HD, every), f32),
            pltpu.VMEM((1, every), f32),
        ],
        compiler_params=params("arbitrary"),
        cost_estimate=cost(per * every * every * HD * 8, 3e6, per * every * every),
        name="attend",
    )(ids, lens, slopes, *blocks)


def attend_back_kernel(n, heads, ids, lens, slopes, *refs):
    inputs = refs[:n]
    grads = refs[n : 2 * n]
    att_ref, den_ref = refs[2 * n], refs[2 * n + 1]
    outs = refs[2 * n + 2 : 3 * n + 2]
    k_s, v_s, q_s, g_s, dn, cor, dq, dk, dv = refs[3 * n + 2 :]
    slots = inputs[0].shape[1]
    z, length, slope = pair_scalars(n, heads, ids, lens, slopes)
    for d in range(n):
        cols = slice(d * slots, (d + 1) * slots)
        k_s[d] = inputs[d][HD : 2 * HD, :].T
        v_s[d] = inputs[d][2 * HD : 3 * HD, :].T
        q_s[d] = inputs[d][0:HD, :].T
        inverse = 1.0 / den_ref[0, :, cols]
        mixed = grads[d][...].astype(f32)
        numer = (mixed * inverse).astype(bf16)
        dn[:, cols] = numer
        g_s[d] = numer.T
        cor[:, cols] = jnp.sum(mixed * att_ref[:, cols], axis=0, keepdims=True) * inverse
    dq[...] = jnp.zeros_like(dq)
    dk[...] = jnp.zeros_like(dk)
    dv[...] = jnp.zeros_like(dv)

    def tile_step(tile, unused):
        keys = gather_rows(k_s, tile, n)
        values = gather_rows(v_s, tile, n)
        keys_t = keys.T
        places = key_place(n, z, tile, length, slope)
        grad_k = jnp.zeros((n * TILE, HD), f32)
        grad_v = jnp.zeros((n * TILE, HD), f32)
        for d in range(n):
            cols = slice(d * slots, (d + 1) * slots)
            there = query_place(n, slots, z, d).astype(f32) * slope
            scores = dot_nn(keys, inputs[d][0:HD, :]) * (0.125 * LOG2E)
            e = jnp.exp2(scores - jnp.abs(there - places))
            inner = dot_nn(values, dn[:, cols])
            ds = (e * (inner - cor[:, cols])).astype(bf16)
            dq[:, cols] += dot_nn(keys_t, ds)
            grad_k += dot_nn(ds, q_s[d])
            grad_v += dot_nn(e.astype(bf16), g_s[d])
        rows = pl.ds(pl.multiple_of(tile * TILE, TILE), TILE)
        for d in range(n):
            dk[d, rows, :] = grad_k[d * TILE : (d + 1) * TILE, :]
            dv[d, rows, :] = grad_v[d * TILE : (d + 1) * TILE, :]
        return unused

    step = TILE * n
    lax.fori_loop(0, (length + step - 1) // step, tile_step, 0)
    for d in range(n):
        cols = slice(d * slots, (d + 1) * slots)
        outs[d][0:HD, :] = (dq[:, cols] * 0.125).astype(bf16)
        outs[d][HD : 2 * HD, :] = (dk[d] * 0.125).astype(bf16).T
        outs[d][2 * HD : 3 * HD, :] = dv[d].astype(bf16).T


def attend_back(ids, lens, slopes, blocks, grads, att, den, n, heads, per):
    slots = blocks[0].shape[1]
    every = n * slots
    rows = [pltpu.VMEM((n, slots, HD), bf16)] * 4
    return pl.pallas_call(
        functools.partial(attend_back_kernel, n, heads),
        grid=(per,),
        out_shape=[shape((per * 3 * HD, slots), bf16)] * n,
        in_specs=[SMEM] * 3
        + [pl.BlockSpec((3 * HD, slots), lambda j: (j, 0))] * n
        + [pl.BlockSpec((HD, slots), lambda j: (j, 0))] * n
        + [
            pl.BlockSpec((HD, every), lambda j: (j, 0)),
            pl.BlockSpec((1, 1, every), lambda j: (j, 0, 0)),
        ],
        out_specs=[pl.BlockSpec((3 * HD, slots), lambda j: (j, 0))] * n,
        scratch_shapes=rows
        + [
            pltpu.VMEM((HD, every), bf16),
            pltpu.VMEM((1, every), f32),
            pltpu.VMEM((HD, every), f32),
            pltpu.VMEM((n, slots, HD), f32),
            pltpu.VMEM((n, slots, HD), f32),
        ],
        compiler_params=params("arbitrary"),
        cost_estimate=cost(per * every * every * HD * 20, 5e6, per * every * every),
        name="attend_back",
    )(ids, lens, slopes, *blocks, *grads, att, den)


def mix_kernel(n, seqs, heads, ids, wo, *refs):
    inputs = refs[:n]
    part, mixed, stage = refs[n], refs[n + 1], refs[n + 2]
    z = ids[2]
    slots = inputs[0].shape[1]
    per = seqs * heads // n
    size = per * HD
    for d in range(n):
        stage[pl.ds(pl.multiple_of((z ^ d) * size, size), size), :] = inputs[d][...]
    for s in range(seqs):
        columns = []
        for h in range(heads):
            i = s * heads + h
            at = (i % n) * per + i // n
            columns.append(stage[at * HD : (at + 1) * HD, :])
        rows = slice(s * slots, (s + 1) * slots)
        ours = jnp.concatenate(columns, axis=0).T
        mixed[rows, :] = ours
        part[rows, :] = dot_nt(ours, wo[...]).astype(bf16)


def mix(ids, packed, blocks, n, seqs, heads):
    slots = blocks[0].shape[1]
    model = packed.shape[0]
    width = heads * HD
    tokens = seqs * slots
    return pl.pallas_call(
        functools.partial(mix_kernel, n, seqs, heads),
        grid=(1,),
        out_shape=[shape((tokens, model), bf16), shape((tokens, width), bf16)],
        in_specs=[SMEM, pl.BlockSpec((model, width), lambda i: (0, 0))] + [VMEM] * n,
        out_specs=[VMEM] * 2,
        scratch_shapes=[pltpu.VMEM((seqs * heads * HD, slots), bf16)],
        compiler_params=params("arbitrary"),
        cost_estimate=cost(2 * tokens * model * width, 3e6),
        name="mix",
    )(ids, packed, *blocks)


def unit_kernel(tok, own, other, vec, wg, wu, wd, hidden, low, act, gel, slope, part, acc):
    j = pl.program_id(0)

    @pl.when(j == 0)
    def _():
        branch = own[...].astype(f32) + other[...].astype(f32) + vec[4:5, :]
        hat, _ = normalise(tok[...].astype(f32) + branch)
        h = hat * vec[0:1, :] + vec[1:2, :]
        hidden[...] = h
        low[...] = h.astype(bf16)
        acc[...] = jnp.zeros_like(acc)

    gate = dot_nn(low[...], wg[...])
    upper = dot_nn(low[...], wu[...])
    phi = 0.5 * (1.0 + lax.erf(gate * math.sqrt(0.5)))
    density = jnp.exp(gate * gate * -0.5) * (1.0 / math.sqrt(2.0 * math.pi))
    unit = gate * phi
    acted = (unit * upper).astype(bf16)
    act[...] = acted
    gel[...] = unit.astype(bf16)
    slope[...] = (upper * (phi + gate * density)).astype(bf16)
    acc[...] += dot_nt(acted, wd[...])

    @pl.when(j == pl.num_programs(0) - 1)
    def _():
        part[...] = acc[...].astype(bf16)


def unit(tok, own, other, vec, packed, width, hidden_units):
    tokens, model = tok.shape
    steps = hidden_units // BLOCK
    first = width // BLOCK
    fixed = lambda j: (0, 0)
    moving = lambda j: (0, j)
    whole = pl.BlockSpec((tokens, model), fixed)
    weight = lambda start: pl.BlockSpec((model, BLOCK), lambda j: (0, start + j))
    inner = pl.BlockSpec((tokens, BLOCK), moving)
    return pl.pallas_call(
        unit_kernel,
        grid=(steps,),
        out_shape=[shape((tokens, model), f32), shape((tokens, model), bf16)]
        + [shape((tokens, hidden_units), bf16)] * 3
        + [shape((tokens, model), bf16)],
        in_specs=[
            whole,
            whole,
            whole,
            pl.BlockSpec(vec.shape, fixed),
            weight(first),
            weight(first + steps),
            weight(first + 2 * steps),
        ],
        out_specs=[whole, whole, inner, inner, inner, whole],
        scratch_shapes=[pltpu.VMEM((tokens, model), f32)],
        compiler_params=params("arbitrary"),
        cost_estimate=cost(6 * tokens * model * hidden_units, 20e6, 2 * tokens * hidden_units),
        name="unit",
    )(tok, own, other, vec, packed, packed, packed)


def unit_back_kernel(
    n, seqs, ids, lens, hidden, own, other, cot, vec, wg, wu, wd, gel, slope,
    output, dz2, dffn, dgate, dup, part, sums, acc,
):
    j = pl.program_id(0)

    @pl.when(j == 0)
    def _():
        live = live_mask(lens, ids[2], n, seqs, hidden.shape[0] // seqs)
        branch = own[...].astype(f32) + other[...].astype(f32) + vec[5:6, :]
        hat, scale = normalise(hidden[...] + branch)
        output[...] = (live * (hat * vec[2:3, :] + vec[3:4, :])).astype(bf16)
        gy = cot[...].astype(f32) * live
        grad = normalise_back(gy * vec[2:3, :], hat, scale)
        dz2[...] = grad
        low = grad.astype(bf16)
        dffn[...] = low
        sums[0:1, :] = jnp.sum(gy * hat, axis=0, keepdims=True)
        sums[1:2, :] = jnp.sum(gy, axis=0, keepdims=True)
        sums[2:3, :] = jnp.sum(low.astype(f32), axis=0, keepdims=True)
        sums[3:8, :] = jnp.zeros_like(sums[3:8, :])
        acc[...] = jnp.zeros_like(acc)

    dact = dot_nn(dffn[...], wd[...])
    upper = (dact * gel[...].astype(f32)).astype(bf16)
    gate = (dact * slope[...].astype(f32)).astype(bf16)
    dgate[...] = gate
    dup[...] = upper
    acc[...] += dot_nt(gate, wg[...]) + dot_nt(upper, wu[...])

    @pl.when(j == pl.num_programs(0) - 1)
    def _():
        part[...] = acc[...].astype(bf16)


def unit_back(ids, lens, hidden, own, other, cot, vec, packed, gel, slope, n, seqs, width):
    tokens, model = hidden.shape
    hidden_units = gel.shape[1]
    steps = hidden_units // BLOCK
    first = width // BLOCK
    fixed = lambda j: (0, 0)
    whole = pl.BlockSpec((tokens, model), fixed)
    weight = lambda start: pl.BlockSpec((model, BLOCK), lambda j: (0, start + j))
    inner = pl.BlockSpec((tokens, BLOCK), lambda j: (0, j))
    return pl.pallas_call(
        functools.partial(unit_back_kernel, n, seqs),
        grid=(steps,),
        out_shape=[
            shape((tokens, model), bf16),
            shape((tokens, model), f32),
            shape((tokens, model), bf16),
            shape((tokens, hidden_units), bf16),
            shape((tokens, hidden_units), bf16),
            shape((tokens, model), bf16),
            shape((8, model), f32),
        ],
        in_specs=[SMEM, SMEM, whole, whole, whole, whole, pl.BlockSpec(vec.shape, fixed)]
        + [weight(first), weight(first + steps), weight(first + 2 * steps), inner, inner],
        out_specs=[whole, whole, whole, inner, inner, whole, pl.BlockSpec((8, model), fixed)],
        scratch_shapes=[pltpu.VMEM((tokens, model), f32)],
        compiler_params=params("arbitrary"),
        cost_estimate=cost(6 * tokens * model * hidden_units, 22e6),
        name="unit_back",
    )(ids, lens, hidden, own, other, cot, vec, packed, packed, packed, gel, slope)


def row_starts(ids, quarter):
    y, c = ids[0], ids[1]
    keep = [(y * 2 + c) * quarter, ((1 - y) * 2 + c) * quarter]
    send = [(y * 2 + 1 - c) * quarter, ((1 - y) * 2 + 1 - c) * quarter]
    return send, keep


def write_rows(ids, turned, right, send, keep):
    quarter = turned.shape[0] // 4
    for ref, starts in zip((send, keep), row_starts(ids, quarter)):
        for k in range(2):
            left = turned[pl.ds(pl.multiple_of(starts[k], quarter), quarter), :]
            ref[k * quarter : (k + 1) * quarter, :] = dot_nn(left, right).astype(bf16)


def weight_kernel(steps, ids, low, dffn, dgate, dup, act, send, keep, left):
    j = pl.program_id(0)

    @pl.when(j == 0)
    def _():
        left[0] = low[...].T
        left[1] = dffn[...].T

    @pl.when(j < steps)
    def _():
        write_rows(ids, left.at[0], dgate[...], send, keep)

    @pl.when((j >= steps) & (j < 2 * steps))
    def _():
        write_rows(ids, left.at[0], dup[...], send, keep)

    @pl.when(j >= 2 * steps)
    def _():
        write_rows(ids, left.at[1], act[...], send, keep)


def weight_grads(ids, low, dffn, dgate, dup, act):
    tokens, model = low.shape
    hidden_units = act.shape[1]
    steps = hidden_units // BLOCK
    fixed = lambda j: (0, 0)
    whole = pl.BlockSpec((tokens, model), fixed)
    column = lambda start: pl.BlockSpec(
        (tokens, BLOCK), lambda j: (0, jnp.clip(j - start, 0, steps - 1))
    )
    out = pl.BlockSpec((model // 2, BLOCK), lambda j: (0, j))
    return pl.pallas_call(
        functools.partial(weight_kernel, steps),
        grid=(3 * steps,),
        out_shape=[shape((model // 2, 3 * hidden_units), bf16)] * 2,
        in_specs=[SMEM, whole, whole, column(0), column(steps), column(2 * steps)],
        out_specs=[out, out],
        scratch_shapes=[pltpu.VMEM((2, model, tokens), bf16)],
        compiler_params=params("arbitrary"),
        cost_estimate=cost(6 * tokens * model * hidden_units, 14e6),
        name="weight_grads",
    )(ids, low, dffn, dgate, dup, act)


def mix_back_kernel(
    n, seqs, heads, ids, tok, own, other, dz2, hown, hother, vec, wo, mixed, *refs
):
    sends = refs[:n]
    dz1, send, keep, sums = refs[n : n + 4]
    stage, left = refs[n + 4 :]
    z = ids[2]
    slots = sends[0].shape[1]
    per = seqs * heads // n
    branch = own[...].astype(f32) + other[...].astype(f32) + vec[4:5, :]
    hat, scale = normalise(tok[...].astype(f32) + branch)
    gh = dz2[...] + (hown[...].astype(f32) + hother[...].astype(f32))
    grad = normalise_back(gh * vec[0:1, :], hat, scale)
    dz1[...] = grad
    low = grad.astype(bf16)
    sums[0:1, :] = jnp.sum(gh * hat, axis=0, keepdims=True)
    sums[1:2, :] = jnp.sum(gh, axis=0, keepdims=True)
    sums[2:3, :] = jnp.sum(low.astype(f32), axis=0, keepdims=True)
    sums[3:8, :] = jnp.zeros_like(sums[3:8, :])
    for s in range(seqs):
        turned = dot_nn(low[s * slots : (s + 1) * slots, :], wo[...]).astype(bf16).T
        for h in range(heads):
            i = s * heads + h
            at = (i % n) * per + i // n
            stage[at * HD : (at + 1) * HD, :] = turned[h * HD : (h + 1) * HD, :]
    size = per * HD
    for d in range(n):
        sends[d][...] = stage[pl.ds(pl.multiple_of((z ^ d) * size, size), size), :]
    left[...] = low.T
    write_rows(ids, left, mixed[...], send, keep)


def mix_back(ids, tok, own, other, dz2, hown, hother, vec, packed, mixed, n, seqs, heads):
    tokens, model = tok.shape
    slots = tokens // seqs
    width = heads * HD
    size = seqs * heads // n * HD
    return pl.pallas_call(
        functools.partial(mix_back_kernel, n, seqs, heads),
        grid=(1,),
        out_shape=[shape((size, slots), bf16)] * n
        + [shape((tokens, model), f32)]
        + [shape((model // 2, width), bf16)] * 2
        + [shape((8, model), f32)],
        in_specs=[SMEM]
        + [VMEM] * 7
        + [pl.BlockSpec((model, width), lambda i: (0, 0)), VMEM],
        out_specs=[VMEM] * (n + 4),
        scratch_shapes=[
            pltpu.VMEM((size * n, slots), bf16),
            pltpu.VMEM((model, tokens), bf16),
        ],
        compiler_params=params("arbitrary"),
        cost_estimate=cost(4 * tokens * model * width, 10e6),
        name="mix_back",
    )(ids, tok, own, other, dz2, hown, hother, vec, packed, mixed)


def project_back_kernel(n, seqs, heads, ids, tok, whole, *refs):
    inputs = refs[:n]
    part, send, keep, sums = refs[n : n + 4]
    stage, right, left = refs[n + 4 :]
    z = ids[2]
    slots = inputs[0].shape[1]
    per = seqs * heads // n
    width = heads * HD
    size = per * 3 * HD
    for d in range(n):
        stage[pl.ds(pl.multiple_of((z ^ d) * size, size), size), :] = inputs[d][...]
    for s in range(seqs):
        for c in range(3):
            columns = []
            for h in range(heads):
                i = s * heads + h
                at = ((i % n) * per + i // n) * 3 + c
                columns.append(stage[at * HD : (at + 1) * HD, :])
            ours = jnp.concatenate(columns, axis=0).T
            right[s * slots : (s + 1) * slots, c * width : (c + 1) * width] = ours
    part[...] = dot_nt(right[...], whole[...]).astype(bf16)
    left[...] = tok[...].T
    for c in range(3):
        cols = slice(c * width, (c + 1) * width)
        write_rows(ids, left, right[:, cols], send.at[:, cols], keep.at[:, cols])
    ones = jnp.ones((8, right.shape[0]), bf16)
    sums[...] = dot_nn(ones, right[...])


def project_back(ids, tok, whole, blocks, n, seqs, heads):
    tokens, model = tok.shape
    slots = tokens // seqs
    wide = whole.shape[1]
    return pl.pallas_call(
        functools.partial(project_back_kernel, n, seqs, heads),
        out_shape=[
            shape((tokens, model), bf16),
            shape((model // 2, wide), bf16),
            shape((model // 2, wide), bf16),
            shape((8, wide), f32),
        ],
        in_specs=[SMEM] + [VMEM] * (2 + n),
        out_specs=[VMEM] * 4,
        scratch_shapes=[
            pltpu.VMEM((seqs * heads * 3 * HD, slots), bf16),
            pltpu.VMEM((tokens, wide), bf16),
            pltpu.VMEM((model, tokens), bf16),
        ],
        compiler_params=params(),
        cost_estimate=cost(4 * tokens * model * wide, 8e6),
        name="project_back",
    )(ids, tok, whole, *blocks)


def own_rows(send, keep, n):
    half = keep.shape[0] // 2
    pair = keep.astype(f32) + swap(send, "shard", 1).astype(f32)
    mine = pair[:half] + swap(pair[half:].astype(bf16), "shard", 2).astype(f32)
    blocks = mine.reshape(n, half // n, mine.shape[1])
    rank = lax.axis_index("ctx")
    total = lax.dynamic_index_in_dim(blocks, rank, 0, keepdims=False)
    for d in range(1, n):
        block = lax.dynamic_index_in_dim(blocks, rank ^ d, 0, keepdims=False)
        total = total + swap(block.astype(bf16), "ctx", d).astype(f32)
    return total


def everywhere_sum(value, n):
    distance = 1
    while distance < n:
        value = value + swap(value, "ctx", distance)
        distance *= 2
    value = value + swap(value, "shard", 2)
    return value + swap(value, "shard", 1)


def fits(tokens, b_qv, w_qkv, w_gu):
    n = lax.axis_size("ctx")
    heads = b_qv.shape[1] // HD
    return (
        n == 4
        and lax.axis_size("shard") == 4
        and lax.axis_size("tp") == 2
        and (tokens.shape[0] * heads) % n == 0
        and w_qkv.shape[0] % 16 == 0
        and tokens.shape[1] % 256 == 0
        and b_qv.shape[1] == BLOCK
        and w_gu.shape[2] % BLOCK == 0
    )


def on_device(tokens, lengths, w_qkv, b_qv, w_out, w_gu, w_down, vectors, cotangent):
    if not fits(tokens, b_qv, w_qkv, w_gu):
        return by_gather(tokens, lengths, w_qkv, b_qv, w_out, w_gu, w_down, vectors, cotangent)
    n = lax.axis_size("ctx")
    seqs, slots, model = tokens.shape
    width = b_qv.shape[1]
    heads = width // HD
    per = seqs * heads // n
    units = w_gu.shape[2]
    rows = w_qkv.shape[0]
    count = seqs * slots
    shard = lax.axis_index("shard")
    ids = jnp.stack(
        [shard // 2, shard % 2, lax.axis_index("ctx"), lax.axis_index("tp")]
    ).astype(jnp.int32)
    slopes = jnp.asarray(slope_table())
    tok = tokens.reshape(count, model)
    cot = cotangent.reshape(count, model)

    first = [w_qkv.astype(bf16).reshape(rows, 3 * width)]
    first += [swap(first[0], "ctx", d) for d in range(1, n)]
    first += [swap(piece, "shard", 2) for piece in first]
    by_core = [swap(piece, "shard", 1) for piece in first]
    pieces = first[:n] + by_core[:n] + first[n:] + by_core[n:]
    packed = jnp.concatenate(
        [w_out.T, w_gu.reshape(rows, 2 * units), w_down.T], axis=1
    ).astype(bf16)
    packed, pieces[0] = lax.optimization_barrier((packed, pieces[0]))
    packed = lax.all_gather(packed, ("shard", "ctx"), axis=0, tiled=True)

    bias = jnp.concatenate([b_qv[0], jnp.zeros_like(b_qv[0]), b_qv[1]])[None, :]
    *sends, whole = project(ids, tok, bias, pieces, n, seqs, heads)
    blocks = [sends[0]] + [swap(sends[d], "ctx", d) for d in range(1, n)]
    *outs, att, den = attend(ids, lengths, slopes, blocks, n, heads, per)
    outs = [outs[0]] + [swap(outs[d], "ctx", d) for d in range(1, n)]
    part, mixed = mix(ids, packed, outs, n, seqs, heads)
    part_other = swap(part, "tp", 1)
    hidden, low, act, gel, slope, ffn = unit(tok, part, part_other, vectors, packed, width, units)
    ffn_other = swap(ffn, "tp", 1)
    output, dz2, dffn, dgate, dup, back, sums_two = unit_back(
        ids, lengths, hidden, ffn, ffn_other, cot, vectors, packed, gel, slope, n, seqs, width
    )
    back_other = swap(back, "tp", 1)
    unit_send, unit_keep = weight_grads(ids, low, dffn, dgate, dup, act)
    *sends, dz1, out_send, out_keep, sums_one = mix_back(
        ids, tok, part, part_other, dz2, back, back_other, vectors, packed, mixed, n, seqs, heads
    )
    grads = [sends[0]] + [swap(sends[d], "ctx", d) for d in range(1, n)]
    outs = attend_back(ids, lengths, slopes, blocks, grads, att, den, n, heads, per)
    outs = [outs[0]] + [swap(outs[d], "ctx", d) for d in range(1, n)]
    dx, qkv_send, qkv_keep, sums_bias = project_back(ids, tok, whole, outs, n, seqs, heads)
    input_grad = dz1 + (dx.astype(f32) + swap(dx, "tp", 1).astype(f32))

    grad_unit = own_rows(unit_send, unit_keep, n)
    grad_out = own_rows(out_send, out_keep, n)
    grad_qkv = own_rows(qkv_send, qkv_keep, n)
    bias_row = jnp.concatenate([sums_bias[0:1, :width], sums_bias[0:1, 2 * width :]], axis=1)
    small = jnp.concatenate(
        [sums_one[0:2], sums_two[0:2], sums_one[2:3], sums_two[2:3], bias_row, jnp.zeros_like(bias_row)]
    )
    small = everywhere_sum(small, n)
    return (
        output.reshape(tokens.shape),
        input_grad.reshape(tokens.shape),
        grad_qkv.reshape(w_qkv.shape),
        small[6].reshape(2, width),
        grad_out.T,
        grad_unit[:, : 2 * units].reshape(w_gu.shape),
        grad_unit[:, 2 * units :].T,
        small[:6],
    )


def alibi_slopes(first_head, head_count):
    power = 2 ** (H.bit_length() - 1)
    heads_index = first_head + jnp.arange(head_count, dtype=jnp.int32)
    early = -8.0 * (heads_index + 1).astype(jnp.float32) / power
    later = -4.0 * (2 * (heads_index - power) + 1).astype(jnp.float32) / power
    return jnp.exp2(jnp.where(heads_index < power, early, later))


def layer_norm(values, gain, shift):
    centred = values - jnp.mean(values, axis=-1, keepdims=True)
    spread = jnp.mean(centred * centred, axis=-1, keepdims=True)
    return centred * lax.rsqrt(spread + epsilon) * gain + shift


def gated_unit(gate_input, upper):
    return jax.nn.gelu(gate_input, approximate=False) * upper


def score_block(query_heads, key_heads, query_place, key_place, slopes, lengths):
    scores = (
        jnp.einsum("sqhe,skhe->shqk", query_heads, key_heads, preferred_element_type=jnp.float32)
        * 0.125
    )
    distance = jnp.abs(query_place[:, None] - key_place[None, :]).astype(jnp.float32)
    scores = scores - slopes[None, :, None, None] * distance[None, None]
    usable = key_place[None, :] < lengths[:, None]
    return jnp.where(usable[:, None, None, :], jnp.exp(scores), 0.0)


def backward_scores(
    query_heads,
    numer_heads,
    correction,
    key_heads,
    value_heads,
    query_place,
    key_place,
    slopes,
    lengths,
):
    weights = score_block(query_heads, key_heads, query_place, key_place, slopes, lengths)
    value_dots = jnp.einsum(
        "sqhe,skhe->shqk", numer_heads, value_heads, preferred_element_type=jnp.float32
    )
    grad_scores = (weights * (value_dots - correction[..., None])).astype(jnp.bfloat16)
    return (weights.astype(jnp.bfloat16), grad_scores)


def split_blocks(shard_piece, slot_count, ctx_count):
    piece_rows = shard_piece.shape[1]
    block_rows = math.gcd(piece_rows, 128)
    block_count = piece_rows // block_rows
    shaped = shard_piece.reshape(
        (shard_piece.shape[0], block_count, block_rows) + shard_piece.shape[2:]
    )
    blocks = jnp.moveaxis(shaped, 1, 0)
    row_ids = jnp.arange(piece_rows, dtype=jnp.int32)
    places = (row_ids % slot_count * ctx_count + row_ids // slot_count).reshape(
        block_count, block_rows
    )
    offsets = block_rows * jnp.arange(block_count, dtype=jnp.int32)
    return (blocks, places, offsets)


def by_gather(tokens, lengths, w_qkv, b_qv, w_out, w_gu, w_down, vectors, cotangent):
    ctx_count = lax.axis_size("ctx")
    ctx_rank = lax.axis_index("ctx")
    seq_count, slot_count, model_width = tokens.shape
    local_width = b_qv.shape[1]
    head_count = local_width // HD
    slopes = alibi_slopes(lax.axis_index("tp") * head_count, head_count)
    slot_ids = jnp.arange(slot_count, dtype=jnp.int32)
    query_place = slot_ids * ctx_count + ctx_rank
    query_live = (query_place[None, :] < lengths[:, None]).astype(jnp.float32)
    live_rows = query_live[:, :, None]
    head_shape = (seq_count, slot_count, head_count, HD)
    whole_qkv, whole_out, whole_gu, whole_down = (
        lax.all_gather(w_qkv.astype(jnp.bfloat16), ("shard", "ctx"), axis=0, tiled=True),
        lax.all_gather(w_out.astype(jnp.bfloat16), ("shard", "ctx"), axis=1, tiled=True),
        lax.all_gather(w_gu.astype(jnp.bfloat16), ("shard", "ctx"), axis=0, tiled=True),
        lax.all_gather(w_down.astype(jnp.bfloat16), ("shard", "ctx"), axis=1, tiled=True),
    )
    inputs = tokens.astype(jnp.float32)
    projected = jnp.einsum("std,dcm->stcm", tokens, whole_qkv, preferred_element_type=jnp.float32)
    query_rows = (projected[:, :, 0] + b_qv[0]).astype(jnp.bfloat16)
    key_rows = projected[:, :, 1].astype(jnp.bfloat16)
    value_rows = (projected[:, :, 2] + b_qv[1]).astype(jnp.bfloat16)
    query_heads = query_rows.reshape(head_shape)
    pairs = jnp.stack([key_rows, value_rows], axis=2)
    start_numer = jnp.zeros((seq_count, head_count, slot_count, HD), jnp.float32)
    start_denom = jnp.zeros((seq_count, head_count, slot_count), jnp.float32)
    blocks, places, offsets = split_blocks(
        lax.all_gather(pairs, "ctx", axis=1, tiled=True), slot_count, ctx_count
    )

    def forward_advance(inner_state, block_item):
        key_block, key_place, row_offset = block_item
        numerator, denominator = inner_state
        key_heads = key_block[:, :, 0].reshape(seq_count, -1, head_count, HD)
        value_heads = key_block[:, :, 1].reshape(seq_count, -1, head_count, HD)
        weights = score_block(query_heads, key_heads, query_place, key_place, slopes, lengths)
        numerator = numerator + jnp.einsum(
            "shqk,skhe->shqe",
            weights.astype(jnp.bfloat16),
            value_heads,
            preferred_element_type=jnp.float32,
        )
        return ((numerator, denominator + jnp.sum(weights, axis=-1)), None)

    result_state, unused = lax.scan(
        forward_advance, (start_numer, start_denom), (blocks, places, offsets)
    )
    numerator, denominator = result_state
    denominator = denominator + (1.0 - query_live)[:, None, :]
    attention_q = jnp.transpose(numerator / denominator[..., None], (0, 2, 1, 3))
    denom_q = jnp.transpose(denominator, (0, 2, 1))
    mixed = attention_q.reshape(seq_count, slot_count, local_width).astype(jnp.bfloat16)
    attn_part = jnp.einsum("stm,mn->stn", mixed, whole_out, preferred_element_type=jnp.float32)
    attn_branch = lax.psum(attn_part, "tp") + vectors[4]
    hidden, first_pull = jax.vjp(layer_norm, inputs + attn_branch, vectors[0], vectors[1])
    hidden_low = hidden.astype(jnp.bfloat16)
    gated = jnp.einsum("std,dcf->stcf", hidden_low, whole_gu, preferred_element_type=jnp.float32)
    activated, unit_pull = jax.vjp(gated_unit, gated[:, :, 0], gated[:, :, 1])
    act_low = activated.astype(jnp.bfloat16)
    ffn_part = jnp.einsum("stf,fn->stn", act_low, whole_down, preferred_element_type=jnp.float32)
    ffn_branch = lax.psum(ffn_part, "tp") + vectors[5]
    normed, second_pull = jax.vjp(layer_norm, hidden + ffn_branch, vectors[2], vectors[3])
    output = (normed * live_rows).astype(jnp.bfloat16)
    upstream = cotangent.astype(jnp.float32) * live_rows
    grad_second, grad_gain_two, grad_shift_two = second_pull(upstream)
    grad_ffn = grad_second.astype(jnp.bfloat16)
    grad_down = jnp.einsum("stf,stn->fn", act_low, grad_ffn, preferred_element_type=jnp.float32)
    grad_ffn_bias = jnp.sum(grad_ffn.astype(jnp.float32), axis=(0, 1))
    grad_act = jnp.einsum("stn,fn->stf", grad_ffn, whole_down, preferred_element_type=jnp.float32)
    grad_gate, grad_upper = unit_pull(grad_act)
    grad_gated = jnp.stack([grad_gate, grad_upper], axis=2).astype(jnp.bfloat16)
    grad_gu = jnp.einsum(
        "std,stcf->dcf", hidden_low, grad_gated, preferred_element_type=jnp.float32
    )
    hidden_part = jnp.einsum(
        "stcf,dcf->std", grad_gated, whole_gu, preferred_element_type=jnp.float32
    )
    grad_hidden = grad_second + lax.psum(hidden_part, "tp")
    grad_first, grad_gain_one, grad_shift_one = first_pull(grad_hidden)
    grad_attn = grad_first.astype(jnp.bfloat16)
    grad_out = jnp.einsum("stm,stn->mn", mixed, grad_attn, preferred_element_type=jnp.float32)
    grad_out_bias = jnp.sum(grad_attn.astype(jnp.float32), axis=(0, 1))
    grad_mixed = jnp.einsum(
        "stn,mn->stm", grad_attn, whole_out, preferred_element_type=jnp.float32
    ).astype(jnp.bfloat16)
    grad_mixed_heads = grad_mixed.reshape(head_shape).astype(jnp.float32)
    correction = jnp.transpose(
        jnp.sum(grad_mixed_heads * attention_q, axis=-1) / denom_q, (0, 2, 1)
    )
    numer_heads = (grad_mixed_heads / denom_q[..., None]).astype(jnp.bfloat16)
    start_query = jnp.zeros(head_shape, jnp.float32)
    start_state = (
        start_query,
        jnp.zeros((seq_count, slot_count * ctx_count, 2, local_width), jnp.float32),
    )
    blocks, places, offsets = split_blocks(
        lax.all_gather(pairs, "ctx", axis=1, tiled=True), slot_count, ctx_count
    )

    def backward_advance(current_state, block_item):
        key_block, key_place, row_offset = block_item
        key_heads = key_block[:, :, 0].reshape(seq_count, -1, head_count, HD)
        value_heads = key_block[:, :, 1].reshape(seq_count, -1, head_count, HD)
        weights_low, grad_scores = backward_scores(
            query_heads,
            numer_heads,
            correction,
            key_heads,
            value_heads,
            query_place,
            key_place,
            slopes,
            lengths,
        )
        grad_query = current_state[0] + jnp.einsum(
            "shqk,skhe->sqhe", grad_scores, key_heads, preferred_element_type=jnp.float32
        )
        grad_key = (
            jnp.einsum(
                "shqk,sqhe->skhe", grad_scores, query_heads, preferred_element_type=jnp.float32
            )
            * 0.125
        )
        grad_value = jnp.einsum(
            "shqk,sqhe->skhe", weights_low, numer_heads, preferred_element_type=jnp.float32
        )
        stacked = jnp.stack(
            [
                grad_key.reshape(seq_count, -1, local_width),
                grad_value.reshape(seq_count, -1, local_width),
            ],
            axis=2,
        )
        buffer = lax.dynamic_update_slice_in_dim(current_state[1], stacked, row_offset, axis=1)
        return ((grad_query, buffer), None)

    result_state, unused = lax.scan(backward_advance, start_state, (blocks, places, offsets))
    grad_pairs = lax.psum_scatter(
        result_state[1].astype(jnp.bfloat16), "ctx", scatter_dimension=1, tiled=True
    )
    grad_query_low = (
        (result_state[0] * 0.125).astype(jnp.bfloat16).reshape(seq_count, slot_count, local_width)
    )
    grad_proj = jnp.concatenate([grad_query_low[:, :, None], grad_pairs], axis=2)
    grad_qkv = jnp.einsum("std,stcm->dcm", tokens, grad_proj, preferred_element_type=jnp.float32)
    bias_terms = jnp.stack(
        [
            jnp.sum(grad_query_low.astype(jnp.float32), axis=(0, 1)),
            jnp.sum(grad_pairs[:, :, 1].astype(jnp.float32), axis=(0, 1)),
        ]
    )
    input_part = jnp.einsum(
        "stcm,dcm->std", grad_proj, whole_qkv, preferred_element_type=jnp.float32
    )
    input_grad = grad_first + lax.psum(input_part.astype(jnp.bfloat16), "tp").astype(jnp.float32)
    grad_weights = (
        lax.psum_scatter(grad_qkv, ("shard", "ctx"), scatter_dimension=0, tiled=True),
        lax.psum_scatter(grad_out, ("shard", "ctx"), scatter_dimension=1, tiled=True),
        lax.psum_scatter(grad_gu, ("shard", "ctx"), scatter_dimension=0, tiled=True),
        lax.psum_scatter(grad_down, ("shard", "ctx"), scatter_dimension=1, tiled=True),
    )
    vector_terms = jnp.stack(
        [grad_gain_one, grad_shift_one, grad_gain_two, grad_shift_two, grad_out_bias, grad_ffn_bias]
    )
    grad_bqv, grad_vectors = lax.psum((bias_terms, vector_terms), ("shard", "ctx"))
    return (
        output,
        input_grad,
        grad_weights[0],
        grad_bqv,
        grad_weights[1],
        grad_weights[2],
        grad_weights[3],
        grad_vectors,
    )


def solution(mesh):
    placed = (
        P("shard", "ctx", None),
        P("shard"),
        P(("shard", "ctx"), None, "tp"),
        P(None, "tp"),
        P("tp", ("shard", "ctx")),
        P(("shard", "ctx"), None, "tp"),
        P("tp", ("shard", "ctx")),
        P(),
        P("shard", "ctx", None),
    )
    return jax.shard_map(
        on_device,
        mesh=mesh,
        in_specs=placed,
        out_specs=(
            P("shard", "ctx", None),
            P("shard", "ctx", None),
            P(("shard", "ctx"), None, "tp"),
            P(None, "tp"),
            P("tp", ("shard", "ctx")),
            P(("shard", "ctx"), None, "tp"),
            P("tp", ("shard", "ctx")),
            P(),
        ),
        check_vma=False,
    )
```

```python
import functools
import math

import jax
import jax.numpy as jnp
import numpy as np
from jax import lax
from jax.experimental import pallas as pl
from jax.experimental.pallas import tpu as pltpu
from jax.sharding import PartitionSpec as P

H = 12
HD = 64
LOG2E = math.log2(math.e)
FAR = 1e30
TILE = 64
BLOCK = 384
EXTRA = 16

epsilon = 1e-12
f32 = jnp.float32
bf16 = jnp.bfloat16
VMEM = pl.BlockSpec(memory_space=pltpu.VMEM)
SMEM = pl.BlockSpec(memory_space=pltpu.SMEM)


def slope_table():
    power = 2 ** (H.bit_length() - 1)
    heads = np.arange(H)
    early = -8.0 * (heads + 1) / power
    later = -4.0 * (2 * (heads - power) + 1) / power
    return np.exp2(np.where(heads < power, early, later)).astype(np.float32)


def dot_nn(a, b):
    return jnp.dot(a, b, preferred_element_type=f32)


def dot_nt(a, b):
    return lax.dot_general(a, b, (((1,), (1,)), ((), ())), preferred_element_type=f32)


def params(*semantics):
    return pltpu.CompilerParams(
        dimension_semantics=semantics or None, vmem_limit_bytes=56 * 1024 * 1024
    )


def cost(flops, nbytes, exps=0):
    return pl.CostEstimate(flops=int(flops), bytes_accessed=int(nbytes), transcendentals=int(exps))


def shape(dims, dtype):
    return jax.ShapeDtypeStruct(dims, dtype)


def xor_pairs(axis, distance):
    return [(i, i ^ distance) for i in range(lax.axis_size(axis))]


def swap(value, axis, distance):
    return lax.ppermute(value, axis, xor_pairs(axis, distance))


def live_mask(lens, rank, n_ctx, seqs, slots):
    slot = lax.broadcasted_iota(jnp.int32, (slots, 1), 0)
    place = slot * n_ctx + rank
    return jnp.concatenate(
        [jnp.where(place < lens[s], 1.0, 0.0).astype(f32) for s in range(seqs)], axis=0
    )


def normalise(z):
    centred = z - jnp.mean(z, axis=-1, keepdims=True)
    spread = jnp.mean(centred * centred, axis=-1, keepdims=True)
    scale = lax.rsqrt(spread + epsilon)
    return centred * scale, scale


def normalise_back(grad_hat, hat, scale):
    inner = jnp.mean(grad_hat * hat, axis=-1, keepdims=True)
    return scale * (grad_hat - jnp.mean(grad_hat, axis=-1, keepdims=True) - hat * inner)


def project_kernel(n, seqs, heads, ids, tok, bias, *refs):
    pieces = refs[: 4 * n]
    sends = refs[4 * n : 5 * n]
    whole = refs[5 * n]
    stage = refs[5 * n + 1]
    y, c, z = ids[0], ids[1], ids[2]
    rows = pieces[0].shape[0]
    for k in range(4 * n):
        ky, kc, kz = k // (2 * n), k // n % 2, k % n
        index = ((y ^ ky) * 2 + (c ^ kc)) * n + (z ^ kz)
        whole[pl.ds(pl.multiple_of(index * rows, rows), rows), :] = pieces[k][...]
    slots = sends[0].shape[1]
    width = heads * HD
    per = seqs * heads // n
    for s in range(seqs):
        acc = dot_nn(tok[s * slots : (s + 1) * slots, :], whole[...]) + bias[...]
        turned = acc.astype(bf16).T
        for h in range(heads):
            i = s * heads + h
            at = ((i % n) * per + i // n) * 3
            for part in range(3):
                first = part * width + h * HD
                stage[(at + part) * HD : (at + part + 1) * HD, :] = turned[first : first + HD, :]
    size = per * 3 * HD
    for d in range(n):
        sends[d][...] = stage[pl.ds(pl.multiple_of((z ^ d) * size, size), size), :]


def project(ids, tok, bias, pieces, n, seqs, heads):
    slots = tok.shape[0] // seqs
    size = seqs * heads // n * 3 * HD
    model, wide = tok.shape[1], bias.shape[1]
    return pl.pallas_call(
        functools.partial(project_kernel, n, seqs, heads),
        out_shape=[shape((size, slots), bf16)] * n + [shape((model, wide), bf16)],
        in_specs=[SMEM] + [VMEM] * (2 + len(pieces)),
        out_specs=[VMEM] * (n + 1),
        scratch_shapes=[pltpu.VMEM((size * n, slots), bf16)],
        compiler_params=params(),
        cost_estimate=cost(2 * tok.shape[0] * model * wide, 6e6),
        name="project",
    )(ids, tok, bias, *pieces)


def pair_scalars(n, heads, ids, lens, slopes):
    j = pl.program_id(0)
    z, t = ids[2], ids[3]
    i = z + n * j
    s = i // heads
    h = i - s * heads
    return z, lens[s], slopes[t * heads + h] * LOG2E


def query_place(n, slots, z, d):
    lane = lax.broadcasted_iota(jnp.int32, (1, slots), 1)
    return lane * n + (z ^ d)


def key_place(n, z, tile, length, slope):
    row = lax.broadcasted_iota(jnp.int32, (TILE, 1), 0)
    places = []
    for d in range(n):
        place = (tile * TILE + row) * n + (z ^ d)
        places.append(jnp.where(place < length, place.astype(f32) * slope, FAR))
    return jnp.concatenate(places, axis=0)


def gather_rows(ref, tile, n):
    rows = pl.ds(pl.multiple_of(tile * TILE, TILE), TILE)
    return jnp.concatenate([ref[d, rows, :] for d in range(n)], axis=0)


def attend_kernel(n, heads, ids, lens, slopes, *refs):
    inputs = refs[:n]
    outs = refs[n : 2 * n]
    att_ref, den_ref = refs[2 * n], refs[2 * n + 1]
    k_s, v_s, acc, den = refs[2 * n + 2 :]
    slots = inputs[0].shape[1]
    z, length, slope = pair_scalars(n, heads, ids, lens, slopes)
    for d in range(n):
        k_s[d] = inputs[d][HD : 2 * HD, :].T
        v_s[d] = inputs[d][2 * HD : 3 * HD, :].T
    acc[...] = jnp.zeros_like(acc)
    den[...] = jnp.zeros_like(den)

    def tile_step(tile, unused):
        keys = gather_rows(k_s, tile, n)
        values = gather_rows(v_s, tile, n).T
        places = key_place(n, z, tile, length, slope)
        for d in range(n):
            cols = slice(d * slots, (d + 1) * slots)
            there = query_place(n, slots, z, d).astype(f32) * slope
            scores = dot_nn(keys, inputs[d][0:HD, :]) * (0.125 * LOG2E)
            e = jnp.exp2(scores - jnp.abs(there - places))
            den[:, cols] += jnp.sum(e, axis=0, keepdims=True)
            acc[:, cols] += dot_nn(values, e.astype(bf16))
        return unused

    step = TILE * n
    lax.fori_loop(0, (length + step - 1) // step, tile_step, 0)
    for d in range(n):
        cols = slice(d * slots, (d + 1) * slots)
        padded = jnp.where(query_place(n, slots, z, d) < length, 0.0, 1.0)
        total = den[:, cols] + padded
        att = acc[:, cols] / total
        att_ref[:, cols] = att
        den_ref[0, :, cols] = total
        outs[d][...] = att.astype(bf16)


def attend(ids, lens, slopes, blocks, n, heads, per):
    slots = blocks[0].shape[1]
    every = n * slots
    return pl.pallas_call(
        functools.partial(attend_kernel, n, heads),
        grid=(per,),
        out_shape=[shape((per * HD, slots), bf16)] * n
        + [shape((per * HD, every), f32), shape((per, 1, every), f32)],
        in_specs=[SMEM] * 3 + [pl.BlockSpec((3 * HD, slots), lambda j: (j, 0))] * n,
        out_specs=[pl.BlockSpec((HD, slots), lambda j: (j, 0))] * n
        + [
            pl.BlockSpec((HD, every), lambda j: (j, 0)),
            pl.BlockSpec((1, 1, every), lambda j: (j, 0, 0)),
        ],
        scratch_shapes=[
            pltpu.VMEM((n, slots, HD), bf16),
            pltpu.VMEM((n, slots, HD), bf16),
            pltpu.VMEM((HD, every), f32),
            pltpu.VMEM((1, every), f32),
        ],
        compiler_params=params("arbitrary"),
        cost_estimate=cost(per * every * every * HD * 8, 3e6, per * every * every),
        name="attend",
    )(ids, lens, slopes, *blocks)


def attend_back_kernel(n, heads, ids, lens, slopes, *refs):
    inputs = refs[:n]
    grads = refs[n : 2 * n]
    att_ref, den_ref = refs[2 * n], refs[2 * n + 1]
    outs = refs[2 * n + 2 : 3 * n + 2]
    k_s, v_s, q_s, g_s, dn, cor, dq, dk, dv = refs[3 * n + 2 :]
    slots = inputs[0].shape[1]
    z, length, slope = pair_scalars(n, heads, ids, lens, slopes)
    for d in range(n):
        cols = slice(d * slots, (d + 1) * slots)
        k_s[d] = inputs[d][HD : 2 * HD, :].T
        v_s[d] = inputs[d][2 * HD : 3 * HD, :].T
        q_s[d] = inputs[d][0:HD, :].T
        inverse = 1.0 / den_ref[0, :, cols]
        mixed = grads[d][...].astype(f32)
        numer = (mixed * inverse).astype(bf16)
        dn[:, cols] = numer
        g_s[d] = numer.T
        cor[:, cols] = jnp.sum(mixed * att_ref[:, cols], axis=0, keepdims=True) * inverse
    dq[...] = jnp.zeros_like(dq)
    dk[...] = jnp.zeros_like(dk)
    dv[...] = jnp.zeros_like(dv)

    def tile_step(tile, unused):
        keys = gather_rows(k_s, tile, n)
        values = gather_rows(v_s, tile, n)
        keys_t = keys.T
        places = key_place(n, z, tile, length, slope)
        grad_k = jnp.zeros((n * TILE, HD), f32)
        grad_v = jnp.zeros((n * TILE, HD), f32)
        for d in range(n):
            cols = slice(d * slots, (d + 1) * slots)
            there = query_place(n, slots, z, d).astype(f32) * slope
            scores = dot_nn(keys, inputs[d][0:HD, :]) * (0.125 * LOG2E)
            e = jnp.exp2(scores - jnp.abs(there - places))
            inner = dot_nn(values, dn[:, cols])
            ds = (e * (inner - cor[:, cols])).astype(bf16)
            dq[:, cols] += dot_nn(keys_t, ds)
            grad_k += dot_nn(ds, q_s[d])
            grad_v += dot_nn(e.astype(bf16), g_s[d])
        rows = pl.ds(pl.multiple_of(tile * TILE, TILE), TILE)
        for d in range(n):
            dk[d, rows, :] = grad_k[d * TILE : (d + 1) * TILE, :]
            dv[d, rows, :] = grad_v[d * TILE : (d + 1) * TILE, :]
        return unused

    step = TILE * n
    lax.fori_loop(0, (length + step - 1) // step, tile_step, 0)
    for d in range(n):
        cols = slice(d * slots, (d + 1) * slots)
        outs[d][0:HD, :] = (dq[:, cols] * 0.125).astype(bf16)
        outs[d][HD : 2 * HD, :] = (dk[d] * 0.125).astype(bf16).T
        outs[d][2 * HD : 3 * HD, :] = dv[d].astype(bf16).T


def attend_back(ids, lens, slopes, blocks, grads, att, den, n, heads, per):
    slots = blocks[0].shape[1]
    every = n * slots
    rows = [pltpu.VMEM((n, slots, HD), bf16)] * 4
    return pl.pallas_call(
        functools.partial(attend_back_kernel, n, heads),
        grid=(per,),
        out_shape=[shape((per * 3 * HD, slots), bf16)] * n,
        in_specs=[SMEM] * 3
        + [pl.BlockSpec((3 * HD, slots), lambda j: (j, 0))] * n
        + [pl.BlockSpec((HD, slots), lambda j: (j, 0))] * n
        + [
            pl.BlockSpec((HD, every), lambda j: (j, 0)),
            pl.BlockSpec((1, 1, every), lambda j: (j, 0, 0)),
        ],
        out_specs=[pl.BlockSpec((3 * HD, slots), lambda j: (j, 0))] * n,
        scratch_shapes=rows
        + [
            pltpu.VMEM((HD, every), bf16),
            pltpu.VMEM((1, every), f32),
            pltpu.VMEM((HD, every), f32),
            pltpu.VMEM((n, slots, HD), f32),
            pltpu.VMEM((n, slots, HD), f32),
        ],
        compiler_params=params("arbitrary"),
        cost_estimate=cost(per * every * every * HD * 20, 5e6, per * every * every),
        name="attend_back",
    )(ids, lens, slopes, *blocks, *grads, att, den)


def mix_kernel(n, seqs, heads, ids, wo, *refs):
    inputs = refs[:n]
    part, mixed, stage = refs[n], refs[n + 1], refs[n + 2]
    z = ids[2]
    slots = inputs[0].shape[1]
    per = seqs * heads // n
    size = per * HD
    for d in range(n):
        stage[pl.ds(pl.multiple_of((z ^ d) * size, size), size), :] = inputs[d][...]
    for s in range(seqs):
        columns = []
        for h in range(heads):
            i = s * heads + h
            at = (i % n) * per + i // n
            columns.append(stage[at * HD : (at + 1) * HD, :])
        rows = slice(s * slots, (s + 1) * slots)
        ours = jnp.concatenate(columns, axis=0).T
        mixed[rows, :] = ours
        part[rows, :] = dot_nt(ours, wo[...]).astype(bf16)


def mix(ids, packed, blocks, n, seqs, heads):
    slots = blocks[0].shape[1]
    model = packed.shape[0]
    width = heads * HD
    tokens = seqs * slots
    return pl.pallas_call(
        functools.partial(mix_kernel, n, seqs, heads),
        grid=(1,),
        out_shape=[shape((tokens, model), bf16), shape((tokens, width), bf16)],
        in_specs=[SMEM, pl.BlockSpec((model, width), lambda i: (0, 0))] + [VMEM] * n,
        out_specs=[VMEM] * 2,
        scratch_shapes=[pltpu.VMEM((seqs * heads * HD, slots), bf16)],
        compiler_params=params("arbitrary"),
        cost_estimate=cost(2 * tokens * model * width, 3e6),
        name="mix",
    )(ids, packed, *blocks)


def unit_kernel(tok, own, other, vec, wg, wu, wd, hidden, low, act, gel, slope, part, acc):
    j = pl.program_id(0)

    @pl.when(j == 0)
    def _():
        branch = own[...].astype(f32) + other[...].astype(f32) + vec[4:5, :]
        hat, _ = normalise(tok[...].astype(f32) + branch)
        h = hat * vec[0:1, :] + vec[1:2, :]
        hidden[...] = h
        low[...] = h.astype(bf16)
        acc[...] = jnp.zeros_like(acc)

    gate = dot_nn(low[...], wg[...])
    upper = dot_nn(low[...], wu[...])
    phi = 0.5 * (1.0 + lax.erf(gate * math.sqrt(0.5)))
    density = jnp.exp(gate * gate * -0.5) * (1.0 / math.sqrt(2.0 * math.pi))
    unit = gate * phi
    acted = (unit * upper).astype(bf16)
    act[...] = acted
    gel[...] = unit.astype(bf16)
    slope[...] = (upper * (phi + gate * density)).astype(bf16)
    acc[...] += dot_nt(acted, wd[...])

    @pl.when(j == pl.num_programs(0) - 1)
    def _():
        part[...] = acc[...].astype(bf16)


def unit(tok, own, other, vec, packed, width, hidden_units):
    tokens, model = tok.shape
    steps = hidden_units // BLOCK
    first = width // BLOCK
    fixed = lambda j: (0, 0)
    moving = lambda j: (0, j)
    whole = pl.BlockSpec((tokens, model), fixed)
    weight = lambda start: pl.BlockSpec((model, BLOCK), lambda j: (0, start + j))
    inner = pl.BlockSpec((tokens, BLOCK), moving)
    return pl.pallas_call(
        unit_kernel,
        grid=(steps,),
        out_shape=[shape((tokens, model), f32), shape((tokens, model), bf16)]
        + [shape((tokens, hidden_units), bf16)] * 3
        + [shape((tokens, model), bf16)],
        in_specs=[
            whole,
            whole,
            whole,
            pl.BlockSpec(vec.shape, fixed),
            weight(first),
            weight(first + steps),
            weight(first + 2 * steps),
        ],
        out_specs=[whole, whole, inner, inner, inner, whole],
        scratch_shapes=[pltpu.VMEM((tokens, model), f32)],
        compiler_params=params("arbitrary"),
        cost_estimate=cost(6 * tokens * model * hidden_units, 20e6, 2 * tokens * hidden_units),
        name="unit",
    )(tok, own, other, vec, packed, packed, packed)


def unit_back_kernel(
    n, seqs, ids, lens, hidden, own, other, cot, vec, wg, wu, wd, gel, slope,
    output, dz2, dffn, dgate, dup, part, sums, acc,
):
    j = pl.program_id(0)

    @pl.when(j == 0)
    def _():
        live = live_mask(lens, ids[2], n, seqs, hidden.shape[0] // seqs)
        branch = own[...].astype(f32) + other[...].astype(f32) + vec[5:6, :]
        hat, scale = normalise(hidden[...] + branch)
        output[...] = (live * (hat * vec[2:3, :] + vec[3:4, :])).astype(bf16)
        gy = cot[...].astype(f32) * live
        grad = normalise_back(gy * vec[2:3, :], hat, scale)
        dz2[...] = grad
        low = grad.astype(bf16)
        dffn[...] = low
        sums[0:1, :] = jnp.sum(gy * hat, axis=0, keepdims=True)
        sums[1:2, :] = jnp.sum(gy, axis=0, keepdims=True)
        sums[2:3, :] = jnp.sum(low.astype(f32), axis=0, keepdims=True)
        sums[3:8, :] = jnp.zeros_like(sums[3:8, :])
        acc[...] = jnp.zeros_like(acc)

    dact = dot_nn(dffn[...], wd[...])
    upper = (dact * gel[...].astype(f32)).astype(bf16)
    gate = (dact * slope[...].astype(f32)).astype(bf16)
    dgate[...] = gate
    dup[...] = upper
    acc[...] += dot_nt(gate, wg[...]) + dot_nt(upper, wu[...])

    @pl.when(j == pl.num_programs(0) - 1)
    def _():
        part[...] = acc[...].astype(bf16)


def unit_back(ids, lens, hidden, own, other, cot, vec, packed, gel, slope, n, seqs, width):
    tokens, model = hidden.shape
    hidden_units = gel.shape[1]
    steps = hidden_units // BLOCK
    first = width // BLOCK
    fixed = lambda j: (0, 0)
    whole = pl.BlockSpec((tokens, model), fixed)
    weight = lambda start: pl.BlockSpec((model, BLOCK), lambda j: (0, start + j))
    inner = pl.BlockSpec((tokens, BLOCK), lambda j: (0, j))
    return pl.pallas_call(
        functools.partial(unit_back_kernel, n, seqs),
        grid=(steps,),
        out_shape=[
            shape((tokens, model), bf16),
            shape((tokens, model), f32),
            shape((tokens, model), bf16),
            shape((tokens, hidden_units), bf16),
            shape((tokens, hidden_units), bf16),
            shape((tokens, model), bf16),
            shape((8, model), f32),
        ],
        in_specs=[SMEM, SMEM, whole, whole, whole, whole, pl.BlockSpec(vec.shape, fixed)]
        + [weight(first), weight(first + steps), weight(first + 2 * steps), inner, inner],
        out_specs=[whole, whole, whole, inner, inner, whole, pl.BlockSpec((8, model), fixed)],
        scratch_shapes=[pltpu.VMEM((tokens, model), f32)],
        compiler_params=params("arbitrary"),
        cost_estimate=cost(6 * tokens * model * hidden_units, 22e6),
        name="unit_back",
    )(ids, lens, hidden, own, other, cot, vec, packed, packed, packed, gel, slope)


def row_starts(ids, quarter):
    y, c = ids[0], ids[1]
    keep = [(y * 2 + c) * quarter, ((1 - y) * 2 + c) * quarter]
    send = [(y * 2 + 1 - c) * quarter, ((1 - y) * 2 + 1 - c) * quarter]
    return send, keep


def write_rows(ids, turned, right, send, keep):
    quarter = turned.shape[0] // 4
    for ref, starts in zip((send, keep), row_starts(ids, quarter)):
        for k in range(2):
            left = turned[pl.ds(pl.multiple_of(starts[k], quarter), quarter), :]
            ref[k * quarter : (k + 1) * quarter, :] = dot_nn(left, right).astype(bf16)


def weight_kernel(steps, ids, low, dffn, dgate, dup, act, send, keep, left):
    j = pl.program_id(0)

    @pl.when(j == 0)
    def _():
        left[0] = low[...].T
        left[1] = dffn[...].T

    @pl.when(j < steps)
    def _():
        write_rows(ids, left.at[0], dgate[...], send, keep)

    @pl.when((j >= steps) & (j < 2 * steps))
    def _():
        write_rows(ids, left.at[0], dup[...], send, keep)

    @pl.when(j >= 2 * steps)
    def _():
        write_rows(ids, left.at[1], act[...], send, keep)


def weight_grads(ids, low, dffn, dgate, dup, act):
    tokens, model = low.shape
    hidden_units = act.shape[1]
    steps = hidden_units // BLOCK
    fixed = lambda j: (0, 0)
    whole = pl.BlockSpec((tokens, model), fixed)
    column = lambda start: pl.BlockSpec(
        (tokens, BLOCK), lambda j: (0, jnp.clip(j - start, 0, steps - 1))
    )
    out = pl.BlockSpec((model // 2, BLOCK), lambda j: (0, j))
    return pl.pallas_call(
        functools.partial(weight_kernel, steps),
        grid=(3 * steps,),
        out_shape=[shape((model // 2, 3 * hidden_units + BLOCK), bf16)] * 2,
        in_specs=[SMEM, whole, whole, column(0), column(steps), column(2 * steps)],
        out_specs=[out, out],
        scratch_shapes=[pltpu.VMEM((2, model, tokens), bf16)],
        compiler_params=params("arbitrary"),
        cost_estimate=cost(6 * tokens * model * hidden_units, 14e6),
        name="weight_grads",
    )(ids, low, dffn, dgate, dup, act)


def mix_back_kernel(
    n, seqs, heads, ids, tok, own, other, dz2, hown, hother, vec, wo, mixed, far, near, *refs
):
    sends = refs[:n]
    dz1, send, keep, sums = refs[n : n + 4]
    stage, left = refs[n + 4 :]
    z = ids[2]
    slots = sends[0].shape[1]
    per = seqs * heads // n
    branch = own[...].astype(f32) + other[...].astype(f32) + vec[4:5, :]
    hat, scale = normalise(tok[...].astype(f32) + branch)
    gh = dz2[...] + (hown[...].astype(f32) + hother[...].astype(f32))
    grad = normalise_back(gh * vec[0:1, :], hat, scale)
    dz1[...] = grad
    low = grad.astype(bf16)
    sums[0:1, :] = jnp.sum(gh * hat, axis=0, keepdims=True)
    sums[1:2, :] = jnp.sum(gh, axis=0, keepdims=True)
    sums[2:3, :] = jnp.sum(low.astype(f32), axis=0, keepdims=True)
    sums[3:8, :] = jnp.zeros_like(sums[3:8, :])
    for s in range(seqs):
        turned = dot_nn(low[s * slots : (s + 1) * slots, :], wo[...]).astype(bf16).T
        for h in range(heads):
            i = s * heads + h
            at = (i % n) * per + i // n
            stage[at * HD : (at + 1) * HD, :] = turned[h * HD : (h + 1) * HD, :]
    size = per * HD
    for d in range(n):
        sends[d][...] = stage[pl.ds(pl.multiple_of((z ^ d) * size, size), size), :]
    left[...] = low.T
    write_rows(ids, left, mixed[...], send, keep)


def mix_back(ids, tok, own, other, dz2, hown, hother, vec, packed, mixed, grads, n, seqs, heads):
    tokens, model = tok.shape
    slots = tokens // seqs
    width = heads * HD
    size = seqs * heads // n * HD
    last = pl.BlockSpec((model // 2, width), lambda i: (0, grads[0].shape[1] // width - 1))
    return pl.pallas_call(
        functools.partial(mix_back_kernel, n, seqs, heads),
        grid=(1,),
        out_shape=[shape((size, slots), bf16)] * n
        + [shape((tokens, model), f32)]
        + [shape(grads[0].shape, bf16)] * 2
        + [shape((8, model), f32)],
        in_specs=[SMEM]
        + [VMEM] * 7
        + [pl.BlockSpec((model, width), lambda i: (0, 0)), VMEM]
        + [pl.BlockSpec(memory_space=pl.ANY)] * 2,
        out_specs=[VMEM] * (n + 1) + [last, last, VMEM],
        input_output_aliases={10: n + 1, 11: n + 2},
        scratch_shapes=[
            pltpu.VMEM((size * n, slots), bf16),
            pltpu.VMEM((model, tokens), bf16),
        ],
        compiler_params=params("arbitrary"),
        cost_estimate=cost(4 * tokens * model * width, 10e6),
        name="mix_back",
    )(ids, tok, own, other, dz2, hown, hother, vec, packed, mixed, *grads)


def project_back_kernel(n, seqs, heads, ids, tok, whole, small, *refs):
    inputs = refs[:n]
    part, send, keep = refs[n : n + 3]
    stage, right, left = refs[n + 3 :]
    z = ids[2]
    slots = inputs[0].shape[1]
    per = seqs * heads // n
    width = heads * HD
    size = per * 3 * HD
    for d in range(n):
        stage[pl.ds(pl.multiple_of((z ^ d) * size, size), size), :] = inputs[d][...]
    for s in range(seqs):
        for c in range(3):
            columns = []
            for h in range(heads):
                i = s * heads + h
                at = ((i % n) * per + i // n) * 3 + c
                columns.append(stage[at * HD : (at + 1) * HD, :])
            ours = jnp.concatenate(columns, axis=0).T
            right[s * slots : (s + 1) * slots, c * width : (c + 1) * width] = ours
    part[...] = dot_nt(right[...], whole[...]).astype(bf16)
    left[...] = tok[...].T
    for c in range(3):
        cols = slice(c * width, (c + 1) * width)
        write_rows(ids, left, right[:, cols], send.at[:, cols], keep.at[:, cols])
    ones = jnp.ones((8, right.shape[0]), bf16)
    sums = dot_nn(ones, right[...])
    line = jnp.concatenate([sums[:, :width], sums[:, 2 * width :]], axis=1)
    row = lax.broadcasted_iota(jnp.int32, (8, 1), 0)
    rows = jnp.where(row == 6, line, small[...])
    rows = jnp.concatenate([rows, jnp.zeros_like(rows)], axis=0).astype(bf16)
    for ref in (send, keep):
        ref[ref.shape[0] - EXTRA :, :] = jnp.zeros((EXTRA, ref.shape[1]), bf16)
        ref[ref.shape[0] - EXTRA :, : 2 * width] = rows


def project_back(ids, tok, whole, small, blocks, n, seqs, heads):
    tokens, model = tok.shape
    slots = tokens // seqs
    wide = whole.shape[1]
    return pl.pallas_call(
        functools.partial(project_back_kernel, n, seqs, heads),
        out_shape=[
            shape((tokens, model), bf16),
            shape((model // 2 + EXTRA, wide), bf16),
            shape((model // 2 + EXTRA, wide), bf16),
        ],
        in_specs=[SMEM] + [VMEM] * (3 + n),
        out_specs=[VMEM] * 3,
        scratch_shapes=[
            pltpu.VMEM((seqs * heads * 3 * HD, slots), bf16),
            pltpu.VMEM((tokens, wide), bf16),
            pltpu.VMEM((model, tokens), bf16),
        ],
        compiler_params=params(),
        cost_estimate=cost(4 * tokens * model * wide, 8e6),
        name="project_back",
    )(ids, tok, whole, small, *blocks)


def fold_core_kernel(extra, keep, recv, mine, send):
    half = (keep.shape[0] - extra) // 2
    mine[0:half, :] = keep[0:half, :].astype(f32) + recv[0:half, :].astype(f32)
    rest = (keep[half:, :].astype(f32) + recv[half:, :].astype(f32)).astype(bf16)
    send[...] = rest
    if extra:
        mine[half:, :] = rest[half:, :].astype(f32)


def fold_core(keep, recv, extra):
    rows, wide = keep.shape
    out = (rows - extra) // 2 + extra
    steps = 1 if extra else 3
    column = lambda size: pl.BlockSpec((size, wide // steps), lambda j: (0, j))
    return pl.pallas_call(
        functools.partial(fold_core_kernel, extra),
        grid=(steps,),
        out_shape=[shape((out, wide), f32), shape((out, wide), bf16)],
        in_specs=[column(rows)] * 2,
        out_specs=[column(out)] * 2,
        compiler_params=params("arbitrary"),
        cost_estimate=cost(rows * wide, 7 * rows * wide),
        name="fold_core",
    )(keep, recv)


def fold_y_kernel(n, extra, ids, mine, recv, own, *refs):
    sends, stage = refs[:-1], refs[-1]
    z = ids[2]
    rows = mine.shape[0] - extra
    size = rows // n
    stage[...] = mine[...] + recv[...].astype(f32)
    for d in range(n):
        block = stage[pl.ds(pl.multiple_of((z ^ d) * size, size), size), :]
        if d:
            sends[d - 1][0:size, :] = block.astype(bf16)
            if extra:
                sends[d - 1][size:, :] = stage[rows:, :].astype(bf16)
        else:
            own[0:size, :] = block
            if extra:
                own[size:, :] = stage[rows:, :].astype(bf16).astype(f32)


def fold_y(ids, mine, recv, n, extra):
    rows, wide = mine.shape
    out = (rows - extra) // n + extra
    steps = 1 if extra else 3
    column = lambda size: pl.BlockSpec((size, wide // steps), lambda j: (0, j))
    return pl.pallas_call(
        functools.partial(fold_y_kernel, n, extra),
        grid=(steps,),
        out_shape=[shape((out, wide), f32)] + [shape((out, wide), bf16)] * (n - 1),
        in_specs=[SMEM] + [column(rows)] * 2,
        out_specs=[column(out)] * n,
        scratch_shapes=[pltpu.VMEM((rows, wide // steps), f32)],
        compiler_params=params("arbitrary"),
        cost_estimate=cost(rows * wide, 9 * rows * wide),
        name="fold_y",
    )(ids, mine, recv)


def fold_z(own, got):
    return (own + got[0].astype(f32)) + (got[1].astype(f32) + got[2].astype(f32))


def fits(tokens, b_qv, w_qkv, w_gu):
    n = lax.axis_size("ctx")
    heads = b_qv.shape[1] // HD
    return (
        n == 4
        and lax.axis_size("shard") == 4
        and lax.axis_size("tp") == 2
        and (tokens.shape[0] * heads) % n == 0
        and w_qkv.shape[0] % 16 == 0
        and tokens.shape[1] % 256 == 0
        and b_qv.shape[1] == BLOCK
        and w_gu.shape[2] % BLOCK == 0
    )


def on_device(tokens, lengths, w_qkv, b_qv, w_out, w_gu, w_down, vectors, cotangent):
    if not fits(tokens, b_qv, w_qkv, w_gu):
        return by_gather(tokens, lengths, w_qkv, b_qv, w_out, w_gu, w_down, vectors, cotangent)
    n = lax.axis_size("ctx")
    seqs, slots, model = tokens.shape
    width = b_qv.shape[1]
    heads = width // HD
    per = seqs * heads // n
    units = w_gu.shape[2]
    rows = w_qkv.shape[0]
    count = seqs * slots
    shard = lax.axis_index("shard")
    ids = jnp.stack(
        [shard // 2, shard % 2, lax.axis_index("ctx"), lax.axis_index("tp")]
    ).astype(jnp.int32)
    slopes = jnp.asarray(slope_table())
    tok = tokens.reshape(count, model)
    cot = cotangent.reshape(count, model)

    first = [w_qkv.astype(bf16).reshape(rows, 3 * width)]
    first += [swap(first[0], "ctx", d) for d in range(1, n)]
    first += [swap(piece, "shard", 2) for piece in first]
    by_core = [swap(piece, "shard", 1) for piece in first]
    pieces = first[:n] + by_core[:n] + first[n:] + by_core[n:]
    packed = jnp.concatenate(
        [w_out.T, w_gu.reshape(rows, 2 * units), w_down.T], axis=1
    ).astype(bf16)
    packed, pieces[0] = lax.optimization_barrier((packed, pieces[0]))
    packed = lax.all_gather(packed, ("shard", "ctx"), axis=0, tiled=True)

    bias = jnp.concatenate([b_qv[0], jnp.zeros_like(b_qv[0]), b_qv[1]])[None, :]
    *sends, whole = project(ids, tok, bias, pieces, n, seqs, heads)
    blocks = [sends[0]] + [swap(sends[d], "ctx", d) for d in range(1, n)]
    *outs, att, den = attend(ids, lengths, slopes, blocks, n, heads, per)
    outs = [outs[0]] + [swap(outs[d], "ctx", d) for d in range(1, n)]
    part, mixed = mix(ids, packed, outs, n, seqs, heads)
    part_other = swap(part, "tp", 1)
    hidden, low, act, gel, slope, ffn = unit(tok, part, part_other, vectors, packed, width, units)
    ffn_other = swap(ffn, "tp", 1)
    output, dz2, dffn, dgate, dup, back, sums_two = unit_back(
        ids, lengths, hidden, ffn, ffn_other, cot, vectors, packed, gel, slope, n, seqs, width
    )
    back_other = swap(back, "tp", 1)
    unit_grads = weight_grads(ids, low, dffn, dgate, dup, act)
    back_other, *unit_grads = lax.optimization_barrier((back_other, *unit_grads))
    *sends, dz1, far, near, sums_one = mix_back(
        ids, tok, part, part_other, dz2, back, back_other, vectors, packed, mixed, unit_grads,
        n, seqs, heads,
    )
    grads = [sends[0]] + [swap(sends[d], "ctx", d) for d in range(1, n)]
    got = swap(far, "shard", 1)
    mine, far = fold_core(near, got, 0)
    *grads, far = lax.optimization_barrier((*grads, far))
    got = swap(far, "shard", 2)
    outs = attend_back(ids, lengths, slopes, blocks, grads, att, den, n, heads, per)
    outs = [outs[0]] + [swap(outs[d], "ctx", d) for d in range(1, n)]
    *outs, got = lax.optimization_barrier((*outs, got))
    rest_own, *rest_sends = fold_y(ids, mine, got, n, 0)
    *outs, rest_own = lax.optimization_barrier((*outs, rest_own))
    small = jnp.concatenate(
        [sums_one[0:2], sums_two[0:2], sums_one[2:3], sums_two[2:3], jnp.zeros_like(sums_one[:2])]
    )
    dx, far, near = project_back(ids, tok, whole, small, outs, n, seqs, heads)
    got = swap(far, "shard", 1)
    dx_other = swap(dx, "tp", 1)
    mine, far = fold_core(near, got, EXTRA)
    got = swap(far, "shard", 2)
    own, *sends = fold_y(ids, mine, got, n, EXTRA)
    rest_got = [swap(block, "ctx", d + 1) for d, block in enumerate(rest_sends)]
    got = [swap(block, "ctx", d + 1) for d, block in enumerate(sends)]
    *rest_got, got[0] = lax.optimization_barrier((*rest_got, got[0]))
    rest = fold_z(rest_own, rest_got)
    last = fold_z(own, got)
    input_grad = dz1 + (dx.astype(f32) + dx_other.astype(f32))
    small = last[rows : rows + 8, : 2 * width]
    return (
        output.reshape(tokens.shape),
        input_grad.reshape(tokens.shape),
        last[:rows].reshape(w_qkv.shape),
        small[6].reshape(2, width),
        rest[:, 3 * units :].T,
        rest[:, : 2 * units].reshape(w_gu.shape),
        rest[:, 2 * units : 3 * units].T,
        small[:6],
    )


def alibi_slopes(first_head, head_count):
    power = 2 ** (H.bit_length() - 1)
    heads_index = first_head + jnp.arange(head_count, dtype=jnp.int32)
    early = -8.0 * (heads_index + 1).astype(jnp.float32) / power
    later = -4.0 * (2 * (heads_index - power) + 1).astype(jnp.float32) / power
    return jnp.exp2(jnp.where(heads_index < power, early, later))


def layer_norm(values, gain, shift):
    centred = values - jnp.mean(values, axis=-1, keepdims=True)
    spread = jnp.mean(centred * centred, axis=-1, keepdims=True)
    return centred * lax.rsqrt(spread + epsilon) * gain + shift


def gated_unit(gate_input, upper):
    return jax.nn.gelu(gate_input, approximate=False) * upper


def score_block(query_heads, key_heads, query_place, key_place, slopes, lengths):
    scores = (
        jnp.einsum("sqhe,skhe->shqk", query_heads, key_heads, preferred_element_type=jnp.float32)
        * 0.125
    )
    distance = jnp.abs(query_place[:, None] - key_place[None, :]).astype(jnp.float32)
    scores = scores - slopes[None, :, None, None] * distance[None, None]
    usable = key_place[None, :] < lengths[:, None]
    return jnp.where(usable[:, None, None, :], jnp.exp(scores), 0.0)


def backward_scores(
    query_heads,
    numer_heads,
    correction,
    key_heads,
    value_heads,
    query_place,
    key_place,
    slopes,
    lengths,
):
    weights = score_block(query_heads, key_heads, query_place, key_place, slopes, lengths)
    value_dots = jnp.einsum(
        "sqhe,skhe->shqk", numer_heads, value_heads, preferred_element_type=jnp.float32
    )
    grad_scores = (weights * (value_dots - correction[..., None])).astype(jnp.bfloat16)
    return (weights.astype(jnp.bfloat16), grad_scores)


def split_blocks(shard_piece, slot_count, ctx_count):
    piece_rows = shard_piece.shape[1]
    block_rows = math.gcd(piece_rows, 128)
    block_count = piece_rows // block_rows
    shaped = shard_piece.reshape(
        (shard_piece.shape[0], block_count, block_rows) + shard_piece.shape[2:]
    )
    blocks = jnp.moveaxis(shaped, 1, 0)
    row_ids = jnp.arange(piece_rows, dtype=jnp.int32)
    places = (row_ids % slot_count * ctx_count + row_ids // slot_count).reshape(
        block_count, block_rows
    )
    offsets = block_rows * jnp.arange(block_count, dtype=jnp.int32)
    return (blocks, places, offsets)


def by_gather(tokens, lengths, w_qkv, b_qv, w_out, w_gu, w_down, vectors, cotangent):
    ctx_count = lax.axis_size("ctx")
    ctx_rank = lax.axis_index("ctx")
    seq_count, slot_count, model_width = tokens.shape
    local_width = b_qv.shape[1]
    head_count = local_width // HD
    slopes = alibi_slopes(lax.axis_index("tp") * head_count, head_count)
    slot_ids = jnp.arange(slot_count, dtype=jnp.int32)
    query_place = slot_ids * ctx_count + ctx_rank
    query_live = (query_place[None, :] < lengths[:, None]).astype(jnp.float32)
    live_rows = query_live[:, :, None]
    head_shape = (seq_count, slot_count, head_count, HD)
    whole_qkv, whole_out, whole_gu, whole_down = (
        lax.all_gather(w_qkv.astype(jnp.bfloat16), ("shard", "ctx"), axis=0, tiled=True),
        lax.all_gather(w_out.astype(jnp.bfloat16), ("shard", "ctx"), axis=1, tiled=True),
        lax.all_gather(w_gu.astype(jnp.bfloat16), ("shard", "ctx"), axis=0, tiled=True),
        lax.all_gather(w_down.astype(jnp.bfloat16), ("shard", "ctx"), axis=1, tiled=True),
    )
    inputs = tokens.astype(jnp.float32)
    projected = jnp.einsum("std,dcm->stcm", tokens, whole_qkv, preferred_element_type=jnp.float32)
    query_rows = (projected[:, :, 0] + b_qv[0]).astype(jnp.bfloat16)
    key_rows = projected[:, :, 1].astype(jnp.bfloat16)
    value_rows = (projected[:, :, 2] + b_qv[1]).astype(jnp.bfloat16)
    query_heads = query_rows.reshape(head_shape)
    pairs = jnp.stack([key_rows, value_rows], axis=2)
    start_numer = jnp.zeros((seq_count, head_count, slot_count, HD), jnp.float32)
    start_denom = jnp.zeros((seq_count, head_count, slot_count), jnp.float32)
    blocks, places, offsets = split_blocks(
        lax.all_gather(pairs, "ctx", axis=1, tiled=True), slot_count, ctx_count
    )

    def forward_advance(inner_state, block_item):
        key_block, key_place, row_offset = block_item
        numerator, denominator = inner_state
        key_heads = key_block[:, :, 0].reshape(seq_count, -1, head_count, HD)
        value_heads = key_block[:, :, 1].reshape(seq_count, -1, head_count, HD)
        weights = score_block(query_heads, key_heads, query_place, key_place, slopes, lengths)
        numerator = numerator + jnp.einsum(
            "shqk,skhe->shqe",
            weights.astype(jnp.bfloat16),
            value_heads,
            preferred_element_type=jnp.float32,
        )
        return ((numerator, denominator + jnp.sum(weights, axis=-1)), None)

    result_state, unused = lax.scan(
        forward_advance, (start_numer, start_denom), (blocks, places, offsets)
    )
    numerator, denominator = result_state
    denominator = denominator + (1.0 - query_live)[:, None, :]
    attention_q = jnp.transpose(numerator / denominator[..., None], (0, 2, 1, 3))
    denom_q = jnp.transpose(denominator, (0, 2, 1))
    mixed = attention_q.reshape(seq_count, slot_count, local_width).astype(jnp.bfloat16)
    attn_part = jnp.einsum("stm,mn->stn", mixed, whole_out, preferred_element_type=jnp.float32)
    attn_branch = lax.psum(attn_part, "tp") + vectors[4]
    hidden, first_pull = jax.vjp(layer_norm, inputs + attn_branch, vectors[0], vectors[1])
    hidden_low = hidden.astype(jnp.bfloat16)
    gated = jnp.einsum("std,dcf->stcf", hidden_low, whole_gu, preferred_element_type=jnp.float32)
    activated, unit_pull = jax.vjp(gated_unit, gated[:, :, 0], gated[:, :, 1])
    act_low = activated.astype(jnp.bfloat16)
    ffn_part = jnp.einsum("stf,fn->stn", act_low, whole_down, preferred_element_type=jnp.float32)
    ffn_branch = lax.psum(ffn_part, "tp") + vectors[5]
    normed, second_pull = jax.vjp(layer_norm, hidden + ffn_branch, vectors[2], vectors[3])
    output = (normed * live_rows).astype(jnp.bfloat16)
    upstream = cotangent.astype(jnp.float32) * live_rows
    grad_second, grad_gain_two, grad_shift_two = second_pull(upstream)
    grad_ffn = grad_second.astype(jnp.bfloat16)
    grad_down = jnp.einsum("stf,stn->fn", act_low, grad_ffn, preferred_element_type=jnp.float32)
    grad_ffn_bias = jnp.sum(grad_ffn.astype(jnp.float32), axis=(0, 1))
    grad_act = jnp.einsum("stn,fn->stf", grad_ffn, whole_down, preferred_element_type=jnp.float32)
    grad_gate, grad_upper = unit_pull(grad_act)
    grad_gated = jnp.stack([grad_gate, grad_upper], axis=2).astype(jnp.bfloat16)
    grad_gu = jnp.einsum(
        "std,stcf->dcf", hidden_low, grad_gated, preferred_element_type=jnp.float32
    )
    hidden_part = jnp.einsum(
        "stcf,dcf->std", grad_gated, whole_gu, preferred_element_type=jnp.float32
    )
    grad_hidden = grad_second + lax.psum(hidden_part, "tp")
    grad_first, grad_gain_one, grad_shift_one = first_pull(grad_hidden)
    grad_attn = grad_first.astype(jnp.bfloat16)
    grad_out = jnp.einsum("stm,stn->mn", mixed, grad_attn, preferred_element_type=jnp.float32)
    grad_out_bias = jnp.sum(grad_attn.astype(jnp.float32), axis=(0, 1))
    grad_mixed = jnp.einsum(
        "stn,mn->stm", grad_attn, whole_out, preferred_element_type=jnp.float32
    ).astype(jnp.bfloat16)
    grad_mixed_heads = grad_mixed.reshape(head_shape).astype(jnp.float32)
    correction = jnp.transpose(
        jnp.sum(grad_mixed_heads * attention_q, axis=-1) / denom_q, (0, 2, 1)
    )
    numer_heads = (grad_mixed_heads / denom_q[..., None]).astype(jnp.bfloat16)
    start_query = jnp.zeros(head_shape, jnp.float32)
    start_state = (
        start_query,
        jnp.zeros((seq_count, slot_count * ctx_count, 2, local_width), jnp.float32),
    )
    blocks, places, offsets = split_blocks(
        lax.all_gather(pairs, "ctx", axis=1, tiled=True), slot_count, ctx_count
    )

    def backward_advance(current_state, block_item):
        key_block, key_place, row_offset = block_item
        key_heads = key_block[:, :, 0].reshape(seq_count, -1, head_count, HD)
        value_heads = key_block[:, :, 1].reshape(seq_count, -1, head_count, HD)
        weights_low, grad_scores = backward_scores(
            query_heads,
            numer_heads,
            correction,
            key_heads,
            value_heads,
            query_place,
            key_place,
            slopes,
            lengths,
        )
        grad_query = current_state[0] + jnp.einsum(
            "shqk,skhe->sqhe", grad_scores, key_heads, preferred_element_type=jnp.float32
        )
        grad_key = (
            jnp.einsum(
                "shqk,sqhe->skhe", grad_scores, query_heads, preferred_element_type=jnp.float32
            )
            * 0.125
        )
        grad_value = jnp.einsum(
            "shqk,sqhe->skhe", weights_low, numer_heads, preferred_element_type=jnp.float32
        )
        stacked = jnp.stack(
            [
                grad_key.reshape(seq_count, -1, local_width),
                grad_value.reshape(seq_count, -1, local_width),
            ],
            axis=2,
        )
        buffer = lax.dynamic_update_slice_in_dim(current_state[1], stacked, row_offset, axis=1)
        return ((grad_query, buffer), None)

    result_state, unused = lax.scan(backward_advance, start_state, (blocks, places, offsets))
    grad_pairs = lax.psum_scatter(
        result_state[1].astype(jnp.bfloat16), "ctx", scatter_dimension=1, tiled=True
    )
    grad_query_low = (
        (result_state[0] * 0.125).astype(jnp.bfloat16).reshape(seq_count, slot_count, local_width)
    )
    grad_proj = jnp.concatenate([grad_query_low[:, :, None], grad_pairs], axis=2)
    grad_qkv = jnp.einsum("std,stcm->dcm", tokens, grad_proj, preferred_element_type=jnp.float32)
    bias_terms = jnp.stack(
        [
            jnp.sum(grad_query_low.astype(jnp.float32), axis=(0, 1)),
            jnp.sum(grad_pairs[:, :, 1].astype(jnp.float32), axis=(0, 1)),
        ]
    )
    input_part = jnp.einsum(
        "stcm,dcm->std", grad_proj, whole_qkv, preferred_element_type=jnp.float32
    )
    input_grad = grad_first + lax.psum(input_part.astype(jnp.bfloat16), "tp").astype(jnp.float32)
    grad_weights = (
        lax.psum_scatter(grad_qkv, ("shard", "ctx"), scatter_dimension=0, tiled=True),
        lax.psum_scatter(grad_out, ("shard", "ctx"), scatter_dimension=1, tiled=True),
        lax.psum_scatter(grad_gu, ("shard", "ctx"), scatter_dimension=0, tiled=True),
        lax.psum_scatter(grad_down, ("shard", "ctx"), scatter_dimension=1, tiled=True),
    )
    vector_terms = jnp.stack(
        [grad_gain_one, grad_shift_one, grad_gain_two, grad_shift_two, grad_out_bias, grad_ffn_bias]
    )
    grad_bqv, grad_vectors = lax.psum((bias_terms, vector_terms), ("shard", "ctx"))
    return (
        output,
        input_grad,
        grad_weights[0],
        grad_bqv,
        grad_weights[1],
        grad_weights[2],
        grad_weights[3],
        grad_vectors,
    )


def solution(mesh):
    placed = (
        P("shard", "ctx", None),
        P("shard"),
        P(("shard", "ctx"), None, "tp"),
        P(None, "tp"),
        P("tp", ("shard", "ctx")),
        P(("shard", "ctx"), None, "tp"),
        P("tp", ("shard", "ctx")),
        P(),
        P("shard", "ctx", None),
    )
    return jax.shard_map(
        on_device,
        mesh=mesh,
        in_specs=placed,
        out_specs=(
            P("shard", "ctx", None),
            P("shard", "ctx", None),
            P(("shard", "ctx"), None, "tp"),
            P(None, "tp"),
            P("tp", ("shard", "ctx")),
            P(("shard", "ctx"), None, "tp"),
            P("tp", ("shard", "ctx")),
            P(),
        ),
        check_vma=False,
    )
```

```python
import functools
import math

import jax
import jax.numpy as jnp
import numpy as np
from jax import lax
from jax.experimental import pallas as pl
from jax.experimental.pallas import tpu as pltpu
from jax.sharding import PartitionSpec as P

H = 12
HD = 64
LOG2E = math.log2(math.e)
FAR = 1e30
TILE = 64
BLOCK = 512
WIDTH = 384
EXTRA = 16

epsilon = 1e-12
f32 = jnp.float32
bf16 = jnp.bfloat16
VMEM = pl.BlockSpec(memory_space=pltpu.VMEM)
SMEM = pl.BlockSpec(memory_space=pltpu.SMEM)


def slope_table():
    power = 2 ** (H.bit_length() - 1)
    heads = np.arange(H)
    early = -8.0 * (heads + 1) / power
    later = -4.0 * (2 * (heads - power) + 1) / power
    return np.exp2(np.where(heads < power, early, later)).astype(np.float32)


def dot_nn(a, b):
    return jnp.dot(a, b, preferred_element_type=f32)


def dot_nt(a, b):
    return lax.dot_general(a, b, (((1,), (1,)), ((), ())), preferred_element_type=f32)


def params(*semantics):
    return pltpu.CompilerParams(
        dimension_semantics=semantics or None, vmem_limit_bytes=56 * 1024 * 1024
    )


def cost(flops, nbytes, exps=0):
    return pl.CostEstimate(flops=int(flops), bytes_accessed=int(nbytes), transcendentals=int(exps))


def shape(dims, dtype):
    return jax.ShapeDtypeStruct(dims, dtype)


def xor_pairs(axis, distance):
    return [(i, i ^ distance) for i in range(lax.axis_size(axis))]


def swap(value, axis, distance):
    return lax.ppermute(value, axis, xor_pairs(axis, distance))


def live_mask(length, rank, n_ctx, slots):
    slot = lax.broadcasted_iota(jnp.int32, (slots, 1), 0)
    return jnp.where(slot * n_ctx + rank < length, 1.0, 0.0).astype(f32)


def normalise(z):
    centred = z - jnp.mean(z, axis=-1, keepdims=True)
    spread = jnp.mean(centred * centred, axis=-1, keepdims=True)
    scale = lax.rsqrt(spread + epsilon)
    return centred * scale, scale


def normalise_back(grad_hat, hat, scale):
    inner = jnp.mean(grad_hat * hat, axis=-1, keepdims=True)
    return scale * (grad_hat - jnp.mean(grad_hat, axis=-1, keepdims=True) - hat * inner)


def project_kernel(n, seqs, heads, ids, tok, bias, *refs):
    pieces = refs[: 4 * n]
    sends = refs[4 * n : 5 * n]
    whole = refs[5 * n]
    stage = refs[5 * n + 1]
    y, c, z = ids[0], ids[1], ids[2]
    rows = pieces[0].shape[0]
    for k in range(4 * n):
        ky, kc, kz = k // (2 * n), k // n % 2, k % n
        index = ((y ^ ky) * 2 + (c ^ kc)) * n + (z ^ kz)
        whole[pl.ds(pl.multiple_of(index * rows, rows), rows), :] = pieces[k][...]
    slots = sends[0].shape[1]
    width = heads * HD
    per = seqs * heads // n
    for s in range(seqs):
        acc = dot_nn(tok[s * slots : (s + 1) * slots, :], whole[...]) + bias[...]
        turned = acc.astype(bf16).T
        for h in range(heads):
            i = s * heads + h
            at = ((i % n) * per + i // n) * 3
            for part in range(3):
                first = part * width + h * HD
                stage[(at + part) * HD : (at + part + 1) * HD, :] = turned[first : first + HD, :]
    size = per * 3 * HD
    for d in range(n):
        sends[d][...] = stage[pl.ds(pl.multiple_of((z ^ d) * size, size), size), :]


def project(ids, tok, bias, pieces, n, seqs, heads):
    slots = tok.shape[0] // seqs
    size = seqs * heads // n * 3 * HD
    model, wide = tok.shape[1], bias.shape[1]
    return pl.pallas_call(
        functools.partial(project_kernel, n, seqs, heads),
        out_shape=[shape((size, slots), bf16)] * n + [shape((model, wide), bf16)],
        in_specs=[SMEM] + [VMEM] * (2 + len(pieces)),
        out_specs=[VMEM] * (n + 1),
        scratch_shapes=[pltpu.VMEM((size * n, slots), bf16)],
        compiler_params=params(),
        cost_estimate=cost(2 * tok.shape[0] * model * wide, 6e6),
        name="project",
    )(ids, tok, bias, *pieces)


def pair_scalars(n, heads, ids, lens, slopes):
    j = pl.program_id(0)
    z, t = ids[2], ids[3]
    i = z + n * j
    s = i // heads
    h = i - s * heads
    return z, lens[s], slopes[t * heads + h] * LOG2E


def query_place(n, slots, z, d):
    lane = lax.broadcasted_iota(jnp.int32, (1, slots), 1)
    return lane * n + (z ^ d)


def key_place(n, z, tile, length, slope):
    row = lax.broadcasted_iota(jnp.int32, (TILE, 1), 0)
    places = []
    for d in range(n):
        place = (tile * TILE + row) * n + (z ^ d)
        places.append(jnp.where(place < length, place.astype(f32) * slope, FAR))
    return jnp.concatenate(places, axis=0)


def gather_rows(ref, tile, n):
    rows = pl.ds(pl.multiple_of(tile * TILE, TILE), TILE)
    return jnp.concatenate([ref[d, rows, :] for d in range(n)], axis=0)


def attend_kernel(n, heads, ids, lens, slopes, *refs):
    inputs = refs[:n]
    outs = refs[n : 2 * n]
    att_ref, den_ref = refs[2 * n], refs[2 * n + 1]
    k_s, v_s, acc, den = refs[2 * n + 2 :]
    slots = inputs[0].shape[1]
    z, length, slope = pair_scalars(n, heads, ids, lens, slopes)
    for d in range(n):
        k_s[d] = inputs[d][HD : 2 * HD, :].T
        v_s[d] = inputs[d][2 * HD : 3 * HD, :].T
    acc[...] = jnp.zeros_like(acc)
    den[...] = jnp.zeros_like(den)

    def tile_step(tile, unused):
        keys = gather_rows(k_s, tile, n)
        values = gather_rows(v_s, tile, n).T
        places = key_place(n, z, tile, length, slope)
        for d in range(n):
            cols = slice(d * slots, (d + 1) * slots)
            there = query_place(n, slots, z, d).astype(f32) * slope
            scores = dot_nn(keys, inputs[d][0:HD, :]) * (0.125 * LOG2E)
            e = jnp.exp2(scores - jnp.abs(there - places))
            den[:, cols] += jnp.sum(e, axis=0, keepdims=True)
            acc[:, cols] += dot_nn(values, e.astype(bf16))
        return unused

    step = TILE * n
    lax.fori_loop(0, (length + step - 1) // step, tile_step, 0)
    for d in range(n):
        cols = slice(d * slots, (d + 1) * slots)
        padded = jnp.where(query_place(n, slots, z, d) < length, 0.0, 1.0)
        total = den[:, cols] + padded
        att = acc[:, cols] / total
        att_ref[:, cols] = att
        den_ref[0, :, cols] = total
        outs[d][...] = att.astype(bf16)


def attend(ids, lens, slopes, blocks, n, heads, per):
    slots = blocks[0].shape[1]
    every = n * slots
    return pl.pallas_call(
        functools.partial(attend_kernel, n, heads),
        grid=(per,),
        out_shape=[shape((per * HD, slots), bf16)] * n
        + [shape((per * HD, every), f32), shape((per, 1, every), f32)],
        in_specs=[SMEM] * 3 + [pl.BlockSpec((3 * HD, slots), lambda j: (j, 0))] * n,
        out_specs=[pl.BlockSpec((HD, slots), lambda j: (j, 0))] * n
        + [
            pl.BlockSpec((HD, every), lambda j: (j, 0)),
            pl.BlockSpec((1, 1, every), lambda j: (j, 0, 0)),
        ],
        scratch_shapes=[
            pltpu.VMEM((n, slots, HD), bf16),
            pltpu.VMEM((n, slots, HD), bf16),
            pltpu.VMEM((HD, every), f32),
            pltpu.VMEM((1, every), f32),
        ],
        compiler_params=params("arbitrary"),
        cost_estimate=cost(per * every * every * HD * 8, 3e6, per * every * every),
        name="attend",
    )(ids, lens, slopes, *blocks)


def attend_back_kernel(n, heads, ids, lens, slopes, *refs):
    inputs = refs[:n]
    grads = refs[n : 2 * n]
    att_ref, den_ref = refs[2 * n], refs[2 * n + 1]
    outs = refs[2 * n + 2 : 3 * n + 2]
    k_s, v_s, q_s, g_s, dn, cor, dq, dk, dv = refs[3 * n + 2 :]
    slots = inputs[0].shape[1]
    z, length, slope = pair_scalars(n, heads, ids, lens, slopes)
    for d in range(n):
        cols = slice(d * slots, (d + 1) * slots)
        k_s[d] = inputs[d][HD : 2 * HD, :].T
        v_s[d] = inputs[d][2 * HD : 3 * HD, :].T
        q_s[d] = inputs[d][0:HD, :].T
        inverse = 1.0 / den_ref[0, :, cols]
        mixed = grads[d][...].astype(f32)
        numer = (mixed * inverse).astype(bf16)
        dn[:, cols] = numer
        g_s[d] = numer.T
        cor[:, cols] = jnp.sum(mixed * att_ref[:, cols], axis=0, keepdims=True) * inverse
    dq[...] = jnp.zeros_like(dq)
    dk[...] = jnp.zeros_like(dk)
    dv[...] = jnp.zeros_like(dv)

    def tile_step(tile, unused):
        keys = gather_rows(k_s, tile, n)
        values = gather_rows(v_s, tile, n)
        keys_t = keys.T
        places = key_place(n, z, tile, length, slope)
        grad_k = jnp.zeros((n * TILE, HD), f32)
        grad_v = jnp.zeros((n * TILE, HD), f32)
        for d in range(n):
            cols = slice(d * slots, (d + 1) * slots)
            there = query_place(n, slots, z, d).astype(f32) * slope
            scores = dot_nn(keys, inputs[d][0:HD, :]) * (0.125 * LOG2E)
            e = jnp.exp2(scores - jnp.abs(there - places))
            inner = dot_nn(values, dn[:, cols])
            ds = (e * (inner - cor[:, cols])).astype(bf16)
            dq[:, cols] += dot_nn(keys_t, ds)
            grad_k += dot_nn(ds, q_s[d])
            grad_v += dot_nn(e.astype(bf16), g_s[d])
        rows = pl.ds(pl.multiple_of(tile * TILE, TILE), TILE)
        for d in range(n):
            dk[d, rows, :] = grad_k[d * TILE : (d + 1) * TILE, :]
            dv[d, rows, :] = grad_v[d * TILE : (d + 1) * TILE, :]
        return unused

    step = TILE * n
    lax.fori_loop(0, (length + step - 1) // step, tile_step, 0)
    for d in range(n):
        cols = slice(d * slots, (d + 1) * slots)
        outs[d][0:HD, :] = (dq[:, cols] * 0.125).astype(bf16)
        outs[d][HD : 2 * HD, :] = (dk[d] * 0.125).astype(bf16).T
        outs[d][2 * HD : 3 * HD, :] = dv[d].astype(bf16).T


def attend_back(ids, lens, slopes, blocks, grads, att, den, n, heads, per):
    slots = blocks[0].shape[1]
    every = n * slots
    rows = [pltpu.VMEM((n, slots, HD), bf16)] * 4
    return pl.pallas_call(
        functools.partial(attend_back_kernel, n, heads),
        grid=(per,),
        out_shape=[shape((per * 3 * HD, slots), bf16)] * n,
        in_specs=[SMEM] * 3
        + [pl.BlockSpec((3 * HD, slots), lambda j: (j, 0))] * n
        + [pl.BlockSpec((HD, slots), lambda j: (j, 0))] * n
        + [
            pl.BlockSpec((HD, every), lambda j: (j, 0)),
            pl.BlockSpec((1, 1, every), lambda j: (j, 0, 0)),
        ],
        out_specs=[pl.BlockSpec((3 * HD, slots), lambda j: (j, 0))] * n,
        scratch_shapes=rows
        + [
            pltpu.VMEM((HD, every), bf16),
            pltpu.VMEM((1, every), f32),
            pltpu.VMEM((HD, every), f32),
            pltpu.VMEM((n, slots, HD), f32),
            pltpu.VMEM((n, slots, HD), f32),
        ],
        compiler_params=params("arbitrary"),
        cost_estimate=cost(per * every * every * HD * 20, 5e6, per * every * every),
        name="attend_back",
    )(ids, lens, slopes, *blocks, *grads, att, den)


def mix_kernel(n, seqs, heads, ids, wo, *refs):
    inputs = refs[:n]
    parts = refs[n : n + seqs]
    mixed, stage = refs[n + seqs :]
    z = ids[2]
    slots = inputs[0].shape[1]
    per = seqs * heads // n
    size = per * HD
    for d in range(n):
        stage[pl.ds(pl.multiple_of((z ^ d) * size, size), size), :] = inputs[d][...]
    for s in range(seqs):
        columns = []
        for h in range(heads):
            i = s * heads + h
            at = (i % n) * per + i // n
            columns.append(stage[at * HD : (at + 1) * HD, :])
        rows = slice(s * slots, (s + 1) * slots)
        ours = jnp.concatenate(columns, axis=0).T
        mixed[rows, :] = ours
        parts[s][...] = dot_nt(ours, wo[...]).astype(bf16)


def mix(ids, packed, blocks, n, seqs, heads):
    slots = blocks[0].shape[1]
    model = packed.shape[0]
    width = heads * HD
    tokens = seqs * slots
    return pl.pallas_call(
        functools.partial(mix_kernel, n, seqs, heads),
        grid=(1,),
        out_shape=[shape((slots, model), bf16)] * seqs + [shape((tokens, width), bf16)],
        in_specs=[SMEM, pl.BlockSpec((model, width), lambda i: (0, packed.shape[1] // width - 1))]
        + [VMEM] * n,
        out_specs=[VMEM] * (seqs + 1),
        scratch_shapes=[pltpu.VMEM((seqs * heads * HD, slots), bf16)],
        compiler_params=params("arbitrary"),
        cost_estimate=cost(2 * tokens * model * width, 3e6),
        name="mix",
    )(ids, packed, *blocks)


def unit_kernel(tok, own, other, vec, wg, wu, wd, hidden, low, act, gel, slope, part, acc):
    j = pl.program_id(0)

    @pl.when(j == 0)
    def _():
        branch = own[...].astype(f32) + other[...].astype(f32) + vec[4:5, :]
        hat, _ = normalise(tok[...].astype(f32) + branch)
        h = hat * vec[0:1, :] + vec[1:2, :]
        hidden[...] = h
        low[...] = h.astype(bf16)
        acc[...] = jnp.zeros_like(acc)

    gate = dot_nn(low[...], wg[...])
    upper = dot_nn(low[...], wu[...])
    phi = 0.5 * (1.0 + lax.erf(gate * math.sqrt(0.5)))
    density = jnp.exp(gate * gate * -0.5) * (1.0 / math.sqrt(2.0 * math.pi))
    unit = gate * phi
    acted = (unit * upper).astype(bf16)
    act[...] = acted
    gel[...] = unit.astype(bf16)
    slope[...] = (upper * (phi + gate * density)).astype(bf16)
    acc[...] += dot_nt(acted, wd[...])

    @pl.when(j == pl.num_programs(0) - 1)
    def _():
        part[...] = acc[...].astype(bf16)


def unit(s, tok, own, other, vec, front, back):
    tokens, model = own.shape
    hidden_units = back.shape[1] // 2
    steps = hidden_units // BLOCK
    fixed = lambda j: (0, 0)
    whole = pl.BlockSpec((tokens, model), fixed)
    weight = lambda start: pl.BlockSpec((model, BLOCK), lambda j: (0, start + j))
    inner = pl.BlockSpec((tokens, BLOCK), lambda j: (0, j))
    return pl.pallas_call(
        unit_kernel,
        grid=(steps,),
        out_shape=[shape((tokens, model), f32), shape((tokens, model), bf16)]
        + [shape((tokens, hidden_units), bf16)] * 3
        + [shape((tokens, model), bf16)],
        in_specs=[
            pl.BlockSpec((tokens, model), lambda j: (s, 0)),
            whole,
            whole,
            pl.BlockSpec(vec.shape, fixed),
            weight(0),
            weight(0),
            weight(steps),
        ],
        out_specs=[whole, whole, inner, inner, inner, whole],
        scratch_shapes=[pltpu.VMEM((tokens, model), f32)],
        compiler_params=params("arbitrary"),
        cost_estimate=cost(6 * tokens * model * hidden_units, 13e6, 2 * tokens * hidden_units),
        name="unit",
    )(tok, own, other, vec, front, back, back)


def unit_back_kernel(
    n, s, ids, lens, hidden, own, other, cot, vec, wg, wu, wd, gel, slope,
    output, dz2, dffn, dgate, dup, part, sums, acc,
):
    j = pl.program_id(0)

    @pl.when(j == 0)
    def _():
        live = live_mask(lens[s], ids[2], n, hidden.shape[0])
        branch = own[...].astype(f32) + other[...].astype(f32) + vec[5:6, :]
        hat, scale = normalise(hidden[...] + branch)
        output[...] = (live * (hat * vec[2:3, :] + vec[3:4, :])).astype(bf16)
        gy = cot[...].astype(f32) * live
        grad = normalise_back(gy * vec[2:3, :], hat, scale)
        dz2[...] = grad
        low = grad.astype(bf16)
        dffn[...] = low
        sums[0:1, :] = jnp.sum(gy * hat, axis=0, keepdims=True)
        sums[1:2, :] = jnp.sum(gy, axis=0, keepdims=True)
        sums[2:3, :] = jnp.sum(low.astype(f32), axis=0, keepdims=True)
        sums[3:8, :] = jnp.zeros_like(sums[3:8, :])
        acc[...] = jnp.zeros_like(acc)

    dact = dot_nn(dffn[...], wd[...])
    upper = (dact * gel[...].astype(f32)).astype(bf16)
    gate = (dact * slope[...].astype(f32)).astype(bf16)
    dgate[...] = gate
    dup[...] = upper
    acc[...] += dot_nt(gate, wg[...]) + dot_nt(upper, wu[...])

    @pl.when(j == pl.num_programs(0) - 1)
    def _():
        part[...] = acc[...].astype(bf16)


def unit_back(s, ids, lens, hidden, own, other, cot, vec, front, back, gel, slope, n):
    tokens, model = hidden.shape
    hidden_units = gel.shape[1]
    steps = hidden_units // BLOCK
    fixed = lambda j: (0, 0)
    whole = pl.BlockSpec((tokens, model), fixed)
    weight = lambda start: pl.BlockSpec((model, BLOCK), lambda j: (0, start + j))
    inner = pl.BlockSpec((tokens, BLOCK), lambda j: (0, j))
    return pl.pallas_call(
        functools.partial(unit_back_kernel, n, s),
        grid=(steps,),
        out_shape=[
            shape((tokens, model), bf16),
            shape((tokens, model), f32),
            shape((tokens, model), bf16),
            shape((tokens, hidden_units), bf16),
            shape((tokens, hidden_units), bf16),
            shape((tokens, model), bf16),
            shape((8, model), f32),
        ],
        in_specs=[SMEM, SMEM, whole, whole, whole]
        + [pl.BlockSpec((tokens, model), lambda j: (s, 0)), pl.BlockSpec(vec.shape, fixed)]
        + [weight(0), weight(0), weight(steps), inner, inner],
        out_specs=[whole, whole, whole, inner, inner, whole, pl.BlockSpec((8, model), fixed)],
        scratch_shapes=[pltpu.VMEM((tokens, model), f32)],
        compiler_params=params("arbitrary"),
        cost_estimate=cost(6 * tokens * model * hidden_units, 14e6),
        name="unit_back",
    )(ids, lens, hidden, own, other, cot, vec, front, back, back, gel, slope)


def row_starts(ids, quarter):
    y, c = ids[0], ids[1]
    keep = [(y * 2 + c) * quarter, ((1 - y) * 2 + c) * quarter]
    send = [(y * 2 + 1 - c) * quarter, ((1 - y) * 2 + 1 - c) * quarter]
    return send, keep


def arrange(ids, turned, left):
    quarter = turned.shape[0] // 4
    send, keep = row_starts(ids, quarter)
    for k, start in enumerate(send + keep):
        rows = pl.ds(pl.multiple_of(start, quarter), quarter)
        left[k * quarter : (k + 1) * quarter, :] = turned[rows, :]


def write_rows(left, right, send, keep):
    grad = dot_nn(left[...], right).astype(bf16)
    half = grad.shape[0] // 2
    send[0:half, :] = grad[:half]
    keep[0:half, :] = grad[half:]


def weight_kernel(steps, seqs, ids, *refs):
    low, dffn, dgate, dup, act = (refs[i * seqs : (i + 1) * seqs] for i in range(5))
    send, keep, left, turned = refs[5 * seqs :]
    j = pl.program_id(0)
    joined = lambda group: jnp.concatenate([ref[...] for ref in group], axis=0)

    @pl.when(j == 0)
    def _():
        for k, group in enumerate((low, dffn)):
            turned[...] = joined(group).T
            arrange(ids, turned, left.at[k])

    @pl.when(j < steps)
    def _():
        write_rows(left.at[0], joined(dgate), send, keep)

    @pl.when((j >= steps) & (j < 2 * steps))
    def _():
        write_rows(left.at[0], joined(dup), send, keep)

    @pl.when(j >= 2 * steps)
    def _():
        write_rows(left.at[1], joined(act), send, keep)


def weight_grads(ids, low, dffn, dgate, dup, act):
    seqs = len(low)
    tokens, model = low[0].shape
    hidden_units = act[0].shape[1]
    steps = hidden_units // BLOCK
    whole = pl.BlockSpec((tokens, model), lambda j: (0, 0))
    column = lambda start: pl.BlockSpec(
        (tokens, BLOCK), lambda j: (0, jnp.clip(j - start, 0, steps - 1))
    )
    out = pl.BlockSpec((model // 2, BLOCK), lambda j: (0, j))
    return pl.pallas_call(
        functools.partial(weight_kernel, steps, seqs),
        grid=(3 * steps,),
        out_shape=[shape((model // 2, 3 * hidden_units + WIDTH), bf16)] * 2,
        in_specs=[SMEM]
        + [whole] * (2 * seqs)
        + [column(0)] * seqs
        + [column(steps)] * seqs
        + [column(2 * steps)] * seqs,
        out_specs=[out, out],
        scratch_shapes=[
            pltpu.VMEM((2, model, tokens * seqs), bf16),
            pltpu.VMEM((model, tokens * seqs), bf16),
        ],
        compiler_params=params("arbitrary"),
        cost_estimate=cost(6 * tokens * seqs * model * hidden_units, 14e6),
        name="weight_grads",
    )(ids, *low, *dffn, *dgate, *dup, *act)


def mix_back_kernel(n, seqs, heads, ids, tok, vec, wo, mixed, far, near, *refs):
    own, other, dz2, hown, hother = (refs[i * seqs : (i + 1) * seqs] for i in range(5))
    refs = refs[5 * seqs :]
    sends = refs[:n]
    dz1, send, keep, sums = refs[n : n + 4]
    stage, left, turned_low = refs[n + 4 :]
    z = ids[2]
    slots = sends[0].shape[1]
    per = seqs * heads // n
    sums[...] = jnp.zeros_like(sums)
    for s in range(seqs):
        rows = slice(s * slots, (s + 1) * slots)
        branch = own[s][...].astype(f32) + other[s][...].astype(f32) + vec[4:5, :]
        hat, scale = normalise(tok[rows, :].astype(f32) + branch)
        gh = dz2[s][...] + (hown[s][...].astype(f32) + hother[s][...].astype(f32))
        grad = normalise_back(gh * vec[0:1, :], hat, scale)
        dz1[rows, :] = grad
        low = grad.astype(bf16)
        sums[0:1, :] += jnp.sum(gh * hat, axis=0, keepdims=True)
        sums[1:2, :] += jnp.sum(gh, axis=0, keepdims=True)
        sums[2:3, :] += jnp.sum(low.astype(f32), axis=0, keepdims=True)
        turned_low[:, rows] = low.T
        turned = dot_nn(low, wo[...]).astype(bf16).T
        for h in range(heads):
            i = s * heads + h
            at = (i % n) * per + i // n
            stage[at * HD : (at + 1) * HD, :] = turned[h * HD : (h + 1) * HD, :]
    size = per * HD
    for d in range(n):
        sends[d][...] = stage[pl.ds(pl.multiple_of((z ^ d) * size, size), size), :]
    arrange(ids, turned_low, left)
    write_rows(left, mixed[...], send, keep)


def mix_back(ids, tok, vec, front, mixed, grads, own, other, dz2, hown, hother, n, heads):
    seqs = len(own)
    tokens, model = tok.shape
    slots = tokens // seqs
    width = heads * HD
    size = seqs * heads // n * HD
    last = pl.BlockSpec((model // 2, width), lambda i: (0, grads[0].shape[1] // width - 1))
    return pl.pallas_call(
        functools.partial(mix_back_kernel, n, seqs, heads),
        grid=(1,),
        out_shape=[shape((size, slots), bf16)] * n
        + [shape((tokens, model), f32)]
        + [shape(grads[0].shape, bf16)] * 2
        + [shape((8, model), f32)],
        in_specs=[SMEM, VMEM, VMEM]
        + [pl.BlockSpec((model, width), lambda i: (0, front.shape[1] // width - 1)), VMEM]
        + [pl.BlockSpec(memory_space=pl.ANY)] * 2
        + [VMEM] * (5 * seqs),
        out_specs=[VMEM] * (n + 1) + [last, last, VMEM],
        input_output_aliases={5: n + 1, 6: n + 2},
        scratch_shapes=[
            pltpu.VMEM((size * n, slots), bf16),
            pltpu.VMEM((model, tokens), bf16),
            pltpu.VMEM((model, tokens), bf16),
        ],
        compiler_params=params("arbitrary"),
        cost_estimate=cost(4 * tokens * model * width, 10e6),
        name="mix_back",
    )(ids, tok, vec, front, mixed, *grads, *own, *other, *dz2, *hown, *hother)


def project_back_kernel(n, seqs, heads, ids, tok, whole, small, *refs):
    inputs = refs[:n]
    part, send, keep = refs[n : n + 3]
    stage, right, left, turned = refs[n + 3 :]
    z = ids[2]
    slots = inputs[0].shape[1]
    per = seqs * heads // n
    width = heads * HD
    size = per * 3 * HD
    for d in range(n):
        stage[pl.ds(pl.multiple_of((z ^ d) * size, size), size), :] = inputs[d][...]
    for s in range(seqs):
        for c in range(3):
            columns = []
            for h in range(heads):
                i = s * heads + h
                at = ((i % n) * per + i // n) * 3 + c
                columns.append(stage[at * HD : (at + 1) * HD, :])
            ours = jnp.concatenate(columns, axis=0).T
            right[s * slots : (s + 1) * slots, c * width : (c + 1) * width] = ours
    part[...] = dot_nt(right[...], whole[...]).astype(bf16)
    turned[...] = tok[...].T
    arrange(ids, turned, left)
    for c in range(3):
        cols = slice(c * width, (c + 1) * width)
        write_rows(left, right[:, cols], send.at[:, cols], keep.at[:, cols])
    ones = jnp.ones((8, right.shape[0]), bf16)
    sums = dot_nn(ones, right[...])
    line = jnp.concatenate([sums[:, :width], sums[:, 2 * width :]], axis=1)
    row = lax.broadcasted_iota(jnp.int32, (8, 1), 0)
    rows = jnp.where(row == 6, line, small[...])
    rows = jnp.concatenate([rows, jnp.zeros_like(rows)], axis=0).astype(bf16)
    for ref in (send, keep):
        ref[ref.shape[0] - EXTRA :, :] = jnp.zeros((EXTRA, ref.shape[1]), bf16)
        ref[ref.shape[0] - EXTRA :, : 2 * width] = rows


def project_back(ids, tok, whole, small, blocks, n, seqs, heads):
    tokens, model = tok.shape
    slots = tokens // seqs
    wide = whole.shape[1]
    return pl.pallas_call(
        functools.partial(project_back_kernel, n, seqs, heads),
        out_shape=[
            shape((tokens, model), bf16),
            shape((model // 2 + EXTRA, wide), bf16),
            shape((model // 2 + EXTRA, wide), bf16),
        ],
        in_specs=[SMEM] + [VMEM] * (3 + n),
        out_specs=[VMEM] * 3,
        scratch_shapes=[
            pltpu.VMEM((seqs * heads * 3 * HD, slots), bf16),
            pltpu.VMEM((tokens, wide), bf16),
            pltpu.VMEM((model, tokens), bf16),
            pltpu.VMEM((model, tokens), bf16),
        ],
        compiler_params=params(),
        cost_estimate=cost(4 * tokens * model * wide, 8e6),
        name="project_back",
    )(ids, tok, whole, small, *blocks)


def fold_core_kernel(extra, keep, recv, mine, send):
    half = (keep.shape[0] - extra) // 2
    mine[0:half, :] = keep[0:half, :].astype(f32) + recv[0:half, :].astype(f32)
    rest = (keep[half:, :].astype(f32) + recv[half:, :].astype(f32)).astype(bf16)
    send[...] = rest
    if extra:
        mine[half:, :] = rest[half:, :].astype(f32)


def fold_core(keep, recv, extra):
    rows, wide = keep.shape
    out = (rows - extra) // 2 + extra
    steps = 1 if extra else 3
    column = lambda size: pl.BlockSpec((size, wide // steps), lambda j: (0, j))
    return pl.pallas_call(
        functools.partial(fold_core_kernel, extra),
        grid=(steps,),
        out_shape=[shape((out, wide), f32), shape((out, wide), bf16)],
        in_specs=[column(rows)] * 2,
        out_specs=[column(out)] * 2,
        compiler_params=params("arbitrary"),
        cost_estimate=cost(rows * wide, 7 * rows * wide),
        name="fold_core",
    )(keep, recv)


def fold_y_kernel(n, extra, ids, mine, recv, own, *refs):
    sends, stage = refs[:-1], refs[-1]
    z = ids[2]
    rows = mine.shape[0] - extra
    size = rows // n
    stage[...] = mine[...] + recv[...].astype(f32)
    for d in range(n):
        block = stage[pl.ds(pl.multiple_of((z ^ d) * size, size), size), :]
        if d:
            sends[d - 1][0:size, :] = block.astype(bf16)
            if extra:
                sends[d - 1][size:, :] = stage[rows:, :].astype(bf16)
        else:
            own[0:size, :] = block
            if extra:
                own[size:, :] = stage[rows:, :].astype(bf16).astype(f32)


def fold_y(ids, mine, recv, n, extra):
    rows, wide = mine.shape
    out = (rows - extra) // n + extra
    steps = 1 if extra else 3
    column = lambda size: pl.BlockSpec((size, wide // steps), lambda j: (0, j))
    return pl.pallas_call(
        functools.partial(fold_y_kernel, n, extra),
        grid=(steps,),
        out_shape=[shape((out, wide), f32)] + [shape((out, wide), bf16)] * (n - 1),
        in_specs=[SMEM] + [column(rows)] * 2,
        out_specs=[column(out)] * n,
        scratch_shapes=[pltpu.VMEM((rows, wide // steps), f32)],
        compiler_params=params("arbitrary"),
        cost_estimate=cost(rows * wide, 9 * rows * wide),
        name="fold_y",
    )(ids, mine, recv)


def fold_z(own, got):
    return (own + got[0].astype(f32)) + (got[1].astype(f32) + got[2].astype(f32))


def fits(tokens, b_qv, w_qkv, w_gu):
    n = lax.axis_size("ctx")
    heads = b_qv.shape[1] // HD
    return (
        n == 4
        and lax.axis_size("shard") == 4
        and lax.axis_size("tp") == 2
        and (tokens.shape[0] * heads) % n == 0
        and w_qkv.shape[0] % 16 == 0
        and tokens.shape[1] % 256 == 0
        and b_qv.shape[1] == WIDTH
        and w_gu.shape[2] % BLOCK == 0
        and w_gu.shape[2] % WIDTH == 0
    )


def on_device(tokens, lengths, w_qkv, b_qv, w_out, w_gu, w_down, vectors, cotangent):
    if not fits(tokens, b_qv, w_qkv, w_gu):
        return by_gather(tokens, lengths, w_qkv, b_qv, w_out, w_gu, w_down, vectors, cotangent)
    n = lax.axis_size("ctx")
    seqs, slots, model = tokens.shape
    width = b_qv.shape[1]
    heads = width // HD
    per = seqs * heads // n
    units = w_gu.shape[2]
    rows = w_qkv.shape[0]
    count = seqs * slots
    shard = lax.axis_index("shard")
    ids = jnp.stack(
        [shard // 2, shard % 2, lax.axis_index("ctx"), lax.axis_index("tp")]
    ).astype(jnp.int32)
    slopes = jnp.asarray(slope_table())
    tok = tokens.reshape(count, model)
    cot = cotangent.reshape(count, model)

    first = [w_qkv.astype(bf16).reshape(rows, 3 * width)]
    first += [swap(first[0], "ctx", d) for d in range(1, n)]
    first += [swap(piece, "shard", 2) for piece in first]
    by_core = [swap(piece, "shard", 1) for piece in first]
    pieces = first[:n] + by_core[:n] + first[n:] + by_core[n:]
    front = jnp.concatenate([w_gu[:, 0], w_out.T], axis=1).astype(bf16)
    back = jnp.concatenate([w_gu[:, 1], w_down.T], axis=1).astype(bf16)
    front, pieces[0] = lax.optimization_barrier((front, pieces[0]))
    front = lax.all_gather(front, ("shard", "ctx"), axis=0, tiled=True)

    bias = jnp.concatenate([b_qv[0], jnp.zeros_like(b_qv[0]), b_qv[1]])[None, :]
    *sends, whole = project(ids, tok, bias, pieces, n, seqs, heads)
    blocks = [sends[0]] + [swap(sends[d], "ctx", d) for d in range(1, n)]
    *blocks, back = lax.optimization_barrier((*blocks, back))
    back = lax.all_gather(back, ("shard", "ctx"), axis=0, tiled=True)
    *outs, att, den = attend(ids, lengths, slopes, blocks, n, heads, per)
    outs = [outs[0]] + [swap(outs[d], "ctx", d) for d in range(1, n)]
    *part, mixed = mix(ids, front, outs, n, seqs, heads)
    part_other = [swap(value, "tp", 1) for value in part]
    hidden, low, act, gel, slope, ffn = zip(
        *(
            unit(s, tok, part[s], part_other[s], vectors, front, back)
            for s in range(seqs)
        )
    )
    ffn_other = [swap(value, "tp", 1) for value in ffn]
    output, dz2, dffn, dgate, dup, dlow, sums_two = zip(
        *(
            unit_back(
                s, ids, lengths, hidden[s], ffn[s], ffn_other[s], cot, vectors, front, back,
                gel[s], slope[s], n,
            )
            for s in range(seqs)
        )
    )
    dlow_other = [swap(value, "tp", 1) for value in dlow]
    unit_grads = weight_grads(ids, low, dffn, dgate, dup, act)
    *dlow_other, far, near = lax.optimization_barrier((*dlow_other, *unit_grads))
    *sends, dz1, far, near, sums_one = mix_back(
        ids, tok, vectors, front, mixed, (far, near), part, part_other, dz2, dlow, dlow_other,
        n, heads,
    )
    sums_two = sum(sums_two)
    grads = [sends[0]] + [swap(sends[d], "ctx", d) for d in range(1, n)]
    got = swap(far, "shard", 1)
    mine, far = fold_core(near, got, 0)
    *grads, far = lax.optimization_barrier((*grads, far))
    got = swap(far, "shard", 2)
    outs = attend_back(ids, lengths, slopes, blocks, grads, att, den, n, heads, per)
    outs = [outs[0]] + [swap(outs[d], "ctx", d) for d in range(1, n)]
    *outs, got = lax.optimization_barrier((*outs, got))
    rest_own, *rest_sends = fold_y(ids, mine, got, n, 0)
    *outs, rest_own = lax.optimization_barrier((*outs, rest_own))
    small = jnp.concatenate(
        [sums_one[0:2], sums_two[0:2], sums_one[2:3], sums_two[2:3], jnp.zeros_like(sums_one[:2])]
    )
    dx, far, near = project_back(ids, tok, whole, small, outs, n, seqs, heads)
    got = swap(far, "shard", 1)
    dx_other = swap(dx, "tp", 1)
    mine, far = fold_core(near, got, EXTRA)
    got = swap(far, "shard", 2)
    own, *sends = fold_y(ids, mine, got, n, EXTRA)
    rest_got = [swap(block, "ctx", d + 1) for d, block in enumerate(rest_sends)]
    got = [swap(block, "ctx", d + 1) for d, block in enumerate(sends)]
    *rest_got, got[0] = lax.optimization_barrier((*rest_got, got[0]))
    rest = fold_z(rest_own, rest_got)
    last = fold_z(own, got)
    input_grad = dz1 + (dx.astype(f32) + dx_other.astype(f32))
    small = last[rows : rows + 8, : 2 * width]
    return (
        jnp.stack(output),
        input_grad.reshape(tokens.shape),
        last[:rows].reshape(w_qkv.shape),
        small[6].reshape(2, width),
        rest[:, 3 * units :].T,
        rest[:, : 2 * units].reshape(w_gu.shape),
        rest[:, 2 * units : 3 * units].T,
        small[:6],
    )


def alibi_slopes(first_head, head_count):
    power = 2 ** (H.bit_length() - 1)
    heads_index = first_head + jnp.arange(head_count, dtype=jnp.int32)
    early = -8.0 * (heads_index + 1).astype(jnp.float32) / power
    later = -4.0 * (2 * (heads_index - power) + 1).astype(jnp.float32) / power
    return jnp.exp2(jnp.where(heads_index < power, early, later))


def layer_norm(values, gain, shift):
    centred = values - jnp.mean(values, axis=-1, keepdims=True)
    spread = jnp.mean(centred * centred, axis=-1, keepdims=True)
    return centred * lax.rsqrt(spread + epsilon) * gain + shift


def gated_unit(gate_input, upper):
    return jax.nn.gelu(gate_input, approximate=False) * upper


def score_block(query_heads, key_heads, query_place, key_place, slopes, lengths):
    scores = (
        jnp.einsum("sqhe,skhe->shqk", query_heads, key_heads, preferred_element_type=jnp.float32)
        * 0.125
    )
    distance = jnp.abs(query_place[:, None] - key_place[None, :]).astype(jnp.float32)
    scores = scores - slopes[None, :, None, None] * distance[None, None]
    usable = key_place[None, :] < lengths[:, None]
    return jnp.where(usable[:, None, None, :], jnp.exp(scores), 0.0)


def backward_scores(
    query_heads,
    numer_heads,
    correction,
    key_heads,
    value_heads,
    query_place,
    key_place,
    slopes,
    lengths,
):
    weights = score_block(query_heads, key_heads, query_place, key_place, slopes, lengths)
    value_dots = jnp.einsum(
        "sqhe,skhe->shqk", numer_heads, value_heads, preferred_element_type=jnp.float32
    )
    grad_scores = (weights * (value_dots - correction[..., None])).astype(jnp.bfloat16)
    return (weights.astype(jnp.bfloat16), grad_scores)


def split_blocks(shard_piece, slot_count, ctx_count):
    piece_rows = shard_piece.shape[1]
    block_rows = math.gcd(piece_rows, 128)
    block_count = piece_rows // block_rows
    shaped = shard_piece.reshape(
        (shard_piece.shape[0], block_count, block_rows) + shard_piece.shape[2:]
    )
    blocks = jnp.moveaxis(shaped, 1, 0)
    row_ids = jnp.arange(piece_rows, dtype=jnp.int32)
    places = (row_ids % slot_count * ctx_count + row_ids // slot_count).reshape(
        block_count, block_rows
    )
    offsets = block_rows * jnp.arange(block_count, dtype=jnp.int32)
    return (blocks, places, offsets)


def by_gather(tokens, lengths, w_qkv, b_qv, w_out, w_gu, w_down, vectors, cotangent):
    ctx_count = lax.axis_size("ctx")
    ctx_rank = lax.axis_index("ctx")
    seq_count, slot_count, model_width = tokens.shape
    local_width = b_qv.shape[1]
    head_count = local_width // HD
    slopes = alibi_slopes(lax.axis_index("tp") * head_count, head_count)
    slot_ids = jnp.arange(slot_count, dtype=jnp.int32)
    query_place = slot_ids * ctx_count + ctx_rank
    query_live = (query_place[None, :] < lengths[:, None]).astype(jnp.float32)
    live_rows = query_live[:, :, None]
    head_shape = (seq_count, slot_count, head_count, HD)
    whole_qkv, whole_out, whole_gu, whole_down = (
        lax.all_gather(w_qkv.astype(jnp.bfloat16), ("shard", "ctx"), axis=0, tiled=True),
        lax.all_gather(w_out.astype(jnp.bfloat16), ("shard", "ctx"), axis=1, tiled=True),
        lax.all_gather(w_gu.astype(jnp.bfloat16), ("shard", "ctx"), axis=0, tiled=True),
        lax.all_gather(w_down.astype(jnp.bfloat16), ("shard", "ctx"), axis=1, tiled=True),
    )
    inputs = tokens.astype(jnp.float32)
    projected = jnp.einsum("std,dcm->stcm", tokens, whole_qkv, preferred_element_type=jnp.float32)
    query_rows = (projected[:, :, 0] + b_qv[0]).astype(jnp.bfloat16)
    key_rows = projected[:, :, 1].astype(jnp.bfloat16)
    value_rows = (projected[:, :, 2] + b_qv[1]).astype(jnp.bfloat16)
    query_heads = query_rows.reshape(head_shape)
    pairs = jnp.stack([key_rows, value_rows], axis=2)
    start_numer = jnp.zeros((seq_count, head_count, slot_count, HD), jnp.float32)
    start_denom = jnp.zeros((seq_count, head_count, slot_count), jnp.float32)
    blocks, places, offsets = split_blocks(
        lax.all_gather(pairs, "ctx", axis=1, tiled=True), slot_count, ctx_count
    )

    def forward_advance(inner_state, block_item):
        key_block, key_place, row_offset = block_item
        numerator, denominator = inner_state
        key_heads = key_block[:, :, 0].reshape(seq_count, -1, head_count, HD)
        value_heads = key_block[:, :, 1].reshape(seq_count, -1, head_count, HD)
        weights = score_block(query_heads, key_heads, query_place, key_place, slopes, lengths)
        numerator = numerator + jnp.einsum(
            "shqk,skhe->shqe",
            weights.astype(jnp.bfloat16),
            value_heads,
            preferred_element_type=jnp.float32,
        )
        return ((numerator, denominator + jnp.sum(weights, axis=-1)), None)

    result_state, unused = lax.scan(
        forward_advance, (start_numer, start_denom), (blocks, places, offsets)
    )
    numerator, denominator = result_state
    denominator = denominator + (1.0 - query_live)[:, None, :]
    attention_q = jnp.transpose(numerator / denominator[..., None], (0, 2, 1, 3))
    denom_q = jnp.transpose(denominator, (0, 2, 1))
    mixed = attention_q.reshape(seq_count, slot_count, local_width).astype(jnp.bfloat16)
    attn_part = jnp.einsum("stm,mn->stn", mixed, whole_out, preferred_element_type=jnp.float32)
    attn_branch = lax.psum(attn_part, "tp") + vectors[4]
    hidden, first_pull = jax.vjp(layer_norm, inputs + attn_branch, vectors[0], vectors[1])
    hidden_low = hidden.astype(jnp.bfloat16)
    gated = jnp.einsum("std,dcf->stcf", hidden_low, whole_gu, preferred_element_type=jnp.float32)
    activated, unit_pull = jax.vjp(gated_unit, gated[:, :, 0], gated[:, :, 1])
    act_low = activated.astype(jnp.bfloat16)
    ffn_part = jnp.einsum("stf,fn->stn", act_low, whole_down, preferred_element_type=jnp.float32)
    ffn_branch = lax.psum(ffn_part, "tp") + vectors[5]
    normed, second_pull = jax.vjp(layer_norm, hidden + ffn_branch, vectors[2], vectors[3])
    output = (normed * live_rows).astype(jnp.bfloat16)
    upstream = cotangent.astype(jnp.float32) * live_rows
    grad_second, grad_gain_two, grad_shift_two = second_pull(upstream)
    grad_ffn = grad_second.astype(jnp.bfloat16)
    grad_down = jnp.einsum("stf,stn->fn", act_low, grad_ffn, preferred_element_type=jnp.float32)
    grad_ffn_bias = jnp.sum(grad_ffn.astype(jnp.float32), axis=(0, 1))
    grad_act = jnp.einsum("stn,fn->stf", grad_ffn, whole_down, preferred_element_type=jnp.float32)
    grad_gate, grad_upper = unit_pull(grad_act)
    grad_gated = jnp.stack([grad_gate, grad_upper], axis=2).astype(jnp.bfloat16)
    grad_gu = jnp.einsum(
        "std,stcf->dcf", hidden_low, grad_gated, preferred_element_type=jnp.float32
    )
    hidden_part = jnp.einsum(
        "stcf,dcf->std", grad_gated, whole_gu, preferred_element_type=jnp.float32
    )
    grad_hidden = grad_second + lax.psum(hidden_part, "tp")
    grad_first, grad_gain_one, grad_shift_one = first_pull(grad_hidden)
    grad_attn = grad_first.astype(jnp.bfloat16)
    grad_out = jnp.einsum("stm,stn->mn", mixed, grad_attn, preferred_element_type=jnp.float32)
    grad_out_bias = jnp.sum(grad_attn.astype(jnp.float32), axis=(0, 1))
    grad_mixed = jnp.einsum(
        "stn,mn->stm", grad_attn, whole_out, preferred_element_type=jnp.float32
    ).astype(jnp.bfloat16)
    grad_mixed_heads = grad_mixed.reshape(head_shape).astype(jnp.float32)
    correction = jnp.transpose(
        jnp.sum(grad_mixed_heads * attention_q, axis=-1) / denom_q, (0, 2, 1)
    )
    numer_heads = (grad_mixed_heads / denom_q[..., None]).astype(jnp.bfloat16)
    start_query = jnp.zeros(head_shape, jnp.float32)
    start_state = (
        start_query,
        jnp.zeros((seq_count, slot_count * ctx_count, 2, local_width), jnp.float32),
    )
    blocks, places, offsets = split_blocks(
        lax.all_gather(pairs, "ctx", axis=1, tiled=True), slot_count, ctx_count
    )

    def backward_advance(current_state, block_item):
        key_block, key_place, row_offset = block_item
        key_heads = key_block[:, :, 0].reshape(seq_count, -1, head_count, HD)
        value_heads = key_block[:, :, 1].reshape(seq_count, -1, head_count, HD)
        weights_low, grad_scores = backward_scores(
            query_heads,
            numer_heads,
            correction,
            key_heads,
            value_heads,
            query_place,
            key_place,
            slopes,
            lengths,
        )
        grad_query = current_state[0] + jnp.einsum(
            "shqk,skhe->sqhe", grad_scores, key_heads, preferred_element_type=jnp.float32
        )
        grad_key = (
            jnp.einsum(
                "shqk,sqhe->skhe", grad_scores, query_heads, preferred_element_type=jnp.float32
            )
            * 0.125
        )
        grad_value = jnp.einsum(
            "shqk,sqhe->skhe", weights_low, numer_heads, preferred_element_type=jnp.float32
        )
        stacked = jnp.stack(
            [
                grad_key.reshape(seq_count, -1, local_width),
                grad_value.reshape(seq_count, -1, local_width),
            ],
            axis=2,
        )
        buffer = lax.dynamic_update_slice_in_dim(current_state[1], stacked, row_offset, axis=1)
        return ((grad_query, buffer), None)

    result_state, unused = lax.scan(backward_advance, start_state, (blocks, places, offsets))
    grad_pairs = lax.psum_scatter(
        result_state[1].astype(jnp.bfloat16), "ctx", scatter_dimension=1, tiled=True
    )
    grad_query_low = (
        (result_state[0] * 0.125).astype(jnp.bfloat16).reshape(seq_count, slot_count, local_width)
    )
    grad_proj = jnp.concatenate([grad_query_low[:, :, None], grad_pairs], axis=2)
    grad_qkv = jnp.einsum("std,stcm->dcm", tokens, grad_proj, preferred_element_type=jnp.float32)
    bias_terms = jnp.stack(
        [
            jnp.sum(grad_query_low.astype(jnp.float32), axis=(0, 1)),
            jnp.sum(grad_pairs[:, :, 1].astype(jnp.float32), axis=(0, 1)),
        ]
    )
    input_part = jnp.einsum(
        "stcm,dcm->std", grad_proj, whole_qkv, preferred_element_type=jnp.float32
    )
    input_grad = grad_first + lax.psum(input_part.astype(jnp.bfloat16), "tp").astype(jnp.float32)
    grad_weights = (
        lax.psum_scatter(grad_qkv, ("shard", "ctx"), scatter_dimension=0, tiled=True),
        lax.psum_scatter(grad_out, ("shard", "ctx"), scatter_dimension=1, tiled=True),
        lax.psum_scatter(grad_gu, ("shard", "ctx"), scatter_dimension=0, tiled=True),
        lax.psum_scatter(grad_down, ("shard", "ctx"), scatter_dimension=1, tiled=True),
    )
    vector_terms = jnp.stack(
        [grad_gain_one, grad_shift_one, grad_gain_two, grad_shift_two, grad_out_bias, grad_ffn_bias]
    )
    grad_bqv, grad_vectors = lax.psum((bias_terms, vector_terms), ("shard", "ctx"))
    return (
        output,
        input_grad,
        grad_weights[0],
        grad_bqv,
        grad_weights[1],
        grad_weights[2],
        grad_weights[3],
        grad_vectors,
    )


def solution(mesh):
    placed = (
        P("shard", "ctx", None),
        P("shard"),
        P(("shard", "ctx"), None, "tp"),
        P(None, "tp"),
        P("tp", ("shard", "ctx")),
        P(("shard", "ctx"), None, "tp"),
        P("tp", ("shard", "ctx")),
        P(),
        P("shard", "ctx", None),
    )
    return jax.shard_map(
        on_device,
        mesh=mesh,
        in_specs=placed,
        out_specs=(
            P("shard", "ctx", None),
            P("shard", "ctx", None),
            P(("shard", "ctx"), None, "tp"),
            P(None, "tp"),
            P("tp", ("shard", "ctx")),
            P(("shard", "ctx"), None, "tp"),
            P("tp", ("shard", "ctx")),
            P(),
        ),
        check_vma=False,
    )
```

```python
import functools
import math

import jax
import jax.numpy as jnp
import numpy as np
from jax import lax
from jax.experimental import pallas as pl
from jax.experimental.pallas import tpu as pltpu
from jax.sharding import PartitionSpec as P

H = 12
HD = 64
LOG2E = math.log2(math.e)
FAR = 1e30
TILE = 64
BLOCK = 512
WIDTH = 384
EXTRA = 16

epsilon = 1e-12
f32 = jnp.float32
bf16 = jnp.bfloat16
VMEM = pl.BlockSpec(memory_space=pltpu.VMEM)
SMEM = pl.BlockSpec(memory_space=pltpu.SMEM)


def slope_table():
    power = 2 ** (H.bit_length() - 1)
    heads = np.arange(H)
    early = -8.0 * (heads + 1) / power
    later = -4.0 * (2 * (heads - power) + 1) / power
    return np.exp2(np.where(heads < power, early, later)).astype(np.float32)


def dot_nn(a, b):
    return jnp.dot(a, b, preferred_element_type=f32)


def dot_nt(a, b):
    return lax.dot_general(a, b, (((1,), (1,)), ((), ())), preferred_element_type=f32)


def params(*semantics):
    return pltpu.CompilerParams(
        dimension_semantics=semantics or None, vmem_limit_bytes=56 * 1024 * 1024
    )


def cost(flops, nbytes, exps=0):
    return pl.CostEstimate(flops=int(flops), bytes_accessed=int(nbytes), transcendentals=int(exps))


def shape(dims, dtype):
    return jax.ShapeDtypeStruct(dims, dtype)


def xor_pairs(axis, distance):
    return [(i, i ^ distance) for i in range(lax.axis_size(axis))]


def swap(value, axis, distance):
    return lax.ppermute(value, axis, xor_pairs(axis, distance))


def after(values, *done):
    return lax.optimization_barrier((*values, *done))[: len(values)]


def live_mask(length, rank, n_ctx, slots):
    slot = lax.broadcasted_iota(jnp.int32, (slots, 1), 0)
    return jnp.where(slot * n_ctx + rank < length, 1.0, 0.0).astype(f32)


def normalise(z):
    centred = z - jnp.mean(z, axis=-1, keepdims=True)
    spread = jnp.mean(centred * centred, axis=-1, keepdims=True)
    scale = lax.rsqrt(spread + epsilon)
    return centred * scale, scale


def normalise_back(grad_hat, hat, scale):
    inner = jnp.mean(grad_hat * hat, axis=-1, keepdims=True)
    return scale * (grad_hat - jnp.mean(grad_hat, axis=-1, keepdims=True) - hat * inner)


def assemble_kernel(n, ids, *refs):
    pieces, whole = refs[:4], refs[4]
    y, c, z = ids[0], ids[1], ids[2]
    rows = pieces[0].shape[0] // n
    for k in range(4):
        for kz in range(n):
            index = ((y ^ (k // 2)) * 2 + (c ^ (k % 2))) * n + (z ^ kz)
            place = pl.ds(pl.multiple_of(index * rows, rows), rows)
            whole[place, :] = pieces[k][kz * rows : (kz + 1) * rows, :]


def assemble(ids, pieces, n):
    rows, wide = pieces[0].shape
    column = lambda size: pl.BlockSpec((size, wide // 3), lambda j: (0, j))
    return pl.pallas_call(
        functools.partial(assemble_kernel, n),
        grid=(3,),
        out_shape=shape((4 * rows, wide), bf16),
        in_specs=[SMEM] + [column(rows)] * 4,
        out_specs=column(4 * rows),
        compiler_params=params("arbitrary"),
        cost_estimate=cost(0, 16 * rows * wide),
        name="assemble",
    )(ids, *pieces)


def project_kernel(n, seqs, heads, ids, tok, bias, *refs):
    pieces = refs[: 4 * n]
    sends = refs[4 * n : 5 * n]
    whole = refs[5 * n]
    stage = refs[5 * n + 1]
    y, c, z = ids[0], ids[1], ids[2]
    rows = pieces[0].shape[0]
    for k in range(4 * n):
        ky, kc, kz = k // (2 * n), k // n % 2, k % n
        index = ((y ^ ky) * 2 + (c ^ kc)) * n + (z ^ kz)
        whole[pl.ds(pl.multiple_of(index * rows, rows), rows), :] = pieces[k][...]
    slots = sends[0].shape[1]
    width = heads * HD
    per = seqs * heads // n
    for s in range(seqs):
        acc = dot_nn(tok[s * slots : (s + 1) * slots, :], whole[...]) + bias[...]
        turned = acc.astype(bf16).T
        for h in range(heads):
            i = s * heads + h
            at = ((i % n) * per + i // n) * 3
            for part in range(3):
                first = part * width + h * HD
                stage[(at + part) * HD : (at + part + 1) * HD, :] = turned[first : first + HD, :]
    size = per * 3 * HD
    for d in range(n):
        sends[d][...] = stage[pl.ds(pl.multiple_of((z ^ d) * size, size), size), :]


def project(ids, tok, bias, pieces, n, seqs, heads):
    slots = tok.shape[0] // seqs
    size = seqs * heads // n * 3 * HD
    model, wide = tok.shape[1], bias.shape[1]
    return pl.pallas_call(
        functools.partial(project_kernel, n, seqs, heads),
        out_shape=[shape((size, slots), bf16)] * n + [shape((model, wide), bf16)],
        in_specs=[SMEM] + [VMEM] * (2 + len(pieces)),
        out_specs=[VMEM] * (n + 1),
        scratch_shapes=[pltpu.VMEM((size * n, slots), bf16)],
        compiler_params=params(),
        cost_estimate=cost(2 * tok.shape[0] * model * wide, 6e6),
        name="project",
    )(ids, tok, bias, *pieces)


def pair_scalars(n, heads, ids, lens, slopes):
    j = pl.program_id(0)
    z, t = ids[2], ids[3]
    i = z + n * j
    s = i // heads
    h = i - s * heads
    return z, lens[s], slopes[t * heads + h] * LOG2E


def query_place(n, slots, z, d):
    lane = lax.broadcasted_iota(jnp.int32, (1, slots), 1)
    return lane * n + (z ^ d)


def key_place(n, z, tile, length, slope):
    row = lax.broadcasted_iota(jnp.int32, (TILE, 1), 0)
    places = []
    for d in range(n):
        place = (tile * TILE + row) * n + (z ^ d)
        places.append(jnp.where(place < length, place.astype(f32) * slope, FAR))
    return jnp.concatenate(places, axis=0)


def gather_rows(ref, tile, n):
    rows = pl.ds(pl.multiple_of(tile * TILE, TILE), TILE)
    return jnp.concatenate([ref[d, rows, :] for d in range(n)], axis=0)


def attend_kernel(n, heads, ids, lens, slopes, *refs):
    inputs = refs[:n]
    outs = refs[n : 2 * n]
    att_ref, den_ref = refs[2 * n], refs[2 * n + 1]
    k_s, v_s, acc, den = refs[2 * n + 2 :]
    slots = inputs[0].shape[1]
    z, length, slope = pair_scalars(n, heads, ids, lens, slopes)
    for d in range(n):
        k_s[d] = inputs[d][HD : 2 * HD, :].T
        v_s[d] = inputs[d][2 * HD : 3 * HD, :].T
    acc[...] = jnp.zeros_like(acc)
    den[...] = jnp.zeros_like(den)

    def tile_step(tile, unused):
        keys = gather_rows(k_s, tile, n)
        values = gather_rows(v_s, tile, n).T
        places = key_place(n, z, tile, length, slope)
        for d in range(n):
            cols = slice(d * slots, (d + 1) * slots)
            there = query_place(n, slots, z, d).astype(f32) * slope
            scores = dot_nn(keys, inputs[d][0:HD, :]) * (0.125 * LOG2E)
            e = jnp.exp2(scores - jnp.abs(there - places))
            den[:, cols] += jnp.sum(e, axis=0, keepdims=True)
            acc[:, cols] += dot_nn(values, e.astype(bf16))
        return unused

    step = TILE * n
    lax.fori_loop(0, (length + step - 1) // step, tile_step, 0)
    for d in range(n):
        cols = slice(d * slots, (d + 1) * slots)
        padded = jnp.where(query_place(n, slots, z, d) < length, 0.0, 1.0)
        total = den[:, cols] + padded
        att = acc[:, cols] / total
        att_ref[:, cols] = att
        den_ref[0, :, cols] = total
        outs[d][...] = att.astype(bf16)


def attend(ids, lens, slopes, blocks, n, heads, per):
    slots = blocks[0].shape[1]
    every = n * slots
    return pl.pallas_call(
        functools.partial(attend_kernel, n, heads),
        grid=(per,),
        out_shape=[shape((per * HD, slots), bf16)] * n
        + [shape((per * HD, every), f32), shape((per, 1, every), f32)],
        in_specs=[SMEM] * 3 + [pl.BlockSpec((3 * HD, slots), lambda j: (j, 0))] * n,
        out_specs=[pl.BlockSpec((HD, slots), lambda j: (j, 0))] * n
        + [
            pl.BlockSpec((HD, every), lambda j: (j, 0)),
            pl.BlockSpec((1, 1, every), lambda j: (j, 0, 0)),
        ],
        scratch_shapes=[
            pltpu.VMEM((n, slots, HD), bf16),
            pltpu.VMEM((n, slots, HD), bf16),
            pltpu.VMEM((HD, every), f32),
            pltpu.VMEM((1, every), f32),
        ],
        compiler_params=params("arbitrary"),
        cost_estimate=cost(per * every * every * HD * 8, 3e6, per * every * every),
        name="attend",
    )(ids, lens, slopes, *blocks)


def attend_back_kernel(n, heads, ids, lens, slopes, *refs):
    inputs = refs[:n]
    grads = refs[n : 2 * n]
    att_ref, den_ref = refs[2 * n], refs[2 * n + 1]
    outs = refs[2 * n + 2 : 3 * n + 2]
    k_s, v_s, q_s, g_s, dn, cor, dq, dk, dv = refs[3 * n + 2 :]
    slots = inputs[0].shape[1]
    z, length, slope = pair_scalars(n, heads, ids, lens, slopes)
    for d in range(n):
        cols = slice(d * slots, (d + 1) * slots)
        k_s[d] = inputs[d][HD : 2 * HD, :].T
        v_s[d] = inputs[d][2 * HD : 3 * HD, :].T
        q_s[d] = inputs[d][0:HD, :].T
        inverse = 1.0 / den_ref[0, :, cols]
        mixed = grads[d][...].astype(f32)
        numer = (mixed * inverse).astype(bf16)
        dn[:, cols] = numer
        g_s[d] = numer.T
        cor[:, cols] = jnp.sum(mixed * att_ref[:, cols], axis=0, keepdims=True) * inverse
    dq[...] = jnp.zeros_like(dq)
    dk[...] = jnp.zeros_like(dk)
    dv[...] = jnp.zeros_like(dv)

    def tile_step(tile, unused):
        keys = gather_rows(k_s, tile, n)
        values = gather_rows(v_s, tile, n)
        keys_t = keys.T
        places = key_place(n, z, tile, length, slope)
        grad_k = jnp.zeros((n * TILE, HD), f32)
        grad_v = jnp.zeros((n * TILE, HD), f32)
        for d in range(n):
            cols = slice(d * slots, (d + 1) * slots)
            there = query_place(n, slots, z, d).astype(f32) * slope
            scores = dot_nn(keys, inputs[d][0:HD, :]) * (0.125 * LOG2E)
            e = jnp.exp2(scores - jnp.abs(there - places))
            inner = dot_nn(values, dn[:, cols])
            ds = (e * (inner - cor[:, cols])).astype(bf16)
            dq[:, cols] += dot_nn(keys_t, ds)
            grad_k += dot_nn(ds, q_s[d])
            grad_v += dot_nn(e.astype(bf16), g_s[d])
        rows = pl.ds(pl.multiple_of(tile * TILE, TILE), TILE)
        for d in range(n):
            dk[d, rows, :] = grad_k[d * TILE : (d + 1) * TILE, :]
            dv[d, rows, :] = grad_v[d * TILE : (d + 1) * TILE, :]
        return unused

    step = TILE * n
    lax.fori_loop(0, (length + step - 1) // step, tile_step, 0)
    for d in range(n):
        cols = slice(d * slots, (d + 1) * slots)
        outs[d][0:HD, :] = (dq[:, cols] * 0.125).astype(bf16)
        outs[d][HD : 2 * HD, :] = (dk[d] * 0.125).astype(bf16).T
        outs[d][2 * HD : 3 * HD, :] = dv[d].astype(bf16).T


def attend_back(ids, lens, slopes, blocks, grads, att, den, n, heads, per):
    slots = blocks[0].shape[1]
    every = n * slots
    rows = [pltpu.VMEM((n, slots, HD), bf16)] * 4
    return pl.pallas_call(
        functools.partial(attend_back_kernel, n, heads),
        grid=(per,),
        out_shape=[shape((per * 3 * HD, slots), bf16)] * n,
        in_specs=[SMEM] * 3
        + [pl.BlockSpec((3 * HD, slots), lambda j: (j, 0))] * n
        + [pl.BlockSpec((HD, slots), lambda j: (j, 0))] * n
        + [
            pl.BlockSpec((HD, every), lambda j: (j, 0)),
            pl.BlockSpec((1, 1, every), lambda j: (j, 0, 0)),
        ],
        out_specs=[pl.BlockSpec((3 * HD, slots), lambda j: (j, 0))] * n,
        scratch_shapes=rows
        + [
            pltpu.VMEM((HD, every), bf16),
            pltpu.VMEM((1, every), f32),
            pltpu.VMEM((HD, every), f32),
            pltpu.VMEM((n, slots, HD), f32),
            pltpu.VMEM((n, slots, HD), f32),
        ],
        compiler_params=params("arbitrary"),
        cost_estimate=cost(per * every * every * HD * 20, 5e6, per * every * every),
        name="attend_back",
    )(ids, lens, slopes, *blocks, *grads, att, den)


def mix_kernel(n, seqs, heads, ids, wo, *refs):
    inputs = refs[:n]
    parts = refs[n : n + seqs]
    mixed, stage = refs[n + seqs :]
    z = ids[2]
    slots = inputs[0].shape[1]
    per = seqs * heads // n
    size = per * HD
    for d in range(n):
        stage[pl.ds(pl.multiple_of((z ^ d) * size, size), size), :] = inputs[d][...]
    for s in range(seqs):
        columns = []
        for h in range(heads):
            i = s * heads + h
            at = (i % n) * per + i // n
            columns.append(stage[at * HD : (at + 1) * HD, :])
        rows = slice(s * slots, (s + 1) * slots)
        ours = jnp.concatenate(columns, axis=0).T
        mixed[rows, :] = ours
        parts[s][...] = dot_nt(ours, wo[...]).astype(bf16)


def mix(ids, packed, blocks, n, seqs, heads):
    slots = blocks[0].shape[1]
    model = packed.shape[0]
    width = heads * HD
    tokens = seqs * slots
    return pl.pallas_call(
        functools.partial(mix_kernel, n, seqs, heads),
        grid=(1,),
        out_shape=[shape((slots, model), bf16)] * seqs + [shape((tokens, width), bf16)],
        in_specs=[SMEM, pl.BlockSpec((model, width), lambda i: (0, packed.shape[1] // width - 1))]
        + [VMEM] * n,
        out_specs=[VMEM] * (seqs + 1),
        scratch_shapes=[pltpu.VMEM((seqs * heads * HD, slots), bf16)],
        compiler_params=params("arbitrary"),
        cost_estimate=cost(2 * tokens * model * width, 3e6),
        name="mix",
    )(ids, packed, *blocks)


def unit_kernel(tok, own, other, vec, wg, wu, wd, hidden, low, act, gel, slope, part, acc):
    j = pl.program_id(0)

    @pl.when(j == 0)
    def _():
        branch = own[...].astype(f32) + other[...].astype(f32) + vec[4:5, :]
        hat, _ = normalise(tok[...].astype(f32) + branch)
        h = hat * vec[0:1, :] + vec[1:2, :]
        hidden[...] = h
        low[...] = h.astype(bf16)
        acc[...] = jnp.zeros_like(acc)

    gate = dot_nn(low[...], wg[...])
    upper = dot_nn(low[...], wu[...])
    phi = 0.5 * (1.0 + lax.erf(gate * math.sqrt(0.5)))
    density = jnp.exp(gate * gate * -0.5) * (1.0 / math.sqrt(2.0 * math.pi))
    unit = gate * phi
    acted = (unit * upper).astype(bf16)
    act[...] = acted
    gel[...] = unit.astype(bf16)
    slope[...] = (upper * (phi + gate * density)).astype(bf16)
    acc[...] += dot_nt(acted, wd[...])

    @pl.when(j == pl.num_programs(0) - 1)
    def _():
        part[...] = acc[...].astype(bf16)


def unit(s, tok, own, other, vec, front, back):
    tokens, model = own.shape
    hidden_units = back.shape[1]
    steps = hidden_units // BLOCK
    fixed = lambda j: (0, 0)
    whole = pl.BlockSpec((tokens, model), fixed)
    weight = lambda start: pl.BlockSpec((model, BLOCK), lambda j: (0, start + j))
    inner = pl.BlockSpec((tokens, BLOCK), lambda j: (0, j))
    return pl.pallas_call(
        unit_kernel,
        grid=(steps,),
        out_shape=[shape((tokens, model), f32), shape((tokens, model), bf16)]
        + [shape((tokens, hidden_units), bf16)] * 3
        + [shape((tokens, model), bf16)],
        in_specs=[
            pl.BlockSpec((tokens, model), lambda j: (s, 0)),
            whole,
            whole,
            pl.BlockSpec(vec.shape, fixed),
            weight(0),
            weight(steps),
            weight(0),
        ],
        out_specs=[whole, whole, inner, inner, inner, whole],
        scratch_shapes=[pltpu.VMEM((tokens, model), f32)],
        compiler_params=params("arbitrary"),
        cost_estimate=cost(6 * tokens * model * hidden_units, 13e6, 2 * tokens * hidden_units),
        name="unit",
    )(tok, own, other, vec, front, front, back)


def unit_back_kernel(
    n, s, ids, lens, hidden, own, other, cot, vec, wg, wu, wd, gel, slope,
    output, dz2, dffn, dgate, dup, part, sums, acc,
):
    j = pl.program_id(0)

    @pl.when(j == 0)
    def _():
        live = live_mask(lens[s], ids[2], n, hidden.shape[0])
        branch = own[...].astype(f32) + other[...].astype(f32) + vec[5:6, :]
        hat, scale = normalise(hidden[...] + branch)
        output[...] = (live * (hat * vec[2:3, :] + vec[3:4, :])).astype(bf16)
        gy = cot[...].astype(f32) * live
        grad = normalise_back(gy * vec[2:3, :], hat, scale)
        dz2[...] = grad
        low = grad.astype(bf16)
        dffn[...] = low
        sums[0:1, :] = jnp.sum(gy * hat, axis=0, keepdims=True)
        sums[1:2, :] = jnp.sum(gy, axis=0, keepdims=True)
        sums[2:3, :] = jnp.sum(low.astype(f32), axis=0, keepdims=True)
        sums[3:8, :] = jnp.zeros_like(sums[3:8, :])
        acc[...] = jnp.zeros_like(acc)

    dact = dot_nn(dffn[...], wd[...])
    upper = (dact * gel[...].astype(f32)).astype(bf16)
    gate = (dact * slope[...].astype(f32)).astype(bf16)
    dgate[...] = gate
    dup[...] = upper
    acc[...] += dot_nt(gate, wg[...]) + dot_nt(upper, wu[...])

    @pl.when(j == pl.num_programs(0) - 1)
    def _():
        part[...] = acc[...].astype(bf16)


def unit_back(s, ids, lens, hidden, own, other, cot, vec, front, back, gel, slope, n):
    tokens, model = hidden.shape
    hidden_units = gel.shape[1]
    steps = hidden_units // BLOCK
    fixed = lambda j: (0, 0)
    whole = pl.BlockSpec((tokens, model), fixed)
    weight = lambda start: pl.BlockSpec((model, BLOCK), lambda j: (0, start + j))
    inner = pl.BlockSpec((tokens, BLOCK), lambda j: (0, j))
    return pl.pallas_call(
        functools.partial(unit_back_kernel, n, s),
        grid=(steps,),
        out_shape=[
            shape((tokens, model), bf16),
            shape((tokens, model), f32),
            shape((tokens, model), bf16),
            shape((tokens, hidden_units), bf16),
            shape((tokens, hidden_units), bf16),
            shape((tokens, model), bf16),
            shape((8, model), f32),
        ],
        in_specs=[SMEM, SMEM, whole, whole, whole]
        + [pl.BlockSpec((tokens, model), lambda j: (s, 0)), pl.BlockSpec(vec.shape, fixed)]
        + [weight(0), weight(steps), weight(0), inner, inner],
        out_specs=[whole, whole, whole, inner, inner, whole, pl.BlockSpec((8, model), fixed)],
        scratch_shapes=[pltpu.VMEM((tokens, model), f32)],
        compiler_params=params("arbitrary"),
        cost_estimate=cost(6 * tokens * model * hidden_units, 14e6),
        name="unit_back",
    )(ids, lens, hidden, own, other, cot, vec, front, front, back, gel, slope)


def row_starts(ids, quarter):
    y, c = ids[0], ids[1]
    keep = [(y * 2 + c) * quarter, ((1 - y) * 2 + c) * quarter]
    send = [(y * 2 + 1 - c) * quarter, ((1 - y) * 2 + 1 - c) * quarter]
    return send, keep


def arrange(ids, turned, left):
    quarter = turned.shape[0] // 4
    send, keep = row_starts(ids, quarter)
    for k, start in enumerate(send + keep):
        rows = pl.ds(pl.multiple_of(start, quarter), quarter)
        left[k * quarter : (k + 1) * quarter, :] = turned[rows, :]


def write_rows(left, right, send, keep):
    grad = dot_nn(left[...], right).astype(bf16)
    half = grad.shape[0] // 2
    send[0:half, :] = grad[:half]
    keep[0:half, :] = grad[half:]


def weight_kernel(steps, seqs, ids, *refs):
    low, dffn, dgate, dup, act = (refs[i * seqs : (i + 1) * seqs] for i in range(5))
    send, keep, left, turned = refs[5 * seqs :]
    j = pl.program_id(0)
    joined = lambda group: jnp.concatenate([ref[...] for ref in group], axis=0)

    @pl.when(j == 0)
    def _():
        for k, group in enumerate((low, dffn)):
            turned[...] = joined(group).T
            arrange(ids, turned, left.at[k])

    @pl.when(j < steps)
    def _():
        write_rows(left.at[0], joined(dgate), send, keep)

    @pl.when((j >= steps) & (j < 2 * steps))
    def _():
        write_rows(left.at[0], joined(dup), send, keep)

    @pl.when(j >= 2 * steps)
    def _():
        write_rows(left.at[1], joined(act), send, keep)


def weight_grads(ids, low, dffn, dgate, dup, act):
    seqs = len(low)
    tokens, model = low[0].shape
    hidden_units = act[0].shape[1]
    steps = hidden_units // BLOCK
    whole = pl.BlockSpec((tokens, model), lambda j: (0, 0))
    column = lambda start: pl.BlockSpec(
        (tokens, BLOCK), lambda j: (0, jnp.clip(j - start, 0, steps - 1))
    )
    out = pl.BlockSpec((model // 2, BLOCK), lambda j: (0, j))
    return pl.pallas_call(
        functools.partial(weight_kernel, steps, seqs),
        grid=(3 * steps,),
        out_shape=[shape((model // 2, 3 * hidden_units), bf16)] * 2,
        in_specs=[SMEM]
        + [whole] * (2 * seqs)
        + [column(0)] * seqs
        + [column(steps)] * seqs
        + [column(2 * steps)] * seqs,
        out_specs=[out, out],
        scratch_shapes=[
            pltpu.VMEM((2, model, tokens * seqs), bf16),
            pltpu.VMEM((model, tokens * seqs), bf16),
        ],
        compiler_params=params("arbitrary"),
        cost_estimate=cost(6 * tokens * seqs * model * hidden_units, 14e6),
        name="weight_grads",
    )(ids, *low, *dffn, *dgate, *dup, *act)


def mix_back_kernel(n, seqs, heads, ids, tok, vec, wo, mixed, *refs):
    own, other, dz2, hown, hother = (refs[i * seqs : (i + 1) * seqs] for i in range(5))
    refs = refs[5 * seqs :]
    sends = refs[:n]
    dz1, send, keep, sums = refs[n : n + 4]
    stage, left, turned_low = refs[n + 4 :]
    z = ids[2]
    slots = sends[0].shape[1]
    per = seqs * heads // n
    sums[...] = jnp.zeros_like(sums)
    for s in range(seqs):
        rows = slice(s * slots, (s + 1) * slots)
        branch = own[s][...].astype(f32) + other[s][...].astype(f32) + vec[4:5, :]
        hat, scale = normalise(tok[rows, :].astype(f32) + branch)
        gh = dz2[s][...] + (hown[s][...].astype(f32) + hother[s][...].astype(f32))
        grad = normalise_back(gh * vec[0:1, :], hat, scale)
        dz1[rows, :] = grad
        low = grad.astype(bf16)
        sums[0:1, :] += jnp.sum(gh * hat, axis=0, keepdims=True)
        sums[1:2, :] += jnp.sum(gh, axis=0, keepdims=True)
        sums[2:3, :] += jnp.sum(low.astype(f32), axis=0, keepdims=True)
        turned_low[:, rows] = low.T
        turned = dot_nn(low, wo[...]).astype(bf16).T
        for h in range(heads):
            i = s * heads + h
            at = (i % n) * per + i // n
            stage[at * HD : (at + 1) * HD, :] = turned[h * HD : (h + 1) * HD, :]
    size = per * HD
    for d in range(n):
        sends[d][...] = stage[pl.ds(pl.multiple_of((z ^ d) * size, size), size), :]
    arrange(ids, turned_low, left)
    write_rows(left, mixed[...], send, keep)
    for ref in (send, keep):
        ref[ref.shape[0] - EXTRA :, :] = jnp.zeros((EXTRA, ref.shape[1]), bf16)


def mix_back(ids, tok, vec, front, mixed, own, other, dz2, hown, hother, n, heads):
    seqs = len(own)
    tokens, model = tok.shape
    slots = tokens // seqs
    width = heads * HD
    size = seqs * heads // n * HD
    rows = model // 2 + EXTRA
    last = pl.BlockSpec((rows, width), lambda i: (0, 3))
    return pl.pallas_call(
        functools.partial(mix_back_kernel, n, seqs, heads),
        grid=(1,),
        out_shape=[shape((size, slots), bf16)] * n
        + [shape((tokens, model), f32)]
        + [shape((rows, 4 * width), bf16)] * 2
        + [shape((8, model), f32)],
        in_specs=[SMEM, VMEM, VMEM]
        + [pl.BlockSpec((model, width), lambda i: (0, front.shape[1] // width - 1)), VMEM]
        + [VMEM] * (5 * seqs),
        out_specs=[VMEM] * (n + 1) + [last, last, VMEM],
        scratch_shapes=[
            pltpu.VMEM((size * n, slots), bf16),
            pltpu.VMEM((model, tokens), bf16),
            pltpu.VMEM((model, tokens), bf16),
        ],
        compiler_params=params("arbitrary"),
        cost_estimate=cost(4 * tokens * model * width, 10e6),
        name="mix_back",
    )(ids, tok, vec, front, mixed, *own, *other, *dz2, *hown, *hother)


def project_back_kernel(n, seqs, heads, ids, tok, whole, small, far, near, *refs):
    inputs = refs[:n]
    part, send, keep = refs[n : n + 3]
    stage, right, left, turned = refs[n + 3 :]
    z = ids[2]
    slots = inputs[0].shape[1]
    per = seqs * heads // n
    width = heads * HD
    size = per * 3 * HD
    for d in range(n):
        stage[pl.ds(pl.multiple_of((z ^ d) * size, size), size), :] = inputs[d][...]
    for s in range(seqs):
        for c in range(3):
            columns = []
            for h in range(heads):
                i = s * heads + h
                at = ((i % n) * per + i // n) * 3 + c
                columns.append(stage[at * HD : (at + 1) * HD, :])
            ours = jnp.concatenate(columns, axis=0).T
            right[s * slots : (s + 1) * slots, c * width : (c + 1) * width] = ours
    part[...] = dot_nt(right[...], whole[...]).astype(bf16)
    turned[...] = tok[...].T
    arrange(ids, turned, left)
    for c in range(3):
        cols = slice(c * width, (c + 1) * width)
        write_rows(left, right[:, cols], send.at[:, cols], keep.at[:, cols])
    ones = jnp.ones((8, right.shape[0]), bf16)
    sums = dot_nn(ones, right[...])
    line = jnp.concatenate([sums[:, :width], sums[:, 2 * width :]], axis=1)
    row = lax.broadcasted_iota(jnp.int32, (8, 1), 0)
    rows = jnp.where(row == 6, line, small[...])
    rows = jnp.concatenate([rows, jnp.zeros_like(rows)], axis=0).astype(bf16)
    for ref in (send, keep):
        ref[ref.shape[0] - EXTRA :, :] = jnp.zeros((EXTRA, ref.shape[1]), bf16)
        ref[ref.shape[0] - EXTRA :, : 2 * width] = rows


def project_back(ids, tok, whole, small, grads, blocks, n, seqs, heads):
    tokens, model = tok.shape
    slots = tokens // seqs
    wide = whole.shape[1]
    return pl.pallas_call(
        functools.partial(project_back_kernel, n, seqs, heads),
        grid=(1,),
        out_shape=[shape((tokens, model), bf16)] + [shape(grads[0].shape, bf16)] * 2,
        in_specs=[SMEM] + [VMEM] * 3 + [pl.BlockSpec(memory_space=pl.ANY)] * 2 + [VMEM] * n,
        out_specs=[VMEM] + [pl.BlockSpec((grads[0].shape[0], wide), lambda i: (0, 0))] * 2,
        input_output_aliases={4: 1, 5: 2},
        scratch_shapes=[
            pltpu.VMEM((seqs * heads * 3 * HD, slots), bf16),
            pltpu.VMEM((tokens, wide), bf16),
            pltpu.VMEM((model, tokens), bf16),
            pltpu.VMEM((model, tokens), bf16),
        ],
        compiler_params=params("arbitrary"),
        cost_estimate=cost(4 * tokens * model * wide, 8e6),
        name="project_back",
    )(ids, tok, whole, small, *grads, *blocks)


def fold_core_kernel(extra, keep, recv, mine, send):
    half = (keep.shape[0] - extra) // 2
    mine[0:half, :] = keep[0:half, :].astype(f32) + recv[0:half, :].astype(f32)
    rest = (keep[half:, :].astype(f32) + recv[half:, :].astype(f32)).astype(bf16)
    send[...] = rest
    if extra:
        mine[half:, :] = rest[half:, :].astype(f32)


def fold_core(keep, recv, extra):
    rows, wide = keep.shape
    out = (rows - extra) // 2 + extra
    steps = 1 if extra else 3
    column = lambda size: pl.BlockSpec((size, wide // steps), lambda j: (0, j))
    return pl.pallas_call(
        functools.partial(fold_core_kernel, extra),
        grid=(steps,),
        out_shape=[shape((out, wide), f32), shape((out, wide), bf16)],
        in_specs=[column(rows)] * 2,
        out_specs=[column(out)] * 2,
        compiler_params=params("arbitrary"),
        cost_estimate=cost(rows * wide, 7 * rows * wide),
        name="fold_core",
    )(keep, recv)


def fold_y_kernel(n, extra, ids, mine, recv, own, *refs):
    sends, stage = refs[:-1], refs[-1]
    z = ids[2]
    rows = mine.shape[0] - extra
    size = rows // n
    stage[...] = mine[...] + recv[...].astype(f32)
    for d in range(n):
        block = stage[pl.ds(pl.multiple_of((z ^ d) * size, size), size), :]
        if d:
            sends[d - 1][0:size, :] = block.astype(bf16)
            if extra:
                sends[d - 1][size:, :] = stage[rows:, :].astype(bf16)
        else:
            own[0:size, :] = block
            if extra:
                own[size:, :] = stage[rows:, :].astype(bf16).astype(f32)


def fold_y(ids, mine, recv, n, extra):
    rows, wide = mine.shape
    out = (rows - extra) // n + extra
    steps = 1 if extra else 3
    column = lambda size: pl.BlockSpec((size, wide // steps), lambda j: (0, j))
    return pl.pallas_call(
        functools.partial(fold_y_kernel, n, extra),
        grid=(steps,),
        out_shape=[shape((out, wide), f32)] + [shape((out, wide), bf16)] * (n - 1),
        in_specs=[SMEM] + [column(rows)] * 2,
        out_specs=[column(out)] * n,
        scratch_shapes=[pltpu.VMEM((rows, wide // steps), f32)],
        compiler_params=params("arbitrary"),
        cost_estimate=cost(rows * wide, 9 * rows * wide),
        name="fold_y",
    )(ids, mine, recv)


def fold_z(own, got):
    return (own + got[0].astype(f32)) + (got[1].astype(f32) + got[2].astype(f32))


def fits(tokens, b_qv, w_qkv, w_gu):
    n = lax.axis_size("ctx")
    heads = b_qv.shape[1] // HD
    return (
        n == 4
        and lax.axis_size("shard") == 4
        and lax.axis_size("tp") == 2
        and (tokens.shape[0] * heads) % n == 0
        and w_qkv.shape[0] % 16 == 0
        and tokens.shape[1] % 256 == 0
        and b_qv.shape[1] == WIDTH
        and w_gu.shape[2] % BLOCK == 0
        and w_gu.shape[2] % WIDTH == 0
    )


def on_device(tokens, lengths, w_qkv, b_qv, w_out, w_gu, w_down, vectors, cotangent):
    if not fits(tokens, b_qv, w_qkv, w_gu):
        return by_gather(tokens, lengths, w_qkv, b_qv, w_out, w_gu, w_down, vectors, cotangent)
    n = lax.axis_size("ctx")
    seqs, slots, model = tokens.shape
    width = b_qv.shape[1]
    heads = width // HD
    per = seqs * heads // n
    units = w_gu.shape[2]
    rows = w_qkv.shape[0]
    count = seqs * slots
    shard = lax.axis_index("shard")
    ids = jnp.stack(
        [shard // 2, shard % 2, lax.axis_index("ctx"), lax.axis_index("tp")]
    ).astype(jnp.int32)
    slopes = jnp.asarray(slope_table())
    tok = tokens.reshape(count, model)
    cot = cotangent.reshape(count, model)

    first = [w_qkv.astype(bf16).reshape(rows, 3 * width)]
    first += [swap(first[0], "ctx", d) for d in range(1, n)]
    first += [swap(piece, "shard", 2) for piece in first]
    by_core = [swap(piece, "shard", 1) for piece in first]
    pieces = first[:n] + by_core[:n] + first[n:] + by_core[n:]
    front = jnp.concatenate([w_gu.reshape(rows, 2 * units), w_out.T], axis=1).astype(bf16)
    back = w_down.T.astype(bf16)
    (front,) = after([front], *pieces[1:n])
    front = [front] + [swap(front, "ctx", d) for d in range(1, n)]

    bias = jnp.concatenate([b_qv[0], jnp.zeros_like(b_qv[0]), b_qv[1]])[None, :]
    *sends, whole = project(ids, tok, bias, pieces, n, seqs, heads)
    blocks = [sends[0]] + [swap(sends[d], "ctx", d) for d in range(1, n)]
    front = jnp.concatenate(after(front, whole), axis=0)
    front_y = swap(front, "shard", 2)
    (back,) = after([back], *blocks)
    back = [back] + [swap(back, "ctx", d) for d in range(1, n)]
    *outs, att, den = attend(ids, lengths, slopes, blocks, n, heads, per)
    front, front_y = after([front, front_y], outs[0])
    front = [front, swap(front, "shard", 1), front_y, swap(front_y, "shard", 1)]
    back = jnp.concatenate(after(back, outs[0]), axis=0)
    back_y = swap(back, "shard", 2)
    outs = [outs[0]] + [swap(outs[d], "ctx", d) for d in range(1, n)]
    front = assemble(ids, front, n)
    *part, mixed = mix(ids, front, outs, n, seqs, heads)
    part_other = [swap(value, "tp", 1) for value in part]
    back, back_y = after([back, back_y], part[0])
    back = [back, swap(back, "shard", 1), back_y, swap(back_y, "shard", 1)]
    back = assemble(ids, back, n)
    hidden, low, act, gel, slope, ffn = zip(
        *(
            unit(s, tok, part[s], part_other[s], vectors, front, back)
            for s in range(seqs)
        )
    )
    ffn_other = [swap(value, "tp", 1) for value in ffn]
    output, dz2, dffn, dgate, dup, dlow, sums_two = zip(
        *(
            unit_back(
                s, ids, lengths, hidden[s], ffn[s], ffn_other[s], cot, vectors, front, back,
                gel[s], slope[s], n,
            )
            for s in range(seqs)
        )
    )
    dlow_other = [swap(value, "tp", 1) for value in dlow]
    far, near = weight_grads(ids, low, dffn, dgate, dup, act)
    *dlow_other, far = lax.optimization_barrier((*dlow_other, far))
    got = swap(far, "shard", 1)
    *sends, dz1, last_far, last_near, sums_one = mix_back(
        ids, tok, vectors, front, mixed, part, part_other, dz2, dlow, dlow_other, n, heads
    )
    sums_two = sum(sums_two)
    grads = [sends[0]] + [swap(sends[d], "ctx", d) for d in range(1, n)]
    got, sends[0] = lax.optimization_barrier((got, sends[0]))
    mine, far = fold_core(near, got, 0)
    *grads, far = lax.optimization_barrier((*grads, far))
    got = swap(far, "shard", 2)
    outs = attend_back(ids, lengths, slopes, blocks, grads, att, den, n, heads, per)
    outs = [outs[0]] + [swap(outs[d], "ctx", d) for d in range(1, n)]
    rest_own, *rest_sends = fold_y(ids, mine, got, n, 0)
    *outs, rest_own = lax.optimization_barrier((*outs, rest_own))
    small = jnp.concatenate(
        [sums_one[0:2], sums_two[0:2], sums_one[2:3], sums_two[2:3], jnp.zeros_like(sums_one[:2])]
    )
    dx, far, near = project_back(
        ids, tok, whole, small, (last_far, last_near), outs, n, seqs, heads
    )
    got = swap(far, "shard", 1)
    dx_other = swap(dx, "tp", 1)
    mine, far = fold_core(near, got, EXTRA)
    got = swap(far, "shard", 2)
    rest_got = [swap(block, "ctx", d + 1) for d, block in enumerate(rest_sends)]
    *rest_got, got = lax.optimization_barrier((*rest_got, got))
    own, *sends = fold_y(ids, mine, got, n, EXTRA)
    got = [swap(block, "ctx", d + 1) for d, block in enumerate(sends)]
    rest = fold_z(rest_own, rest_got)
    last = fold_z(own, got)
    input_grad = dz1 + (dx.astype(f32) + dx_other.astype(f32))
    small = last[rows : rows + 8, : 2 * width]
    return (
        jnp.stack(output),
        input_grad.reshape(tokens.shape),
        last[:rows, : 3 * width].reshape(w_qkv.shape),
        small[6].reshape(2, width),
        last[:rows, 3 * width :].T,
        rest[:, : 2 * units].reshape(w_gu.shape),
        rest[:, 2 * units :].T,
        small[:6],
    )


def alibi_slopes(first_head, head_count):
    power = 2 ** (H.bit_length() - 1)
    heads_index = first_head + jnp.arange(head_count, dtype=jnp.int32)
    early = -8.0 * (heads_index + 1).astype(jnp.float32) / power
    later = -4.0 * (2 * (heads_index - power) + 1).astype(jnp.float32) / power
    return jnp.exp2(jnp.where(heads_index < power, early, later))


def layer_norm(values, gain, shift):
    centred = values - jnp.mean(values, axis=-1, keepdims=True)
    spread = jnp.mean(centred * centred, axis=-1, keepdims=True)
    return centred * lax.rsqrt(spread + epsilon) * gain + shift


def gated_unit(gate_input, upper):
    return jax.nn.gelu(gate_input, approximate=False) * upper


def score_block(query_heads, key_heads, query_place, key_place, slopes, lengths):
    scores = (
        jnp.einsum("sqhe,skhe->shqk", query_heads, key_heads, preferred_element_type=jnp.float32)
        * 0.125
    )
    distance = jnp.abs(query_place[:, None] - key_place[None, :]).astype(jnp.float32)
    scores = scores - slopes[None, :, None, None] * distance[None, None]
    usable = key_place[None, :] < lengths[:, None]
    return jnp.where(usable[:, None, None, :], jnp.exp(scores), 0.0)


def backward_scores(
    query_heads,
    numer_heads,
    correction,
    key_heads,
    value_heads,
    query_place,
    key_place,
    slopes,
    lengths,
):
    weights = score_block(query_heads, key_heads, query_place, key_place, slopes, lengths)
    value_dots = jnp.einsum(
        "sqhe,skhe->shqk", numer_heads, value_heads, preferred_element_type=jnp.float32
    )
    grad_scores = (weights * (value_dots - correction[..., None])).astype(jnp.bfloat16)
    return (weights.astype(jnp.bfloat16), grad_scores)


def split_blocks(shard_piece, slot_count, ctx_count):
    piece_rows = shard_piece.shape[1]
    block_rows = math.gcd(piece_rows, 128)
    block_count = piece_rows // block_rows
    shaped = shard_piece.reshape(
        (shard_piece.shape[0], block_count, block_rows) + shard_piece.shape[2:]
    )
    blocks = jnp.moveaxis(shaped, 1, 0)
    row_ids = jnp.arange(piece_rows, dtype=jnp.int32)
    places = (row_ids % slot_count * ctx_count + row_ids // slot_count).reshape(
        block_count, block_rows
    )
    offsets = block_rows * jnp.arange(block_count, dtype=jnp.int32)
    return (blocks, places, offsets)


def by_gather(tokens, lengths, w_qkv, b_qv, w_out, w_gu, w_down, vectors, cotangent):
    ctx_count = lax.axis_size("ctx")
    ctx_rank = lax.axis_index("ctx")
    seq_count, slot_count, model_width = tokens.shape
    local_width = b_qv.shape[1]
    head_count = local_width // HD
    slopes = alibi_slopes(lax.axis_index("tp") * head_count, head_count)
    slot_ids = jnp.arange(slot_count, dtype=jnp.int32)
    query_place = slot_ids * ctx_count + ctx_rank
    query_live = (query_place[None, :] < lengths[:, None]).astype(jnp.float32)
    live_rows = query_live[:, :, None]
    head_shape = (seq_count, slot_count, head_count, HD)
    whole_qkv, whole_out, whole_gu, whole_down = (
        lax.all_gather(w_qkv.astype(jnp.bfloat16), ("shard", "ctx"), axis=0, tiled=True),
        lax.all_gather(w_out.astype(jnp.bfloat16), ("shard", "ctx"), axis=1, tiled=True),
        lax.all_gather(w_gu.astype(jnp.bfloat16), ("shard", "ctx"), axis=0, tiled=True),
        lax.all_gather(w_down.astype(jnp.bfloat16), ("shard", "ctx"), axis=1, tiled=True),
    )
    inputs = tokens.astype(jnp.float32)
    projected = jnp.einsum("std,dcm->stcm", tokens, whole_qkv, preferred_element_type=jnp.float32)
    query_rows = (projected[:, :, 0] + b_qv[0]).astype(jnp.bfloat16)
    key_rows = projected[:, :, 1].astype(jnp.bfloat16)
    value_rows = (projected[:, :, 2] + b_qv[1]).astype(jnp.bfloat16)
    query_heads = query_rows.reshape(head_shape)
    pairs = jnp.stack([key_rows, value_rows], axis=2)
    start_numer = jnp.zeros((seq_count, head_count, slot_count, HD), jnp.float32)
    start_denom = jnp.zeros((seq_count, head_count, slot_count), jnp.float32)
    blocks, places, offsets = split_blocks(
        lax.all_gather(pairs, "ctx", axis=1, tiled=True), slot_count, ctx_count
    )

    def forward_advance(inner_state, block_item):
        key_block, key_place, row_offset = block_item
        numerator, denominator = inner_state
        key_heads = key_block[:, :, 0].reshape(seq_count, -1, head_count, HD)
        value_heads = key_block[:, :, 1].reshape(seq_count, -1, head_count, HD)
        weights = score_block(query_heads, key_heads, query_place, key_place, slopes, lengths)
        numerator = numerator + jnp.einsum(
            "shqk,skhe->shqe",
            weights.astype(jnp.bfloat16),
            value_heads,
            preferred_element_type=jnp.float32,
        )
        return ((numerator, denominator + jnp.sum(weights, axis=-1)), None)

    result_state, unused = lax.scan(
        forward_advance, (start_numer, start_denom), (blocks, places, offsets)
    )
    numerator, denominator = result_state
    denominator = denominator + (1.0 - query_live)[:, None, :]
    attention_q = jnp.transpose(numerator / denominator[..., None], (0, 2, 1, 3))
    denom_q = jnp.transpose(denominator, (0, 2, 1))
    mixed = attention_q.reshape(seq_count, slot_count, local_width).astype(jnp.bfloat16)
    attn_part = jnp.einsum("stm,mn->stn", mixed, whole_out, preferred_element_type=jnp.float32)
    attn_branch = lax.psum(attn_part, "tp") + vectors[4]
    hidden, first_pull = jax.vjp(layer_norm, inputs + attn_branch, vectors[0], vectors[1])
    hidden_low = hidden.astype(jnp.bfloat16)
    gated = jnp.einsum("std,dcf->stcf", hidden_low, whole_gu, preferred_element_type=jnp.float32)
    activated, unit_pull = jax.vjp(gated_unit, gated[:, :, 0], gated[:, :, 1])
    act_low = activated.astype(jnp.bfloat16)
    ffn_part = jnp.einsum("stf,fn->stn", act_low, whole_down, preferred_element_type=jnp.float32)
    ffn_branch = lax.psum(ffn_part, "tp") + vectors[5]
    normed, second_pull = jax.vjp(layer_norm, hidden + ffn_branch, vectors[2], vectors[3])
    output = (normed * live_rows).astype(jnp.bfloat16)
    upstream = cotangent.astype(jnp.float32) * live_rows
    grad_second, grad_gain_two, grad_shift_two = second_pull(upstream)
    grad_ffn = grad_second.astype(jnp.bfloat16)
    grad_down = jnp.einsum("stf,stn->fn", act_low, grad_ffn, preferred_element_type=jnp.float32)
    grad_ffn_bias = jnp.sum(grad_ffn.astype(jnp.float32), axis=(0, 1))
    grad_act = jnp.einsum("stn,fn->stf", grad_ffn, whole_down, preferred_element_type=jnp.float32)
    grad_gate, grad_upper = unit_pull(grad_act)
    grad_gated = jnp.stack([grad_gate, grad_upper], axis=2).astype(jnp.bfloat16)
    grad_gu = jnp.einsum(
        "std,stcf->dcf", hidden_low, grad_gated, preferred_element_type=jnp.float32
    )
    hidden_part = jnp.einsum(
        "stcf,dcf->std", grad_gated, whole_gu, preferred_element_type=jnp.float32
    )
    grad_hidden = grad_second + lax.psum(hidden_part, "tp")
    grad_first, grad_gain_one, grad_shift_one = first_pull(grad_hidden)
    grad_attn = grad_first.astype(jnp.bfloat16)
    grad_out = jnp.einsum("stm,stn->mn", mixed, grad_attn, preferred_element_type=jnp.float32)
    grad_out_bias = jnp.sum(grad_attn.astype(jnp.float32), axis=(0, 1))
    grad_mixed = jnp.einsum(
        "stn,mn->stm", grad_attn, whole_out, preferred_element_type=jnp.float32
    ).astype(jnp.bfloat16)
    grad_mixed_heads = grad_mixed.reshape(head_shape).astype(jnp.float32)
    correction = jnp.transpose(
        jnp.sum(grad_mixed_heads * attention_q, axis=-1) / denom_q, (0, 2, 1)
    )
    numer_heads = (grad_mixed_heads / denom_q[..., None]).astype(jnp.bfloat16)
    start_query = jnp.zeros(head_shape, jnp.float32)
    start_state = (
        start_query,
        jnp.zeros((seq_count, slot_count * ctx_count, 2, local_width), jnp.float32),
    )
    blocks, places, offsets = split_blocks(
        lax.all_gather(pairs, "ctx", axis=1, tiled=True), slot_count, ctx_count
    )

    def backward_advance(current_state, block_item):
        key_block, key_place, row_offset = block_item
        key_heads = key_block[:, :, 0].reshape(seq_count, -1, head_count, HD)
        value_heads = key_block[:, :, 1].reshape(seq_count, -1, head_count, HD)
        weights_low, grad_scores = backward_scores(
            query_heads,
            numer_heads,
            correction,
            key_heads,
            value_heads,
            query_place,
            key_place,
            slopes,
            lengths,
        )
        grad_query = current_state[0] + jnp.einsum(
            "shqk,skhe->sqhe", grad_scores, key_heads, preferred_element_type=jnp.float32
        )
        grad_key = (
            jnp.einsum(
                "shqk,sqhe->skhe", grad_scores, query_heads, preferred_element_type=jnp.float32
            )
            * 0.125
        )
        grad_value = jnp.einsum(
            "shqk,sqhe->skhe", weights_low, numer_heads, preferred_element_type=jnp.float32
        )
        stacked = jnp.stack(
            [
                grad_key.reshape(seq_count, -1, local_width),
                grad_value.reshape(seq_count, -1, local_width),
            ],
            axis=2,
        )
        buffer = lax.dynamic_update_slice_in_dim(current_state[1], stacked, row_offset, axis=1)
        return ((grad_query, buffer), None)

    result_state, unused = lax.scan(backward_advance, start_state, (blocks, places, offsets))
    grad_pairs = lax.psum_scatter(
        result_state[1].astype(jnp.bfloat16), "ctx", scatter_dimension=1, tiled=True
    )
    grad_query_low = (
        (result_state[0] * 0.125).astype(jnp.bfloat16).reshape(seq_count, slot_count, local_width)
    )
    grad_proj = jnp.concatenate([grad_query_low[:, :, None], grad_pairs], axis=2)
    grad_qkv = jnp.einsum("std,stcm->dcm", tokens, grad_proj, preferred_element_type=jnp.float32)
    bias_terms = jnp.stack(
        [
            jnp.sum(grad_query_low.astype(jnp.float32), axis=(0, 1)),
            jnp.sum(grad_pairs[:, :, 1].astype(jnp.float32), axis=(0, 1)),
        ]
    )
    input_part = jnp.einsum(
        "stcm,dcm->std", grad_proj, whole_qkv, preferred_element_type=jnp.float32
    )
    input_grad = grad_first + lax.psum(input_part.astype(jnp.bfloat16), "tp").astype(jnp.float32)
    grad_weights = (
        lax.psum_scatter(grad_qkv, ("shard", "ctx"), scatter_dimension=0, tiled=True),
        lax.psum_scatter(grad_out, ("shard", "ctx"), scatter_dimension=1, tiled=True),
        lax.psum_scatter(grad_gu, ("shard", "ctx"), scatter_dimension=0, tiled=True),
        lax.psum_scatter(grad_down, ("shard", "ctx"), scatter_dimension=1, tiled=True),
    )
    vector_terms = jnp.stack(
        [grad_gain_one, grad_shift_one, grad_gain_two, grad_shift_two, grad_out_bias, grad_ffn_bias]
    )
    grad_bqv, grad_vectors = lax.psum((bias_terms, vector_terms), ("shard", "ctx"))
    return (
        output,
        input_grad,
        grad_weights[0],
        grad_bqv,
        grad_weights[1],
        grad_weights[2],
        grad_weights[3],
        grad_vectors,
    )


def solution(mesh):
    placed = (
        P("shard", "ctx", None),
        P("shard"),
        P(("shard", "ctx"), None, "tp"),
        P(None, "tp"),
        P("tp", ("shard", "ctx")),
        P(("shard", "ctx"), None, "tp"),
        P("tp", ("shard", "ctx")),
        P(),
        P("shard", "ctx", None),
    )
    return jax.shard_map(
        on_device,
        mesh=mesh,
        in_specs=placed,
        out_specs=(
            P("shard", "ctx", None),
            P("shard", "ctx", None),
            P(("shard", "ctx"), None, "tp"),
            P(None, "tp"),
            P("tp", ("shard", "ctx")),
            P(("shard", "ctx"), None, "tp"),
            P("tp", ("shard", "ctx")),
            P(),
        ),
        check_vma=False,
    )
```

```python
import functools
import math

import jax
import jax.numpy as jnp
import numpy as np
from jax import lax
from jax.experimental import pallas as pl
from jax.experimental.pallas import tpu as pltpu
from jax.sharding import PartitionSpec as P

H = 12
HD = 64
LOG2E = math.log2(math.e)
FAR = 1e30
TILE = 64
BLOCK = 512
WIDTH = 384
EXTRA = 16

epsilon = 1e-12
f32 = jnp.float32
bf16 = jnp.bfloat16
VMEM = pl.BlockSpec(memory_space=pltpu.VMEM)
SMEM = pl.BlockSpec(memory_space=pltpu.SMEM)


def slope_table():
    power = 2 ** (H.bit_length() - 1)
    heads = np.arange(H)
    early = -8.0 * (heads + 1) / power
    later = -4.0 * (2 * (heads - power) + 1) / power
    return np.exp2(np.where(heads < power, early, later)).astype(np.float32)


def dot_nn(a, b):
    return jnp.dot(a, b, preferred_element_type=f32)


def dot_nt(a, b):
    return lax.dot_general(a, b, (((1,), (1,)), ((), ())), preferred_element_type=f32)


def params(*semantics):
    return pltpu.CompilerParams(
        dimension_semantics=semantics or None, vmem_limit_bytes=56 * 1024 * 1024
    )


def cost(flops, nbytes, exps=0):
    return pl.CostEstimate(flops=int(flops), bytes_accessed=int(nbytes), transcendentals=int(exps))


def shape(dims, dtype):
    return jax.ShapeDtypeStruct(dims, dtype)


def xor_pairs(axis, distance):
    return [(i, i ^ distance) for i in range(lax.axis_size(axis))]


def swap(value, axis, distance):
    return lax.ppermute(value, axis, xor_pairs(axis, distance))


def after(values, *done):
    return lax.optimization_barrier((*values, *done))[: len(values)]


def live_mask(length, rank, n_ctx, slots):
    slot = lax.broadcasted_iota(jnp.int32, (slots, 1), 0)
    return jnp.where(slot * n_ctx + rank < length, 1.0, 0.0).astype(f32)


def normalise(z):
    centred = z - jnp.mean(z, axis=-1, keepdims=True)
    spread = jnp.mean(centred * centred, axis=-1, keepdims=True)
    scale = lax.rsqrt(spread + epsilon)
    return centred * scale, scale


def normalise_back(grad_hat, hat, scale):
    inner = jnp.mean(grad_hat * hat, axis=-1, keepdims=True)
    return scale * (grad_hat - jnp.mean(grad_hat, axis=-1, keepdims=True) - hat * inner)


def assemble_kernel(n, ids, *refs):
    pieces, whole = refs[:4], refs[4]
    y, c, z = ids[0], ids[1], ids[2]
    rows = pieces[0].shape[0] // n
    for k in range(4):
        for kz in range(n):
            index = ((y ^ (k // 2)) * 2 + (c ^ (k % 2))) * n + (z ^ kz)
            place = pl.ds(pl.multiple_of(index * rows, rows), rows)
            whole[place, :] = pieces[k][kz * rows : (kz + 1) * rows, :]


def assemble(ids, pieces, n):
    rows, wide = pieces[0].shape
    column = lambda size: pl.BlockSpec((size, wide // 3), lambda j: (0, j))
    return pl.pallas_call(
        functools.partial(assemble_kernel, n),
        grid=(3,),
        out_shape=shape((4 * rows, wide), bf16),
        in_specs=[SMEM] + [column(rows)] * 4,
        out_specs=column(4 * rows),
        compiler_params=params("arbitrary"),
        cost_estimate=cost(0, 16 * rows * wide),
        name="assemble",
    )(ids, *pieces)


def project_kernel(n, seqs, heads, ids, tok, bias, *refs):
    pieces = refs[: 4 * n]
    sends = refs[4 * n : 5 * n]
    whole = refs[5 * n]
    stage = refs[5 * n + 1]
    y, c, z = ids[0], ids[1], ids[2]
    rows = pieces[0].shape[0]
    for k in range(4 * n):
        ky, kc, kz = k // (2 * n), k // n % 2, k % n
        index = ((y ^ ky) * 2 + (c ^ kc)) * n + (z ^ kz)
        whole[pl.ds(pl.multiple_of(index * rows, rows), rows), :] = pieces[k][...]
    slots = sends[0].shape[1]
    width = heads * HD
    per = seqs * heads // n
    for s in range(seqs):
        acc = dot_nn(tok[s * slots : (s + 1) * slots, :], whole[...]) + bias[...]
        turned = acc.astype(bf16).T
        for h in range(heads):
            i = s * heads + h
            at = ((i % n) * per + i // n) * 3
            for part in range(3):
                first = part * width + h * HD
                stage[(at + part) * HD : (at + part + 1) * HD, :] = turned[first : first + HD, :]
    size = per * 3 * HD
    for d in range(n):
        sends[d][...] = stage[pl.ds(pl.multiple_of((z ^ d) * size, size), size), :]


def project(ids, tok, bias, pieces, n, seqs, heads):
    slots = tok.shape[0] // seqs
    size = seqs * heads // n * 3 * HD
    model, wide = tok.shape[1], bias.shape[1]
    return pl.pallas_call(
        functools.partial(project_kernel, n, seqs, heads),
        out_shape=[shape((size, slots), bf16)] * n + [shape((model, wide), bf16)],
        in_specs=[SMEM] + [VMEM] * (2 + len(pieces)),
        out_specs=[VMEM] * (n + 1),
        scratch_shapes=[pltpu.VMEM((size * n, slots), bf16)],
        compiler_params=params(),
        cost_estimate=cost(2 * tok.shape[0] * model * wide, 6e6),
        name="project",
    )(ids, tok, bias, *pieces)


def pair_scalars(n, heads, ids, lens, slopes):
    j = pl.program_id(0)
    z, t = ids[2], ids[3]
    i = z + n * j
    s = i // heads
    h = i - s * heads
    return z, lens[s], slopes[t * heads + h] * LOG2E


def query_place(n, slots, z, d):
    lane = lax.broadcasted_iota(jnp.int32, (1, slots), 1)
    return lane * n + (z ^ d)


def key_place(n, z, tile, length, slope):
    row = lax.broadcasted_iota(jnp.int32, (TILE, 1), 0)
    places = []
    for d in range(n):
        place = (tile * TILE + row) * n + (z ^ d)
        places.append(jnp.where(place < length, place.astype(f32) * slope, FAR))
    return jnp.concatenate(places, axis=0)


def gather_rows(ref, tile, n):
    rows = pl.ds(pl.multiple_of(tile * TILE, TILE), TILE)
    return jnp.concatenate([ref[d, rows, :] for d in range(n)], axis=0)


def attend_kernel(n, heads, ids, lens, slopes, *refs):
    inputs = refs[:n]
    outs = refs[n : 2 * n]
    att_ref, den_ref = refs[2 * n], refs[2 * n + 1]
    k_s, v_s, acc, den = refs[2 * n + 2 :]
    slots = inputs[0].shape[1]
    z, length, slope = pair_scalars(n, heads, ids, lens, slopes)
    for d in range(n):
        k_s[d] = inputs[d][HD : 2 * HD, :].T
        v_s[d] = inputs[d][2 * HD : 3 * HD, :].T
    acc[...] = jnp.zeros_like(acc)
    den[...] = jnp.zeros_like(den)

    def tile_step(tile, unused):
        keys = gather_rows(k_s, tile, n)
        values = gather_rows(v_s, tile, n).T
        places = key_place(n, z, tile, length, slope)
        for d in range(n):
            cols = slice(d * slots, (d + 1) * slots)
            there = query_place(n, slots, z, d).astype(f32) * slope
            scores = dot_nn(keys, inputs[d][0:HD, :]) * (0.125 * LOG2E)
            e = jnp.exp2(scores - jnp.abs(there - places))
            den[:, cols] += jnp.sum(e, axis=0, keepdims=True)
            acc[:, cols] += dot_nn(values, e.astype(bf16))
        return unused

    step = TILE * n
    lax.fori_loop(0, (length + step - 1) // step, tile_step, 0)
    for d in range(n):
        cols = slice(d * slots, (d + 1) * slots)
        padded = jnp.where(query_place(n, slots, z, d) < length, 0.0, 1.0)
        total = den[:, cols] + padded
        att = acc[:, cols] / total
        att_ref[:, cols] = att
        den_ref[0, :, cols] = total
        outs[d][...] = att.astype(bf16)


def attend(ids, lens, slopes, blocks, n, heads, per):
    slots = blocks[0].shape[1]
    every = n * slots
    return pl.pallas_call(
        functools.partial(attend_kernel, n, heads),
        grid=(per,),
        out_shape=[shape((per * HD, slots), bf16)] * n
        + [shape((per * HD, every), f32), shape((per, 1, every), f32)],
        in_specs=[SMEM] * 3 + [pl.BlockSpec((3 * HD, slots), lambda j: (j, 0))] * n,
        out_specs=[pl.BlockSpec((HD, slots), lambda j: (j, 0))] * n
        + [
            pl.BlockSpec((HD, every), lambda j: (j, 0)),
            pl.BlockSpec((1, 1, every), lambda j: (j, 0, 0)),
        ],
        scratch_shapes=[
            pltpu.VMEM((n, slots, HD), bf16),
            pltpu.VMEM((n, slots, HD), bf16),
            pltpu.VMEM((HD, every), f32),
            pltpu.VMEM((1, every), f32),
        ],
        compiler_params=params("arbitrary"),
        cost_estimate=cost(per * every * every * HD * 8, 3e6, per * every * every),
        name="attend",
    )(ids, lens, slopes, *blocks)


def attend_back_kernel(n, heads, ids, lens, slopes, *refs):
    inputs = refs[:n]
    grads = refs[n : 2 * n]
    att_ref, den_ref = refs[2 * n], refs[2 * n + 1]
    outs = refs[2 * n + 2 : 3 * n + 2]
    k_s, v_s, q_s, g_s, dn, cor, dq, dk, dv = refs[3 * n + 2 :]
    slots = inputs[0].shape[1]
    z, length, slope = pair_scalars(n, heads, ids, lens, slopes)
    for d in range(n):
        cols = slice(d * slots, (d + 1) * slots)
        k_s[d] = inputs[d][HD : 2 * HD, :].T
        v_s[d] = inputs[d][2 * HD : 3 * HD, :].T
        q_s[d] = inputs[d][0:HD, :].T
        inverse = 1.0 / den_ref[0, :, cols]
        mixed = grads[d][...].astype(f32)
        numer = (mixed * inverse).astype(bf16)
        dn[:, cols] = numer
        g_s[d] = numer.T
        cor[:, cols] = jnp.sum(mixed * att_ref[:, cols], axis=0, keepdims=True) * inverse
    dq[...] = jnp.zeros_like(dq)
    dk[...] = jnp.zeros_like(dk)
    dv[...] = jnp.zeros_like(dv)

    def tile_step(tile, unused):
        keys = gather_rows(k_s, tile, n)
        values = gather_rows(v_s, tile, n)
        keys_t = keys.T
        places = key_place(n, z, tile, length, slope)
        grad_k = jnp.zeros((n * TILE, HD), f32)
        grad_v = jnp.zeros((n * TILE, HD), f32)
        for d in range(n):
            cols = slice(d * slots, (d + 1) * slots)
            there = query_place(n, slots, z, d).astype(f32) * slope
            scores = dot_nn(keys, inputs[d][0:HD, :]) * (0.125 * LOG2E)
            e = jnp.exp2(scores - jnp.abs(there - places))
            inner = dot_nn(values, dn[:, cols])
            ds = (e * (inner - cor[:, cols])).astype(bf16)
            dq[:, cols] += dot_nn(keys_t, ds)
            grad_k += dot_nn(ds, q_s[d])
            grad_v += dot_nn(e.astype(bf16), g_s[d])
        rows = pl.ds(pl.multiple_of(tile * TILE, TILE), TILE)
        for d in range(n):
            dk[d, rows, :] = grad_k[d * TILE : (d + 1) * TILE, :]
            dv[d, rows, :] = grad_v[d * TILE : (d + 1) * TILE, :]
        return unused

    step = TILE * n
    lax.fori_loop(0, (length + step - 1) // step, tile_step, 0)
    for d in range(n):
        cols = slice(d * slots, (d + 1) * slots)
        outs[d][0:HD, :] = (dq[:, cols] * 0.125).astype(bf16)
        outs[d][HD : 2 * HD, :] = (dk[d] * 0.125).astype(bf16).T
        outs[d][2 * HD : 3 * HD, :] = dv[d].astype(bf16).T


def attend_back(ids, lens, slopes, blocks, grads, att, den, n, heads, per):
    slots = blocks[0].shape[1]
    every = n * slots
    rows = [pltpu.VMEM((n, slots, HD), bf16)] * 4
    return pl.pallas_call(
        functools.partial(attend_back_kernel, n, heads),
        grid=(per,),
        out_shape=[shape((per * 3 * HD, slots), bf16)] * n,
        in_specs=[SMEM] * 3
        + [pl.BlockSpec((3 * HD, slots), lambda j: (j, 0))] * n
        + [pl.BlockSpec((HD, slots), lambda j: (j, 0))] * n
        + [
            pl.BlockSpec((HD, every), lambda j: (j, 0)),
            pl.BlockSpec((1, 1, every), lambda j: (j, 0, 0)),
        ],
        out_specs=[pl.BlockSpec((3 * HD, slots), lambda j: (j, 0))] * n,
        scratch_shapes=rows
        + [
            pltpu.VMEM((HD, every), bf16),
            pltpu.VMEM((1, every), f32),
            pltpu.VMEM((HD, every), f32),
            pltpu.VMEM((n, slots, HD), f32),
            pltpu.VMEM((n, slots, HD), f32),
        ],
        compiler_params=params("arbitrary"),
        cost_estimate=cost(per * every * every * HD * 20, 5e6, per * every * every),
        name="attend_back",
    )(ids, lens, slopes, *blocks, *grads, att, den)


def mix_kernel(n, seqs, heads, ids, wo, *refs):
    inputs = refs[:n]
    parts = refs[n : n + seqs]
    mixed, stage = refs[n + seqs :]
    z = ids[2]
    slots = inputs[0].shape[1]
    per = seqs * heads // n
    size = per * HD
    for d in range(n):
        stage[pl.ds(pl.multiple_of((z ^ d) * size, size), size), :] = inputs[d][...]
    for s in range(seqs):
        columns = []
        for h in range(heads):
            i = s * heads + h
            at = (i % n) * per + i // n
            columns.append(stage[at * HD : (at + 1) * HD, :])
        rows = slice(s * slots, (s + 1) * slots)
        ours = jnp.concatenate(columns, axis=0).T
        mixed[rows, :] = ours
        parts[s][...] = dot_nt(ours, wo[...]).astype(bf16)


def mix(ids, packed, blocks, n, seqs, heads):
    slots = blocks[0].shape[1]
    model = packed.shape[0]
    width = heads * HD
    tokens = seqs * slots
    return pl.pallas_call(
        functools.partial(mix_kernel, n, seqs, heads),
        grid=(1,),
        out_shape=[shape((slots, model), bf16)] * seqs + [shape((tokens, width), bf16)],
        in_specs=[SMEM, pl.BlockSpec((model, width), lambda i: (0, packed.shape[1] // width - 1))]
        + [VMEM] * n,
        out_specs=[VMEM] * (seqs + 1),
        scratch_shapes=[pltpu.VMEM((seqs * heads * HD, slots), bf16)],
        compiler_params=params("arbitrary"),
        cost_estimate=cost(2 * tokens * model * width, 3e6),
        name="mix",
    )(ids, packed, *blocks)


def unit_kernel(tok, own, other, vec, wg, wu, wd, hidden, low, act, gel, slope, part, acc):
    j = pl.program_id(0)

    @pl.when(j == 0)
    def _():
        branch = own[...].astype(f32) + other[...].astype(f32) + vec[4:5, :]
        hat, _ = normalise(tok[...].astype(f32) + branch)
        h = hat * vec[0:1, :] + vec[1:2, :]
        hidden[...] = h
        low[...] = h.astype(bf16)
        acc[...] = jnp.zeros_like(acc)

    gate = dot_nn(low[...], wg[...])
    upper = dot_nn(low[...], wu[...])
    phi = 0.5 * (1.0 + lax.erf(gate * math.sqrt(0.5)))
    density = jnp.exp(gate * gate * -0.5) * (1.0 / math.sqrt(2.0 * math.pi))
    unit = gate * phi
    acted = (unit * upper).astype(bf16)
    act[...] = acted
    gel[...] = unit.astype(bf16)
    slope[...] = (upper * (phi + gate * density)).astype(bf16)
    acc[...] += dot_nt(acted, wd[...])

    @pl.when(j == pl.num_programs(0) - 1)
    def _():
        part[...] = acc[...].astype(bf16)


def unit(s, tok, own, other, vec, front, back):
    tokens, model = own.shape
    hidden_units = back.shape[1]
    steps = hidden_units // BLOCK
    fixed = lambda j: (0, 0)
    whole = pl.BlockSpec((tokens, model), fixed)
    weight = lambda start: pl.BlockSpec((model, BLOCK), lambda j: (0, start + j))
    inner = pl.BlockSpec((tokens, BLOCK), lambda j: (0, j))
    return pl.pallas_call(
        unit_kernel,
        grid=(steps,),
        out_shape=[shape((tokens, model), f32), shape((tokens, model), bf16)]
        + [shape((tokens, hidden_units), bf16)] * 3
        + [shape((tokens, model), bf16)],
        in_specs=[
            pl.BlockSpec((tokens, model), lambda j: (s, 0)),
            whole,
            whole,
            pl.BlockSpec(vec.shape, fixed),
            weight(0),
            weight(steps),
            weight(0),
        ],
        out_specs=[whole, whole, inner, inner, inner, whole],
        scratch_shapes=[pltpu.VMEM((tokens, model), f32)],
        compiler_params=params("arbitrary"),
        cost_estimate=cost(6 * tokens * model * hidden_units, 13e6, 2 * tokens * hidden_units),
        name="unit",
    )(tok, own, other, vec, front, front, back)


def unit_back_kernel(
    n, s, ids, lens, hidden, own, other, cot, vec, wg, wu, wd, gel, slope,
    output, dz2, dffn, dgate, dup, part, sums, acc,
):
    j = pl.program_id(0)

    @pl.when(j == 0)
    def _():
        live = live_mask(lens[s], ids[2], n, hidden.shape[0])
        branch = own[...].astype(f32) + other[...].astype(f32) + vec[5:6, :]
        hat, scale = normalise(hidden[...] + branch)
        output[...] = (live * (hat * vec[2:3, :] + vec[3:4, :])).astype(bf16)
        gy = cot[...].astype(f32) * live
        grad = normalise_back(gy * vec[2:3, :], hat, scale)
        dz2[...] = grad
        low = grad.astype(bf16)
        dffn[...] = low
        sums[0:1, :] = jnp.sum(gy * hat, axis=0, keepdims=True)
        sums[1:2, :] = jnp.sum(gy, axis=0, keepdims=True)
        sums[2:3, :] = jnp.sum(low.astype(f32), axis=0, keepdims=True)
        sums[3:8, :] = jnp.zeros_like(sums[3:8, :])
        acc[...] = jnp.zeros_like(acc)

    dact = dot_nn(dffn[...], wd[...])
    upper = (dact * gel[...].astype(f32)).astype(bf16)
    gate = (dact * slope[...].astype(f32)).astype(bf16)
    dgate[...] = gate
    dup[...] = upper
    acc[...] += dot_nt(gate, wg[...]) + dot_nt(upper, wu[...])

    @pl.when(j == pl.num_programs(0) - 1)
    def _():
        part[...] = acc[...].astype(bf16)


def unit_back(s, ids, lens, hidden, own, other, cot, vec, front, back, gel, slope, n):
    tokens, model = hidden.shape
    hidden_units = gel.shape[1]
    steps = hidden_units // BLOCK
    fixed = lambda j: (0, 0)
    whole = pl.BlockSpec((tokens, model), fixed)
    weight = lambda start: pl.BlockSpec((model, BLOCK), lambda j: (0, start + j))
    inner = pl.BlockSpec((tokens, BLOCK), lambda j: (0, j))
    return pl.pallas_call(
        functools.partial(unit_back_kernel, n, s),
        grid=(steps,),
        out_shape=[
            shape((tokens, model), bf16),
            shape((tokens, model), f32),
            shape((tokens, model), bf16),
            shape((tokens, hidden_units), bf16),
            shape((tokens, hidden_units), bf16),
            shape((tokens, model), bf16),
            shape((8, model), f32),
        ],
        in_specs=[SMEM, SMEM, whole, whole, whole]
        + [pl.BlockSpec((tokens, model), lambda j: (s, 0)), pl.BlockSpec(vec.shape, fixed)]
        + [weight(0), weight(steps), weight(0), inner, inner],
        out_specs=[whole, whole, whole, inner, inner, whole, pl.BlockSpec((8, model), fixed)],
        scratch_shapes=[pltpu.VMEM((tokens, model), f32)],
        compiler_params=params("arbitrary"),
        cost_estimate=cost(6 * tokens * model * hidden_units, 14e6),
        name="unit_back",
    )(ids, lens, hidden, own, other, cot, vec, front, front, back, gel, slope)


def row_starts(ids, quarter):
    y, c = ids[0], ids[1]
    keep = [(y * 2 + c) * quarter, ((1 - y) * 2 + c) * quarter]
    send = [(y * 2 + 1 - c) * quarter, ((1 - y) * 2 + 1 - c) * quarter]
    return send, keep


def arrange(ids, turned, left):
    quarter = turned.shape[0] // 4
    send, keep = row_starts(ids, quarter)
    for k, start in enumerate(send + keep):
        rows = pl.ds(pl.multiple_of(start, quarter), quarter)
        left[k * quarter : (k + 1) * quarter, :] = turned[rows, :]


def write_rows(left, right, send, keep):
    grad = dot_nn(left[...], right).astype(bf16)
    half = grad.shape[0] // 2
    send[0:half, :] = grad[:half]
    keep[0:half, :] = grad[half:]


def weight_kernel(steps, seqs, ids, *refs):
    low, dffn, dgate, dup, act = (refs[i * seqs : (i + 1) * seqs] for i in range(5))
    send, keep, left, turned = refs[5 * seqs :]
    j = pl.program_id(0)
    joined = lambda group: jnp.concatenate([ref[...] for ref in group], axis=0)

    @pl.when(j == 0)
    def _():
        for k, group in enumerate((low, dffn)):
            turned[...] = joined(group).T
            arrange(ids, turned, left.at[k])

    @pl.when(j < steps)
    def _():
        write_rows(left.at[0], joined(dgate), send, keep)

    @pl.when((j >= steps) & (j < 2 * steps))
    def _():
        write_rows(left.at[0], joined(dup), send, keep)

    @pl.when(j >= 2 * steps)
    def _():
        write_rows(left.at[1], joined(act), send, keep)


def weight_grads(ids, low, dffn, dgate, dup, act):
    seqs = len(low)
    tokens, model = low[0].shape
    hidden_units = act[0].shape[1]
    steps = hidden_units // BLOCK
    whole = pl.BlockSpec((tokens, model), lambda j: (0, 0))
    column = lambda start: pl.BlockSpec(
        (tokens, BLOCK), lambda j: (0, jnp.clip(j - start, 0, steps - 1))
    )
    out = pl.BlockSpec((model // 2, BLOCK), lambda j: (0, j))
    return pl.pallas_call(
        functools.partial(weight_kernel, steps, seqs),
        grid=(3 * steps,),
        out_shape=[shape((model // 2, 3 * hidden_units), bf16)] * 2,
        in_specs=[SMEM]
        + [whole] * (2 * seqs)
        + [column(0)] * seqs
        + [column(steps)] * seqs
        + [column(2 * steps)] * seqs,
        out_specs=[out, out],
        scratch_shapes=[
            pltpu.VMEM((2, model, tokens * seqs), bf16),
            pltpu.VMEM((model, tokens * seqs), bf16),
        ],
        compiler_params=params("arbitrary"),
        cost_estimate=cost(6 * tokens * seqs * model * hidden_units, 14e6),
        name="weight_grads",
    )(ids, *low, *dffn, *dgate, *dup, *act)


def mix_back_kernel(n, seqs, heads, ids, tok, vec, wo, mixed, *refs):
    own, other, dz2, hown, hother = (refs[i * seqs : (i + 1) * seqs] for i in range(5))
    refs = refs[5 * seqs :]
    sends = refs[:n]
    dz1, send, keep, sums = refs[n : n + 4]
    stage, left, turned_low = refs[n + 4 :]
    z = ids[2]
    slots = sends[0].shape[1]
    per = seqs * heads // n
    sums[...] = jnp.zeros_like(sums)
    for s in range(seqs):
        rows = slice(s * slots, (s + 1) * slots)
        branch = own[s][...].astype(f32) + other[s][...].astype(f32) + vec[4:5, :]
        hat, scale = normalise(tok[rows, :].astype(f32) + branch)
        gh = dz2[s][...] + (hown[s][...].astype(f32) + hother[s][...].astype(f32))
        grad = normalise_back(gh * vec[0:1, :], hat, scale)
        dz1[rows, :] = grad
        low = grad.astype(bf16)
        sums[0:1, :] += jnp.sum(gh * hat, axis=0, keepdims=True)
        sums[1:2, :] += jnp.sum(gh, axis=0, keepdims=True)
        sums[2:3, :] += jnp.sum(low.astype(f32), axis=0, keepdims=True)
        turned_low[:, rows] = low.T
        turned = dot_nn(low, wo[...]).astype(bf16).T
        for h in range(heads):
            i = s * heads + h
            at = (i % n) * per + i // n
            stage[at * HD : (at + 1) * HD, :] = turned[h * HD : (h + 1) * HD, :]
    size = per * HD
    for d in range(n):
        sends[d][...] = stage[pl.ds(pl.multiple_of((z ^ d) * size, size), size), :]
    arrange(ids, turned_low, left)
    write_rows(left, mixed[...], send, keep)
    for ref in (send, keep):
        ref[ref.shape[0] - EXTRA :, :] = jnp.zeros((EXTRA, ref.shape[1]), bf16)


def mix_back(ids, tok, vec, front, mixed, own, other, dz2, hown, hother, n, heads):
    seqs = len(own)
    tokens, model = tok.shape
    slots = tokens // seqs
    width = heads * HD
    size = seqs * heads // n * HD
    rows = model // 2 + EXTRA
    last = pl.BlockSpec((rows, width), lambda i: (0, 3))
    return pl.pallas_call(
        functools.partial(mix_back_kernel, n, seqs, heads),
        grid=(1,),
        out_shape=[shape((size, slots), bf16)] * n
        + [shape((tokens, model), f32)]
        + [shape((rows, 4 * width), bf16)] * 2
        + [shape((8, model), f32)],
        in_specs=[SMEM, VMEM, VMEM]
        + [pl.BlockSpec((model, width), lambda i: (0, front.shape[1] // width - 1)), VMEM]
        + [VMEM] * (5 * seqs),
        out_specs=[VMEM] * (n + 1) + [last, last, VMEM],
        scratch_shapes=[
            pltpu.VMEM((size * n, slots), bf16),
            pltpu.VMEM((model, tokens), bf16),
            pltpu.VMEM((model, tokens), bf16),
        ],
        compiler_params=params("arbitrary"),
        cost_estimate=cost(4 * tokens * model * width, 10e6),
        name="mix_back",
    )(ids, tok, vec, front, mixed, *own, *other, *dz2, *hown, *hother)


def project_back_kernel(n, seqs, heads, ids, tok, whole, small, far, near, *refs):
    inputs = refs[:n]
    part, send, keep = refs[n : n + 3]
    stage, right, left, turned = refs[n + 3 :]
    z = ids[2]
    slots = inputs[0].shape[1]
    per = seqs * heads // n
    width = heads * HD
    size = per * 3 * HD
    for d in range(n):
        stage[pl.ds(pl.multiple_of((z ^ d) * size, size), size), :] = inputs[d][...]
    for s in range(seqs):
        for c in range(3):
            columns = []
            for h in range(heads):
                i = s * heads + h
                at = ((i % n) * per + i // n) * 3 + c
                columns.append(stage[at * HD : (at + 1) * HD, :])
            ours = jnp.concatenate(columns, axis=0).T
            right[s * slots : (s + 1) * slots, c * width : (c + 1) * width] = ours
    part[...] = dot_nt(right[...], whole[...]).astype(bf16)
    turned[...] = tok[...].T
    arrange(ids, turned, left)
    for c in range(3):
        cols = slice(c * width, (c + 1) * width)
        write_rows(left, right[:, cols], send.at[:, cols], keep.at[:, cols])
    ones = jnp.ones((8, right.shape[0]), bf16)
    sums = dot_nn(ones, right[...])
    line = jnp.concatenate([sums[:, :width], sums[:, 2 * width :]], axis=1)
    row = lax.broadcasted_iota(jnp.int32, (8, 1), 0)
    rows = jnp.where(row == 6, line, small[...])
    rows = jnp.concatenate([rows, jnp.zeros_like(rows)], axis=0).astype(bf16)
    for ref in (send, keep):
        ref[ref.shape[0] - EXTRA :, :] = jnp.zeros((EXTRA, ref.shape[1]), bf16)
        ref[ref.shape[0] - EXTRA :, : 2 * width] = rows


def project_back(ids, tok, whole, small, grads, blocks, n, seqs, heads):
    tokens, model = tok.shape
    slots = tokens // seqs
    wide = whole.shape[1]
    return pl.pallas_call(
        functools.partial(project_back_kernel, n, seqs, heads),
        grid=(1,),
        out_shape=[shape((tokens, model), bf16)] + [shape(grads[0].shape, bf16)] * 2,
        in_specs=[SMEM] + [VMEM] * 3 + [pl.BlockSpec(memory_space=pl.ANY)] * 2 + [VMEM] * n,
        out_specs=[VMEM] + [pl.BlockSpec((grads[0].shape[0], wide), lambda i: (0, 0))] * 2,
        input_output_aliases={4: 1, 5: 2},
        scratch_shapes=[
            pltpu.VMEM((seqs * heads * 3 * HD, slots), bf16),
            pltpu.VMEM((tokens, wide), bf16),
            pltpu.VMEM((model, tokens), bf16),
            pltpu.VMEM((model, tokens), bf16),
        ],
        compiler_params=params("arbitrary"),
        cost_estimate=cost(4 * tokens * model * wide, 8e6),
        name="project_back",
    )(ids, tok, whole, small, *grads, *blocks)


def fold_core_kernel(extra, keep, recv, mine, *sends):
    half = (keep.shape[0] - extra) // 2
    mine[0:half, :] = keep[0:half, :].astype(f32) + recv[0:half, :].astype(f32)
    rest = (keep[half:, :].astype(f32) + recv[half:, :].astype(f32)).astype(bf16)
    size = sends[0].shape[1]
    for k, send in enumerate(sends):
        send[...] = rest[:, k * size : (k + 1) * size]
    if extra:
        mine[half:, :] = rest[half:, :].astype(f32)


def fold_core(keep, recv, extra):
    rows, wide = keep.shape
    out = (rows - extra) // 2 + extra
    steps = 1 if extra else 3
    parts = 2 if extra else 1
    column = lambda size: pl.BlockSpec((size, wide // steps), lambda j: (0, j))
    return pl.pallas_call(
        functools.partial(fold_core_kernel, extra),
        grid=(steps,),
        out_shape=[shape((out, wide), f32)] + [shape((out, wide // parts), bf16)] * parts,
        in_specs=[column(rows)] * 2,
        out_specs=[column(out)]
        + [pl.BlockSpec((out, wide // steps // parts), lambda j: (0, j))] * parts,
        compiler_params=params("arbitrary"),
        cost_estimate=cost(rows * wide, 7 * rows * wide),
        name="fold_core",
    )(keep, recv)


def fold_y_kernel(n, extra, parts, ids, mine, *refs):
    recvs, own, sends, stage = refs[:parts], refs[parts], refs[parts + 1 : -1], refs[-1]
    z = ids[2]
    rows = mine.shape[0] - extra
    size = rows // n
    recv = jnp.concatenate([ref[...] for ref in recvs], axis=1)
    stage[...] = mine[...] + recv.astype(f32)
    for d in range(n):
        block = stage[pl.ds(pl.multiple_of((z ^ d) * size, size), size), :]
        if d:
            sends[d - 1][0:size, :] = block.astype(bf16)
            if extra:
                sends[d - 1][size:, :] = stage[rows:, :].astype(bf16)
        else:
            own[0:size, :] = block
            if extra:
                own[size:, :] = stage[rows:, :].astype(bf16).astype(f32)


def fold_y(ids, mine, recvs, n, extra):
    rows, wide = mine.shape
    out = (rows - extra) // n + extra
    steps = 1 if extra else 3
    parts = len(recvs)
    column = lambda size: pl.BlockSpec((size, wide // steps), lambda j: (0, j))
    return pl.pallas_call(
        functools.partial(fold_y_kernel, n, extra, parts),
        grid=(steps,),
        out_shape=[shape((out, wide), f32)] + [shape((out, wide), bf16)] * (n - 1),
        in_specs=[SMEM, column(rows)]
        + [pl.BlockSpec((rows, wide // steps // parts), lambda j: (0, j))] * parts,
        out_specs=[column(out)] * n,
        scratch_shapes=[pltpu.VMEM((rows, wide // steps), f32)],
        compiler_params=params("arbitrary"),
        cost_estimate=cost(rows * wide, 9 * rows * wide),
        name="fold_y",
    )(ids, mine, *recvs)


def fold_z(own, got):
    return (own + got[0].astype(f32)) + (got[1].astype(f32) + got[2].astype(f32))


def fits(tokens, b_qv, w_qkv, w_gu):
    n = lax.axis_size("ctx")
    heads = b_qv.shape[1] // HD
    return (
        n == 4
        and lax.axis_size("shard") == 4
        and lax.axis_size("tp") == 2
        and (tokens.shape[0] * heads) % n == 0
        and w_qkv.shape[0] % 16 == 0
        and tokens.shape[1] % 256 == 0
        and b_qv.shape[1] == WIDTH
        and w_gu.shape[2] % BLOCK == 0
        and w_gu.shape[2] % WIDTH == 0
    )


def on_device(tokens, lengths, w_qkv, b_qv, w_out, w_gu, w_down, vectors, cotangent):
    if not fits(tokens, b_qv, w_qkv, w_gu):
        return by_gather(tokens, lengths, w_qkv, b_qv, w_out, w_gu, w_down, vectors, cotangent)
    n = lax.axis_size("ctx")
    seqs, slots, model = tokens.shape
    width = b_qv.shape[1]
    heads = width // HD
    per = seqs * heads // n
    units = w_gu.shape[2]
    rows = w_qkv.shape[0]
    count = seqs * slots
    shard = lax.axis_index("shard")
    ids = jnp.stack(
        [shard // 2, shard % 2, lax.axis_index("ctx"), lax.axis_index("tp")]
    ).astype(jnp.int32)
    slopes = jnp.asarray(slope_table())
    tok = tokens.reshape(count, model)
    cot = cotangent.reshape(count, model)

    first = [w_qkv.astype(bf16).reshape(rows, 3 * width)]
    first += [swap(first[0], "ctx", d) for d in range(1, n)]
    first += [swap(piece, "shard", 2) for piece in first]
    by_core = [swap(piece, "shard", 1) for piece in first]
    pieces = first[:n] + by_core[:n] + first[n:] + by_core[n:]
    front = jnp.concatenate([w_gu.reshape(rows, 2 * units), w_out.T], axis=1).astype(bf16)
    back = w_down.T.astype(bf16)
    (front,) = after([front], *pieces[1:n])
    front = [front] + [swap(front, "ctx", d) for d in range(1, n)]

    bias = jnp.concatenate([b_qv[0], jnp.zeros_like(b_qv[0]), b_qv[1]])[None, :]
    *sends, whole = project(ids, tok, bias, pieces, n, seqs, heads)
    blocks = [sends[0]] + [swap(sends[d], "ctx", d) for d in range(1, n)]
    front = jnp.concatenate(after(front, whole), axis=0)
    front_y = swap(front, "shard", 2)
    (back,) = after([back], *blocks)
    back = [back] + [swap(back, "ctx", d) for d in range(1, n)]
    *outs, att, den = attend(ids, lengths, slopes, blocks, n, heads, per)
    front, front_y = after([front, front_y], outs[0])
    front = [front, swap(front, "shard", 1), front_y, swap(front_y, "shard", 1)]
    back = jnp.concatenate(after(back, outs[0]), axis=0)
    back_y = swap(back, "shard", 2)
    outs = [outs[0]] + [swap(outs[d], "ctx", d) for d in range(1, n)]
    front = assemble(ids, front, n)
    *part, mixed = mix(ids, front, outs, n, seqs, heads)
    part_other = [swap(value, "tp", 1) for value in part]
    back, back_y = after([back, back_y], part[0])
    back = [back, swap(back, "shard", 1), back_y, swap(back_y, "shard", 1)]
    back = assemble(ids, back, n)
    hidden, low, act, gel, slope, ffn = zip(
        *(
            unit(s, tok, part[s], part_other[s], vectors, front, back)
            for s in range(seqs)
        )
    )
    ffn_other = [swap(value, "tp", 1) for value in ffn]
    output, dz2, dffn, dgate, dup, dlow, sums_two = zip(
        *(
            unit_back(
                s, ids, lengths, hidden[s], ffn[s], ffn_other[s], cot, vectors, front, back,
                gel[s], slope[s], n,
            )
            for s in range(seqs)
        )
    )
    dlow_other = [swap(value, "tp", 1) for value in dlow]
    far, near = weight_grads(ids, low, dffn, dgate, dup, act)
    *dlow_other, far = lax.optimization_barrier((*dlow_other, far))
    got = swap(far, "shard", 1)
    *sends, dz1, last_far, last_near, sums_one = mix_back(
        ids, tok, vectors, front, mixed, part, part_other, dz2, dlow, dlow_other, n, heads
    )
    sums_two = sum(sums_two)
    grads = [sends[0]] + [swap(sends[d], "ctx", d) for d in range(1, n)]
    got, sends[0] = lax.optimization_barrier((got, sends[0]))
    mine, far = fold_core(near, got, 0)
    *grads, far = lax.optimization_barrier((*grads, far))
    got = swap(far, "shard", 2)
    outs = attend_back(ids, lengths, slopes, blocks, grads, att, den, n, heads, per)
    outs = [outs[0]] + [swap(outs[d], "ctx", d) for d in range(1, n)]
    rest_own, *rest_sends = fold_y(ids, mine, [got], n, 0)
    *outs, rest_own = lax.optimization_barrier((*outs, rest_own))
    small = jnp.concatenate(
        [sums_one[0:2], sums_two[0:2], sums_one[2:3], sums_two[2:3], jnp.zeros_like(sums_one[:2])]
    )
    dx, far, near = project_back(
        ids, tok, whole, small, (last_far, last_near), outs, n, seqs, heads
    )
    got = swap(far, "shard", 1)
    mine, *far = fold_core(near, got, EXTRA)
    got = [swap(half, "shard", 2) for half in far]
    dx_other = swap(dx, "tp", 1)
    rest_got = [swap(block, "ctx", d + 1) for d, block in enumerate(rest_sends)]
    rest_got[0], got[0] = lax.optimization_barrier((rest_got[0], got[0]))
    own, *sends = fold_y(ids, mine, got, n, EXTRA)
    got = [swap(block, "ctx", d + 1) for d, block in enumerate(sends)]
    rest = fold_z(rest_own, rest_got)
    last = fold_z(own, got)
    input_grad = dz1 + (dx.astype(f32) + dx_other.astype(f32))
    small = last[rows : rows + 8, : 2 * width]
    return (
        jnp.stack(output),
        input_grad.reshape(tokens.shape),
        last[:rows, : 3 * width].reshape(w_qkv.shape),
        small[6].reshape(2, width),
        last[:rows, 3 * width :].T,
        rest[:, : 2 * units].reshape(w_gu.shape),
        rest[:, 2 * units :].T,
        small[:6],
    )


def alibi_slopes(first_head, head_count):
    power = 2 ** (H.bit_length() - 1)
    heads_index = first_head + jnp.arange(head_count, dtype=jnp.int32)
    early = -8.0 * (heads_index + 1).astype(jnp.float32) / power
    later = -4.0 * (2 * (heads_index - power) + 1).astype(jnp.float32) / power
    return jnp.exp2(jnp.where(heads_index < power, early, later))


def layer_norm(values, gain, shift):
    centred = values - jnp.mean(values, axis=-1, keepdims=True)
    spread = jnp.mean(centred * centred, axis=-1, keepdims=True)
    return centred * lax.rsqrt(spread + epsilon) * gain + shift


def gated_unit(gate_input, upper):
    return jax.nn.gelu(gate_input, approximate=False) * upper


def score_block(query_heads, key_heads, query_place, key_place, slopes, lengths):
    scores = (
        jnp.einsum("sqhe,skhe->shqk", query_heads, key_heads, preferred_element_type=jnp.float32)
        * 0.125
    )
    distance = jnp.abs(query_place[:, None] - key_place[None, :]).astype(jnp.float32)
    scores = scores - slopes[None, :, None, None] * distance[None, None]
    usable = key_place[None, :] < lengths[:, None]
    return jnp.where(usable[:, None, None, :], jnp.exp(scores), 0.0)


def backward_scores(
    query_heads,
    numer_heads,
    correction,
    key_heads,
    value_heads,
    query_place,
    key_place,
    slopes,
    lengths,
):
    weights = score_block(query_heads, key_heads, query_place, key_place, slopes, lengths)
    value_dots = jnp.einsum(
        "sqhe,skhe->shqk", numer_heads, value_heads, preferred_element_type=jnp.float32
    )
    grad_scores = (weights * (value_dots - correction[..., None])).astype(jnp.bfloat16)
    return (weights.astype(jnp.bfloat16), grad_scores)


def split_blocks(shard_piece, slot_count, ctx_count):
    piece_rows = shard_piece.shape[1]
    block_rows = math.gcd(piece_rows, 128)
    block_count = piece_rows // block_rows
    shaped = shard_piece.reshape(
        (shard_piece.shape[0], block_count, block_rows) + shard_piece.shape[2:]
    )
    blocks = jnp.moveaxis(shaped, 1, 0)
    row_ids = jnp.arange(piece_rows, dtype=jnp.int32)
    places = (row_ids % slot_count * ctx_count + row_ids // slot_count).reshape(
        block_count, block_rows
    )
    offsets = block_rows * jnp.arange(block_count, dtype=jnp.int32)
    return (blocks, places, offsets)


def by_gather(tokens, lengths, w_qkv, b_qv, w_out, w_gu, w_down, vectors, cotangent):
    ctx_count = lax.axis_size("ctx")
    ctx_rank = lax.axis_index("ctx")
    seq_count, slot_count, model_width = tokens.shape
    local_width = b_qv.shape[1]
    head_count = local_width // HD
    slopes = alibi_slopes(lax.axis_index("tp") * head_count, head_count)
    slot_ids = jnp.arange(slot_count, dtype=jnp.int32)
    query_place = slot_ids * ctx_count + ctx_rank
    query_live = (query_place[None, :] < lengths[:, None]).astype(jnp.float32)
    live_rows = query_live[:, :, None]
    head_shape = (seq_count, slot_count, head_count, HD)
    whole_qkv, whole_out, whole_gu, whole_down = (
        lax.all_gather(w_qkv.astype(jnp.bfloat16), ("shard", "ctx"), axis=0, tiled=True),
        lax.all_gather(w_out.astype(jnp.bfloat16), ("shard", "ctx"), axis=1, tiled=True),
        lax.all_gather(w_gu.astype(jnp.bfloat16), ("shard", "ctx"), axis=0, tiled=True),
        lax.all_gather(w_down.astype(jnp.bfloat16), ("shard", "ctx"), axis=1, tiled=True),
    )
    inputs = tokens.astype(jnp.float32)
    projected = jnp.einsum("std,dcm->stcm", tokens, whole_qkv, preferred_element_type=jnp.float32)
    query_rows = (projected[:, :, 0] + b_qv[0]).astype(jnp.bfloat16)
    key_rows = projected[:, :, 1].astype(jnp.bfloat16)
    value_rows = (projected[:, :, 2] + b_qv[1]).astype(jnp.bfloat16)
    query_heads = query_rows.reshape(head_shape)
    pairs = jnp.stack([key_rows, value_rows], axis=2)
    start_numer = jnp.zeros((seq_count, head_count, slot_count, HD), jnp.float32)
    start_denom = jnp.zeros((seq_count, head_count, slot_count), jnp.float32)
    blocks, places, offsets = split_blocks(
        lax.all_gather(pairs, "ctx", axis=1, tiled=True), slot_count, ctx_count
    )

    def forward_advance(inner_state, block_item):
        key_block, key_place, row_offset = block_item
        numerator, denominator = inner_state
        key_heads = key_block[:, :, 0].reshape(seq_count, -1, head_count, HD)
        value_heads = key_block[:, :, 1].reshape(seq_count, -1, head_count, HD)
        weights = score_block(query_heads, key_heads, query_place, key_place, slopes, lengths)
        numerator = numerator + jnp.einsum(
            "shqk,skhe->shqe",
            weights.astype(jnp.bfloat16),
            value_heads,
            preferred_element_type=jnp.float32,
        )
        return ((numerator, denominator + jnp.sum(weights, axis=-1)), None)

    result_state, unused = lax.scan(
        forward_advance, (start_numer, start_denom), (blocks, places, offsets)
    )
    numerator, denominator = result_state
    denominator = denominator + (1.0 - query_live)[:, None, :]
    attention_q = jnp.transpose(numerator / denominator[..., None], (0, 2, 1, 3))
    denom_q = jnp.transpose(denominator, (0, 2, 1))
    mixed = attention_q.reshape(seq_count, slot_count, local_width).astype(jnp.bfloat16)
    attn_part = jnp.einsum("stm,mn->stn", mixed, whole_out, preferred_element_type=jnp.float32)
    attn_branch = lax.psum(attn_part, "tp") + vectors[4]
    hidden, first_pull = jax.vjp(layer_norm, inputs + attn_branch, vectors[0], vectors[1])
    hidden_low = hidden.astype(jnp.bfloat16)
    gated = jnp.einsum("std,dcf->stcf", hidden_low, whole_gu, preferred_element_type=jnp.float32)
    activated, unit_pull = jax.vjp(gated_unit, gated[:, :, 0], gated[:, :, 1])
    act_low = activated.astype(jnp.bfloat16)
    ffn_part = jnp.einsum("stf,fn->stn", act_low, whole_down, preferred_element_type=jnp.float32)
    ffn_branch = lax.psum(ffn_part, "tp") + vectors[5]
    normed, second_pull = jax.vjp(layer_norm, hidden + ffn_branch, vectors[2], vectors[3])
    output = (normed * live_rows).astype(jnp.bfloat16)
    upstream = cotangent.astype(jnp.float32) * live_rows
    grad_second, grad_gain_two, grad_shift_two = second_pull(upstream)
    grad_ffn = grad_second.astype(jnp.bfloat16)
    grad_down = jnp.einsum("stf,stn->fn", act_low, grad_ffn, preferred_element_type=jnp.float32)
    grad_ffn_bias = jnp.sum(grad_ffn.astype(jnp.float32), axis=(0, 1))
    grad_act = jnp.einsum("stn,fn->stf", grad_ffn, whole_down, preferred_element_type=jnp.float32)
    grad_gate, grad_upper = unit_pull(grad_act)
    grad_gated = jnp.stack([grad_gate, grad_upper], axis=2).astype(jnp.bfloat16)
    grad_gu = jnp.einsum(
        "std,stcf->dcf", hidden_low, grad_gated, preferred_element_type=jnp.float32
    )
    hidden_part = jnp.einsum(
        "stcf,dcf->std", grad_gated, whole_gu, preferred_element_type=jnp.float32
    )
    grad_hidden = grad_second + lax.psum(hidden_part, "tp")
    grad_first, grad_gain_one, grad_shift_one = first_pull(grad_hidden)
    grad_attn = grad_first.astype(jnp.bfloat16)
    grad_out = jnp.einsum("stm,stn->mn", mixed, grad_attn, preferred_element_type=jnp.float32)
    grad_out_bias = jnp.sum(grad_attn.astype(jnp.float32), axis=(0, 1))
    grad_mixed = jnp.einsum(
        "stn,mn->stm", grad_attn, whole_out, preferred_element_type=jnp.float32
    ).astype(jnp.bfloat16)
    grad_mixed_heads = grad_mixed.reshape(head_shape).astype(jnp.float32)
    correction = jnp.transpose(
        jnp.sum(grad_mixed_heads * attention_q, axis=-1) / denom_q, (0, 2, 1)
    )
    numer_heads = (grad_mixed_heads / denom_q[..., None]).astype(jnp.bfloat16)
    start_query = jnp.zeros(head_shape, jnp.float32)
    start_state = (
        start_query,
        jnp.zeros((seq_count, slot_count * ctx_count, 2, local_width), jnp.float32),
    )
    blocks, places, offsets = split_blocks(
        lax.all_gather(pairs, "ctx", axis=1, tiled=True), slot_count, ctx_count
    )

    def backward_advance(current_state, block_item):
        key_block, key_place, row_offset = block_item
        key_heads = key_block[:, :, 0].reshape(seq_count, -1, head_count, HD)
        value_heads = key_block[:, :, 1].reshape(seq_count, -1, head_count, HD)
        weights_low, grad_scores = backward_scores(
            query_heads,
            numer_heads,
            correction,
            key_heads,
            value_heads,
            query_place,
            key_place,
            slopes,
            lengths,
        )
        grad_query = current_state[0] + jnp.einsum(
            "shqk,skhe->sqhe", grad_scores, key_heads, preferred_element_type=jnp.float32
        )
        grad_key = (
            jnp.einsum(
                "shqk,sqhe->skhe", grad_scores, query_heads, preferred_element_type=jnp.float32
            )
            * 0.125
        )
        grad_value = jnp.einsum(
            "shqk,sqhe->skhe", weights_low, numer_heads, preferred_element_type=jnp.float32
        )
        stacked = jnp.stack(
            [
                grad_key.reshape(seq_count, -1, local_width),
                grad_value.reshape(seq_count, -1, local_width),
            ],
            axis=2,
        )
        buffer = lax.dynamic_update_slice_in_dim(current_state[1], stacked, row_offset, axis=1)
        return ((grad_query, buffer), None)

    result_state, unused = lax.scan(backward_advance, start_state, (blocks, places, offsets))
    grad_pairs = lax.psum_scatter(
        result_state[1].astype(jnp.bfloat16), "ctx", scatter_dimension=1, tiled=True
    )
    grad_query_low = (
        (result_state[0] * 0.125).astype(jnp.bfloat16).reshape(seq_count, slot_count, local_width)
    )
    grad_proj = jnp.concatenate([grad_query_low[:, :, None], grad_pairs], axis=2)
    grad_qkv = jnp.einsum("std,stcm->dcm", tokens, grad_proj, preferred_element_type=jnp.float32)
    bias_terms = jnp.stack(
        [
            jnp.sum(grad_query_low.astype(jnp.float32), axis=(0, 1)),
            jnp.sum(grad_pairs[:, :, 1].astype(jnp.float32), axis=(0, 1)),
        ]
    )
    input_part = jnp.einsum(
        "stcm,dcm->std", grad_proj, whole_qkv, preferred_element_type=jnp.float32
    )
    input_grad = grad_first + lax.psum(input_part.astype(jnp.bfloat16), "tp").astype(jnp.float32)
    grad_weights = (
        lax.psum_scatter(grad_qkv, ("shard", "ctx"), scatter_dimension=0, tiled=True),
        lax.psum_scatter(grad_out, ("shard", "ctx"), scatter_dimension=1, tiled=True),
        lax.psum_scatter(grad_gu, ("shard", "ctx"), scatter_dimension=0, tiled=True),
        lax.psum_scatter(grad_down, ("shard", "ctx"), scatter_dimension=1, tiled=True),
    )
    vector_terms = jnp.stack(
        [grad_gain_one, grad_shift_one, grad_gain_two, grad_shift_two, grad_out_bias, grad_ffn_bias]
    )
    grad_bqv, grad_vectors = lax.psum((bias_terms, vector_terms), ("shard", "ctx"))
    return (
        output,
        input_grad,
        grad_weights[0],
        grad_bqv,
        grad_weights[1],
        grad_weights[2],
        grad_weights[3],
        grad_vectors,
    )


def solution(mesh):
    placed = (
        P("shard", "ctx", None),
        P("shard"),
        P(("shard", "ctx"), None, "tp"),
        P(None, "tp"),
        P("tp", ("shard", "ctx")),
        P(("shard", "ctx"), None, "tp"),
        P("tp", ("shard", "ctx")),
        P(),
        P("shard", "ctx", None),
    )
    return jax.shard_map(
        on_device,
        mesh=mesh,
        in_specs=placed,
        out_specs=(
            P("shard", "ctx", None),
            P("shard", "ctx", None),
            P(("shard", "ctx"), None, "tp"),
            P(None, "tp"),
            P("tp", ("shard", "ctx")),
            P(("shard", "ctx"), None, "tp"),
            P("tp", ("shard", "ctx")),
            P(),
        ),
        check_vma=False,
    )
```

```python
import functools
import math

import jax
import jax.numpy as jnp
import numpy as np
from jax import lax
from jax.experimental import pallas as pl
from jax.experimental.pallas import tpu as pltpu
from jax.sharding import PartitionSpec as P

H = 12
HD = 64
LOG2E = math.log2(math.e)
FAR = 1e30
TILE = 64
BLOCK = 512
WIDTH = 384
EXTRA = 16

epsilon = 1e-12
f32 = jnp.float32
bf16 = jnp.bfloat16
VMEM = pl.BlockSpec(memory_space=pltpu.VMEM)
SMEM = pl.BlockSpec(memory_space=pltpu.SMEM)


def slope_table():
    power = 2 ** (H.bit_length() - 1)
    heads = np.arange(H)
    early = -8.0 * (heads + 1) / power
    later = -4.0 * (2 * (heads - power) + 1) / power
    return np.exp2(np.where(heads < power, early, later)).astype(np.float32)


def dot_nn(a, b):
    return jnp.dot(a, b, preferred_element_type=f32)


def dot_nt(a, b):
    return lax.dot_general(a, b, (((1,), (1,)), ((), ())), preferred_element_type=f32)


def params(*semantics):
    return pltpu.CompilerParams(
        dimension_semantics=semantics or None, vmem_limit_bytes=20 * 1024 * 1024
    )


def cost(flops, nbytes, exps=0):
    return pl.CostEstimate(flops=int(flops), bytes_accessed=int(nbytes), transcendentals=int(exps))


def shape(dims, dtype):
    return jax.ShapeDtypeStruct(dims, dtype)


def xor_pairs(axis, distance):
    return [(i, i ^ distance) for i in range(lax.axis_size(axis))]


def swap(value, axis, distance):
    return lax.ppermute(value, axis, xor_pairs(axis, distance))


def after(values, *done):
    return lax.optimization_barrier((*values, *done))[: len(values)]


def live_mask(length, rank, n_ctx, slots):
    slot = lax.broadcasted_iota(jnp.int32, (slots, 1), 0)
    return jnp.where(slot * n_ctx + rank < length, 1.0, 0.0).astype(f32)


def normalise(z):
    centred = z - jnp.mean(z, axis=-1, keepdims=True)
    spread = jnp.mean(centred * centred, axis=-1, keepdims=True)
    scale = lax.rsqrt(spread + epsilon)
    return centred * scale, scale


def normalise_back(grad_hat, hat, scale):
    inner = jnp.mean(grad_hat * hat, axis=-1, keepdims=True)
    return scale * (grad_hat - jnp.mean(grad_hat, axis=-1, keepdims=True) - hat * inner)


def assemble_kernel(n, ids, *refs):
    pieces, whole = refs[:4], refs[4]
    y, c, z = ids[0], ids[1], ids[2]
    rows = pieces[0].shape[0] // n
    for k in range(4):
        for kz in range(n):
            index = ((y ^ (k // 2)) * 2 + (c ^ (k % 2))) * n + (z ^ kz)
            place = pl.ds(pl.multiple_of(index * rows, rows), rows)
            whole[place, :] = pieces[k][kz * rows : (kz + 1) * rows, :]


def assemble(ids, pieces, n):
    rows, wide = pieces[0].shape
    column = lambda size: pl.BlockSpec((size, wide // 3), lambda j: (0, j))
    return pl.pallas_call(
        functools.partial(assemble_kernel, n),
        grid=(3,),
        out_shape=shape((4 * rows, wide), bf16),
        in_specs=[SMEM] + [column(rows)] * 4,
        out_specs=column(4 * rows),
        compiler_params=params("arbitrary"),
        cost_estimate=cost(0, 16 * rows * wide),
        name="assemble",
    )(ids, *pieces)


def project_kernel(n, seqs, heads, ids, tok, bias, *refs):
    pieces = refs[: 4 * n]
    sends = refs[4 * n : 5 * n]
    whole = refs[5 * n]
    stage = refs[5 * n + 1]
    y, c, z = ids[0], ids[1], ids[2]
    rows = pieces[0].shape[0]
    for k in range(4 * n):
        ky, kc, kz = k // (2 * n), k // n % 2, k % n
        index = ((y ^ ky) * 2 + (c ^ kc)) * n + (z ^ kz)
        whole[pl.ds(pl.multiple_of(index * rows, rows), rows), :] = pieces[k][...]
    slots = sends[0].shape[1]
    width = heads * HD
    per = seqs * heads // n
    for s in range(seqs):
        acc = dot_nn(tok[s * slots : (s + 1) * slots, :], whole[...]) + bias[...]
        turned = acc.astype(bf16).T
        for h in range(heads):
            i = s * heads + h
            at = ((i % n) * per + i // n) * 3
            for part in range(3):
                first = part * width + h * HD
                stage[(at + part) * HD : (at + part + 1) * HD, :] = turned[first : first + HD, :]
    size = per * 3 * HD
    for d in range(n):
        sends[d][...] = stage[pl.ds(pl.multiple_of((z ^ d) * size, size), size), :]


def project(ids, tok, bias, pieces, n, seqs, heads):
    slots = tok.shape[0] // seqs
    size = seqs * heads // n * 3 * HD
    model, wide = tok.shape[1], bias.shape[1]
    return pl.pallas_call(
        functools.partial(project_kernel, n, seqs, heads),
        out_shape=[shape((size, slots), bf16)] * n + [shape((model, wide), bf16)],
        in_specs=[SMEM] + [VMEM] * (2 + len(pieces)),
        out_specs=[VMEM] * (n + 1),
        scratch_shapes=[pltpu.VMEM((size * n, slots), bf16)],
        compiler_params=params(),
        cost_estimate=cost(2 * tok.shape[0] * model * wide, 6e6),
        name="project",
    )(ids, tok, bias, *pieces)


def pair_scalars(n, heads, ids, lens, slopes):
    j = pl.program_id(0)
    z, t = ids[2], ids[3]
    i = z + n * j
    s = i // heads
    h = i - s * heads
    return z, lens[s], slopes[t * heads + h] * LOG2E


def query_place(n, slots, z, d):
    lane = lax.broadcasted_iota(jnp.int32, (1, slots), 1)
    return lane * n + (z ^ d)


def key_place(n, z, tile, length, slope):
    row = lax.broadcasted_iota(jnp.int32, (TILE, 1), 0)
    places = []
    for d in range(n):
        place = (tile * TILE + row) * n + (z ^ d)
        places.append(jnp.where(place < length, place.astype(f32) * slope, FAR))
    return jnp.concatenate(places, axis=0)


def gather_rows(ref, tile, n):
    rows = pl.ds(pl.multiple_of(tile * TILE, TILE), TILE)
    return jnp.concatenate([ref[d, rows, :] for d in range(n)], axis=0)


def attend_kernel(n, heads, ids, lens, slopes, *refs):
    inputs = refs[:n]
    outs = refs[n : 2 * n]
    att_ref, den_ref = refs[2 * n], refs[2 * n + 1]
    k_s, v_s, acc, den = refs[2 * n + 2 :]
    slots = inputs[0].shape[1]
    z, length, slope = pair_scalars(n, heads, ids, lens, slopes)
    for d in range(n):
        k_s[d] = inputs[d][HD : 2 * HD, :].T
        v_s[d] = inputs[d][2 * HD : 3 * HD, :].T
    acc[...] = jnp.zeros_like(acc)
    den[...] = jnp.zeros_like(den)

    def tile_step(tile, unused):
        keys = gather_rows(k_s, tile, n)
        values = gather_rows(v_s, tile, n).T
        places = key_place(n, z, tile, length, slope)
        for d in range(n):
            cols = slice(d * slots, (d + 1) * slots)
            there = query_place(n, slots, z, d).astype(f32) * slope
            scores = dot_nn(keys, inputs[d][0:HD, :]) * (0.125 * LOG2E)
            e = jnp.exp2(scores - jnp.abs(there - places))
            den[:, cols] += jnp.sum(e, axis=0, keepdims=True)
            acc[:, cols] += dot_nn(values, e.astype(bf16))
        return unused

    step = TILE * n
    lax.fori_loop(0, (length + step - 1) // step, tile_step, 0)
    for d in range(n):
        cols = slice(d * slots, (d + 1) * slots)
        padded = jnp.where(query_place(n, slots, z, d) < length, 0.0, 1.0)
        total = den[:, cols] + padded
        att = acc[:, cols] / total
        att_ref[:, cols] = att
        den_ref[0, :, cols] = total
        outs[d][...] = att.astype(bf16)


def attend(ids, lens, slopes, blocks, n, heads, per):
    slots = blocks[0].shape[1]
    every = n * slots
    return pl.pallas_call(
        functools.partial(attend_kernel, n, heads),
        grid=(per,),
        out_shape=[shape((per * HD, slots), bf16)] * n
        + [shape((per * HD, every), f32), shape((per, 1, every), f32)],
        in_specs=[SMEM] * 3 + [pl.BlockSpec((3 * HD, slots), lambda j: (j, 0))] * n,
        out_specs=[pl.BlockSpec((HD, slots), lambda j: (j, 0))] * n
        + [
            pl.BlockSpec((HD, every), lambda j: (j, 0)),
            pl.BlockSpec((1, 1, every), lambda j: (j, 0, 0)),
        ],
        scratch_shapes=[
            pltpu.VMEM((n, slots, HD), bf16),
            pltpu.VMEM((n, slots, HD), bf16),
            pltpu.VMEM((HD, every), f32),
            pltpu.VMEM((1, every), f32),
        ],
        compiler_params=params("arbitrary"),
        cost_estimate=cost(per * every * every * HD * 8, 3e6, per * every * every),
        name="attend",
    )(ids, lens, slopes, *blocks)


def attend_back_kernel(n, heads, ids, lens, slopes, *refs):
    inputs = refs[:n]
    grads = refs[n : 2 * n]
    att_ref, den_ref = refs[2 * n], refs[2 * n + 1]
    outs = refs[2 * n + 2 : 3 * n + 2]
    k_s, v_s, q_s, g_s, dn, cor, dq, dk, dv = refs[3 * n + 2 :]
    slots = inputs[0].shape[1]
    z, length, slope = pair_scalars(n, heads, ids, lens, slopes)
    for d in range(n):
        cols = slice(d * slots, (d + 1) * slots)
        k_s[d] = inputs[d][HD : 2 * HD, :].T
        v_s[d] = inputs[d][2 * HD : 3 * HD, :].T
        q_s[d] = inputs[d][0:HD, :].T
        inverse = 1.0 / den_ref[0, :, cols]
        mixed = grads[d][...].astype(f32)
        numer = (mixed * inverse).astype(bf16)
        dn[:, cols] = numer
        g_s[d] = numer.T
        cor[:, cols] = jnp.sum(mixed * att_ref[:, cols], axis=0, keepdims=True) * inverse
    dq[...] = jnp.zeros_like(dq)
    dk[...] = jnp.zeros_like(dk)
    dv[...] = jnp.zeros_like(dv)

    def tile_step(tile, unused):
        keys = gather_rows(k_s, tile, n)
        values = gather_rows(v_s, tile, n)
        keys_t = keys.T
        places = key_place(n, z, tile, length, slope)
        grad_k = jnp.zeros((n * TILE, HD), f32)
        grad_v = jnp.zeros((n * TILE, HD), f32)
        for d in range(n):
            cols = slice(d * slots, (d + 1) * slots)
            there = query_place(n, slots, z, d).astype(f32) * slope
            scores = dot_nn(keys, inputs[d][0:HD, :]) * (0.125 * LOG2E)
            e = jnp.exp2(scores - jnp.abs(there - places))
            inner = dot_nn(values, dn[:, cols])
            ds = (e * (inner - cor[:, cols])).astype(bf16)
            dq[:, cols] += dot_nn(keys_t, ds)
            grad_k += dot_nn(ds, q_s[d])
            grad_v += dot_nn(e.astype(bf16), g_s[d])
        rows = pl.ds(pl.multiple_of(tile * TILE, TILE), TILE)
        for d in range(n):
            dk[d, rows, :] = grad_k[d * TILE : (d + 1) * TILE, :]
            dv[d, rows, :] = grad_v[d * TILE : (d + 1) * TILE, :]
        return unused

    step = TILE * n
    lax.fori_loop(0, (length + step - 1) // step, tile_step, 0)
    for d in range(n):
        cols = slice(d * slots, (d + 1) * slots)
        outs[d][0:HD, :] = (dq[:, cols] * 0.125).astype(bf16)
        outs[d][HD : 2 * HD, :] = (dk[d] * 0.125).astype(bf16).T
        outs[d][2 * HD : 3 * HD, :] = dv[d].astype(bf16).T


def attend_back(ids, lens, slopes, blocks, grads, att, den, n, heads, per):
    slots = blocks[0].shape[1]
    every = n * slots
    rows = [pltpu.VMEM((n, slots, HD), bf16)] * 4
    return pl.pallas_call(
        functools.partial(attend_back_kernel, n, heads),
        grid=(per,),
        out_shape=[shape((per * 3 * HD, slots), bf16)] * n,
        in_specs=[SMEM] * 3
        + [pl.BlockSpec((3 * HD, slots), lambda j: (j, 0))] * n
        + [pl.BlockSpec((HD, slots), lambda j: (j, 0))] * n
        + [
            pl.BlockSpec((HD, every), lambda j: (j, 0)),
            pl.BlockSpec((1, 1, every), lambda j: (j, 0, 0)),
        ],
        out_specs=[pl.BlockSpec((3 * HD, slots), lambda j: (j, 0))] * n,
        scratch_shapes=rows
        + [
            pltpu.VMEM((HD, every), bf16),
            pltpu.VMEM((1, every), f32),
            pltpu.VMEM((HD, every), f32),
            pltpu.VMEM((n, slots, HD), f32),
            pltpu.VMEM((n, slots, HD), f32),
        ],
        compiler_params=params("arbitrary"),
        cost_estimate=cost(per * every * every * HD * 20, 5e6, per * every * every),
        name="attend_back",
    )(ids, lens, slopes, *blocks, *grads, att, den)


def mix_kernel(n, seqs, heads, ids, wo, *refs):
    inputs = refs[:n]
    parts = refs[n : n + seqs]
    mixed, stage = refs[n + seqs :]
    z = ids[2]
    slots = inputs[0].shape[1]
    per = seqs * heads // n
    size = per * HD
    for d in range(n):
        stage[pl.ds(pl.multiple_of((z ^ d) * size, size), size), :] = inputs[d][...]
    for s in range(seqs):
        columns = []
        for h in range(heads):
            i = s * heads + h
            at = (i % n) * per + i // n
            columns.append(stage[at * HD : (at + 1) * HD, :])
        rows = slice(s * slots, (s + 1) * slots)
        ours = jnp.concatenate(columns, axis=0).T
        mixed[rows, :] = ours
        parts[s][...] = dot_nt(ours, wo[...]).astype(bf16)


def mix(ids, packed, blocks, n, seqs, heads):
    slots = blocks[0].shape[1]
    model = packed.shape[0]
    width = heads * HD
    tokens = seqs * slots
    return pl.pallas_call(
        functools.partial(mix_kernel, n, seqs, heads),
        grid=(1,),
        out_shape=[shape((slots, model), bf16)] * seqs + [shape((tokens, width), bf16)],
        in_specs=[SMEM, pl.BlockSpec((model, width), lambda i: (0, packed.shape[1] // width - 1))]
        + [VMEM] * n,
        out_specs=[VMEM] * (seqs + 1),
        scratch_shapes=[pltpu.VMEM((seqs * heads * HD, slots), bf16)],
        compiler_params=params("arbitrary"),
        cost_estimate=cost(2 * tokens * model * width, 3e6),
        name="mix",
    )(ids, packed, *blocks)


def unit_kernel(tok, own, other, vec, wg, wu, wd, hidden, low, act, gel, slope, part, acc):
    j = pl.program_id(0)

    @pl.when(j == 0)
    def _():
        branch = own[...].astype(f32) + other[...].astype(f32) + vec[4:5, :]
        hat, _ = normalise(tok[...].astype(f32) + branch)
        h = hat * vec[0:1, :] + vec[1:2, :]
        hidden[...] = h
        low[...] = h.astype(bf16)
        acc[...] = jnp.zeros_like(acc)

    gate = dot_nn(low[...], wg[...])
    upper = dot_nn(low[...], wu[...])
    phi = 0.5 * (1.0 + lax.erf(gate * math.sqrt(0.5)))
    density = jnp.exp(gate * gate * -0.5) * (1.0 / math.sqrt(2.0 * math.pi))
    unit = gate * phi
    acted = (unit * upper).astype(bf16)
    act[...] = acted
    gel[...] = unit.astype(bf16)
    slope[...] = (upper * (phi + gate * density)).astype(bf16)
    acc[...] += dot_nt(acted, wd[...])

    @pl.when(j == pl.num_programs(0) - 1)
    def _():
        part[...] = acc[...].astype(bf16)


def unit(s, tok, own, other, vec, front, back):
    tokens, model = own.shape
    hidden_units = back.shape[1]
    steps = hidden_units // BLOCK
    fixed = lambda j: (0, 0)
    whole = pl.BlockSpec((tokens, model), fixed)
    weight = lambda start: pl.BlockSpec((model, BLOCK), lambda j: (0, start + j))
    inner = pl.BlockSpec((tokens, BLOCK), lambda j: (0, j))
    return pl.pallas_call(
        unit_kernel,
        grid=(steps,),
        out_shape=[shape((tokens, model), f32), shape((tokens, model), bf16)]
        + [shape((tokens, hidden_units), bf16)] * 3
        + [shape((tokens, model), bf16)],
        in_specs=[
            pl.BlockSpec((tokens, model), lambda j: (s, 0)),
            whole,
            whole,
            pl.BlockSpec(vec.shape, fixed),
            weight(0),
            weight(steps),
            weight(0),
        ],
        out_specs=[whole, whole, inner, inner, inner, whole],
        scratch_shapes=[pltpu.VMEM((tokens, model), f32)],
        compiler_params=params("arbitrary"),
        cost_estimate=cost(6 * tokens * model * hidden_units, 13e6, 2 * tokens * hidden_units),
        name="unit",
    )(tok, own, other, vec, front, front, back)


def unit_back_kernel(
    n, s, ids, lens, hidden, own, other, cot, vec, wg, wu, wd, gel, slope,
    output, dz2, dffn, dgate, dup, part, sums, acc,
):
    j = pl.program_id(0)

    @pl.when(j == 0)
    def _():
        live = live_mask(lens[s], ids[2], n, hidden.shape[0])
        branch = own[...].astype(f32) + other[...].astype(f32) + vec[5:6, :]
        hat, scale = normalise(hidden[...] + branch)
        output[...] = (live * (hat * vec[2:3, :] + vec[3:4, :])).astype(bf16)
        gy = cot[...].astype(f32) * live
        grad = normalise_back(gy * vec[2:3, :], hat, scale)
        dz2[...] = grad
        low = grad.astype(bf16)
        dffn[...] = low
        sums[0:1, :] = jnp.sum(gy * hat, axis=0, keepdims=True)
        sums[1:2, :] = jnp.sum(gy, axis=0, keepdims=True)
        sums[2:3, :] = jnp.sum(low.astype(f32), axis=0, keepdims=True)
        sums[3:8, :] = jnp.zeros_like(sums[3:8, :])
        acc[...] = jnp.zeros_like(acc)

    dact = dot_nn(dffn[...], wd[...])
    upper = (dact * gel[...].astype(f32)).astype(bf16)
    gate = (dact * slope[...].astype(f32)).astype(bf16)
    dgate[...] = gate
    dup[...] = upper
    acc[...] += dot_nt(gate, wg[...]) + dot_nt(upper, wu[...])

    @pl.when(j == pl.num_programs(0) - 1)
    def _():
        part[...] = acc[...].astype(bf16)


def unit_back(s, ids, lens, hidden, own, other, cot, vec, front, back, gel, slope, n):
    tokens, model = hidden.shape
    hidden_units = gel.shape[1]
    steps = hidden_units // BLOCK
    fixed = lambda j: (0, 0)
    whole = pl.BlockSpec((tokens, model), fixed)
    weight = lambda start: pl.BlockSpec((model, BLOCK), lambda j: (0, start + j))
    inner = pl.BlockSpec((tokens, BLOCK), lambda j: (0, j))
    return pl.pallas_call(
        functools.partial(unit_back_kernel, n, s),
        grid=(steps,),
        out_shape=[
            shape((tokens, model), bf16),
            shape((tokens, model), f32),
            shape((tokens, model), bf16),
            shape((tokens, hidden_units), bf16),
            shape((tokens, hidden_units), bf16),
            shape((tokens, model), bf16),
            shape((8, model), f32),
        ],
        in_specs=[SMEM, SMEM, whole, whole, whole]
        + [pl.BlockSpec((tokens, model), lambda j: (s, 0)), pl.BlockSpec(vec.shape, fixed)]
        + [weight(0), weight(steps), weight(0), inner, inner],
        out_specs=[whole, whole, whole, inner, inner, whole, pl.BlockSpec((8, model), fixed)],
        scratch_shapes=[pltpu.VMEM((tokens, model), f32)],
        compiler_params=params("arbitrary"),
        cost_estimate=cost(6 * tokens * model * hidden_units, 14e6),
        name="unit_back",
    )(ids, lens, hidden, own, other, cot, vec, front, front, back, gel, slope)


def row_starts(ids, quarter):
    y, c = ids[0], ids[1]
    keep = [(y * 2 + c) * quarter, ((1 - y) * 2 + c) * quarter]
    send = [(y * 2 + 1 - c) * quarter, ((1 - y) * 2 + 1 - c) * quarter]
    return send, keep


def arrange(ids, turned, left):
    quarter = turned.shape[0] // 4
    send, keep = row_starts(ids, quarter)
    for k, start in enumerate(send + keep):
        rows = pl.ds(pl.multiple_of(start, quarter), quarter)
        left[k * quarter : (k + 1) * quarter, :] = turned[rows, :]


def write_rows(left, right, send, keep):
    grad = dot_nn(left[...], right).astype(bf16)
    half = grad.shape[0] // 2
    send[0:half, :] = grad[:half]
    keep[0:half, :] = grad[half:]


def weight_kernel(steps, seqs, ids, *refs):
    low, dffn, dgate, dup, act = (refs[i * seqs : (i + 1) * seqs] for i in range(5))
    send, keep, left, turned = refs[5 * seqs :]
    j = pl.program_id(0)
    joined = lambda group: jnp.concatenate([ref[...] for ref in group], axis=0)

    @pl.when(j == 0)
    def _():
        for k, group in enumerate((low, dffn)):
            turned[...] = joined(group).T
            arrange(ids, turned, left.at[k])

    @pl.when(j < steps)
    def _():
        write_rows(left.at[0], joined(dgate), send, keep)

    @pl.when((j >= steps) & (j < 2 * steps))
    def _():
        write_rows(left.at[0], joined(dup), send, keep)

    @pl.when(j >= 2 * steps)
    def _():
        write_rows(left.at[1], joined(act), send, keep)


def weight_grads(ids, low, dffn, dgate, dup, act):
    seqs = len(low)
    tokens, model = low[0].shape
    hidden_units = act[0].shape[1]
    steps = hidden_units // BLOCK
    whole = pl.BlockSpec((tokens, model), lambda j: (0, 0))
    column = lambda start: pl.BlockSpec(
        (tokens, BLOCK), lambda j: (0, jnp.clip(j - start, 0, steps - 1))
    )
    out = pl.BlockSpec((model // 2, BLOCK), lambda j: (0, j))
    return pl.pallas_call(
        functools.partial(weight_kernel, steps, seqs),
        grid=(3 * steps,),
        out_shape=[shape((model // 2, 3 * hidden_units), bf16)] * 2,
        in_specs=[SMEM]
        + [whole] * (2 * seqs)
        + [column(0)] * seqs
        + [column(steps)] * seqs
        + [column(2 * steps)] * seqs,
        out_specs=[out, out],
        scratch_shapes=[
            pltpu.VMEM((2, model, tokens * seqs), bf16),
            pltpu.VMEM((model, tokens * seqs), bf16),
        ],
        compiler_params=params("arbitrary"),
        cost_estimate=cost(6 * tokens * seqs * model * hidden_units, 14e6),
        name="weight_grads",
    )(ids, *low, *dffn, *dgate, *dup, *act)


def mix_back_kernel(n, seqs, heads, ids, tok, vec, wo, mixed, *refs):
    own, other, dz2, hown, hother = (refs[i * seqs : (i + 1) * seqs] for i in range(5))
    refs = refs[5 * seqs :]
    sends = refs[:n]
    dz1, send, keep, sums = refs[n : n + 4]
    stage, left, turned_low = refs[n + 4 :]
    z = ids[2]
    slots = sends[0].shape[1]
    per = seqs * heads // n
    sums[...] = jnp.zeros_like(sums)
    for s in range(seqs):
        rows = slice(s * slots, (s + 1) * slots)
        branch = own[s][...].astype(f32) + other[s][...].astype(f32) + vec[4:5, :]
        hat, scale = normalise(tok[rows, :].astype(f32) + branch)
        gh = dz2[s][...] + (hown[s][...].astype(f32) + hother[s][...].astype(f32))
        grad = normalise_back(gh * vec[0:1, :], hat, scale)
        dz1[rows, :] = grad
        low = grad.astype(bf16)
        sums[0:1, :] += jnp.sum(gh * hat, axis=0, keepdims=True)
        sums[1:2, :] += jnp.sum(gh, axis=0, keepdims=True)
        sums[2:3, :] += jnp.sum(low.astype(f32), axis=0, keepdims=True)
        turned_low[:, rows] = low.T
        turned = dot_nn(low, wo[...]).astype(bf16).T
        for h in range(heads):
            i = s * heads + h
            at = (i % n) * per + i // n
            stage[at * HD : (at + 1) * HD, :] = turned[h * HD : (h + 1) * HD, :]
    size = per * HD
    for d in range(n):
        sends[d][...] = stage[pl.ds(pl.multiple_of((z ^ d) * size, size), size), :]
    arrange(ids, turned_low, left)
    write_rows(left, mixed[...], send, keep)
    for ref in (send, keep):
        ref[ref.shape[0] - EXTRA :, :] = jnp.zeros((EXTRA, ref.shape[1]), bf16)


def mix_back(ids, tok, vec, front, mixed, own, other, dz2, hown, hother, n, heads):
    seqs = len(own)
    tokens, model = tok.shape
    slots = tokens // seqs
    width = heads * HD
    size = seqs * heads // n * HD
    rows = model // 2 + EXTRA
    last = pl.BlockSpec((rows, width), lambda i: (0, 3))
    return pl.pallas_call(
        functools.partial(mix_back_kernel, n, seqs, heads),
        grid=(1,),
        out_shape=[shape((size, slots), bf16)] * n
        + [shape((tokens, model), f32)]
        + [shape((rows, 4 * width), bf16)] * 2
        + [shape((8, model), f32)],
        in_specs=[SMEM, VMEM, VMEM]
        + [pl.BlockSpec((model, width), lambda i: (0, front.shape[1] // width - 1)), VMEM]
        + [VMEM] * (5 * seqs),
        out_specs=[VMEM] * (n + 1) + [last, last, VMEM],
        scratch_shapes=[
            pltpu.VMEM((size * n, slots), bf16),
            pltpu.VMEM((model, tokens), bf16),
            pltpu.VMEM((model, tokens), bf16),
        ],
        compiler_params=params("arbitrary"),
        cost_estimate=cost(4 * tokens * model * width, 10e6),
        name="mix_back",
    )(ids, tok, vec, front, mixed, *own, *other, *dz2, *hown, *hother)


def project_back_kernel(n, seqs, heads, ids, tok, whole, small, far, near, *refs):
    inputs = refs[:n]
    part, send, keep = refs[n : n + 3]
    stage, right, left, turned = refs[n + 3 :]
    z = ids[2]
    slots = inputs[0].shape[1]
    per = seqs * heads // n
    width = heads * HD
    size = per * 3 * HD
    for d in range(n):
        stage[pl.ds(pl.multiple_of((z ^ d) * size, size), size), :] = inputs[d][...]
    for s in range(seqs):
        for c in range(3):
            columns = []
            for h in range(heads):
                i = s * heads + h
                at = ((i % n) * per + i // n) * 3 + c
                columns.append(stage[at * HD : (at + 1) * HD, :])
            ours = jnp.concatenate(columns, axis=0).T
            right[s * slots : (s + 1) * slots, c * width : (c + 1) * width] = ours
    part[...] = dot_nt(right[...], whole[...]).astype(bf16)
    turned[...] = tok[...].T
    arrange(ids, turned, left)
    for c in range(3):
        cols = slice(c * width, (c + 1) * width)
        write_rows(left, right[:, cols], send.at[:, cols], keep.at[:, cols])
    ones = jnp.ones((8, right.shape[0]), bf16)
    sums = dot_nn(ones, right[...])
    line = jnp.concatenate([sums[:, :width], sums[:, 2 * width :]], axis=1)
    row = lax.broadcasted_iota(jnp.int32, (8, 1), 0)
    rows = jnp.where(row == 6, line, small[...])
    rows = jnp.concatenate([rows, jnp.zeros_like(rows)], axis=0).astype(bf16)
    for ref in (send, keep):
        ref[ref.shape[0] - EXTRA :, :] = jnp.zeros((EXTRA, ref.shape[1]), bf16)
        ref[ref.shape[0] - EXTRA :, : 2 * width] = rows


def project_back(ids, tok, whole, small, grads, blocks, n, seqs, heads):
    tokens, model = tok.shape
    slots = tokens // seqs
    wide = whole.shape[1]
    return pl.pallas_call(
        functools.partial(project_back_kernel, n, seqs, heads),
        grid=(1,),
        out_shape=[shape((tokens, model), bf16)] + [shape(grads[0].shape, bf16)] * 2,
        in_specs=[SMEM] + [VMEM] * 3 + [pl.BlockSpec(memory_space=pl.ANY)] * 2 + [VMEM] * n,
        out_specs=[VMEM] + [pl.BlockSpec((grads[0].shape[0], wide), lambda i: (0, 0))] * 2,
        input_output_aliases={4: 1, 5: 2},
        scratch_shapes=[
            pltpu.VMEM((seqs * heads * 3 * HD, slots), bf16),
            pltpu.VMEM((tokens, wide), bf16),
            pltpu.VMEM((model, tokens), bf16),
            pltpu.VMEM((model, tokens), bf16),
        ],
        compiler_params=params("arbitrary"),
        cost_estimate=cost(4 * tokens * model * wide, 8e6),
        name="project_back",
    )(ids, tok, whole, small, *grads, *blocks)


def fold_core_kernel(extra, keep, recv, mine, *sends):
    half = (keep.shape[0] - extra) // 2
    mine[0:half, :] = keep[0:half, :].astype(f32) + recv[0:half, :].astype(f32)
    rest = (keep[half:, :].astype(f32) + recv[half:, :].astype(f32)).astype(bf16)
    size = sends[0].shape[1]
    for k, send in enumerate(sends):
        send[...] = rest[:, k * size : (k + 1) * size]
    if extra:
        mine[half:, :] = rest[half:, :].astype(f32)


def fold_core(keep, recv, extra):
    rows, wide = keep.shape
    out = (rows - extra) // 2 + extra
    steps = 1 if extra else 3
    parts = 2 if extra else 1
    column = lambda size: pl.BlockSpec((size, wide // steps), lambda j: (0, j))
    return pl.pallas_call(
        functools.partial(fold_core_kernel, extra),
        grid=(steps,),
        out_shape=[shape((out, wide), f32)] + [shape((out, wide // parts), bf16)] * parts,
        in_specs=[column(rows)] * 2,
        out_specs=[column(out)]
        + [pl.BlockSpec((out, wide // steps // parts), lambda j: (0, j))] * parts,
        compiler_params=params("arbitrary"),
        cost_estimate=cost(rows * wide, 7 * rows * wide),
        name="fold_core",
    )(keep, recv)


def fold_y_kernel(n, extra, parts, ids, mine, *refs):
    recvs, own, sends, stage = refs[:parts], refs[parts], refs[parts + 1 : -1], refs[-1]
    z = ids[2]
    rows = mine.shape[0] - extra
    size = rows // n
    recv = jnp.concatenate([ref[...] for ref in recvs], axis=1)
    stage[...] = mine[...] + recv.astype(f32)
    for d in range(n):
        block = stage[pl.ds(pl.multiple_of((z ^ d) * size, size), size), :]
        if d:
            sends[d - 1][0:size, :] = block.astype(bf16)
            if extra:
                sends[d - 1][size:, :] = stage[rows:, :].astype(bf16)
        else:
            own[0:size, :] = block
            if extra:
                own[size:, :] = stage[rows:, :].astype(bf16).astype(f32)


def fold_y(ids, mine, recvs, n, extra):
    rows, wide = mine.shape
    out = (rows - extra) // n + extra
    steps = 1 if extra else 3
    parts = len(recvs)
    column = lambda size: pl.BlockSpec((size, wide // steps), lambda j: (0, j))
    return pl.pallas_call(
        functools.partial(fold_y_kernel, n, extra, parts),
        grid=(steps,),
        out_shape=[shape((out, wide), f32)] + [shape((out, wide), bf16)] * (n - 1),
        in_specs=[SMEM, column(rows)]
        + [pl.BlockSpec((rows, wide // steps // parts), lambda j: (0, j))] * parts,
        out_specs=[column(out)] * n,
        scratch_shapes=[pltpu.VMEM((rows, wide // steps), f32)],
        compiler_params=params("arbitrary"),
        cost_estimate=cost(rows * wide, 9 * rows * wide),
        name="fold_y",
    )(ids, mine, *recvs)


def fold_z(own, got):
    return (own + got[0].astype(f32)) + (got[1].astype(f32) + got[2].astype(f32))


def fits(tokens, b_qv, w_qkv, w_gu):
    n = lax.axis_size("ctx")
    heads = b_qv.shape[1] // HD
    return (
        n == 4
        and lax.axis_size("shard") == 4
        and lax.axis_size("tp") == 2
        and (tokens.shape[0] * heads) % n == 0
        and w_qkv.shape[0] % 16 == 0
        and tokens.shape[1] % 256 == 0
        and b_qv.shape[1] == WIDTH
        and w_gu.shape[2] % BLOCK == 0
        and w_gu.shape[2] % WIDTH == 0
    )


def on_device(tokens, lengths, w_qkv, b_qv, w_out, w_gu, w_down, vectors, cotangent):
    if not fits(tokens, b_qv, w_qkv, w_gu):
        return by_gather(tokens, lengths, w_qkv, b_qv, w_out, w_gu, w_down, vectors, cotangent)
    n = lax.axis_size("ctx")
    seqs, slots, model = tokens.shape
    width = b_qv.shape[1]
    heads = width // HD
    per = seqs * heads // n
    units = w_gu.shape[2]
    rows = w_qkv.shape[0]
    count = seqs * slots
    shard = lax.axis_index("shard")
    ids = jnp.stack(
        [shard // 2, shard % 2, lax.axis_index("ctx"), lax.axis_index("tp")]
    ).astype(jnp.int32)
    slopes = jnp.asarray(slope_table())
    tok = tokens.reshape(count, model)
    cot = cotangent.reshape(count, model)

    first = [w_qkv.astype(bf16).reshape(rows, 3 * width)]
    first += [swap(first[0], "ctx", d) for d in range(1, n)]
    first += [swap(piece, "shard", 2) for piece in first]
    by_core = [swap(piece, "shard", 1) for piece in first]
    pieces = first[:n] + by_core[:n] + first[n:] + by_core[n:]
    front = jnp.concatenate([w_gu.reshape(rows, 2 * units), w_out.T], axis=1).astype(bf16)
    back = w_down.T.astype(bf16)
    (front,) = after([front], *pieces[1:n])
    front = [front] + [swap(front, "ctx", d) for d in range(1, n)]

    bias = jnp.concatenate([b_qv[0], jnp.zeros_like(b_qv[0]), b_qv[1]])[None, :]
    *sends, whole = project(ids, tok, bias, pieces, n, seqs, heads)
    blocks = [sends[0]] + [swap(sends[d], "ctx", d) for d in range(1, n)]
    front = jnp.concatenate(after(front, whole), axis=0)
    front_y = swap(front, "shard", 2)
    (back,) = after([back], *blocks)
    back = [back] + [swap(back, "ctx", d) for d in range(1, n)]
    *outs, att, den = attend(ids, lengths, slopes, blocks, n, heads, per)
    front, front_y = after([front, front_y], outs[0])
    front = [front, swap(front, "shard", 1), front_y, swap(front_y, "shard", 1)]
    back = jnp.concatenate(after(back, outs[0]), axis=0)
    back_y = swap(back, "shard", 2)
    outs = [outs[0]] + [swap(outs[d], "ctx", d) for d in range(1, n)]
    front = assemble(ids, front, n)
    *part, mixed = mix(ids, front, outs, n, seqs, heads)
    part_other = [swap(value, "tp", 1) for value in part]
    back, back_y = after([back, back_y], part[0])
    back = [back, swap(back, "shard", 1), back_y, swap(back_y, "shard", 1)]
    back = assemble(ids, back, n)
    hidden, low, act, gel, slope, ffn = zip(
        *(
            unit(s, tok, part[s], part_other[s], vectors, front, back)
            for s in range(seqs)
        )
    )
    ffn_other = [swap(value, "tp", 1) for value in ffn]
    output, dz2, dffn, dgate, dup, dlow, sums_two = zip(
        *(
            unit_back(
                s, ids, lengths, hidden[s], ffn[s], ffn_other[s], cot, vectors, front, back,
                gel[s], slope[s], n,
            )
            for s in range(seqs)
        )
    )
    dlow_other = [swap(value, "tp", 1) for value in dlow]
    far, near = weight_grads(ids, low, dffn, dgate, dup, act)
    *dlow_other, far = lax.optimization_barrier((*dlow_other, far))
    got = swap(far, "shard", 1)
    *sends, dz1, last_far, last_near, sums_one = mix_back(
        ids, tok, vectors, front, mixed, part, part_other, dz2, dlow, dlow_other, n, heads
    )
    sums_two = sum(sums_two)
    grads = [sends[0]] + [swap(sends[d], "ctx", d) for d in range(1, n)]
    got, sends[0] = lax.optimization_barrier((got, sends[0]))
    mine, far = fold_core(near, got, 0)
    *grads, far = lax.optimization_barrier((*grads, far))
    got = swap(far, "shard", 2)
    outs = attend_back(ids, lengths, slopes, blocks, grads, att, den, n, heads, per)
    outs = [outs[0]] + [swap(outs[d], "ctx", d) for d in range(1, n)]
    rest_own, *rest_sends = fold_y(ids, mine, [got], n, 0)
    *outs, rest_own = lax.optimization_barrier((*outs, rest_own))
    small = jnp.concatenate(
        [sums_one[0:2], sums_two[0:2], sums_one[2:3], sums_two[2:3], jnp.zeros_like(sums_one[:2])]
    )
    dx, far, near = project_back(
        ids, tok, whole, small, (last_far, last_near), outs, n, seqs, heads
    )
    got = swap(far, "shard", 1)
    mine, *far = fold_core(near, got, EXTRA)
    got = [swap(half, "shard", 2) for half in far]
    dx_other = swap(dx, "tp", 1)
    rest_got = [swap(block, "ctx", d + 1) for d, block in enumerate(rest_sends)]
    rest_got[0], got[0] = lax.optimization_barrier((rest_got[0], got[0]))
    own, *sends = fold_y(ids, mine, got, n, EXTRA)
    got = [swap(block, "ctx", d + 1) for d, block in enumerate(sends)]
    rest = fold_z(rest_own, rest_got)
    last = fold_z(own, got)
    input_grad = dz1 + (dx.astype(f32) + dx_other.astype(f32))
    small = last[rows : rows + 8, : 2 * width]
    return (
        jnp.stack(output),
        input_grad.reshape(tokens.shape),
        last[:rows, : 3 * width].reshape(w_qkv.shape),
        small[6].reshape(2, width),
        last[:rows, 3 * width :].T,
        rest[:, : 2 * units].reshape(w_gu.shape),
        rest[:, 2 * units :].T,
        small[:6],
    )


def alibi_slopes(first_head, head_count):
    power = 2 ** (H.bit_length() - 1)
    heads_index = first_head + jnp.arange(head_count, dtype=jnp.int32)
    early = -8.0 * (heads_index + 1).astype(jnp.float32) / power
    later = -4.0 * (2 * (heads_index - power) + 1).astype(jnp.float32) / power
    return jnp.exp2(jnp.where(heads_index < power, early, later))


def layer_norm(values, gain, shift):
    centred = values - jnp.mean(values, axis=-1, keepdims=True)
    spread = jnp.mean(centred * centred, axis=-1, keepdims=True)
    return centred * lax.rsqrt(spread + epsilon) * gain + shift


def gated_unit(gate_input, upper):
    return jax.nn.gelu(gate_input, approximate=False) * upper


def score_block(query_heads, key_heads, query_place, key_place, slopes, lengths):
    scores = (
        jnp.einsum("sqhe,skhe->shqk", query_heads, key_heads, preferred_element_type=jnp.float32)
        * 0.125
    )
    distance = jnp.abs(query_place[:, None] - key_place[None, :]).astype(jnp.float32)
    scores = scores - slopes[None, :, None, None] * distance[None, None]
    usable = key_place[None, :] < lengths[:, None]
    return jnp.where(usable[:, None, None, :], jnp.exp(scores), 0.0)


def backward_scores(
    query_heads,
    numer_heads,
    correction,
    key_heads,
    value_heads,
    query_place,
    key_place,
    slopes,
    lengths,
):
    weights = score_block(query_heads, key_heads, query_place, key_place, slopes, lengths)
    value_dots = jnp.einsum(
        "sqhe,skhe->shqk", numer_heads, value_heads, preferred_element_type=jnp.float32
    )
    grad_scores = (weights * (value_dots - correction[..., None])).astype(jnp.bfloat16)
    return (weights.astype(jnp.bfloat16), grad_scores)


def split_blocks(shard_piece, slot_count, ctx_count):
    piece_rows = shard_piece.shape[1]
    block_rows = math.gcd(piece_rows, 128)
    block_count = piece_rows // block_rows
    shaped = shard_piece.reshape(
        (shard_piece.shape[0], block_count, block_rows) + shard_piece.shape[2:]
    )
    blocks = jnp.moveaxis(shaped, 1, 0)
    row_ids = jnp.arange(piece_rows, dtype=jnp.int32)
    places = (row_ids % slot_count * ctx_count + row_ids // slot_count).reshape(
        block_count, block_rows
    )
    offsets = block_rows * jnp.arange(block_count, dtype=jnp.int32)
    return (blocks, places, offsets)


def by_gather(tokens, lengths, w_qkv, b_qv, w_out, w_gu, w_down, vectors, cotangent):
    ctx_count = lax.axis_size("ctx")
    ctx_rank = lax.axis_index("ctx")
    seq_count, slot_count, model_width = tokens.shape
    local_width = b_qv.shape[1]
    head_count = local_width // HD
    slopes = alibi_slopes(lax.axis_index("tp") * head_count, head_count)
    slot_ids = jnp.arange(slot_count, dtype=jnp.int32)
    query_place = slot_ids * ctx_count + ctx_rank
    query_live = (query_place[None, :] < lengths[:, None]).astype(jnp.float32)
    live_rows = query_live[:, :, None]
    head_shape = (seq_count, slot_count, head_count, HD)
    whole_qkv, whole_out, whole_gu, whole_down = (
        lax.all_gather(w_qkv.astype(jnp.bfloat16), ("shard", "ctx"), axis=0, tiled=True),
        lax.all_gather(w_out.astype(jnp.bfloat16), ("shard", "ctx"), axis=1, tiled=True),
        lax.all_gather(w_gu.astype(jnp.bfloat16), ("shard", "ctx"), axis=0, tiled=True),
        lax.all_gather(w_down.astype(jnp.bfloat16), ("shard", "ctx"), axis=1, tiled=True),
    )
    inputs = tokens.astype(jnp.float32)
    projected = jnp.einsum("std,dcm->stcm", tokens, whole_qkv, preferred_element_type=jnp.float32)
    query_rows = (projected[:, :, 0] + b_qv[0]).astype(jnp.bfloat16)
    key_rows = projected[:, :, 1].astype(jnp.bfloat16)
    value_rows = (projected[:, :, 2] + b_qv[1]).astype(jnp.bfloat16)
    query_heads = query_rows.reshape(head_shape)
    pairs = jnp.stack([key_rows, value_rows], axis=2)
    start_numer = jnp.zeros((seq_count, head_count, slot_count, HD), jnp.float32)
    start_denom = jnp.zeros((seq_count, head_count, slot_count), jnp.float32)
    blocks, places, offsets = split_blocks(
        lax.all_gather(pairs, "ctx", axis=1, tiled=True), slot_count, ctx_count
    )

    def forward_advance(inner_state, block_item):
        key_block, key_place, row_offset = block_item
        numerator, denominator = inner_state
        key_heads = key_block[:, :, 0].reshape(seq_count, -1, head_count, HD)
        value_heads = key_block[:, :, 1].reshape(seq_count, -1, head_count, HD)
        weights = score_block(query_heads, key_heads, query_place, key_place, slopes, lengths)
        numerator = numerator + jnp.einsum(
            "shqk,skhe->shqe",
            weights.astype(jnp.bfloat16),
            value_heads,
            preferred_element_type=jnp.float32,
        )
        return ((numerator, denominator + jnp.sum(weights, axis=-1)), None)

    result_state, unused = lax.scan(
        forward_advance, (start_numer, start_denom), (blocks, places, offsets)
    )
    numerator, denominator = result_state
    denominator = denominator + (1.0 - query_live)[:, None, :]
    attention_q = jnp.transpose(numerator / denominator[..., None], (0, 2, 1, 3))
    denom_q = jnp.transpose(denominator, (0, 2, 1))
    mixed = attention_q.reshape(seq_count, slot_count, local_width).astype(jnp.bfloat16)
    attn_part = jnp.einsum("stm,mn->stn", mixed, whole_out, preferred_element_type=jnp.float32)
    attn_branch = lax.psum(attn_part, "tp") + vectors[4]
    hidden, first_pull = jax.vjp(layer_norm, inputs + attn_branch, vectors[0], vectors[1])
    hidden_low = hidden.astype(jnp.bfloat16)
    gated = jnp.einsum("std,dcf->stcf", hidden_low, whole_gu, preferred_element_type=jnp.float32)
    activated, unit_pull = jax.vjp(gated_unit, gated[:, :, 0], gated[:, :, 1])
    act_low = activated.astype(jnp.bfloat16)
    ffn_part = jnp.einsum("stf,fn->stn", act_low, whole_down, preferred_element_type=jnp.float32)
    ffn_branch = lax.psum(ffn_part, "tp") + vectors[5]
    normed, second_pull = jax.vjp(layer_norm, hidden + ffn_branch, vectors[2], vectors[3])
    output = (normed * live_rows).astype(jnp.bfloat16)
    upstream = cotangent.astype(jnp.float32) * live_rows
    grad_second, grad_gain_two, grad_shift_two = second_pull(upstream)
    grad_ffn = grad_second.astype(jnp.bfloat16)
    grad_down = jnp.einsum("stf,stn->fn", act_low, grad_ffn, preferred_element_type=jnp.float32)
    grad_ffn_bias = jnp.sum(grad_ffn.astype(jnp.float32), axis=(0, 1))
    grad_act = jnp.einsum("stn,fn->stf", grad_ffn, whole_down, preferred_element_type=jnp.float32)
    grad_gate, grad_upper = unit_pull(grad_act)
    grad_gated = jnp.stack([grad_gate, grad_upper], axis=2).astype(jnp.bfloat16)
    grad_gu = jnp.einsum(
        "std,stcf->dcf", hidden_low, grad_gated, preferred_element_type=jnp.float32
    )
    hidden_part = jnp.einsum(
        "stcf,dcf->std", grad_gated, whole_gu, preferred_element_type=jnp.float32
    )
    grad_hidden = grad_second + lax.psum(hidden_part, "tp")
    grad_first, grad_gain_one, grad_shift_one = first_pull(grad_hidden)
    grad_attn = grad_first.astype(jnp.bfloat16)
    grad_out = jnp.einsum("stm,stn->mn", mixed, grad_attn, preferred_element_type=jnp.float32)
    grad_out_bias = jnp.sum(grad_attn.astype(jnp.float32), axis=(0, 1))
    grad_mixed = jnp.einsum(
        "stn,mn->stm", grad_attn, whole_out, preferred_element_type=jnp.float32
    ).astype(jnp.bfloat16)
    grad_mixed_heads = grad_mixed.reshape(head_shape).astype(jnp.float32)
    correction = jnp.transpose(
        jnp.sum(grad_mixed_heads * attention_q, axis=-1) / denom_q, (0, 2, 1)
    )
    numer_heads = (grad_mixed_heads / denom_q[..., None]).astype(jnp.bfloat16)
    start_query = jnp.zeros(head_shape, jnp.float32)
    start_state = (
        start_query,
        jnp.zeros((seq_count, slot_count * ctx_count, 2, local_width), jnp.float32),
    )
    blocks, places, offsets = split_blocks(
        lax.all_gather(pairs, "ctx", axis=1, tiled=True), slot_count, ctx_count
    )

    def backward_advance(current_state, block_item):
        key_block, key_place, row_offset = block_item
        key_heads = key_block[:, :, 0].reshape(seq_count, -1, head_count, HD)
        value_heads = key_block[:, :, 1].reshape(seq_count, -1, head_count, HD)
        weights_low, grad_scores = backward_scores(
            query_heads,
            numer_heads,
            correction,
            key_heads,
            value_heads,
            query_place,
            key_place,
            slopes,
            lengths,
        )
        grad_query = current_state[0] + jnp.einsum(
            "shqk,skhe->sqhe", grad_scores, key_heads, preferred_element_type=jnp.float32
        )
        grad_key = (
            jnp.einsum(
                "shqk,sqhe->skhe", grad_scores, query_heads, preferred_element_type=jnp.float32
            )
            * 0.125
        )
        grad_value = jnp.einsum(
            "shqk,sqhe->skhe", weights_low, numer_heads, preferred_element_type=jnp.float32
        )
        stacked = jnp.stack(
            [
                grad_key.reshape(seq_count, -1, local_width),
                grad_value.reshape(seq_count, -1, local_width),
            ],
            axis=2,
        )
        buffer = lax.dynamic_update_slice_in_dim(current_state[1], stacked, row_offset, axis=1)
        return ((grad_query, buffer), None)

    result_state, unused = lax.scan(backward_advance, start_state, (blocks, places, offsets))
    grad_pairs = lax.psum_scatter(
        result_state[1].astype(jnp.bfloat16), "ctx", scatter_dimension=1, tiled=True
    )
    grad_query_low = (
        (result_state[0] * 0.125).astype(jnp.bfloat16).reshape(seq_count, slot_count, local_width)
    )
    grad_proj = jnp.concatenate([grad_query_low[:, :, None], grad_pairs], axis=2)
    grad_qkv = jnp.einsum("std,stcm->dcm", tokens, grad_proj, preferred_element_type=jnp.float32)
    bias_terms = jnp.stack(
        [
            jnp.sum(grad_query_low.astype(jnp.float32), axis=(0, 1)),
            jnp.sum(grad_pairs[:, :, 1].astype(jnp.float32), axis=(0, 1)),
        ]
    )
    input_part = jnp.einsum(
        "stcm,dcm->std", grad_proj, whole_qkv, preferred_element_type=jnp.float32
    )
    input_grad = grad_first + lax.psum(input_part.astype(jnp.bfloat16), "tp").astype(jnp.float32)
    grad_weights = (
        lax.psum_scatter(grad_qkv, ("shard", "ctx"), scatter_dimension=0, tiled=True),
        lax.psum_scatter(grad_out, ("shard", "ctx"), scatter_dimension=1, tiled=True),
        lax.psum_scatter(grad_gu, ("shard", "ctx"), scatter_dimension=0, tiled=True),
        lax.psum_scatter(grad_down, ("shard", "ctx"), scatter_dimension=1, tiled=True),
    )
    vector_terms = jnp.stack(
        [grad_gain_one, grad_shift_one, grad_gain_two, grad_shift_two, grad_out_bias, grad_ffn_bias]
    )
    grad_bqv, grad_vectors = lax.psum((bias_terms, vector_terms), ("shard", "ctx"))
    return (
        output,
        input_grad,
        grad_weights[0],
        grad_bqv,
        grad_weights[1],
        grad_weights[2],
        grad_weights[3],
        grad_vectors,
    )


def solution(mesh):
    placed = (
        P("shard", "ctx", None),
        P("shard"),
        P(("shard", "ctx"), None, "tp"),
        P(None, "tp"),
        P("tp", ("shard", "ctx")),
        P(("shard", "ctx"), None, "tp"),
        P("tp", ("shard", "ctx")),
        P(),
        P("shard", "ctx", None),
    )
    return jax.shard_map(
        on_device,
        mesh=mesh,
        in_specs=placed,
        out_specs=(
            P("shard", "ctx", None),
            P("shard", "ctx", None),
            P(("shard", "ctx"), None, "tp"),
            P(None, "tp"),
            P("tp", ("shard", "ctx")),
            P(("shard", "ctx"), None, "tp"),
            P("tp", ("shard", "ctx")),
            P(),
        ),
        check_vma=False,
    )
```

```python
import functools
import math

import jax
import jax.numpy as jnp
import numpy as np
from jax import lax
from jax.experimental import pallas as pl
from jax.experimental.pallas import tpu as pltpu
from jax.sharding import PartitionSpec as P

H = 12
HD = 64
LOG2E = math.log2(math.e)
FAR = 1e30
TILE = 64
BLOCK = 512
WIDTH = 384
EXTRA = 16

epsilon = 1e-12
f32 = jnp.float32
bf16 = jnp.bfloat16
VMEM = pl.BlockSpec(memory_space=pltpu.VMEM)
SMEM = pl.BlockSpec(memory_space=pltpu.SMEM)


def slope_table():
    power = 2 ** (H.bit_length() - 1)
    heads = np.arange(H)
    early = -8.0 * (heads + 1) / power
    later = -4.0 * (2 * (heads - power) + 1) / power
    return np.exp2(np.where(heads < power, early, later)).astype(np.float32)


def dot_nn(a, b):
    return jnp.dot(a, b, preferred_element_type=f32)


def dot_nt(a, b):
    return lax.dot_general(a, b, (((1,), (1,)), ((), ())), preferred_element_type=f32)


def params(*semantics):
    return pltpu.CompilerParams(
        dimension_semantics=semantics or None, vmem_limit_bytes=20 * 1024 * 1024
    )


def cost(flops, nbytes, exps=0):
    return pl.CostEstimate(flops=int(flops), bytes_accessed=int(nbytes), transcendentals=int(exps))


def shape(dims, dtype):
    return jax.ShapeDtypeStruct(dims, dtype)


def xor_pairs(axis, distance):
    return [(i, i ^ distance) for i in range(lax.axis_size(axis))]


def swap(value, axis, distance):
    return lax.ppermute(value, axis, xor_pairs(axis, distance))


def after(values, *done):
    return lax.optimization_barrier((*values, *done))[: len(values)]


def live_mask(length, rank, n_ctx, slots):
    slot = lax.broadcasted_iota(jnp.int32, (slots, 1), 0)
    return jnp.where(slot * n_ctx + rank < length, 1.0, 0.0).astype(f32)


def normalise(z):
    centred = z - jnp.mean(z, axis=-1, keepdims=True)
    spread = jnp.mean(centred * centred, axis=-1, keepdims=True)
    scale = lax.rsqrt(spread + epsilon)
    return centred * scale, scale


def normalise_back(grad_hat, hat, scale):
    inner = jnp.mean(grad_hat * hat, axis=-1, keepdims=True)
    return scale * (grad_hat - jnp.mean(grad_hat, axis=-1, keepdims=True) - hat * inner)


def assemble_kernel(n, ids, *refs):
    pieces, whole = refs[:4], refs[4]
    y, c, z = ids[0], ids[1], ids[2]
    rows = pieces[0].shape[0] // n
    for k in range(4):
        for kz in range(n):
            index = ((y ^ (k // 2)) * 2 + (c ^ (k % 2))) * n + (z ^ kz)
            place = pl.ds(pl.multiple_of(index * rows, rows), rows)
            whole[place, :] = pieces[k][kz * rows : (kz + 1) * rows, :]


def assemble(ids, pieces, n):
    rows, wide = pieces[0].shape
    column = lambda size: pl.BlockSpec((size, wide // 3), lambda j: (0, j))
    return pl.pallas_call(
        functools.partial(assemble_kernel, n),
        grid=(3,),
        out_shape=shape((4 * rows, wide), bf16),
        in_specs=[SMEM] + [column(rows)] * 4,
        out_specs=column(4 * rows),
        compiler_params=params("arbitrary"),
        cost_estimate=cost(0, 16 * rows * wide),
        name="assemble",
    )(ids, *pieces)


def project_kernel(n, seqs, heads, ids, tok, bias, *refs):
    pieces = refs[: 4 * n]
    sends = refs[4 * n : 5 * n]
    whole = refs[5 * n]
    stage = refs[5 * n + 1]
    y, c, z = ids[0], ids[1], ids[2]
    rows = pieces[0].shape[0]
    for k in range(4 * n):
        ky, kc, kz = k // (2 * n), k // n % 2, k % n
        index = ((y ^ ky) * 2 + (c ^ kc)) * n + (z ^ kz)
        whole[pl.ds(pl.multiple_of(index * rows, rows), rows), :] = pieces[k][...]
    slots = sends[0].shape[1]
    width = heads * HD
    per = seqs * heads // n
    for s in range(seqs):
        acc = dot_nn(tok[s * slots : (s + 1) * slots, :], whole[...]) + bias[...]
        turned = acc.astype(bf16).T
        for h in range(heads):
            i = s * heads + h
            at = ((i % n) * per + i // n) * 3
            for part in range(3):
                first = part * width + h * HD
                stage[(at + part) * HD : (at + part + 1) * HD, :] = turned[first : first + HD, :]
    size = per * 3 * HD
    for d in range(n):
        sends[d][...] = stage[pl.ds(pl.multiple_of((z ^ d) * size, size), size), :]


def project(ids, tok, bias, pieces, n, seqs, heads):
    slots = tok.shape[0] // seqs
    size = seqs * heads // n * 3 * HD
    model, wide = tok.shape[1], bias.shape[1]
    return pl.pallas_call(
        functools.partial(project_kernel, n, seqs, heads),
        out_shape=[shape((size, slots), bf16)] * n + [shape((model, wide), bf16)],
        in_specs=[SMEM] + [VMEM] * (2 + len(pieces)),
        out_specs=[VMEM] * (n + 1),
        scratch_shapes=[pltpu.VMEM((size * n, slots), bf16)],
        compiler_params=params(),
        cost_estimate=cost(2 * tok.shape[0] * model * wide, 6e6),
        name="project",
    )(ids, tok, bias, *pieces)


def pair_scalars(n, heads, ids, lens, slopes):
    j = pl.program_id(0)
    z, t = ids[2], ids[3]
    i = z + n * j
    s = i // heads
    h = i - s * heads
    return z, lens[s], slopes[t * heads + h] * LOG2E


def query_place(n, slots, z, d):
    lane = lax.broadcasted_iota(jnp.int32, (1, slots), 1)
    return lane * n + (z ^ d)


def key_place(n, z, tile, length, slope):
    row = lax.broadcasted_iota(jnp.int32, (TILE, 1), 0)
    places = []
    for d in range(n):
        place = (tile * TILE + row) * n + (z ^ d)
        places.append(jnp.where(place < length, place.astype(f32) * slope, FAR))
    return jnp.concatenate(places, axis=0)


def gather_rows(ref, tile, n):
    rows = pl.ds(pl.multiple_of(tile * TILE, TILE), TILE)
    return jnp.concatenate([ref[d, rows, :] for d in range(n)], axis=0)


def attend_kernel(n, heads, ids, lens, slopes, *refs):
    inputs = refs[:n]
    outs = refs[n : 2 * n]
    att_ref, den_ref = refs[2 * n], refs[2 * n + 1]
    k_s, v_s, acc, den = refs[2 * n + 2 :]
    slots = inputs[0].shape[1]
    z, length, slope = pair_scalars(n, heads, ids, lens, slopes)
    for d in range(n):
        k_s[d] = inputs[d][HD : 2 * HD, :].T
        v_s[d] = inputs[d][2 * HD : 3 * HD, :].T
    acc[...] = jnp.zeros_like(acc)
    den[...] = jnp.zeros_like(den)

    def tile_step(tile, unused):
        keys = gather_rows(k_s, tile, n)
        values = gather_rows(v_s, tile, n).T
        places = key_place(n, z, tile, length, slope)
        for d in range(n):
            cols = slice(d * slots, (d + 1) * slots)
            there = query_place(n, slots, z, d).astype(f32) * slope
            scores = dot_nn(keys, inputs[d][0:HD, :]) * (0.125 * LOG2E)
            e = jnp.exp2(scores - jnp.abs(there - places))
            den[:, cols] += jnp.sum(e, axis=0, keepdims=True)
            acc[:, cols] += dot_nn(values, e.astype(bf16))
        return unused

    step = TILE * n
    lax.fori_loop(0, (length + step - 1) // step, tile_step, 0)
    for d in range(n):
        cols = slice(d * slots, (d + 1) * slots)
        padded = jnp.where(query_place(n, slots, z, d) < length, 0.0, 1.0)
        total = den[:, cols] + padded
        att = acc[:, cols] / total
        att_ref[:, cols] = att
        den_ref[0, :, cols] = total
        outs[d][...] = att.astype(bf16)


def attend(ids, lens, slopes, blocks, n, heads, per):
    slots = blocks[0].shape[1]
    every = n * slots
    return pl.pallas_call(
        functools.partial(attend_kernel, n, heads),
        grid=(per,),
        out_shape=[shape((per * HD, slots), bf16)] * n
        + [shape((per * HD, every), f32), shape((per, 1, every), f32)],
        in_specs=[SMEM] * 3 + [pl.BlockSpec((3 * HD, slots), lambda j: (j, 0))] * n,
        out_specs=[pl.BlockSpec((HD, slots), lambda j: (j, 0))] * n
        + [
            pl.BlockSpec((HD, every), lambda j: (j, 0)),
            pl.BlockSpec((1, 1, every), lambda j: (j, 0, 0)),
        ],
        scratch_shapes=[
            pltpu.VMEM((n, slots, HD), bf16),
            pltpu.VMEM((n, slots, HD), bf16),
            pltpu.VMEM((HD, every), f32),
            pltpu.VMEM((1, every), f32),
        ],
        compiler_params=params("arbitrary"),
        cost_estimate=cost(per * every * every * HD * 8, 3e6, per * every * every),
        name="attend",
    )(ids, lens, slopes, *blocks)


def attend_back_kernel(n, heads, ids, lens, slopes, *refs):
    inputs = refs[:n]
    grads = refs[n : 2 * n]
    att_ref, den_ref = refs[2 * n], refs[2 * n + 1]
    outs = refs[2 * n + 2 : 3 * n + 2]
    k_s, v_s, q_s, g_s, dn, cor, dq, dk, dv = refs[3 * n + 2 :]
    slots = inputs[0].shape[1]
    z, length, slope = pair_scalars(n, heads, ids, lens, slopes)
    for d in range(n):
        cols = slice(d * slots, (d + 1) * slots)
        k_s[d] = inputs[d][HD : 2 * HD, :].T
        v_s[d] = inputs[d][2 * HD : 3 * HD, :].T
        q_s[d] = inputs[d][0:HD, :].T
        inverse = 1.0 / den_ref[0, :, cols]
        mixed = grads[d][...].astype(f32)
        numer = (mixed * inverse).astype(bf16)
        dn[:, cols] = numer
        g_s[d] = numer.T
        cor[:, cols] = jnp.sum(mixed * att_ref[:, cols], axis=0, keepdims=True) * inverse
    dq[...] = jnp.zeros_like(dq)
    dk[...] = jnp.zeros_like(dk)
    dv[...] = jnp.zeros_like(dv)

    def tile_step(tile, unused):
        keys = gather_rows(k_s, tile, n)
        values = gather_rows(v_s, tile, n)
        keys_t = keys.T
        places = key_place(n, z, tile, length, slope)
        grad_k = jnp.zeros((n * TILE, HD), f32)
        grad_v = jnp.zeros((n * TILE, HD), f32)
        for d in range(n):
            cols = slice(d * slots, (d + 1) * slots)
            there = query_place(n, slots, z, d).astype(f32) * slope
            scores = dot_nn(keys, inputs[d][0:HD, :]) * (0.125 * LOG2E)
            e = jnp.exp2(scores - jnp.abs(there - places))
            inner = dot_nn(values, dn[:, cols])
            ds = (e * (inner - cor[:, cols])).astype(bf16)
            dq[:, cols] += dot_nn(keys_t, ds)
            grad_k += dot_nn(ds, q_s[d])
            grad_v += dot_nn(e.astype(bf16), g_s[d])
        rows = pl.ds(pl.multiple_of(tile * TILE, TILE), TILE)
        for d in range(n):
            dk[d, rows, :] = grad_k[d * TILE : (d + 1) * TILE, :]
            dv[d, rows, :] = grad_v[d * TILE : (d + 1) * TILE, :]
        return unused

    step = TILE * n
    lax.fori_loop(0, (length + step - 1) // step, tile_step, 0)
    for d in range(n):
        cols = slice(d * slots, (d + 1) * slots)
        outs[d][0:HD, :] = (dq[:, cols] * 0.125).astype(bf16)
        outs[d][HD : 2 * HD, :] = (dk[d] * 0.125).astype(bf16).T
        outs[d][2 * HD : 3 * HD, :] = dv[d].astype(bf16).T


def attend_back(ids, lens, slopes, blocks, grads, att, den, n, heads, per):
    slots = blocks[0].shape[1]
    every = n * slots
    rows = [pltpu.VMEM((n, slots, HD), bf16)] * 4
    return pl.pallas_call(
        functools.partial(attend_back_kernel, n, heads),
        grid=(per,),
        out_shape=[shape((per * 3 * HD, slots), bf16)] * n,
        in_specs=[SMEM] * 3
        + [pl.BlockSpec((3 * HD, slots), lambda j: (j, 0))] * n
        + [pl.BlockSpec((HD, slots), lambda j: (j, 0))] * n
        + [
            pl.BlockSpec((HD, every), lambda j: (j, 0)),
            pl.BlockSpec((1, 1, every), lambda j: (j, 0, 0)),
        ],
        out_specs=[pl.BlockSpec((3 * HD, slots), lambda j: (j, 0))] * n,
        scratch_shapes=rows
        + [
            pltpu.VMEM((HD, every), bf16),
            pltpu.VMEM((1, every), f32),
            pltpu.VMEM((HD, every), f32),
            pltpu.VMEM((n, slots, HD), f32),
            pltpu.VMEM((n, slots, HD), f32),
        ],
        compiler_params=params("arbitrary"),
        cost_estimate=cost(per * every * every * HD * 20, 5e6, per * every * every),
        name="attend_back",
    )(ids, lens, slopes, *blocks, *grads, att, den)


def mix_kernel(n, seqs, heads, ids, wo, *refs):
    inputs = refs[:n]
    parts = refs[n : n + seqs]
    mixed, stage = refs[n + seqs :]
    z = ids[2]
    slots = inputs[0].shape[1]
    per = seqs * heads // n
    size = per * HD
    for d in range(n):
        stage[pl.ds(pl.multiple_of((z ^ d) * size, size), size), :] = inputs[d][...]
    for s in range(seqs):
        columns = []
        for h in range(heads):
            i = s * heads + h
            at = (i % n) * per + i // n
            columns.append(stage[at * HD : (at + 1) * HD, :])
        rows = slice(s * slots, (s + 1) * slots)
        ours = jnp.concatenate(columns, axis=0).T
        mixed[rows, :] = ours
        parts[s][...] = dot_nt(ours, wo[...]).astype(bf16)


def mix(ids, packed, blocks, n, seqs, heads):
    slots = blocks[0].shape[1]
    model = packed.shape[0]
    width = heads * HD
    tokens = seqs * slots
    return pl.pallas_call(
        functools.partial(mix_kernel, n, seqs, heads),
        grid=(1,),
        out_shape=[shape((slots, model), bf16)] * seqs + [shape((tokens, width), bf16)],
        in_specs=[SMEM, pl.BlockSpec((model, width), lambda i: (0, packed.shape[1] // width - 1))]
        + [VMEM] * n,
        out_specs=[VMEM] * (seqs + 1),
        scratch_shapes=[pltpu.VMEM((seqs * heads * HD, slots), bf16)],
        compiler_params=params("arbitrary"),
        cost_estimate=cost(2 * tokens * model * width, 3e6),
        name="mix",
    )(ids, packed, *blocks)


def unit_kernel(tok, own, other, vec, wg, wu, wd, hidden, low, act, gel, slope, part, acc):
    j = pl.program_id(0)

    @pl.when(j == 0)
    def _():
        branch = own[...].astype(f32) + other[...].astype(f32) + vec[4:5, :]
        hat, _ = normalise(tok[...].astype(f32) + branch)
        h = hat * vec[0:1, :] + vec[1:2, :]
        hidden[...] = h
        low[...] = h.astype(bf16)
        acc[...] = jnp.zeros_like(acc)

    gate = dot_nn(low[...], wg[...])
    upper = dot_nn(low[...], wu[...])
    phi = 0.5 * (1.0 + lax.erf(gate * math.sqrt(0.5)))
    density = jnp.exp(gate * gate * -0.5) * (1.0 / math.sqrt(2.0 * math.pi))
    unit = gate * phi
    acted = (unit * upper).astype(bf16)
    act[...] = acted
    gel[...] = unit.astype(bf16)
    slope[...] = (upper * (phi + gate * density)).astype(bf16)
    acc[...] += dot_nt(acted, wd[...])

    @pl.when(j == pl.num_programs(0) - 1)
    def _():
        part[...] = acc[...].astype(bf16)


def unit(s, tok, own, other, vec, front, back):
    tokens, model = own.shape
    hidden_units = back.shape[1]
    steps = hidden_units // BLOCK
    fixed = lambda j: (0, 0)
    whole = pl.BlockSpec((tokens, model), fixed)
    weight = lambda start: pl.BlockSpec((model, BLOCK), lambda j: (0, start + j))
    inner = pl.BlockSpec((tokens, BLOCK), lambda j: (0, j))
    return pl.pallas_call(
        unit_kernel,
        grid=(steps,),
        out_shape=[shape((tokens, model), f32), shape((tokens, model), bf16)]
        + [shape((tokens, hidden_units), bf16)] * 3
        + [shape((tokens, model), bf16)],
        in_specs=[
            pl.BlockSpec((tokens, model), lambda j: (s, 0)),
            whole,
            whole,
            pl.BlockSpec(vec.shape, fixed),
            weight(0),
            weight(steps),
            weight(0),
        ],
        out_specs=[whole, whole, inner, inner, inner, whole],
        scratch_shapes=[pltpu.VMEM((tokens, model), f32)],
        compiler_params=params("arbitrary"),
        cost_estimate=cost(6 * tokens * model * hidden_units, 13e6, 2 * tokens * hidden_units),
        name="unit",
    )(tok, own, other, vec, front, front, back)


def unit_back_kernel(
    n, s, ids, lens, hidden, own, other, cot, vec, wg, wu, wd, gel, slope,
    output, dz2, dffn, dgate, dup, part, sums, acc,
):
    j = pl.program_id(0)

    @pl.when(j == 0)
    def _():
        live = live_mask(lens[s], ids[2], n, hidden.shape[0])
        branch = own[...].astype(f32) + other[...].astype(f32) + vec[5:6, :]
        hat, scale = normalise(hidden[...] + branch)
        output[...] = (live * (hat * vec[2:3, :] + vec[3:4, :])).astype(bf16)
        gy = cot[...].astype(f32) * live
        grad = normalise_back(gy * vec[2:3, :], hat, scale)
        dz2[...] = grad
        low = grad.astype(bf16)
        dffn[...] = low
        sums[0:1, :] = jnp.sum(gy * hat, axis=0, keepdims=True)
        sums[1:2, :] = jnp.sum(gy, axis=0, keepdims=True)
        sums[2:3, :] = jnp.sum(low.astype(f32), axis=0, keepdims=True)
        sums[3:8, :] = jnp.zeros_like(sums[3:8, :])
        acc[...] = jnp.zeros_like(acc)

    dact = dot_nn(dffn[...], wd[...])
    upper = (dact * gel[...].astype(f32)).astype(bf16)
    gate = (dact * slope[...].astype(f32)).astype(bf16)
    dgate[...] = gate
    dup[...] = upper
    acc[...] += dot_nt(gate, wg[...]) + dot_nt(upper, wu[...])

    @pl.when(j == pl.num_programs(0) - 1)
    def _():
        part[...] = acc[...].astype(bf16)


def unit_back(s, ids, lens, hidden, own, other, cot, vec, front, back, gel, slope, n):
    tokens, model = hidden.shape
    hidden_units = gel.shape[1]
    steps = hidden_units // BLOCK
    fixed = lambda j: (0, 0)
    whole = pl.BlockSpec((tokens, model), fixed)
    weight = lambda start: pl.BlockSpec((model, BLOCK), lambda j: (0, start + j))
    inner = pl.BlockSpec((tokens, BLOCK), lambda j: (0, j))
    return pl.pallas_call(
        functools.partial(unit_back_kernel, n, s),
        grid=(steps,),
        out_shape=[
            shape((tokens, model), bf16),
            shape((tokens, model), f32),
            shape((tokens, model), bf16),
            shape((tokens, hidden_units), bf16),
            shape((tokens, hidden_units), bf16),
            shape((tokens, model), bf16),
            shape((8, model), f32),
        ],
        in_specs=[SMEM, SMEM, whole, whole, whole]
        + [pl.BlockSpec((tokens, model), lambda j: (s, 0)), pl.BlockSpec(vec.shape, fixed)]
        + [weight(0), weight(steps), weight(0), inner, inner],
        out_specs=[whole, whole, whole, inner, inner, whole, pl.BlockSpec((8, model), fixed)],
        scratch_shapes=[pltpu.VMEM((tokens, model), f32)],
        compiler_params=params("arbitrary"),
        cost_estimate=cost(6 * tokens * model * hidden_units, 14e6),
        name="unit_back",
    )(ids, lens, hidden, own, other, cot, vec, front, front, back, gel, slope)


def row_starts(ids, quarter):
    y, c = ids[0], ids[1]
    keep = [(y * 2 + c) * quarter, ((1 - y) * 2 + c) * quarter]
    send = [(y * 2 + 1 - c) * quarter, ((1 - y) * 2 + 1 - c) * quarter]
    return send, keep


def arrange(ids, turned, left):
    quarter = turned.shape[0] // 4
    send, keep = row_starts(ids, quarter)
    for k, start in enumerate(send + keep):
        rows = pl.ds(pl.multiple_of(start, quarter), quarter)
        left[k * quarter : (k + 1) * quarter, :] = turned[rows, :]


def write_rows(left, right, send, keep):
    grad = dot_nn(left[...], right).astype(bf16)
    half = grad.shape[0] // 2
    send[0:half, :] = grad[:half]
    keep[0:half, :] = grad[half:]


def weight_kernel(steps, seqs, ids, *refs):
    low, dffn, dgate, dup, act = (refs[i * seqs : (i + 1) * seqs] for i in range(5))
    send, keep, left, turned = refs[5 * seqs :]
    j = pl.program_id(0)
    joined = lambda group: jnp.concatenate([ref[...] for ref in group], axis=0)

    @pl.when(j == 0)
    def _():
        for k, group in enumerate((low, dffn)):
            turned[...] = joined(group).T
            arrange(ids, turned, left.at[k])

    @pl.when(j < steps)
    def _():
        write_rows(left.at[0], joined(dgate), send, keep)

    @pl.when((j >= steps) & (j < 2 * steps))
    def _():
        write_rows(left.at[0], joined(dup), send, keep)

    @pl.when(j >= 2 * steps)
    def _():
        write_rows(left.at[1], joined(act), send, keep)


def weight_grads(ids, low, dffn, dgate, dup, act):
    seqs = len(low)
    tokens, model = low[0].shape
    hidden_units = act[0].shape[1]
    steps = hidden_units // BLOCK
    whole = pl.BlockSpec((tokens, model), lambda j: (0, 0))
    column = lambda start: pl.BlockSpec(
        (tokens, BLOCK), lambda j: (0, jnp.clip(j - start, 0, steps - 1))
    )
    out = pl.BlockSpec((model // 2, BLOCK), lambda j: (0, j))
    return pl.pallas_call(
        functools.partial(weight_kernel, steps, seqs),
        grid=(3 * steps,),
        out_shape=[shape((model // 2, 3 * hidden_units), bf16)] * 2,
        in_specs=[SMEM]
        + [whole] * (2 * seqs)
        + [column(0)] * seqs
        + [column(steps)] * seqs
        + [column(2 * steps)] * seqs,
        out_specs=[out, out],
        scratch_shapes=[
            pltpu.VMEM((2, model, tokens * seqs), bf16),
            pltpu.VMEM((model, tokens * seqs), bf16),
        ],
        compiler_params=params("arbitrary"),
        cost_estimate=cost(6 * tokens * seqs * model * hidden_units, 14e6),
        name="weight_grads",
    )(ids, *low, *dffn, *dgate, *dup, *act)


def mix_back_kernel(n, seqs, heads, ids, tok, vec, wo, mixed, *refs):
    own, other, dz2, hown, hother = (refs[i * seqs : (i + 1) * seqs] for i in range(5))
    refs = refs[5 * seqs :]
    sends = refs[:n]
    dz1, send, keep, sums = refs[n : n + 4]
    stage, left, turned_low = refs[n + 4 :]
    z = ids[2]
    slots = sends[0].shape[1]
    per = seqs * heads // n
    sums[...] = jnp.zeros_like(sums)
    for s in range(seqs):
        rows = slice(s * slots, (s + 1) * slots)
        branch = own[s][...].astype(f32) + other[s][...].astype(f32) + vec[4:5, :]
        hat, scale = normalise(tok[rows, :].astype(f32) + branch)
        gh = dz2[s][...] + (hown[s][...].astype(f32) + hother[s][...].astype(f32))
        grad = normalise_back(gh * vec[0:1, :], hat, scale)
        dz1[rows, :] = grad
        low = grad.astype(bf16)
        sums[0:1, :] += jnp.sum(gh * hat, axis=0, keepdims=True)
        sums[1:2, :] += jnp.sum(gh, axis=0, keepdims=True)
        sums[2:3, :] += jnp.sum(low.astype(f32), axis=0, keepdims=True)
        turned_low[:, rows] = low.T
        turned = dot_nn(low, wo[...]).astype(bf16).T
        for h in range(heads):
            i = s * heads + h
            at = (i % n) * per + i // n
            stage[at * HD : (at + 1) * HD, :] = turned[h * HD : (h + 1) * HD, :]
    size = per * HD
    for d in range(n):
        sends[d][...] = stage[pl.ds(pl.multiple_of((z ^ d) * size, size), size), :]
    arrange(ids, turned_low, left)
    write_rows(left, mixed[...], send, keep)
    for ref in (send, keep):
        ref[ref.shape[0] - EXTRA :, :] = jnp.zeros((EXTRA, ref.shape[1]), bf16)


def mix_back(ids, tok, vec, front, mixed, own, other, dz2, hown, hother, n, heads):
    seqs = len(own)
    tokens, model = tok.shape
    slots = tokens // seqs
    width = heads * HD
    size = seqs * heads // n * HD
    rows = model // 2 + EXTRA
    return pl.pallas_call(
        functools.partial(mix_back_kernel, n, seqs, heads),
        grid=(1,),
        out_shape=[shape((size, slots), bf16)] * n
        + [shape((tokens, model), f32)]
        + [shape((rows, width), bf16)] * 2
        + [shape((8, model), f32)],
        in_specs=[SMEM, VMEM, VMEM]
        + [pl.BlockSpec((model, width), lambda i: (0, front.shape[1] // width - 1)), VMEM]
        + [VMEM] * (5 * seqs),
        out_specs=[VMEM] * (n + 4),
        scratch_shapes=[
            pltpu.VMEM((size * n, slots), bf16),
            pltpu.VMEM((model, tokens), bf16),
            pltpu.VMEM((model, tokens), bf16),
        ],
        compiler_params=params("arbitrary"),
        cost_estimate=cost(4 * tokens * model * width, 10e6),
        name="mix_back",
    )(ids, tok, vec, front, mixed, *own, *other, *dz2, *hown, *hother)


def project_back_kernel(n, seqs, heads, ids, tok, whole, small, far, near, *refs):
    inputs = refs[:n]
    part, send, keep = refs[n : n + 3]
    stage, right, left, turned = refs[n + 3 :]
    z = ids[2]
    slots = inputs[0].shape[1]
    per = seqs * heads // n
    width = heads * HD
    size = per * 3 * HD
    for d in range(n):
        stage[pl.ds(pl.multiple_of((z ^ d) * size, size), size), :] = inputs[d][...]
    for s in range(seqs):
        for c in range(3):
            columns = []
            for h in range(heads):
                i = s * heads + h
                at = ((i % n) * per + i // n) * 3 + c
                columns.append(stage[at * HD : (at + 1) * HD, :])
            ours = jnp.concatenate(columns, axis=0).T
            right[s * slots : (s + 1) * slots, c * width : (c + 1) * width] = ours
    part[...] = dot_nt(right[...], whole[...]).astype(bf16)
    turned[...] = tok[...].T
    arrange(ids, turned, left)
    for c in range(3):
        cols = slice(c * width, (c + 1) * width)
        write_rows(left, right[:, cols], send.at[:, cols], keep.at[:, cols])
    ones = jnp.ones((8, right.shape[0]), bf16)
    sums = dot_nn(ones, right[...])
    line = jnp.concatenate([sums[:, :width], sums[:, 2 * width :]], axis=1)
    row = lax.broadcasted_iota(jnp.int32, (8, 1), 0)
    rows = jnp.where(row == 6, line, small[...])
    rows = jnp.concatenate([rows, jnp.zeros_like(rows)], axis=0).astype(bf16)
    for ref, before in ((send, far), (keep, near)):
        ref[ref.shape[0] - EXTRA :, : 2 * width] = rows
        ref[ref.shape[0] - EXTRA :, 2 * width : 3 * width] = jnp.zeros((EXTRA, width), bf16)
        ref[:, 3 * width :] = before[...]


def project_back(ids, tok, whole, small, grads, blocks, n, seqs, heads):
    tokens, model = tok.shape
    slots = tokens // seqs
    wide = whole.shape[1]
    return pl.pallas_call(
        functools.partial(project_back_kernel, n, seqs, heads),
        out_shape=[shape((tokens, model), bf16)] + [shape((grads[0].shape[0], 4 * heads * HD), bf16)] * 2,
        in_specs=[SMEM] + [VMEM] * (5 + n),
        out_specs=[VMEM] * 3,
        scratch_shapes=[
            pltpu.VMEM((seqs * heads * 3 * HD, slots), bf16),
            pltpu.VMEM((tokens, wide), bf16),
            pltpu.VMEM((model, tokens), bf16),
            pltpu.VMEM((model, tokens), bf16),
        ],
        compiler_params=params(),
        cost_estimate=cost(4 * tokens * model * wide, 8e6),
        name="project_back",
    )(ids, tok, whole, small, *grads, *blocks)


def fold_core_kernel(extra, keep, recv, mine, *sends):
    half = (keep.shape[0] - extra) // 2
    mine[0:half, :] = keep[0:half, :].astype(f32) + recv[0:half, :].astype(f32)
    rest = (keep[half:, :].astype(f32) + recv[half:, :].astype(f32)).astype(bf16)
    size = sends[0].shape[1]
    for k, send in enumerate(sends):
        send[...] = rest[:, k * size : (k + 1) * size]
    if extra:
        mine[half:, :] = rest[half:, :].astype(f32)


def fold_core(keep, recv, extra):
    rows, wide = keep.shape
    out = (rows - extra) // 2 + extra
    steps = 1 if extra else 3
    parts = 2 if extra else 1
    column = lambda size: pl.BlockSpec((size, wide // steps), lambda j: (0, j))
    return pl.pallas_call(
        functools.partial(fold_core_kernel, extra),
        grid=(steps,),
        out_shape=[shape((out, wide), f32)] + [shape((out, wide // parts), bf16)] * parts,
        in_specs=[column(rows)] * 2,
        out_specs=[column(out)]
        + [pl.BlockSpec((out, wide // steps // parts), lambda j: (0, j))] * parts,
        compiler_params=params("arbitrary"),
        cost_estimate=cost(rows * wide, 7 * rows * wide),
        name="fold_core",
    )(keep, recv)


def fold_y_kernel(n, extra, parts, ids, mine, *refs):
    recvs, own, sends, stage = refs[:parts], refs[parts], refs[parts + 1 : -1], refs[-1]
    z = ids[2]
    rows = mine.shape[0] - extra
    size = rows // n
    recv = jnp.concatenate([ref[...] for ref in recvs], axis=1)
    stage[...] = mine[...] + recv.astype(f32)
    for d in range(n):
        block = stage[pl.ds(pl.multiple_of((z ^ d) * size, size), size), :]
        if d:
            sends[d - 1][0:size, :] = block.astype(bf16)
            if extra:
                sends[d - 1][size:, :] = stage[rows:, :].astype(bf16)
        else:
            own[0:size, :] = block
            if extra:
                own[size:, :] = stage[rows:, :].astype(bf16).astype(f32)


def fold_y(ids, mine, recvs, n, extra):
    rows, wide = mine.shape
    out = (rows - extra) // n + extra
    steps = 1 if extra else 3
    parts = len(recvs)
    column = lambda size: pl.BlockSpec((size, wide // steps), lambda j: (0, j))
    return pl.pallas_call(
        functools.partial(fold_y_kernel, n, extra, parts),
        grid=(steps,),
        out_shape=[shape((out, wide), f32)] + [shape((out, wide), bf16)] * (n - 1),
        in_specs=[SMEM, column(rows)]
        + [pl.BlockSpec((rows, wide // steps // parts), lambda j: (0, j))] * parts,
        out_specs=[column(out)] * n,
        scratch_shapes=[pltpu.VMEM((rows, wide // steps), f32)],
        compiler_params=params("arbitrary"),
        cost_estimate=cost(rows * wide, 9 * rows * wide),
        name="fold_y",
    )(ids, mine, *recvs)


def fold_z(own, got):
    return (own + got[0].astype(f32)) + (got[1].astype(f32) + got[2].astype(f32))


def fits(tokens, b_qv, w_qkv, w_gu):
    n = lax.axis_size("ctx")
    heads = b_qv.shape[1] // HD
    return (
        n == 4
        and lax.axis_size("shard") == 4
        and lax.axis_size("tp") == 2
        and (tokens.shape[0] * heads) % n == 0
        and w_qkv.shape[0] % 16 == 0
        and tokens.shape[1] % 256 == 0
        and b_qv.shape[1] == WIDTH
        and w_gu.shape[2] % BLOCK == 0
        and w_gu.shape[2] % WIDTH == 0
    )


def on_device(tokens, lengths, w_qkv, b_qv, w_out, w_gu, w_down, vectors, cotangent):
    if not fits(tokens, b_qv, w_qkv, w_gu):
        return by_gather(tokens, lengths, w_qkv, b_qv, w_out, w_gu, w_down, vectors, cotangent)
    n = lax.axis_size("ctx")
    seqs, slots, model = tokens.shape
    width = b_qv.shape[1]
    heads = width // HD
    per = seqs * heads // n
    units = w_gu.shape[2]
    rows = w_qkv.shape[0]
    count = seqs * slots
    shard = lax.axis_index("shard")
    ids = jnp.stack(
        [shard // 2, shard % 2, lax.axis_index("ctx"), lax.axis_index("tp")]
    ).astype(jnp.int32)
    slopes = jnp.asarray(slope_table())
    tok = tokens.reshape(count, model)
    cot = cotangent.reshape(count, model)

    first = [w_qkv.astype(bf16).reshape(rows, 3 * width)]
    first += [swap(first[0], "ctx", d) for d in range(1, n)]
    first += [swap(piece, "shard", 2) for piece in first]
    by_core = [swap(piece, "shard", 1) for piece in first]
    pieces = first[:n] + by_core[:n] + first[n:] + by_core[n:]
    front = jnp.concatenate([w_gu.reshape(rows, 2 * units), w_out.T], axis=1).astype(bf16)
    back = w_down.T.astype(bf16)
    (front,) = after([front], *pieces[1:n])
    front = [front] + [swap(front, "ctx", d) for d in range(1, n)]

    bias = jnp.concatenate([b_qv[0], jnp.zeros_like(b_qv[0]), b_qv[1]])[None, :]
    *sends, whole = project(ids, tok, bias, pieces, n, seqs, heads)
    blocks = [sends[0]] + [swap(sends[d], "ctx", d) for d in range(1, n)]
    front = jnp.concatenate(after(front, whole), axis=0)
    front_y = swap(front, "shard", 2)
    (back,) = after([back], *blocks)
    back = [back] + [swap(back, "ctx", d) for d in range(1, n)]
    *outs, att, den = attend(ids, lengths, slopes, blocks, n, heads, per)
    front, front_y = after([front, front_y], outs[0])
    front = [front, swap(front, "shard", 1), front_y, swap(front_y, "shard", 1)]
    back = jnp.concatenate(after(back, outs[0]), axis=0)
    back_y = swap(back, "shard", 2)
    outs = [outs[0]] + [swap(outs[d], "ctx", d) for d in range(1, n)]
    front = assemble(ids, front, n)
    *part, mixed = mix(ids, front, outs, n, seqs, heads)
    part_other = [swap(value, "tp", 1) for value in part]
    back, back_y = after([back, back_y], part[0])
    back = [back, swap(back, "shard", 1), back_y, swap(back_y, "shard", 1)]
    back = assemble(ids, back, n)
    hidden, low, act, gel, slope, ffn = zip(
        *(
            unit(s, tok, part[s], part_other[s], vectors, front, back)
            for s in range(seqs)
        )
    )
    ffn_other = [swap(value, "tp", 1) for value in ffn]
    output, dz2, dffn, dgate, dup, dlow, sums_two = zip(
        *(
            unit_back(
                s, ids, lengths, hidden[s], ffn[s], ffn_other[s], cot, vectors, front, back,
                gel[s], slope[s], n,
            )
            for s in range(seqs)
        )
    )
    dlow_other = [swap(value, "tp", 1) for value in dlow]
    far, near = weight_grads(ids, low, dffn, dgate, dup, act)
    *dlow_other, far = lax.optimization_barrier((*dlow_other, far))
    got = swap(far, "shard", 1)
    *sends, dz1, last_far, last_near, sums_one = mix_back(
        ids, tok, vectors, front, mixed, part, part_other, dz2, dlow, dlow_other, n, heads
    )
    sums_two = sum(sums_two)
    grads = [sends[0]] + [swap(sends[d], "ctx", d) for d in range(1, n)]
    got, sends[0] = lax.optimization_barrier((got, sends[0]))
    mine, far = fold_core(near, got, 0)
    *grads, far = lax.optimization_barrier((*grads, far))
    got = swap(far, "shard", 2)
    outs = attend_back(ids, lengths, slopes, blocks, grads, att, den, n, heads, per)
    outs = [outs[0]] + [swap(outs[d], "ctx", d) for d in range(1, n)]
    rest_own, *rest_sends = fold_y(ids, mine, [got], n, 0)
    *outs, rest_own = lax.optimization_barrier((*outs, rest_own))
    small = jnp.concatenate(
        [sums_one[0:2], sums_two[0:2], sums_one[2:3], sums_two[2:3], jnp.zeros_like(sums_one[:2])]
    )
    dx, far, near = project_back(
        ids, tok, whole, small, (last_far, last_near), outs, n, seqs, heads
    )
    got = swap(far, "shard", 1)
    mine, *far = fold_core(near, got, EXTRA)
    got = [swap(half, "shard", 2) for half in far]
    dx_other = swap(dx, "tp", 1)
    rest_got = [swap(block, "ctx", d + 1) for d, block in enumerate(rest_sends)]
    rest_got[0], got[0] = lax.optimization_barrier((rest_got[0], got[0]))
    own, *sends = fold_y(ids, mine, got, n, EXTRA)
    got = [swap(block, "ctx", d + 1) for d, block in enumerate(sends)]
    rest = fold_z(rest_own, rest_got)
    last = fold_z(own, got)
    input_grad = dz1 + (dx.astype(f32) + dx_other.astype(f32))
    small = last[rows : rows + 8, : 2 * width]
    return (
        jnp.stack(output),
        input_grad.reshape(tokens.shape),
        last[:rows, : 3 * width].reshape(w_qkv.shape),
        small[6].reshape(2, width),
        last[:rows, 3 * width :].T,
        rest[:, : 2 * units].reshape(w_gu.shape),
        rest[:, 2 * units :].T,
        small[:6],
    )


def alibi_slopes(first_head, head_count):
    power = 2 ** (H.bit_length() - 1)
    heads_index = first_head + jnp.arange(head_count, dtype=jnp.int32)
    early = -8.0 * (heads_index + 1).astype(jnp.float32) / power
    later = -4.0 * (2 * (heads_index - power) + 1).astype(jnp.float32) / power
    return jnp.exp2(jnp.where(heads_index < power, early, later))


def layer_norm(values, gain, shift):
    centred = values - jnp.mean(values, axis=-1, keepdims=True)
    spread = jnp.mean(centred * centred, axis=-1, keepdims=True)
    return centred * lax.rsqrt(spread + epsilon) * gain + shift


def gated_unit(gate_input, upper):
    return jax.nn.gelu(gate_input, approximate=False) * upper


def score_block(query_heads, key_heads, query_place, key_place, slopes, lengths):
    scores = (
        jnp.einsum("sqhe,skhe->shqk", query_heads, key_heads, preferred_element_type=jnp.float32)
        * 0.125
    )
    distance = jnp.abs(query_place[:, None] - key_place[None, :]).astype(jnp.float32)
    scores = scores - slopes[None, :, None, None] * distance[None, None]
    usable = key_place[None, :] < lengths[:, None]
    return jnp.where(usable[:, None, None, :], jnp.exp(scores), 0.0)


def backward_scores(
    query_heads,
    numer_heads,
    correction,
    key_heads,
    value_heads,
    query_place,
    key_place,
    slopes,
    lengths,
):
    weights = score_block(query_heads, key_heads, query_place, key_place, slopes, lengths)
    value_dots = jnp.einsum(
        "sqhe,skhe->shqk", numer_heads, value_heads, preferred_element_type=jnp.float32
    )
    grad_scores = (weights * (value_dots - correction[..., None])).astype(jnp.bfloat16)
    return (weights.astype(jnp.bfloat16), grad_scores)


def split_blocks(shard_piece, slot_count, ctx_count):
    piece_rows = shard_piece.shape[1]
    block_rows = math.gcd(piece_rows, 128)
    block_count = piece_rows // block_rows
    shaped = shard_piece.reshape(
        (shard_piece.shape[0], block_count, block_rows) + shard_piece.shape[2:]
    )
    blocks = jnp.moveaxis(shaped, 1, 0)
    row_ids = jnp.arange(piece_rows, dtype=jnp.int32)
    places = (row_ids % slot_count * ctx_count + row_ids // slot_count).reshape(
        block_count, block_rows
    )
    offsets = block_rows * jnp.arange(block_count, dtype=jnp.int32)
    return (blocks, places, offsets)


def by_gather(tokens, lengths, w_qkv, b_qv, w_out, w_gu, w_down, vectors, cotangent):
    ctx_count = lax.axis_size("ctx")
    ctx_rank = lax.axis_index("ctx")
    seq_count, slot_count, model_width = tokens.shape
    local_width = b_qv.shape[1]
    head_count = local_width // HD
    slopes = alibi_slopes(lax.axis_index("tp") * head_count, head_count)
    slot_ids = jnp.arange(slot_count, dtype=jnp.int32)
    query_place = slot_ids * ctx_count + ctx_rank
    query_live = (query_place[None, :] < lengths[:, None]).astype(jnp.float32)
    live_rows = query_live[:, :, None]
    head_shape = (seq_count, slot_count, head_count, HD)
    whole_qkv, whole_out, whole_gu, whole_down = (
        lax.all_gather(w_qkv.astype(jnp.bfloat16), ("shard", "ctx"), axis=0, tiled=True),
        lax.all_gather(w_out.astype(jnp.bfloat16), ("shard", "ctx"), axis=1, tiled=True),
        lax.all_gather(w_gu.astype(jnp.bfloat16), ("shard", "ctx"), axis=0, tiled=True),
        lax.all_gather(w_down.astype(jnp.bfloat16), ("shard", "ctx"), axis=1, tiled=True),
    )
    inputs = tokens.astype(jnp.float32)
    projected = jnp.einsum("std,dcm->stcm", tokens, whole_qkv, preferred_element_type=jnp.float32)
    query_rows = (projected[:, :, 0] + b_qv[0]).astype(jnp.bfloat16)
    key_rows = projected[:, :, 1].astype(jnp.bfloat16)
    value_rows = (projected[:, :, 2] + b_qv[1]).astype(jnp.bfloat16)
    query_heads = query_rows.reshape(head_shape)
    pairs = jnp.stack([key_rows, value_rows], axis=2)
    start_numer = jnp.zeros((seq_count, head_count, slot_count, HD), jnp.float32)
    start_denom = jnp.zeros((seq_count, head_count, slot_count), jnp.float32)
    blocks, places, offsets = split_blocks(
        lax.all_gather(pairs, "ctx", axis=1, tiled=True), slot_count, ctx_count
    )

    def forward_advance(inner_state, block_item):
        key_block, key_place, row_offset = block_item
        numerator, denominator = inner_state
        key_heads = key_block[:, :, 0].reshape(seq_count, -1, head_count, HD)
        value_heads = key_block[:, :, 1].reshape(seq_count, -1, head_count, HD)
        weights = score_block(query_heads, key_heads, query_place, key_place, slopes, lengths)
        numerator = numerator + jnp.einsum(
            "shqk,skhe->shqe",
            weights.astype(jnp.bfloat16),
            value_heads,
            preferred_element_type=jnp.float32,
        )
        return ((numerator, denominator + jnp.sum(weights, axis=-1)), None)

    result_state, unused = lax.scan(
        forward_advance, (start_numer, start_denom), (blocks, places, offsets)
    )
    numerator, denominator = result_state
    denominator = denominator + (1.0 - query_live)[:, None, :]
    attention_q = jnp.transpose(numerator / denominator[..., None], (0, 2, 1, 3))
    denom_q = jnp.transpose(denominator, (0, 2, 1))
    mixed = attention_q.reshape(seq_count, slot_count, local_width).astype(jnp.bfloat16)
    attn_part = jnp.einsum("stm,mn->stn", mixed, whole_out, preferred_element_type=jnp.float32)
    attn_branch = lax.psum(attn_part, "tp") + vectors[4]
    hidden, first_pull = jax.vjp(layer_norm, inputs + attn_branch, vectors[0], vectors[1])
    hidden_low = hidden.astype(jnp.bfloat16)
    gated = jnp.einsum("std,dcf->stcf", hidden_low, whole_gu, preferred_element_type=jnp.float32)
    activated, unit_pull = jax.vjp(gated_unit, gated[:, :, 0], gated[:, :, 1])
    act_low = activated.astype(jnp.bfloat16)
    ffn_part = jnp.einsum("stf,fn->stn", act_low, whole_down, preferred_element_type=jnp.float32)
    ffn_branch = lax.psum(ffn_part, "tp") + vectors[5]
    normed, second_pull = jax.vjp(layer_norm, hidden + ffn_branch, vectors[2], vectors[3])
    output = (normed * live_rows).astype(jnp.bfloat16)
    upstream = cotangent.astype(jnp.float32) * live_rows
    grad_second, grad_gain_two, grad_shift_two = second_pull(upstream)
    grad_ffn = grad_second.astype(jnp.bfloat16)
    grad_down = jnp.einsum("stf,stn->fn", act_low, grad_ffn, preferred_element_type=jnp.float32)
    grad_ffn_bias = jnp.sum(grad_ffn.astype(jnp.float32), axis=(0, 1))
    grad_act = jnp.einsum("stn,fn->stf", grad_ffn, whole_down, preferred_element_type=jnp.float32)
    grad_gate, grad_upper = unit_pull(grad_act)
    grad_gated = jnp.stack([grad_gate, grad_upper], axis=2).astype(jnp.bfloat16)
    grad_gu = jnp.einsum(
        "std,stcf->dcf", hidden_low, grad_gated, preferred_element_type=jnp.float32
    )
    hidden_part = jnp.einsum(
        "stcf,dcf->std", grad_gated, whole_gu, preferred_element_type=jnp.float32
    )
    grad_hidden = grad_second + lax.psum(hidden_part, "tp")
    grad_first, grad_gain_one, grad_shift_one = first_pull(grad_hidden)
    grad_attn = grad_first.astype(jnp.bfloat16)
    grad_out = jnp.einsum("stm,stn->mn", mixed, grad_attn, preferred_element_type=jnp.float32)
    grad_out_bias = jnp.sum(grad_attn.astype(jnp.float32), axis=(0, 1))
    grad_mixed = jnp.einsum(
        "stn,mn->stm", grad_attn, whole_out, preferred_element_type=jnp.float32
    ).astype(jnp.bfloat16)
    grad_mixed_heads = grad_mixed.reshape(head_shape).astype(jnp.float32)
    correction = jnp.transpose(
        jnp.sum(grad_mixed_heads * attention_q, axis=-1) / denom_q, (0, 2, 1)
    )
    numer_heads = (grad_mixed_heads / denom_q[..., None]).astype(jnp.bfloat16)
    start_query = jnp.zeros(head_shape, jnp.float32)
    start_state = (
        start_query,
        jnp.zeros((seq_count, slot_count * ctx_count, 2, local_width), jnp.float32),
    )
    blocks, places, offsets = split_blocks(
        lax.all_gather(pairs, "ctx", axis=1, tiled=True), slot_count, ctx_count
    )

    def backward_advance(current_state, block_item):
        key_block, key_place, row_offset = block_item
        key_heads = key_block[:, :, 0].reshape(seq_count, -1, head_count, HD)
        value_heads = key_block[:, :, 1].reshape(seq_count, -1, head_count, HD)
        weights_low, grad_scores = backward_scores(
            query_heads,
            numer_heads,
            correction,
            key_heads,
            value_heads,
            query_place,
            key_place,
            slopes,
            lengths,
        )
        grad_query = current_state[0] + jnp.einsum(
            "shqk,skhe->sqhe", grad_scores, key_heads, preferred_element_type=jnp.float32
        )
        grad_key = (
            jnp.einsum(
                "shqk,sqhe->skhe", grad_scores, query_heads, preferred_element_type=jnp.float32
            )
            * 0.125
        )
        grad_value = jnp.einsum(
            "shqk,sqhe->skhe", weights_low, numer_heads, preferred_element_type=jnp.float32
        )
        stacked = jnp.stack(
            [
                grad_key.reshape(seq_count, -1, local_width),
                grad_value.reshape(seq_count, -1, local_width),
            ],
            axis=2,
        )
        buffer = lax.dynamic_update_slice_in_dim(current_state[1], stacked, row_offset, axis=1)
        return ((grad_query, buffer), None)

    result_state, unused = lax.scan(backward_advance, start_state, (blocks, places, offsets))
    grad_pairs = lax.psum_scatter(
        result_state[1].astype(jnp.bfloat16), "ctx", scatter_dimension=1, tiled=True
    )
    grad_query_low = (
        (result_state[0] * 0.125).astype(jnp.bfloat16).reshape(seq_count, slot_count, local_width)
    )
    grad_proj = jnp.concatenate([grad_query_low[:, :, None], grad_pairs], axis=2)
    grad_qkv = jnp.einsum("std,stcm->dcm", tokens, grad_proj, preferred_element_type=jnp.float32)
    bias_terms = jnp.stack(
        [
            jnp.sum(grad_query_low.astype(jnp.float32), axis=(0, 1)),
            jnp.sum(grad_pairs[:, :, 1].astype(jnp.float32), axis=(0, 1)),
        ]
    )
    input_part = jnp.einsum(
        "stcm,dcm->std", grad_proj, whole_qkv, preferred_element_type=jnp.float32
    )
    input_grad = grad_first + lax.psum(input_part.astype(jnp.bfloat16), "tp").astype(jnp.float32)
    grad_weights = (
        lax.psum_scatter(grad_qkv, ("shard", "ctx"), scatter_dimension=0, tiled=True),
        lax.psum_scatter(grad_out, ("shard", "ctx"), scatter_dimension=1, tiled=True),
        lax.psum_scatter(grad_gu, ("shard", "ctx"), scatter_dimension=0, tiled=True),
        lax.psum_scatter(grad_down, ("shard", "ctx"), scatter_dimension=1, tiled=True),
    )
    vector_terms = jnp.stack(
        [grad_gain_one, grad_shift_one, grad_gain_two, grad_shift_two, grad_out_bias, grad_ffn_bias]
    )
    grad_bqv, grad_vectors = lax.psum((bias_terms, vector_terms), ("shard", "ctx"))
    return (
        output,
        input_grad,
        grad_weights[0],
        grad_bqv,
        grad_weights[1],
        grad_weights[2],
        grad_weights[3],
        grad_vectors,
    )


def solution(mesh):
    placed = (
        P("shard", "ctx", None),
        P("shard"),
        P(("shard", "ctx"), None, "tp"),
        P(None, "tp"),
        P("tp", ("shard", "ctx")),
        P(("shard", "ctx"), None, "tp"),
        P("tp", ("shard", "ctx")),
        P(),
        P("shard", "ctx", None),
    )
    return jax.shard_map(
        on_device,
        mesh=mesh,
        in_specs=placed,
        out_specs=(
            P("shard", "ctx", None),
            P("shard", "ctx", None),
            P(("shard", "ctx"), None, "tp"),
            P(None, "tp"),
            P("tp", ("shard", "ctx")),
            P(("shard", "ctx"), None, "tp"),
            P("tp", ("shard", "ctx")),
            P(),
        ),
        check_vma=False,
    )
```

```python
import functools
import math

import jax
import jax.numpy as jnp
import numpy as np
from jax import lax
from jax.experimental import pallas as pl
from jax.experimental.pallas import tpu as pltpu
from jax.sharding import PartitionSpec as P

H = 12
HD = 64
LOG2E = math.log2(math.e)
FAR = 1e30
TILE = 128
BLOCK = 512
WIDTH = 384
EXTRA = 16

epsilon = 1e-12
f32 = jnp.float32
bf16 = jnp.bfloat16
VMEM = pl.BlockSpec(memory_space=pltpu.VMEM)
SMEM = pl.BlockSpec(memory_space=pltpu.SMEM)


def slope_table():
    power = 2 ** (H.bit_length() - 1)
    heads = np.arange(H)
    early = -8.0 * (heads + 1) / power
    later = -4.0 * (2 * (heads - power) + 1) / power
    return np.exp2(np.where(heads < power, early, later)).astype(np.float32)


def dot_nn(a, b):
    return jnp.dot(a, b, preferred_element_type=f32)


def dot_nt(a, b):
    return lax.dot_general(a, b, (((1,), (1,)), ((), ())), preferred_element_type=f32)


def params(*semantics):
    return pltpu.CompilerParams(
        dimension_semantics=semantics or None, vmem_limit_bytes=20 * 1024 * 1024
    )


def cost(flops, nbytes, exps=0):
    return pl.CostEstimate(flops=int(flops), bytes_accessed=int(nbytes), transcendentals=int(exps))


def shape(dims, dtype):
    return jax.ShapeDtypeStruct(dims, dtype)


def xor_pairs(axis, distance):
    return [(i, i ^ distance) for i in range(lax.axis_size(axis))]


def swap(value, axis, distance):
    return lax.ppermute(value, axis, xor_pairs(axis, distance))


def after(values, *done):
    return lax.optimization_barrier((*values, *done))[: len(values)]


def live_mask(length, rank, n_ctx, slots):
    slot = lax.broadcasted_iota(jnp.int32, (slots, 1), 0)
    return jnp.where(slot * n_ctx + rank < length, 1.0, 0.0).astype(f32)


def normalise(z):
    centred = z - jnp.mean(z, axis=-1, keepdims=True)
    spread = jnp.mean(centred * centred, axis=-1, keepdims=True)
    scale = lax.rsqrt(spread + epsilon)
    return centred * scale, scale


def normalise_back(grad_hat, hat, scale):
    inner = jnp.mean(grad_hat * hat, axis=-1, keepdims=True)
    return scale * (grad_hat - jnp.mean(grad_hat, axis=-1, keepdims=True) - hat * inner)


def assemble_kernel(n, ids, *refs):
    pieces, whole = refs[:4], refs[4]
    y, c, z = ids[0], ids[1], ids[2]
    rows = pieces[0].shape[0] // n
    for k in range(4):
        for kz in range(n):
            index = ((y ^ (k // 2)) * 2 + (c ^ (k % 2))) * n + (z ^ kz)
            place = pl.ds(pl.multiple_of(index * rows, rows), rows)
            whole[place, :] = pieces[k][kz * rows : (kz + 1) * rows, :]


def assemble(ids, pieces, n):
    rows, wide = pieces[0].shape
    column = lambda size: pl.BlockSpec((size, wide // 3), lambda j: (0, j))
    return pl.pallas_call(
        functools.partial(assemble_kernel, n),
        grid=(3,),
        out_shape=shape((4 * rows, wide), bf16),
        in_specs=[SMEM] + [column(rows)] * 4,
        out_specs=column(4 * rows),
        compiler_params=params("arbitrary"),
        cost_estimate=cost(0, 16 * rows * wide),
        name="assemble",
    )(ids, *pieces)


def project_kernel(n, seqs, heads, ids, tok, bias, *refs):
    pieces = refs[: 4 * n]
    sends = refs[4 * n : 5 * n]
    whole = refs[5 * n]
    stage = refs[5 * n + 1]
    y, c, z = ids[0], ids[1], ids[2]
    rows = pieces[0].shape[0]
    for k in range(4 * n):
        ky, kc, kz = k // (2 * n), k // n % 2, k % n
        index = ((y ^ ky) * 2 + (c ^ kc)) * n + (z ^ kz)
        whole[pl.ds(pl.multiple_of(index * rows, rows), rows), :] = pieces[k][...]
    slots = sends[0].shape[1]
    width = heads * HD
    per = seqs * heads // n
    for s in range(seqs):
        acc = dot_nn(tok[s * slots : (s + 1) * slots, :], whole[...]) + bias[...]
        turned = acc.astype(bf16).T
        for h in range(heads):
            i = s * heads + h
            at = ((i % n) * per + i // n) * 3
            for part in range(3):
                first = part * width + h * HD
                stage[(at + part) * HD : (at + part + 1) * HD, :] = turned[first : first + HD, :]
    size = per * 3 * HD
    for d in range(n):
        sends[d][...] = stage[pl.ds(pl.multiple_of((z ^ d) * size, size), size), :]


def project(ids, tok, bias, pieces, n, seqs, heads):
    slots = tok.shape[0] // seqs
    size = seqs * heads // n * 3 * HD
    model, wide = tok.shape[1], bias.shape[1]
    return pl.pallas_call(
        functools.partial(project_kernel, n, seqs, heads),
        out_shape=[shape((size, slots), bf16)] * n + [shape((model, wide), bf16)],
        in_specs=[SMEM] + [VMEM] * (2 + len(pieces)),
        out_specs=[VMEM] * (n + 1),
        scratch_shapes=[pltpu.VMEM((size * n, slots), bf16)],
        compiler_params=params(),
        cost_estimate=cost(2 * tok.shape[0] * model * wide, 6e6),
        name="project",
    )(ids, tok, bias, *pieces)


def pair_scalars(n, heads, ids, lens, slopes):
    j = pl.program_id(0)
    z, t = ids[2], ids[3]
    i = z + n * j
    s = i // heads
    h = i - s * heads
    return z, lens[s], slopes[t * heads + h] * LOG2E


def query_place(n, slots, z, d):
    lane = lax.broadcasted_iota(jnp.int32, (1, slots), 1)
    return lane * n + (z ^ d)


def key_place(n, z, tile, length, slope):
    row = lax.broadcasted_iota(jnp.int32, (TILE, 1), 0)
    places = []
    for d in range(n):
        place = (tile * TILE + row) * n + (z ^ d)
        places.append(jnp.where(place < length, place.astype(f32) * slope, FAR))
    return jnp.concatenate(places, axis=0)


def gather_rows(ref, tile, n):
    rows = pl.ds(pl.multiple_of(tile * TILE, TILE), TILE)
    return jnp.concatenate([ref[d, rows, :] for d in range(n)], axis=0)


def attend_kernel(n, heads, ids, lens, slopes, *refs):
    inputs = refs[:n]
    outs = refs[n : 2 * n]
    att_ref, den_ref = refs[2 * n], refs[2 * n + 1]
    k_s, v_s, acc, den = refs[2 * n + 2 :]
    slots = inputs[0].shape[1]
    z, length, slope = pair_scalars(n, heads, ids, lens, slopes)
    for d in range(n):
        k_s[d] = inputs[d][HD : 2 * HD, :].T
        v_s[d] = inputs[d][2 * HD : 3 * HD, :].T
    acc[...] = jnp.zeros_like(acc)
    den[...] = jnp.zeros_like(den)

    def tile_step(tile, unused):
        keys = gather_rows(k_s, tile, n)
        values = gather_rows(v_s, tile, n).T
        places = key_place(n, z, tile, length, slope)
        for d in range(n):
            cols = slice(d * slots, (d + 1) * slots)
            there = query_place(n, slots, z, d).astype(f32) * slope
            scores = dot_nn(keys, inputs[d][0:HD, :]) * (0.125 * LOG2E)
            e = jnp.exp2(scores - jnp.abs(there - places))
            den[:, cols] += jnp.sum(e, axis=0, keepdims=True)
            acc[:, cols] += dot_nn(values, e.astype(bf16))
        return unused

    step = TILE * n
    lax.fori_loop(0, (length + step - 1) // step, tile_step, 0)
    for d in range(n):
        cols = slice(d * slots, (d + 1) * slots)
        padded = jnp.where(query_place(n, slots, z, d) < length, 0.0, 1.0)
        total = den[:, cols] + padded
        att = acc[:, cols] / total
        att_ref[:, cols] = att
        den_ref[0, :, cols] = total
        outs[d][...] = att.astype(bf16)


def attend(ids, lens, slopes, blocks, n, heads, per):
    slots = blocks[0].shape[1]
    every = n * slots
    return pl.pallas_call(
        functools.partial(attend_kernel, n, heads),
        grid=(per,),
        out_shape=[shape((per * HD, slots), bf16)] * n
        + [shape((per * HD, every), f32), shape((per, 1, every), f32)],
        in_specs=[SMEM] * 3 + [pl.BlockSpec((3 * HD, slots), lambda j: (j, 0))] * n,
        out_specs=[pl.BlockSpec((HD, slots), lambda j: (j, 0))] * n
        + [
            pl.BlockSpec((HD, every), lambda j: (j, 0)),
            pl.BlockSpec((1, 1, every), lambda j: (j, 0, 0)),
        ],
        scratch_shapes=[
            pltpu.VMEM((n, slots, HD), bf16),
            pltpu.VMEM((n, slots, HD), bf16),
            pltpu.VMEM((HD, every), f32),
            pltpu.VMEM((1, every), f32),
        ],
        compiler_params=params("arbitrary"),
        cost_estimate=cost(per * every * every * HD * 8, 3e6, per * every * every),
        name="attend",
    )(ids, lens, slopes, *blocks)


def attend_back_kernel(n, heads, ids, lens, slopes, *refs):
    inputs = refs[:n]
    grads = refs[n : 2 * n]
    att_ref, den_ref = refs[2 * n], refs[2 * n + 1]
    outs = refs[2 * n + 2 : 3 * n + 2]
    k_s, v_s, q_s, g_s, dn, cor, dq, dk, dv = refs[3 * n + 2 :]
    slots = inputs[0].shape[1]
    z, length, slope = pair_scalars(n, heads, ids, lens, slopes)
    for d in range(n):
        cols = slice(d * slots, (d + 1) * slots)
        k_s[d] = inputs[d][HD : 2 * HD, :].T
        v_s[d] = inputs[d][2 * HD : 3 * HD, :].T
        q_s[d] = inputs[d][0:HD, :].T
        inverse = 1.0 / den_ref[0, :, cols]
        mixed = grads[d][...].astype(f32)
        numer = (mixed * inverse).astype(bf16)
        dn[:, cols] = numer
        g_s[d] = numer.T
        cor[:, cols] = jnp.sum(mixed * att_ref[:, cols], axis=0, keepdims=True) * inverse
    dq[...] = jnp.zeros_like(dq)
    dk[...] = jnp.zeros_like(dk)
    dv[...] = jnp.zeros_like(dv)

    def tile_step(tile, unused):
        keys = gather_rows(k_s, tile, n)
        values = gather_rows(v_s, tile, n)
        keys_t = keys.T
        places = key_place(n, z, tile, length, slope)
        grad_k = jnp.zeros((n * TILE, HD), f32)
        grad_v = jnp.zeros((n * TILE, HD), f32)
        for d in range(n):
            cols = slice(d * slots, (d + 1) * slots)
            there = query_place(n, slots, z, d).astype(f32) * slope
            scores = dot_nn(keys, inputs[d][0:HD, :]) * (0.125 * LOG2E)
            e = jnp.exp2(scores - jnp.abs(there - places))
            inner = dot_nn(values, dn[:, cols])
            ds = (e * (inner - cor[:, cols])).astype(bf16)
            dq[:, cols] += dot_nn(keys_t, ds)
            grad_k += dot_nn(ds, q_s[d])
            grad_v += dot_nn(e.astype(bf16), g_s[d])
        rows = pl.ds(pl.multiple_of(tile * TILE, TILE), TILE)
        for d in range(n):
            dk[d, rows, :] = grad_k[d * TILE : (d + 1) * TILE, :]
            dv[d, rows, :] = grad_v[d * TILE : (d + 1) * TILE, :]
        return unused

    step = TILE * n
    lax.fori_loop(0, (length + step - 1) // step, tile_step, 0)
    for d in range(n):
        cols = slice(d * slots, (d + 1) * slots)
        outs[d][0:HD, :] = (dq[:, cols] * 0.125).astype(bf16)
        outs[d][HD : 2 * HD, :] = (dk[d] * 0.125).astype(bf16).T
        outs[d][2 * HD : 3 * HD, :] = dv[d].astype(bf16).T


def attend_back(ids, lens, slopes, blocks, grads, att, den, n, heads, per):
    slots = blocks[0].shape[1]
    every = n * slots
    rows = [pltpu.VMEM((n, slots, HD), bf16)] * 4
    return pl.pallas_call(
        functools.partial(attend_back_kernel, n, heads),
        grid=(per,),
        out_shape=[shape((per * 3 * HD, slots), bf16)] * n,
        in_specs=[SMEM] * 3
        + [pl.BlockSpec((3 * HD, slots), lambda j: (j, 0))] * n
        + [pl.BlockSpec((HD, slots), lambda j: (j, 0))] * n
        + [
            pl.BlockSpec((HD, every), lambda j: (j, 0)),
            pl.BlockSpec((1, 1, every), lambda j: (j, 0, 0)),
        ],
        out_specs=[pl.BlockSpec((3 * HD, slots), lambda j: (j, 0))] * n,
        scratch_shapes=rows
        + [
            pltpu.VMEM((HD, every), bf16),
            pltpu.VMEM((1, every), f32),
            pltpu.VMEM((HD, every), f32),
            pltpu.VMEM((n, slots, HD), f32),
            pltpu.VMEM((n, slots, HD), f32),
        ],
        compiler_params=params("arbitrary"),
        cost_estimate=cost(per * every * every * HD * 20, 5e6, per * every * every),
        name="attend_back",
    )(ids, lens, slopes, *blocks, *grads, att, den)


def mix_kernel(n, seqs, heads, ids, wo, *refs):
    inputs = refs[:n]
    parts = refs[n : n + seqs]
    mixed, stage = refs[n + seqs :]
    z = ids[2]
    slots = inputs[0].shape[1]
    per = seqs * heads // n
    size = per * HD
    for d in range(n):
        stage[pl.ds(pl.multiple_of((z ^ d) * size, size), size), :] = inputs[d][...]
    for s in range(seqs):
        columns = []
        for h in range(heads):
            i = s * heads + h
            at = (i % n) * per + i // n
            columns.append(stage[at * HD : (at + 1) * HD, :])
        rows = slice(s * slots, (s + 1) * slots)
        ours = jnp.concatenate(columns, axis=0).T
        mixed[rows, :] = ours
        parts[s][...] = dot_nt(ours, wo[...]).astype(bf16)


def mix(ids, packed, blocks, n, seqs, heads):
    slots = blocks[0].shape[1]
    model = packed.shape[0]
    width = heads * HD
    tokens = seqs * slots
    return pl.pallas_call(
        functools.partial(mix_kernel, n, seqs, heads),
        grid=(1,),
        out_shape=[shape((slots, model), bf16)] * seqs + [shape((tokens, width), bf16)],
        in_specs=[SMEM, pl.BlockSpec((model, width), lambda i: (0, packed.shape[1] // width - 1))]
        + [VMEM] * n,
        out_specs=[VMEM] * (seqs + 1),
        scratch_shapes=[pltpu.VMEM((seqs * heads * HD, slots), bf16)],
        compiler_params=params("arbitrary"),
        cost_estimate=cost(2 * tokens * model * width, 3e6),
        name="mix",
    )(ids, packed, *blocks)


def unit_kernel(tok, own, other, vec, wg, wu, wd, hidden, low, act, gel, slope, part, acc):
    j = pl.program_id(0)

    @pl.when(j == 0)
    def _():
        branch = own[...].astype(f32) + other[...].astype(f32) + vec[4:5, :]
        hat, _ = normalise(tok[...].astype(f32) + branch)
        h = hat * vec[0:1, :] + vec[1:2, :]
        hidden[...] = h
        low[...] = h.astype(bf16)
        acc[...] = jnp.zeros_like(acc)

    gate = dot_nn(low[...], wg[...])
    upper = dot_nn(low[...], wu[...])
    phi = 0.5 * (1.0 + lax.erf(gate * math.sqrt(0.5)))
    density = jnp.exp(gate * gate * -0.5) * (1.0 / math.sqrt(2.0 * math.pi))
    unit = gate * phi
    acted = (unit * upper).astype(bf16)
    act[...] = acted
    gel[...] = unit.astype(bf16)
    slope[...] = (upper * (phi + gate * density)).astype(bf16)
    acc[...] += dot_nt(acted, wd[...])

    @pl.when(j == pl.num_programs(0) - 1)
    def _():
        part[...] = acc[...].astype(bf16)


def unit(s, tok, own, other, vec, front, back):
    tokens, model = own.shape
    hidden_units = back.shape[1]
    steps = hidden_units // BLOCK
    fixed = lambda j: (0, 0)
    whole = pl.BlockSpec((tokens, model), fixed)
    weight = lambda start: pl.BlockSpec((model, BLOCK), lambda j: (0, start + j))
    inner = pl.BlockSpec((tokens, BLOCK), lambda j: (0, j))
    return pl.pallas_call(
        unit_kernel,
        grid=(steps,),
        out_shape=[shape((tokens, model), f32), shape((tokens, model), bf16)]
        + [shape((tokens, hidden_units), bf16)] * 3
        + [shape((tokens, model), bf16)],
        in_specs=[
            pl.BlockSpec((tokens, model), lambda j: (s, 0)),
            whole,
            whole,
            pl.BlockSpec(vec.shape, fixed),
            weight(0),
            weight(steps),
            weight(0),
        ],
        out_specs=[whole, whole, inner, inner, inner, whole],
        scratch_shapes=[pltpu.VMEM((tokens, model), f32)],
        compiler_params=params("arbitrary"),
        cost_estimate=cost(6 * tokens * model * hidden_units, 13e6, 2 * tokens * hidden_units),
        name="unit",
    )(tok, own, other, vec, front, front, back)


def unit_back_kernel(
    n, s, ids, lens, hidden, own, other, cot, vec, wg, wu, wd, gel, slope,
    output, dz2, dffn, dgate, dup, part, sums, acc,
):
    j = pl.program_id(0)

    @pl.when(j == 0)
    def _():
        live = live_mask(lens[s], ids[2], n, hidden.shape[0])
        branch = own[...].astype(f32) + other[...].astype(f32) + vec[5:6, :]
        hat, scale = normalise(hidden[...] + branch)
        output[...] = (live * (hat * vec[2:3, :] + vec[3:4, :])).astype(bf16)
        gy = cot[...].astype(f32) * live
        grad = normalise_back(gy * vec[2:3, :], hat, scale)
        dz2[...] = grad
        low = grad.astype(bf16)
        dffn[...] = low
        sums[0:1, :] = jnp.sum(gy * hat, axis=0, keepdims=True)
        sums[1:2, :] = jnp.sum(gy, axis=0, keepdims=True)
        sums[2:3, :] = jnp.sum(low.astype(f32), axis=0, keepdims=True)
        sums[3:8, :] = jnp.zeros_like(sums[3:8, :])
        acc[...] = jnp.zeros_like(acc)

    dact = dot_nn(dffn[...], wd[...])
    upper = (dact * gel[...].astype(f32)).astype(bf16)
    gate = (dact * slope[...].astype(f32)).astype(bf16)
    dgate[...] = gate
    dup[...] = upper
    acc[...] += dot_nt(gate, wg[...]) + dot_nt(upper, wu[...])

    @pl.when(j == pl.num_programs(0) - 1)
    def _():
        part[...] = acc[...].astype(bf16)


def unit_back(s, ids, lens, hidden, own, other, cot, vec, front, back, gel, slope, n):
    tokens, model = hidden.shape
    hidden_units = gel.shape[1]
    steps = hidden_units // BLOCK
    fixed = lambda j: (0, 0)
    whole = pl.BlockSpec((tokens, model), fixed)
    weight = lambda start: pl.BlockSpec((model, BLOCK), lambda j: (0, start + j))
    inner = pl.BlockSpec((tokens, BLOCK), lambda j: (0, j))
    return pl.pallas_call(
        functools.partial(unit_back_kernel, n, s),
        grid=(steps,),
        out_shape=[
            shape((tokens, model), bf16),
            shape((tokens, model), f32),
            shape((tokens, model), bf16),
            shape((tokens, hidden_units), bf16),
            shape((tokens, hidden_units), bf16),
            shape((tokens, model), bf16),
            shape((8, model), f32),
        ],
        in_specs=[SMEM, SMEM, whole, whole, whole]
        + [pl.BlockSpec((tokens, model), lambda j: (s, 0)), pl.BlockSpec(vec.shape, fixed)]
        + [weight(0), weight(steps), weight(0), inner, inner],
        out_specs=[whole, whole, whole, inner, inner, whole, pl.BlockSpec((8, model), fixed)],
        scratch_shapes=[pltpu.VMEM((tokens, model), f32)],
        compiler_params=params("arbitrary"),
        cost_estimate=cost(6 * tokens * model * hidden_units, 14e6),
        name="unit_back",
    )(ids, lens, hidden, own, other, cot, vec, front, front, back, gel, slope)


def row_starts(ids, quarter):
    y, c = ids[0], ids[1]
    keep = [(y * 2 + c) * quarter, ((1 - y) * 2 + c) * quarter]
    send = [(y * 2 + 1 - c) * quarter, ((1 - y) * 2 + 1 - c) * quarter]
    return send, keep


def arrange(ids, turned, left):
    quarter = turned.shape[0] // 4
    send, keep = row_starts(ids, quarter)
    for k, start in enumerate(send + keep):
        rows = pl.ds(pl.multiple_of(start, quarter), quarter)
        left[k * quarter : (k + 1) * quarter, :] = turned[rows, :]


def write_rows(left, right, send, keep):
    grad = dot_nn(left[...], right).astype(bf16)
    half = grad.shape[0] // 2
    send[0:half, :] = grad[:half]
    keep[0:half, :] = grad[half:]


def weight_kernel(steps, seqs, ids, *refs):
    low, dffn, dgate, dup, act = (refs[i * seqs : (i + 1) * seqs] for i in range(5))
    send, keep, left, turned = refs[5 * seqs :]
    j = pl.program_id(0)
    joined = lambda group: jnp.concatenate([ref[...] for ref in group], axis=0)

    @pl.when(j == 0)
    def _():
        for k, group in enumerate((low, dffn)):
            turned[...] = joined(group).T
            arrange(ids, turned, left.at[k])

    @pl.when(j < steps)
    def _():
        write_rows(left.at[0], joined(dgate), send, keep)

    @pl.when((j >= steps) & (j < 2 * steps))
    def _():
        write_rows(left.at[0], joined(dup), send, keep)

    @pl.when(j >= 2 * steps)
    def _():
        write_rows(left.at[1], joined(act), send, keep)


def weight_grads(ids, low, dffn, dgate, dup, act):
    seqs = len(low)
    tokens, model = low[0].shape
    hidden_units = act[0].shape[1]
    steps = hidden_units // BLOCK
    whole = pl.BlockSpec((tokens, model), lambda j: (0, 0))
    column = lambda start: pl.BlockSpec(
        (tokens, BLOCK), lambda j: (0, jnp.clip(j - start, 0, steps - 1))
    )
    out = pl.BlockSpec((model // 2, BLOCK), lambda j: (0, j))
    return pl.pallas_call(
        functools.partial(weight_kernel, steps, seqs),
        grid=(3 * steps,),
        out_shape=[shape((model // 2, 3 * hidden_units), bf16)] * 2,
        in_specs=[SMEM]
        + [whole] * (2 * seqs)
        + [column(0)] * seqs
        + [column(steps)] * seqs
        + [column(2 * steps)] * seqs,
        out_specs=[out, out],
        scratch_shapes=[
            pltpu.VMEM((2, model, tokens * seqs), bf16),
            pltpu.VMEM((model, tokens * seqs), bf16),
        ],
        compiler_params=params("arbitrary"),
        cost_estimate=cost(6 * tokens * seqs * model * hidden_units, 14e6),
        name="weight_grads",
    )(ids, *low, *dffn, *dgate, *dup, *act)


def mix_back_kernel(n, seqs, heads, ids, tok, vec, wo, mixed, *refs):
    own, other, dz2, hown, hother = (refs[i * seqs : (i + 1) * seqs] for i in range(5))
    refs = refs[5 * seqs :]
    sends = refs[:n]
    dz1, send, keep, sums = refs[n : n + 4]
    stage, left, turned_low = refs[n + 4 :]
    z = ids[2]
    slots = sends[0].shape[1]
    per = seqs * heads // n
    sums[...] = jnp.zeros_like(sums)
    for s in range(seqs):
        rows = slice(s * slots, (s + 1) * slots)
        branch = own[s][...].astype(f32) + other[s][...].astype(f32) + vec[4:5, :]
        hat, scale = normalise(tok[rows, :].astype(f32) + branch)
        gh = dz2[s][...] + (hown[s][...].astype(f32) + hother[s][...].astype(f32))
        grad = normalise_back(gh * vec[0:1, :], hat, scale)
        dz1[rows, :] = grad
        low = grad.astype(bf16)
        sums[0:1, :] += jnp.sum(gh * hat, axis=0, keepdims=True)
        sums[1:2, :] += jnp.sum(gh, axis=0, keepdims=True)
        sums[2:3, :] += jnp.sum(low.astype(f32), axis=0, keepdims=True)
        turned_low[:, rows] = low.T
        turned = dot_nn(low, wo[...]).astype(bf16).T
        for h in range(heads):
            i = s * heads + h
            at = (i % n) * per + i // n
            stage[at * HD : (at + 1) * HD, :] = turned[h * HD : (h + 1) * HD, :]
    size = per * HD
    for d in range(n):
        sends[d][...] = stage[pl.ds(pl.multiple_of((z ^ d) * size, size), size), :]
    arrange(ids, turned_low, left)
    write_rows(left, mixed[...], send, keep)
    for ref in (send, keep):
        ref[ref.shape[0] - EXTRA :, :] = jnp.zeros((EXTRA, ref.shape[1]), bf16)


def mix_back(ids, tok, vec, front, mixed, own, other, dz2, hown, hother, n, heads):
    seqs = len(own)
    tokens, model = tok.shape
    slots = tokens // seqs
    width = heads * HD
    size = seqs * heads // n * HD
    rows = model // 2 + EXTRA
    return pl.pallas_call(
        functools.partial(mix_back_kernel, n, seqs, heads),
        grid=(1,),
        out_shape=[shape((size, slots), bf16)] * n
        + [shape((tokens, model), f32)]
        + [shape((rows, width), bf16)] * 2
        + [shape((8, model), f32)],
        in_specs=[SMEM, VMEM, VMEM]
        + [pl.BlockSpec((model, width), lambda i: (0, front.shape[1] // width - 1)), VMEM]
        + [VMEM] * (5 * seqs),
        out_specs=[VMEM] * (n + 4),
        scratch_shapes=[
            pltpu.VMEM((size * n, slots), bf16),
            pltpu.VMEM((model, tokens), bf16),
            pltpu.VMEM((model, tokens), bf16),
        ],
        compiler_params=params("arbitrary"),
        cost_estimate=cost(4 * tokens * model * width, 10e6),
        name="mix_back",
    )(ids, tok, vec, front, mixed, *own, *other, *dz2, *hown, *hother)


def project_back_kernel(n, seqs, heads, ids, tok, whole, small, far, near, *refs):
    inputs = refs[:n]
    part, send, keep = refs[n : n + 3]
    stage, right, left, turned = refs[n + 3 :]
    z = ids[2]
    slots = inputs[0].shape[1]
    per = seqs * heads // n
    width = heads * HD
    size = per * 3 * HD
    for d in range(n):
        stage[pl.ds(pl.multiple_of((z ^ d) * size, size), size), :] = inputs[d][...]
    for s in range(seqs):
        for c in range(3):
            columns = []
            for h in range(heads):
                i = s * heads + h
                at = ((i % n) * per + i // n) * 3 + c
                columns.append(stage[at * HD : (at + 1) * HD, :])
            ours = jnp.concatenate(columns, axis=0).T
            right[s * slots : (s + 1) * slots, c * width : (c + 1) * width] = ours
    part[...] = dot_nt(right[...], whole[...]).astype(bf16)
    turned[...] = tok[...].T
    arrange(ids, turned, left)
    for c in range(3):
        cols = slice(c * width, (c + 1) * width)
        write_rows(left, right[:, cols], send.at[:, cols], keep.at[:, cols])
    ones = jnp.ones((8, right.shape[0]), bf16)
    sums = dot_nn(ones, right[...])
    line = jnp.concatenate([sums[:, :width], sums[:, 2 * width :]], axis=1)
    row = lax.broadcasted_iota(jnp.int32, (8, 1), 0)
    rows = jnp.where(row == 6, line, small[...])
    rows = jnp.concatenate([rows, jnp.zeros_like(rows)], axis=0).astype(bf16)
    for ref, before in ((send, far), (keep, near)):
        ref[ref.shape[0] - EXTRA :, : 2 * width] = rows
        ref[ref.shape[0] - EXTRA :, 2 * width : 3 * width] = jnp.zeros((EXTRA, width), bf16)
        ref[:, 3 * width :] = before[...]


def project_back(ids, tok, whole, small, grads, blocks, n, seqs, heads):
    tokens, model = tok.shape
    slots = tokens // seqs
    wide = whole.shape[1]
    return pl.pallas_call(
        functools.partial(project_back_kernel, n, seqs, heads),
        out_shape=[shape((tokens, model), bf16)] + [shape((grads[0].shape[0], 4 * heads * HD), bf16)] * 2,
        in_specs=[SMEM] + [VMEM] * (5 + n),
        out_specs=[VMEM] * 3,
        scratch_shapes=[
            pltpu.VMEM((seqs * heads * 3 * HD, slots), bf16),
            pltpu.VMEM((tokens, wide), bf16),
            pltpu.VMEM((model, tokens), bf16),
            pltpu.VMEM((model, tokens), bf16),
        ],
        compiler_params=params(),
        cost_estimate=cost(4 * tokens * model * wide, 8e6),
        name="project_back",
    )(ids, tok, whole, small, *grads, *blocks)


def fold_core_kernel(extra, keep, recv, mine, *sends):
    half = (keep.shape[0] - extra) // 2
    mine[0:half, :] = keep[0:half, :].astype(f32) + recv[0:half, :].astype(f32)
    rest = (keep[half:, :].astype(f32) + recv[half:, :].astype(f32)).astype(bf16)
    size = sends[0].shape[1]
    for k, send in enumerate(sends):
        send[...] = rest[:, k * size : (k + 1) * size]
    if extra:
        mine[half:, :] = rest[half:, :].astype(f32)


def fold_core(keep, recv, extra):
    rows, wide = keep.shape
    out = (rows - extra) // 2 + extra
    steps = 1 if extra else 3
    parts = 2 if extra else 1
    column = lambda size: pl.BlockSpec((size, wide // steps), lambda j: (0, j))
    return pl.pallas_call(
        functools.partial(fold_core_kernel, extra),
        grid=(steps,),
        out_shape=[shape((out, wide), f32)] + [shape((out, wide // parts), bf16)] * parts,
        in_specs=[column(rows)] * 2,
        out_specs=[column(out)]
        + [pl.BlockSpec((out, wide // steps // parts), lambda j: (0, j))] * parts,
        compiler_params=params("arbitrary"),
        cost_estimate=cost(rows * wide, 7 * rows * wide),
        name="fold_core",
    )(keep, recv)


def fold_y_kernel(n, extra, parts, ids, mine, *refs):
    recvs, own, sends, stage = refs[:parts], refs[parts], refs[parts + 1 : -1], refs[-1]
    z = ids[2]
    rows = mine.shape[0] - extra
    size = rows // n
    recv = jnp.concatenate([ref[...] for ref in recvs], axis=1)
    stage[...] = mine[...] + recv.astype(f32)
    for d in range(n):
        block = stage[pl.ds(pl.multiple_of((z ^ d) * size, size), size), :]
        if d:
            sends[d - 1][0:size, :] = block.astype(bf16)
            if extra:
                sends[d - 1][size:, :] = stage[rows:, :].astype(bf16)
        else:
            own[0:size, :] = block
            if extra:
                own[size:, :] = stage[rows:, :].astype(bf16).astype(f32)


def fold_y(ids, mine, recvs, n, extra):
    rows, wide = mine.shape
    out = (rows - extra) // n + extra
    steps = 1 if extra else 3
    parts = len(recvs)
    column = lambda size: pl.BlockSpec((size, wide // steps), lambda j: (0, j))
    return pl.pallas_call(
        functools.partial(fold_y_kernel, n, extra, parts),
        grid=(steps,),
        out_shape=[shape((out, wide), f32)] + [shape((out, wide), bf16)] * (n - 1),
        in_specs=[SMEM, column(rows)]
        + [pl.BlockSpec((rows, wide // steps // parts), lambda j: (0, j))] * parts,
        out_specs=[column(out)] * n,
        scratch_shapes=[pltpu.VMEM((rows, wide // steps), f32)],
        compiler_params=params("arbitrary"),
        cost_estimate=cost(rows * wide, 9 * rows * wide),
        name="fold_y",
    )(ids, mine, *recvs)


def fold_z(own, got):
    return (own + got[0].astype(f32)) + (got[1].astype(f32) + got[2].astype(f32))


def fits(tokens, b_qv, w_qkv, w_gu):
    n = lax.axis_size("ctx")
    heads = b_qv.shape[1] // HD
    return (
        n == 4
        and lax.axis_size("shard") == 4
        and lax.axis_size("tp") == 2
        and (tokens.shape[0] * heads) % n == 0
        and w_qkv.shape[0] % 16 == 0
        and tokens.shape[1] % 256 == 0
        and b_qv.shape[1] == WIDTH
        and w_gu.shape[2] % BLOCK == 0
        and w_gu.shape[2] % WIDTH == 0
    )


def on_device(tokens, lengths, w_qkv, b_qv, w_out, w_gu, w_down, vectors, cotangent):
    if not fits(tokens, b_qv, w_qkv, w_gu):
        return by_gather(tokens, lengths, w_qkv, b_qv, w_out, w_gu, w_down, vectors, cotangent)
    n = lax.axis_size("ctx")
    seqs, slots, model = tokens.shape
    width = b_qv.shape[1]
    heads = width // HD
    per = seqs * heads // n
    units = w_gu.shape[2]
    rows = w_qkv.shape[0]
    count = seqs * slots
    shard = lax.axis_index("shard")
    ids = jnp.stack(
        [shard // 2, shard % 2, lax.axis_index("ctx"), lax.axis_index("tp")]
    ).astype(jnp.int32)
    slopes = jnp.asarray(slope_table())
    tok = tokens.reshape(count, model)
    cot = cotangent.reshape(count, model)

    first = [w_qkv.astype(bf16).reshape(rows, 3 * width)]
    first += [swap(first[0], "ctx", d) for d in range(1, n)]
    first += [swap(piece, "shard", 2) for piece in first]
    by_core = [swap(piece, "shard", 1) for piece in first]
    pieces = first[:n] + by_core[:n] + first[n:] + by_core[n:]
    front = jnp.concatenate([w_gu.reshape(rows, 2 * units), w_out.T], axis=1).astype(bf16)
    back = w_down.T.astype(bf16)
    (front,) = after([front], *pieces[1:n])
    front = [front] + [swap(front, "ctx", d) for d in range(1, n)]

    bias = jnp.concatenate([b_qv[0], jnp.zeros_like(b_qv[0]), b_qv[1]])[None, :]
    *sends, whole = project(ids, tok, bias, pieces, n, seqs, heads)
    blocks = [sends[0]] + [swap(sends[d], "ctx", d) for d in range(1, n)]
    front = jnp.concatenate(after(front, whole), axis=0)
    front_y = swap(front, "shard", 2)
    (back,) = after([back], *blocks)
    back = [back] + [swap(back, "ctx", d) for d in range(1, n)]
    *outs, att, den = attend(ids, lengths, slopes, blocks, n, heads, per)
    front, front_y = after([front, front_y], outs[0])
    front = [front, swap(front, "shard", 1), front_y, swap(front_y, "shard", 1)]
    back = jnp.concatenate(after(back, outs[0]), axis=0)
    back_y = swap(back, "shard", 2)
    outs = [outs[0]] + [swap(outs[d], "ctx", d) for d in range(1, n)]
    front = assemble(ids, front, n)
    *part, mixed = mix(ids, front, outs, n, seqs, heads)
    part_other = [swap(value, "tp", 1) for value in part]
    back, back_y = after([back, back_y], part[0])
    back = [back, swap(back, "shard", 1), back_y, swap(back_y, "shard", 1)]
    back = assemble(ids, back, n)
    hidden, low, act, gel, slope, ffn = zip(
        *(
            unit(s, tok, part[s], part_other[s], vectors, front, back)
            for s in range(seqs)
        )
    )
    ffn_other = [swap(value, "tp", 1) for value in ffn]
    output, dz2, dffn, dgate, dup, dlow, sums_two = zip(
        *(
            unit_back(
                s, ids, lengths, hidden[s], ffn[s], ffn_other[s], cot, vectors, front, back,
                gel[s], slope[s], n,
            )
            for s in range(seqs)
        )
    )
    dlow_other = [swap(value, "tp", 1) for value in dlow]
    far, near = weight_grads(ids, low, dffn, dgate, dup, act)
    *dlow_other, far = lax.optimization_barrier((*dlow_other, far))
    got = swap(far, "shard", 1)
    *sends, dz1, last_far, last_near, sums_one = mix_back(
        ids, tok, vectors, front, mixed, part, part_other, dz2, dlow, dlow_other, n, heads
    )
    sums_two = sum(sums_two)
    grads = [sends[0]] + [swap(sends[d], "ctx", d) for d in range(1, n)]
    got, sends[0] = lax.optimization_barrier((got, sends[0]))
    mine, far = fold_core(near, got, 0)
    *grads, far = lax.optimization_barrier((*grads, far))
    got = swap(far, "shard", 2)
    outs = attend_back(ids, lengths, slopes, blocks, grads, att, den, n, heads, per)
    outs = [outs[0]] + [swap(outs[d], "ctx", d) for d in range(1, n)]
    rest_own, *rest_sends = fold_y(ids, mine, [got], n, 0)
    *outs, rest_own = lax.optimization_barrier((*outs, rest_own))
    small = jnp.concatenate(
        [sums_one[0:2], sums_two[0:2], sums_one[2:3], sums_two[2:3], jnp.zeros_like(sums_one[:2])]
    )
    dx, far, near = project_back(
        ids, tok, whole, small, (last_far, last_near), outs, n, seqs, heads
    )
    got = swap(far, "shard", 1)
    mine, *far = fold_core(near, got, EXTRA)
    got = [swap(half, "shard", 2) for half in far]
    dx_other = swap(dx, "tp", 1)
    rest_got = [swap(block, "ctx", d + 1) for d, block in enumerate(rest_sends)]
    rest_got[0], got[0] = lax.optimization_barrier((rest_got[0], got[0]))
    own, *sends = fold_y(ids, mine, got, n, EXTRA)
    got = [swap(block, "ctx", d + 1) for d, block in enumerate(sends)]
    rest = fold_z(rest_own, rest_got)
    last = fold_z(own, got)
    input_grad = dz1 + (dx.astype(f32) + dx_other.astype(f32))
    small = last[rows : rows + 8, : 2 * width]
    return (
        jnp.stack(output),
        input_grad.reshape(tokens.shape),
        last[:rows, : 3 * width].reshape(w_qkv.shape),
        small[6].reshape(2, width),
        last[:rows, 3 * width :].T,
        rest[:, : 2 * units].reshape(w_gu.shape),
        rest[:, 2 * units :].T,
        small[:6],
    )


def alibi_slopes(first_head, head_count):
    power = 2 ** (H.bit_length() - 1)
    heads_index = first_head + jnp.arange(head_count, dtype=jnp.int32)
    early = -8.0 * (heads_index + 1).astype(jnp.float32) / power
    later = -4.0 * (2 * (heads_index - power) + 1).astype(jnp.float32) / power
    return jnp.exp2(jnp.where(heads_index < power, early, later))


def layer_norm(values, gain, shift):
    centred = values - jnp.mean(values, axis=-1, keepdims=True)
    spread = jnp.mean(centred * centred, axis=-1, keepdims=True)
    return centred * lax.rsqrt(spread + epsilon) * gain + shift


def gated_unit(gate_input, upper):
    return jax.nn.gelu(gate_input, approximate=False) * upper


def score_block(query_heads, key_heads, query_place, key_place, slopes, lengths):
    scores = (
        jnp.einsum("sqhe,skhe->shqk", query_heads, key_heads, preferred_element_type=jnp.float32)
        * 0.125
    )
    distance = jnp.abs(query_place[:, None] - key_place[None, :]).astype(jnp.float32)
    scores = scores - slopes[None, :, None, None] * distance[None, None]
    usable = key_place[None, :] < lengths[:, None]
    return jnp.where(usable[:, None, None, :], jnp.exp(scores), 0.0)


def backward_scores(
    query_heads,
    numer_heads,
    correction,
    key_heads,
    value_heads,
    query_place,
    key_place,
    slopes,
    lengths,
):
    weights = score_block(query_heads, key_heads, query_place, key_place, slopes, lengths)
    value_dots = jnp.einsum(
        "sqhe,skhe->shqk", numer_heads, value_heads, preferred_element_type=jnp.float32
    )
    grad_scores = (weights * (value_dots - correction[..., None])).astype(jnp.bfloat16)
    return (weights.astype(jnp.bfloat16), grad_scores)


def split_blocks(shard_piece, slot_count, ctx_count):
    piece_rows = shard_piece.shape[1]
    block_rows = math.gcd(piece_rows, 128)
    block_count = piece_rows // block_rows
    shaped = shard_piece.reshape(
        (shard_piece.shape[0], block_count, block_rows) + shard_piece.shape[2:]
    )
    blocks = jnp.moveaxis(shaped, 1, 0)
    row_ids = jnp.arange(piece_rows, dtype=jnp.int32)
    places = (row_ids % slot_count * ctx_count + row_ids // slot_count).reshape(
        block_count, block_rows
    )
    offsets = block_rows * jnp.arange(block_count, dtype=jnp.int32)
    return (blocks, places, offsets)


def by_gather(tokens, lengths, w_qkv, b_qv, w_out, w_gu, w_down, vectors, cotangent):
    ctx_count = lax.axis_size("ctx")
    ctx_rank = lax.axis_index("ctx")
    seq_count, slot_count, model_width = tokens.shape
    local_width = b_qv.shape[1]
    head_count = local_width // HD
    slopes = alibi_slopes(lax.axis_index("tp") * head_count, head_count)
    slot_ids = jnp.arange(slot_count, dtype=jnp.int32)
    query_place = slot_ids * ctx_count + ctx_rank
    query_live = (query_place[None, :] < lengths[:, None]).astype(jnp.float32)
    live_rows = query_live[:, :, None]
    head_shape = (seq_count, slot_count, head_count, HD)
    whole_qkv, whole_out, whole_gu, whole_down = (
        lax.all_gather(w_qkv.astype(jnp.bfloat16), ("shard", "ctx"), axis=0, tiled=True),
        lax.all_gather(w_out.astype(jnp.bfloat16), ("shard", "ctx"), axis=1, tiled=True),
        lax.all_gather(w_gu.astype(jnp.bfloat16), ("shard", "ctx"), axis=0, tiled=True),
        lax.all_gather(w_down.astype(jnp.bfloat16), ("shard", "ctx"), axis=1, tiled=True),
    )
    inputs = tokens.astype(jnp.float32)
    projected = jnp.einsum("std,dcm->stcm", tokens, whole_qkv, preferred_element_type=jnp.float32)
    query_rows = (projected[:, :, 0] + b_qv[0]).astype(jnp.bfloat16)
    key_rows = projected[:, :, 1].astype(jnp.bfloat16)
    value_rows = (projected[:, :, 2] + b_qv[1]).astype(jnp.bfloat16)
    query_heads = query_rows.reshape(head_shape)
    pairs = jnp.stack([key_rows, value_rows], axis=2)
    start_numer = jnp.zeros((seq_count, head_count, slot_count, HD), jnp.float32)
    start_denom = jnp.zeros((seq_count, head_count, slot_count), jnp.float32)
    blocks, places, offsets = split_blocks(
        lax.all_gather(pairs, "ctx", axis=1, tiled=True), slot_count, ctx_count
    )

    def forward_advance(inner_state, block_item):
        key_block, key_place, row_offset = block_item
        numerator, denominator = inner_state
        key_heads = key_block[:, :, 0].reshape(seq_count, -1, head_count, HD)
        value_heads = key_block[:, :, 1].reshape(seq_count, -1, head_count, HD)
        weights = score_block(query_heads, key_heads, query_place, key_place, slopes, lengths)
        numerator = numerator + jnp.einsum(
            "shqk,skhe->shqe",
            weights.astype(jnp.bfloat16),
            value_heads,
            preferred_element_type=jnp.float32,
        )
        return ((numerator, denominator + jnp.sum(weights, axis=-1)), None)

    result_state, unused = lax.scan(
        forward_advance, (start_numer, start_denom), (blocks, places, offsets)
    )
    numerator, denominator = result_state
    denominator = denominator + (1.0 - query_live)[:, None, :]
    attention_q = jnp.transpose(numerator / denominator[..., None], (0, 2, 1, 3))
    denom_q = jnp.transpose(denominator, (0, 2, 1))
    mixed = attention_q.reshape(seq_count, slot_count, local_width).astype(jnp.bfloat16)
    attn_part = jnp.einsum("stm,mn->stn", mixed, whole_out, preferred_element_type=jnp.float32)
    attn_branch = lax.psum(attn_part, "tp") + vectors[4]
    hidden, first_pull = jax.vjp(layer_norm, inputs + attn_branch, vectors[0], vectors[1])
    hidden_low = hidden.astype(jnp.bfloat16)
    gated = jnp.einsum("std,dcf->stcf", hidden_low, whole_gu, preferred_element_type=jnp.float32)
    activated, unit_pull = jax.vjp(gated_unit, gated[:, :, 0], gated[:, :, 1])
    act_low = activated.astype(jnp.bfloat16)
    ffn_part = jnp.einsum("stf,fn->stn", act_low, whole_down, preferred_element_type=jnp.float32)
    ffn_branch = lax.psum(ffn_part, "tp") + vectors[5]
    normed, second_pull = jax.vjp(layer_norm, hidden + ffn_branch, vectors[2], vectors[3])
    output = (normed * live_rows).astype(jnp.bfloat16)
    upstream = cotangent.astype(jnp.float32) * live_rows
    grad_second, grad_gain_two, grad_shift_two = second_pull(upstream)
    grad_ffn = grad_second.astype(jnp.bfloat16)
    grad_down = jnp.einsum("stf,stn->fn", act_low, grad_ffn, preferred_element_type=jnp.float32)
    grad_ffn_bias = jnp.sum(grad_ffn.astype(jnp.float32), axis=(0, 1))
    grad_act = jnp.einsum("stn,fn->stf", grad_ffn, whole_down, preferred_element_type=jnp.float32)
    grad_gate, grad_upper = unit_pull(grad_act)
    grad_gated = jnp.stack([grad_gate, grad_upper], axis=2).astype(jnp.bfloat16)
    grad_gu = jnp.einsum(
        "std,stcf->dcf", hidden_low, grad_gated, preferred_element_type=jnp.float32
    )
    hidden_part = jnp.einsum(
        "stcf,dcf->std", grad_gated, whole_gu, preferred_element_type=jnp.float32
    )
    grad_hidden = grad_second + lax.psum(hidden_part, "tp")
    grad_first, grad_gain_one, grad_shift_one = first_pull(grad_hidden)
    grad_attn = grad_first.astype(jnp.bfloat16)
    grad_out = jnp.einsum("stm,stn->mn", mixed, grad_attn, preferred_element_type=jnp.float32)
    grad_out_bias = jnp.sum(grad_attn.astype(jnp.float32), axis=(0, 1))
    grad_mixed = jnp.einsum(
        "stn,mn->stm", grad_attn, whole_out, preferred_element_type=jnp.float32
    ).astype(jnp.bfloat16)
    grad_mixed_heads = grad_mixed.reshape(head_shape).astype(jnp.float32)
    correction = jnp.transpose(
        jnp.sum(grad_mixed_heads * attention_q, axis=-1) / denom_q, (0, 2, 1)
    )
    numer_heads = (grad_mixed_heads / denom_q[..., None]).astype(jnp.bfloat16)
    start_query = jnp.zeros(head_shape, jnp.float32)
    start_state = (
        start_query,
        jnp.zeros((seq_count, slot_count * ctx_count, 2, local_width), jnp.float32),
    )
    blocks, places, offsets = split_blocks(
        lax.all_gather(pairs, "ctx", axis=1, tiled=True), slot_count, ctx_count
    )

    def backward_advance(current_state, block_item):
        key_block, key_place, row_offset = block_item
        key_heads = key_block[:, :, 0].reshape(seq_count, -1, head_count, HD)
        value_heads = key_block[:, :, 1].reshape(seq_count, -1, head_count, HD)
        weights_low, grad_scores = backward_scores(
            query_heads,
            numer_heads,
            correction,
            key_heads,
            value_heads,
            query_place,
            key_place,
            slopes,
            lengths,
        )
        grad_query = current_state[0] + jnp.einsum(
            "shqk,skhe->sqhe", grad_scores, key_heads, preferred_element_type=jnp.float32
        )
        grad_key = (
            jnp.einsum(
                "shqk,sqhe->skhe", grad_scores, query_heads, preferred_element_type=jnp.float32
            )
            * 0.125
        )
        grad_value = jnp.einsum(
            "shqk,sqhe->skhe", weights_low, numer_heads, preferred_element_type=jnp.float32
        )
        stacked = jnp.stack(
            [
                grad_key.reshape(seq_count, -1, local_width),
                grad_value.reshape(seq_count, -1, local_width),
            ],
            axis=2,
        )
        buffer = lax.dynamic_update_slice_in_dim(current_state[1], stacked, row_offset, axis=1)
        return ((grad_query, buffer), None)

    result_state, unused = lax.scan(backward_advance, start_state, (blocks, places, offsets))
    grad_pairs = lax.psum_scatter(
        result_state[1].astype(jnp.bfloat16), "ctx", scatter_dimension=1, tiled=True
    )
    grad_query_low = (
        (result_state[0] * 0.125).astype(jnp.bfloat16).reshape(seq_count, slot_count, local_width)
    )
    grad_proj = jnp.concatenate([grad_query_low[:, :, None], grad_pairs], axis=2)
    grad_qkv = jnp.einsum("std,stcm->dcm", tokens, grad_proj, preferred_element_type=jnp.float32)
    bias_terms = jnp.stack(
        [
            jnp.sum(grad_query_low.astype(jnp.float32), axis=(0, 1)),
            jnp.sum(grad_pairs[:, :, 1].astype(jnp.float32), axis=(0, 1)),
        ]
    )
    input_part = jnp.einsum(
        "stcm,dcm->std", grad_proj, whole_qkv, preferred_element_type=jnp.float32
    )
    input_grad = grad_first + lax.psum(input_part.astype(jnp.bfloat16), "tp").astype(jnp.float32)
    grad_weights = (
        lax.psum_scatter(grad_qkv, ("shard", "ctx"), scatter_dimension=0, tiled=True),
        lax.psum_scatter(grad_out, ("shard", "ctx"), scatter_dimension=1, tiled=True),
        lax.psum_scatter(grad_gu, ("shard", "ctx"), scatter_dimension=0, tiled=True),
        lax.psum_scatter(grad_down, ("shard", "ctx"), scatter_dimension=1, tiled=True),
    )
    vector_terms = jnp.stack(
        [grad_gain_one, grad_shift_one, grad_gain_two, grad_shift_two, grad_out_bias, grad_ffn_bias]
    )
    grad_bqv, grad_vectors = lax.psum((bias_terms, vector_terms), ("shard", "ctx"))
    return (
        output,
        input_grad,
        grad_weights[0],
        grad_bqv,
        grad_weights[1],
        grad_weights[2],
        grad_weights[3],
        grad_vectors,
    )


def solution(mesh):
    placed = (
        P("shard", "ctx", None),
        P("shard"),
        P(("shard", "ctx"), None, "tp"),
        P(None, "tp"),
        P("tp", ("shard", "ctx")),
        P(("shard", "ctx"), None, "tp"),
        P("tp", ("shard", "ctx")),
        P(),
        P("shard", "ctx", None),
    )
    return jax.shard_map(
        on_device,
        mesh=mesh,
        in_specs=placed,
        out_specs=(
            P("shard", "ctx", None),
            P("shard", "ctx", None),
            P(("shard", "ctx"), None, "tp"),
            P(None, "tp"),
            P("tp", ("shard", "ctx")),
            P(("shard", "ctx"), None, "tp"),
            P("tp", ("shard", "ctx")),
            P(),
        ),
        check_vma=False,
    )
```

```python
import functools
import math

import jax
import jax.numpy as jnp
import numpy as np
from jax import lax
from jax.experimental import pallas as pl
from jax.experimental.pallas import tpu as pltpu
from jax.sharding import PartitionSpec as P

H = 12
HD = 64
LOG2E = math.log2(math.e)
FAR = 1e30
TILE = 128
BLOCK = 512
WIDTH = 384
EXTRA = 16

epsilon = 1e-12
f32 = jnp.float32
bf16 = jnp.bfloat16
VMEM = pl.BlockSpec(memory_space=pltpu.VMEM)
SMEM = pl.BlockSpec(memory_space=pltpu.SMEM)


def slope_table():
    power = 2 ** (H.bit_length() - 1)
    heads = np.arange(H)
    early = -8.0 * (heads + 1) / power
    later = -4.0 * (2 * (heads - power) + 1) / power
    return np.exp2(np.where(heads < power, early, later)).astype(np.float32)


def dot_nn(a, b):
    return jnp.dot(a, b, preferred_element_type=f32)


def dot_nt(a, b):
    return lax.dot_general(a, b, (((1,), (1,)), ((), ())), preferred_element_type=f32)


def params(*semantics):
    return pltpu.CompilerParams(
        dimension_semantics=semantics or None, vmem_limit_bytes=20 * 1024 * 1024
    )


def cost(flops, nbytes, exps=0):
    return pl.CostEstimate(flops=int(flops), bytes_accessed=int(nbytes), transcendentals=int(exps))


def shape(dims, dtype):
    return jax.ShapeDtypeStruct(dims, dtype)


def xor_pairs(axis, distance):
    return [(i, i ^ distance) for i in range(lax.axis_size(axis))]


def swap(value, axis, distance):
    return lax.ppermute(value, axis, xor_pairs(axis, distance))


def after(values, *done):
    return lax.optimization_barrier((*values, *done))[: len(values)]


def live_mask(length, rank, n_ctx, slots):
    slot = lax.broadcasted_iota(jnp.int32, (slots, 1), 0)
    return jnp.where(slot * n_ctx + rank < length, 1.0, 0.0).astype(f32)


def normalise(z):
    centred = z - jnp.mean(z, axis=-1, keepdims=True)
    spread = jnp.mean(centred * centred, axis=-1, keepdims=True)
    scale = lax.rsqrt(spread + epsilon)
    return centred * scale, scale


def normalise_back(grad_hat, hat, scale):
    inner = jnp.mean(grad_hat * hat, axis=-1, keepdims=True)
    return scale * (grad_hat - jnp.mean(grad_hat, axis=-1, keepdims=True) - hat * inner)


def assemble_kernel(n, ids, *refs):
    pieces, whole = refs[:4], refs[4]
    y, c, z = ids[0], ids[1], ids[2]
    rows = pieces[0].shape[0] // n
    for k in range(4):
        for kz in range(n):
            index = ((y ^ (k // 2)) * 2 + (c ^ (k % 2))) * n + (z ^ kz)
            place = pl.ds(pl.multiple_of(index * rows, rows), rows)
            whole[place, :] = pieces[k][kz * rows : (kz + 1) * rows, :]


def assemble(ids, pieces, n):
    rows, wide = pieces[0].shape
    column = lambda size: pl.BlockSpec((size, wide // 3), lambda j: (0, j))
    return pl.pallas_call(
        functools.partial(assemble_kernel, n),
        grid=(3,),
        out_shape=shape((4 * rows, wide), bf16),
        in_specs=[SMEM] + [column(rows)] * 4,
        out_specs=column(4 * rows),
        compiler_params=params("arbitrary"),
        cost_estimate=cost(0, 16 * rows * wide),
        name="assemble",
    )(ids, *pieces)


def project_kernel(n, seqs, heads, ids, tok, bias, *refs):
    pieces = refs[: 4 * n]
    sends = refs[4 * n : 5 * n]
    whole = refs[5 * n]
    stage = refs[5 * n + 1]
    y, c, z = ids[0], ids[1], ids[2]
    rows = pieces[0].shape[0]
    for k in range(4 * n):
        ky, kc, kz = k // (2 * n), k // n % 2, k % n
        index = ((y ^ ky) * 2 + (c ^ kc)) * n + (z ^ kz)
        whole[pl.ds(pl.multiple_of(index * rows, rows), rows), :] = pieces[k][...]
    slots = sends[0].shape[1]
    width = heads * HD
    per = seqs * heads // n
    for s in range(seqs):
        acc = dot_nn(tok[s * slots : (s + 1) * slots, :], whole[...]) + bias[...]
        turned = acc.astype(bf16).T
        for h in range(heads):
            i = s * heads + h
            at = ((i % n) * per + i // n) * 3
            for part in range(3):
                first = part * width + h * HD
                stage[(at + part) * HD : (at + part + 1) * HD, :] = turned[first : first + HD, :]
    size = per * 3 * HD
    for d in range(n):
        sends[d][...] = stage[pl.ds(pl.multiple_of((z ^ d) * size, size), size), :]


def project(ids, tok, bias, pieces, n, seqs, heads):
    slots = tok.shape[0] // seqs
    size = seqs * heads // n * 3 * HD
    model, wide = tok.shape[1], bias.shape[1]
    return pl.pallas_call(
        functools.partial(project_kernel, n, seqs, heads),
        out_shape=[shape((size, slots), bf16)] * n + [shape((model, wide), bf16)],
        in_specs=[SMEM] + [VMEM] * (2 + len(pieces)),
        out_specs=[VMEM] * (n + 1),
        scratch_shapes=[pltpu.VMEM((size * n, slots), bf16)],
        compiler_params=params(),
        cost_estimate=cost(2 * tok.shape[0] * model * wide, 6e6),
        name="project",
    )(ids, tok, bias, *pieces)


def pair_scalars(n, heads, ids, lens, slopes):
    j = pl.program_id(0)
    z, t = ids[2], ids[3]
    i = z + n * j
    s = i // heads
    h = i - s * heads
    return z, lens[s], slopes[t * heads + h] * LOG2E


def query_place(n, slots, z, d):
    lane = lax.broadcasted_iota(jnp.int32, (1, slots), 1)
    return lane * n + (z ^ d)


def key_place(n, z, tile, length, slope):
    row = lax.broadcasted_iota(jnp.int32, (TILE, 1), 0)
    places = []
    for d in range(n):
        place = (tile * TILE + row) * n + (z ^ d)
        places.append(jnp.where(place < length, place.astype(f32) * slope, FAR))
    return jnp.concatenate(places, axis=0)


def gather_rows(ref, tile, n):
    rows = pl.ds(pl.multiple_of(tile * TILE, TILE), TILE)
    return jnp.concatenate([ref[d, rows, :] for d in range(n)], axis=0)


def attend_kernel(n, heads, ids, lens, slopes, *refs):
    inputs = refs[:n]
    outs = refs[n : 2 * n]
    att_ref, den_ref = refs[2 * n], refs[2 * n + 1]
    k_s, v_s, acc, den = refs[2 * n + 2 :]
    slots = inputs[0].shape[1]
    z, length, slope = pair_scalars(n, heads, ids, lens, slopes)
    for d in range(n):
        k_s[d] = inputs[d][HD : 2 * HD, :].T
        v_s[d] = inputs[d][2 * HD : 3 * HD, :].T
    acc[...] = jnp.zeros_like(acc)
    den[...] = jnp.zeros_like(den)

    def tile_step(tile, unused):
        keys = gather_rows(k_s, tile, n)
        values = gather_rows(v_s, tile, n).T
        places = key_place(n, z, tile, length, slope)
        for d in range(n):
            cols = slice(d * slots, (d + 1) * slots)
            there = query_place(n, slots, z, d).astype(f32) * slope
            scores = dot_nn(keys, inputs[d][0:HD, :]) * (0.125 * LOG2E)
            e = jnp.exp2(scores - jnp.abs(there - places))
            den[:, cols] += jnp.sum(e, axis=0, keepdims=True)
            acc[:, cols] += dot_nn(values, e.astype(bf16))
        return unused

    step = TILE * n
    lax.fori_loop(0, (length + step - 1) // step, tile_step, 0)
    for d in range(n):
        cols = slice(d * slots, (d + 1) * slots)
        padded = jnp.where(query_place(n, slots, z, d) < length, 0.0, 1.0)
        total = den[:, cols] + padded
        att = acc[:, cols] / total
        att_ref[:, cols] = att
        den_ref[0, :, cols] = total
        outs[d][...] = att.astype(bf16)


def attend(ids, lens, slopes, blocks, n, heads, per):
    slots = blocks[0].shape[1]
    every = n * slots
    return pl.pallas_call(
        functools.partial(attend_kernel, n, heads),
        grid=(per,),
        out_shape=[shape((per * HD, slots), bf16)] * n
        + [shape((per * HD, every), f32), shape((per, 1, every), f32)],
        in_specs=[SMEM] * 3 + [pl.BlockSpec((3 * HD, slots), lambda j: (j, 0))] * n,
        out_specs=[pl.BlockSpec((HD, slots), lambda j: (j, 0))] * n
        + [
            pl.BlockSpec((HD, every), lambda j: (j, 0)),
            pl.BlockSpec((1, 1, every), lambda j: (j, 0, 0)),
        ],
        scratch_shapes=[
            pltpu.VMEM((n, slots, HD), bf16),
            pltpu.VMEM((n, slots, HD), bf16),
            pltpu.VMEM((HD, every), f32),
            pltpu.VMEM((1, every), f32),
        ],
        compiler_params=params("arbitrary"),
        cost_estimate=cost(per * every * every * HD * 8, 3e6, per * every * every),
        name="attend",
    )(ids, lens, slopes, *blocks)


def attend_back_kernel(n, heads, ids, lens, slopes, *refs):
    inputs = refs[:n]
    grads = refs[n : 2 * n]
    att_ref, den_ref = refs[2 * n], refs[2 * n + 1]
    outs = refs[2 * n + 2 : 3 * n + 2]
    k_s, v_s, q_s, g_s, dn, cor, dq, dk, dv = refs[3 * n + 2 :]
    slots = inputs[0].shape[1]
    z, length, slope = pair_scalars(n, heads, ids, lens, slopes)
    for d in range(n):
        cols = slice(d * slots, (d + 1) * slots)
        k_s[d] = inputs[d][HD : 2 * HD, :].T
        v_s[d] = inputs[d][2 * HD : 3 * HD, :].T
        q_s[d] = inputs[d][0:HD, :].T
        inverse = 1.0 / den_ref[0, :, cols]
        mixed = grads[d][...].astype(f32)
        numer = (mixed * inverse).astype(bf16)
        dn[:, cols] = numer
        g_s[d] = numer.T
        cor[:, cols] = jnp.sum(mixed * att_ref[:, cols], axis=0, keepdims=True) * inverse
    dq[...] = jnp.zeros_like(dq)
    dk[...] = jnp.zeros_like(dk)
    dv[...] = jnp.zeros_like(dv)

    def tile_step(tile, unused):
        keys = gather_rows(k_s, tile, n)
        values = gather_rows(v_s, tile, n)
        keys_t = keys.T
        places = key_place(n, z, tile, length, slope)
        grad_k = jnp.zeros((n * TILE, HD), f32)
        grad_v = jnp.zeros((n * TILE, HD), f32)
        for d in range(n):
            cols = slice(d * slots, (d + 1) * slots)
            there = query_place(n, slots, z, d).astype(f32) * slope
            scores = dot_nn(keys, inputs[d][0:HD, :]) * (0.125 * LOG2E)
            e = jnp.exp2(scores - jnp.abs(there - places))
            inner = dot_nn(values, dn[:, cols])
            ds = (e * (inner - cor[:, cols])).astype(bf16)
            dq[:, cols] += dot_nn(keys_t, ds)
            grad_k += dot_nn(ds, q_s[d])
            grad_v += dot_nn(e.astype(bf16), g_s[d])
        rows = pl.ds(pl.multiple_of(tile * TILE, TILE), TILE)
        for d in range(n):
            dk[d, rows, :] = grad_k[d * TILE : (d + 1) * TILE, :]
            dv[d, rows, :] = grad_v[d * TILE : (d + 1) * TILE, :]
        return unused

    step = TILE * n
    lax.fori_loop(0, (length + step - 1) // step, tile_step, 0)
    for d in range(n):
        cols = slice(d * slots, (d + 1) * slots)
        outs[d][0:HD, :] = (dq[:, cols] * 0.125).astype(bf16)
        outs[d][HD : 2 * HD, :] = (dk[d] * 0.125).astype(bf16).T
        outs[d][2 * HD : 3 * HD, :] = dv[d].astype(bf16).T


def attend_back(ids, lens, slopes, blocks, grads, att, den, n, heads, per):
    slots = blocks[0].shape[1]
    every = n * slots
    rows = [pltpu.VMEM((n, slots, HD), bf16)] * 4
    return pl.pallas_call(
        functools.partial(attend_back_kernel, n, heads),
        grid=(per,),
        out_shape=[shape((per * 3 * HD, slots), bf16)] * n,
        in_specs=[SMEM] * 3
        + [pl.BlockSpec((3 * HD, slots), lambda j: (j, 0))] * n
        + [pl.BlockSpec((HD, slots), lambda j: (j, 0))] * n
        + [
            pl.BlockSpec((HD, every), lambda j: (j, 0)),
            pl.BlockSpec((1, 1, every), lambda j: (j, 0, 0)),
        ],
        out_specs=[pl.BlockSpec((3 * HD, slots), lambda j: (j, 0))] * n,
        scratch_shapes=rows
        + [
            pltpu.VMEM((HD, every), bf16),
            pltpu.VMEM((1, every), f32),
            pltpu.VMEM((HD, every), f32),
            pltpu.VMEM((n, slots, HD), f32),
            pltpu.VMEM((n, slots, HD), f32),
        ],
        compiler_params=params("arbitrary"),
        cost_estimate=cost(per * every * every * HD * 20, 5e6, per * every * every),
        name="attend_back",
    )(ids, lens, slopes, *blocks, *grads, att, den)


def mix_kernel(n, seqs, heads, ids, wo, *refs):
    inputs = refs[:n]
    parts = refs[n : n + seqs]
    mixed, stage = refs[n + seqs :]
    z = ids[2]
    slots = inputs[0].shape[1]
    per = seqs * heads // n
    size = per * HD
    for d in range(n):
        stage[pl.ds(pl.multiple_of((z ^ d) * size, size), size), :] = inputs[d][...]
    for s in range(seqs):
        columns = []
        for h in range(heads):
            i = s * heads + h
            at = (i % n) * per + i // n
            columns.append(stage[at * HD : (at + 1) * HD, :])
        rows = slice(s * slots, (s + 1) * slots)
        ours = jnp.concatenate(columns, axis=0).T
        mixed[rows, :] = ours
        parts[s][...] = dot_nt(ours, wo[...]).astype(bf16)


def mix(ids, packed, blocks, n, seqs, heads):
    slots = blocks[0].shape[1]
    model = packed.shape[0]
    width = heads * HD
    tokens = seqs * slots
    return pl.pallas_call(
        functools.partial(mix_kernel, n, seqs, heads),
        grid=(1,),
        out_shape=[shape((slots, model), bf16)] * seqs + [shape((tokens, width), bf16)],
        in_specs=[SMEM, pl.BlockSpec((model, width), lambda i: (0, packed.shape[1] // width - 1))]
        + [VMEM] * n,
        out_specs=[VMEM] * (seqs + 1),
        scratch_shapes=[pltpu.VMEM((seqs * heads * HD, slots), bf16)],
        compiler_params=params("arbitrary"),
        cost_estimate=cost(2 * tokens * model * width, 3e6),
        name="mix",
    )(ids, packed, *blocks)


def unit_kernel(tok, own, other, vec, wg, wu, wd, hidden, low, act, gel, slope, part, acc):
    j = pl.program_id(0)

    @pl.when(j == 0)
    def _():
        branch = own[...].astype(f32) + other[...].astype(f32) + vec[4:5, :]
        hat, _ = normalise(tok[...].astype(f32) + branch)
        h = hat * vec[0:1, :] + vec[1:2, :]
        hidden[...] = h
        low[...] = h.astype(bf16)
        acc[...] = jnp.zeros_like(acc)

    gate = dot_nn(low[...], wg[...])
    upper = dot_nn(low[...], wu[...])
    phi = 0.5 * (1.0 + lax.erf(gate * math.sqrt(0.5)))
    density = jnp.exp(gate * gate * -0.5) * (1.0 / math.sqrt(2.0 * math.pi))
    unit = gate * phi
    acted = (unit * upper).astype(bf16)
    act[...] = acted
    gel[...] = unit.astype(bf16)
    slope[...] = (upper * (phi + gate * density)).astype(bf16)
    acc[...] += dot_nt(acted, wd[...])

    @pl.when(j == pl.num_programs(0) - 1)
    def _():
        part[...] = acc[...].astype(bf16)


def unit(s, tok, own, other, vec, front, back):
    tokens, model = own.shape
    hidden_units = back.shape[1]
    steps = hidden_units // BLOCK
    fixed = lambda j: (0, 0)
    whole = pl.BlockSpec((tokens, model), fixed)
    weight = lambda start: pl.BlockSpec((model, BLOCK), lambda j: (0, start + j))
    inner = pl.BlockSpec((tokens, BLOCK), lambda j: (0, j))
    return pl.pallas_call(
        unit_kernel,
        grid=(steps,),
        out_shape=[shape((tokens, model), f32), shape((tokens, model), bf16)]
        + [shape((tokens, hidden_units), bf16)] * 3
        + [shape((tokens, model), bf16)],
        in_specs=[
            pl.BlockSpec((tokens, model), lambda j: (s, 0)),
            whole,
            whole,
            pl.BlockSpec(vec.shape, fixed),
            weight(0),
            weight(steps),
            weight(0),
        ],
        out_specs=[whole, whole, inner, inner, inner, whole],
        scratch_shapes=[pltpu.VMEM((tokens, model), f32)],
        compiler_params=params("arbitrary"),
        cost_estimate=cost(6 * tokens * model * hidden_units, 13e6, 2 * tokens * hidden_units),
        name="unit",
    )(tok, own, other, vec, front, front, back)


def unit_back_kernel(
    n, s, ids, lens, hidden, own, other, cot, vec, wg, wu, wd, gel, slope,
    output, dz2, dffn, dgate, dup, part, sums, acc,
):
    j = pl.program_id(0)

    @pl.when(j == 0)
    def _():
        live = live_mask(lens[s], ids[2], n, hidden.shape[0])
        branch = own[...].astype(f32) + other[...].astype(f32) + vec[5:6, :]
        hat, scale = normalise(hidden[...] + branch)
        output[...] = (live * (hat * vec[2:3, :] + vec[3:4, :])).astype(bf16)
        gy = cot[...].astype(f32) * live
        grad = normalise_back(gy * vec[2:3, :], hat, scale)
        dz2[...] = grad
        low = grad.astype(bf16)
        dffn[...] = low
        sums[0:1, :] = jnp.sum(gy * hat, axis=0, keepdims=True)
        sums[1:2, :] = jnp.sum(gy, axis=0, keepdims=True)
        sums[2:3, :] = jnp.sum(low.astype(f32), axis=0, keepdims=True)
        sums[3:8, :] = jnp.zeros_like(sums[3:8, :])
        acc[...] = jnp.zeros_like(acc)

    dact = dot_nn(dffn[...], wd[...])
    upper = (dact * gel[...].astype(f32)).astype(bf16)
    gate = (dact * slope[...].astype(f32)).astype(bf16)
    dgate[...] = gate
    dup[...] = upper
    acc[...] += dot_nt(gate, wg[...]) + dot_nt(upper, wu[...])

    @pl.when(j == pl.num_programs(0) - 1)
    def _():
        part[...] = acc[...].astype(bf16)


def unit_back(s, ids, lens, hidden, own, other, cot, vec, front, back, gel, slope, n):
    tokens, model = hidden.shape
    hidden_units = gel.shape[1]
    steps = hidden_units // BLOCK
    fixed = lambda j: (0, 0)
    whole = pl.BlockSpec((tokens, model), fixed)
    weight = lambda start: pl.BlockSpec((model, BLOCK), lambda j: (0, start + j))
    inner = pl.BlockSpec((tokens, BLOCK), lambda j: (0, j))
    return pl.pallas_call(
        functools.partial(unit_back_kernel, n, s),
        grid=(steps,),
        out_shape=[
            shape((tokens, model), bf16),
            shape((tokens, model), f32),
            shape((tokens, model), bf16),
            shape((tokens, hidden_units), bf16),
            shape((tokens, hidden_units), bf16),
            shape((tokens, model), bf16),
            shape((8, model), f32),
        ],
        in_specs=[SMEM, SMEM, whole, whole, whole]
        + [pl.BlockSpec((tokens, model), lambda j: (s, 0)), pl.BlockSpec(vec.shape, fixed)]
        + [weight(0), weight(steps), weight(0), inner, inner],
        out_specs=[whole, whole, whole, inner, inner, whole, pl.BlockSpec((8, model), fixed)],
        scratch_shapes=[pltpu.VMEM((tokens, model), f32)],
        compiler_params=params("arbitrary"),
        cost_estimate=cost(6 * tokens * model * hidden_units, 14e6),
        name="unit_back",
    )(ids, lens, hidden, own, other, cot, vec, front, front, back, gel, slope)


def row_starts(ids, quarter):
    y, c = ids[0], ids[1]
    keep = [(y * 2 + c) * quarter, ((1 - y) * 2 + c) * quarter]
    send = [(y * 2 + 1 - c) * quarter, ((1 - y) * 2 + 1 - c) * quarter]
    return send, keep


def arrange(ids, turned, left):
    quarter = turned.shape[0] // 4
    send, keep = row_starts(ids, quarter)
    for k, start in enumerate(send + keep):
        rows = pl.ds(pl.multiple_of(start, quarter), quarter)
        left[k * quarter : (k + 1) * quarter, :] = turned[rows, :]


def write_rows(left, right, send, keep):
    grad = dot_nn(left[...], right).astype(bf16)
    half = grad.shape[0] // 2
    send[0:half, :] = grad[:half]
    keep[0:half, :] = grad[half:]


def weight_kernel(steps, seqs, ids, *refs):
    low, dffn, dgate, dup, act = (refs[i * seqs : (i + 1) * seqs] for i in range(5))
    send, keep, left, turned = refs[5 * seqs :]
    j = pl.program_id(0)
    joined = lambda group: jnp.concatenate([ref[...] for ref in group], axis=0)

    @pl.when(j == 0)
    def _():
        for k, group in enumerate((low, dffn)):
            turned[...] = joined(group).T
            arrange(ids, turned, left.at[k])

    @pl.when(j < steps)
    def _():
        write_rows(left.at[0], joined(dgate), send, keep)

    @pl.when((j >= steps) & (j < 2 * steps))
    def _():
        write_rows(left.at[0], joined(dup), send, keep)

    @pl.when(j >= 2 * steps)
    def _():
        write_rows(left.at[1], joined(act), send, keep)


def weight_grads(ids, low, dffn, dgate, dup, act):
    seqs = len(low)
    tokens, model = low[0].shape
    hidden_units = act[0].shape[1]
    steps = hidden_units // BLOCK
    whole = pl.BlockSpec((tokens, model), lambda j: (0, 0))
    column = lambda start: pl.BlockSpec(
        (tokens, BLOCK), lambda j: (0, jnp.clip(j - start, 0, steps - 1))
    )
    out = pl.BlockSpec((model // 2, BLOCK), lambda j: (0, j))
    return pl.pallas_call(
        functools.partial(weight_kernel, steps, seqs),
        grid=(3 * steps,),
        out_shape=[shape((model // 2, 3 * hidden_units), bf16)] * 2,
        in_specs=[SMEM]
        + [whole] * (2 * seqs)
        + [column(0)] * seqs
        + [column(steps)] * seqs
        + [column(2 * steps)] * seqs,
        out_specs=[out, out],
        scratch_shapes=[
            pltpu.VMEM((2, model, tokens * seqs), bf16),
            pltpu.VMEM((model, tokens * seqs), bf16),
        ],
        compiler_params=params("arbitrary"),
        cost_estimate=cost(6 * tokens * seqs * model * hidden_units, 14e6),
        name="weight_grads",
    )(ids, *low, *dffn, *dgate, *dup, *act)


def mix_back_kernel(n, seqs, heads, ids, tok, vec, wo, mixed, *refs):
    own, other, dz2, hown, hother = (refs[i * seqs : (i + 1) * seqs] for i in range(5))
    refs = refs[5 * seqs :]
    sends = refs[:n]
    dz1, send, keep, sums = refs[n : n + 4]
    stage, left, turned_low = refs[n + 4 :]
    z = ids[2]
    slots = sends[0].shape[1]
    per = seqs * heads // n
    sums[...] = jnp.zeros_like(sums)
    for s in range(seqs):
        rows = slice(s * slots, (s + 1) * slots)
        branch = own[s][...].astype(f32) + other[s][...].astype(f32) + vec[4:5, :]
        hat, scale = normalise(tok[rows, :].astype(f32) + branch)
        gh = dz2[s][...] + (hown[s][...].astype(f32) + hother[s][...].astype(f32))
        grad = normalise_back(gh * vec[0:1, :], hat, scale)
        dz1[rows, :] = grad
        low = grad.astype(bf16)
        sums[0:1, :] += jnp.sum(gh * hat, axis=0, keepdims=True)
        sums[1:2, :] += jnp.sum(gh, axis=0, keepdims=True)
        sums[2:3, :] += jnp.sum(low.astype(f32), axis=0, keepdims=True)
        turned_low[:, rows] = low.T
        turned = dot_nn(low, wo[...]).astype(bf16).T
        for h in range(heads):
            i = s * heads + h
            at = (i % n) * per + i // n
            stage[at * HD : (at + 1) * HD, :] = turned[h * HD : (h + 1) * HD, :]
    size = per * HD
    for d in range(n):
        sends[d][...] = stage[pl.ds(pl.multiple_of((z ^ d) * size, size), size), :]
    arrange(ids, turned_low, left)
    write_rows(left, mixed[...], send, keep)
    for ref in (send, keep):
        ref[ref.shape[0] - EXTRA :, :] = jnp.zeros((EXTRA, ref.shape[1]), bf16)


def mix_back(ids, tok, vec, front, mixed, own, other, dz2, hown, hother, n, heads):
    seqs = len(own)
    tokens, model = tok.shape
    slots = tokens // seqs
    width = heads * HD
    size = seqs * heads // n * HD
    rows = model // 2 + EXTRA
    return pl.pallas_call(
        functools.partial(mix_back_kernel, n, seqs, heads),
        grid=(1,),
        out_shape=[shape((size, slots), bf16)] * n
        + [shape((tokens, model), f32)]
        + [shape((rows, width), bf16)] * 2
        + [shape((8, model), f32)],
        in_specs=[SMEM, VMEM, VMEM]
        + [pl.BlockSpec((model, width), lambda i: (0, front.shape[1] // width - 1)), VMEM]
        + [VMEM] * (5 * seqs),
        out_specs=[VMEM] * (n + 4),
        scratch_shapes=[
            pltpu.VMEM((size * n, slots), bf16),
            pltpu.VMEM((model, tokens), bf16),
            pltpu.VMEM((model, tokens), bf16),
        ],
        compiler_params=params("arbitrary"),
        cost_estimate=cost(4 * tokens * model * width, 10e6),
        name="mix_back",
    )(ids, tok, vec, front, mixed, *own, *other, *dz2, *hown, *hother)


def project_back_kernel(n, seqs, heads, ids, tok, whole, small, far, near, *refs):
    inputs = refs[:n]
    part, send, keep = refs[n : n + 3]
    stage, right, left, turned = refs[n + 3 :]
    z = ids[2]
    slots = inputs[0].shape[1]
    per = seqs * heads // n
    width = heads * HD
    size = per * 3 * HD
    for d in range(n):
        stage[pl.ds(pl.multiple_of((z ^ d) * size, size), size), :] = inputs[d][...]
    for s in range(seqs):
        for c in range(3):
            columns = []
            for h in range(heads):
                i = s * heads + h
                at = ((i % n) * per + i // n) * 3 + c
                columns.append(stage[at * HD : (at + 1) * HD, :])
            ours = jnp.concatenate(columns, axis=0).T
            right[s * slots : (s + 1) * slots, c * width : (c + 1) * width] = ours
    part[...] = dot_nt(right[...], whole[...]).astype(bf16)
    turned[...] = tok[...].T
    arrange(ids, turned, left)
    for c in range(3):
        cols = slice(c * width, (c + 1) * width)
        write_rows(left, right[:, cols], send.at[:, cols], keep.at[:, cols])
    ones = jnp.ones((8, right.shape[0]), bf16)
    sums = dot_nn(ones, right[...])
    line = jnp.concatenate([sums[:, :width], sums[:, 2 * width :]], axis=1)
    row = lax.broadcasted_iota(jnp.int32, (8, 1), 0)
    rows = jnp.where(row == 6, line, small[...])
    rows = jnp.concatenate([rows, jnp.zeros_like(rows)], axis=0).astype(bf16)
    for ref, before in ((send, far), (keep, near)):
        ref[ref.shape[0] - EXTRA :, : 2 * width] = rows
        ref[ref.shape[0] - EXTRA :, 2 * width : 3 * width] = jnp.zeros((EXTRA, width), bf16)
        ref[:, 3 * width :] = before[...]


def project_back(ids, tok, whole, small, grads, blocks, n, seqs, heads):
    tokens, model = tok.shape
    slots = tokens // seqs
    wide = whole.shape[1]
    return pl.pallas_call(
        functools.partial(project_back_kernel, n, seqs, heads),
        out_shape=[shape((tokens, model), bf16)] + [shape((grads[0].shape[0], 4 * heads * HD), bf16)] * 2,
        in_specs=[SMEM] + [VMEM] * (5 + n),
        out_specs=[VMEM] * 3,
        scratch_shapes=[
            pltpu.VMEM((seqs * heads * 3 * HD, slots), bf16),
            pltpu.VMEM((tokens, wide), bf16),
            pltpu.VMEM((model, tokens), bf16),
            pltpu.VMEM((model, tokens), bf16),
        ],
        compiler_params=params(),
        cost_estimate=cost(4 * tokens * model * wide, 8e6),
        name="project_back",
    )(ids, tok, whole, small, *grads, *blocks)


def fold_core_kernel(extra, keep, recv, mine, *sends):
    half = (keep.shape[0] - extra) // 2
    total = keep[0:half, :].astype(f32) + recv[0:half, :].astype(f32)
    mine[0:half, :] = total.astype(mine.dtype)
    rest = (keep[half:, :].astype(f32) + recv[half:, :].astype(f32)).astype(bf16)
    size = sends[0].shape[1]
    for k, send in enumerate(sends):
        send[...] = rest[:, k * size : (k + 1) * size]
    if extra:
        mine[half:, :] = rest[half:, :].astype(f32)


def fold_core(keep, recv, extra):
    rows, wide = keep.shape
    out = (rows - extra) // 2 + extra
    steps = 1 if extra else 3
    parts = 2 if extra else 1
    column = lambda size: pl.BlockSpec((size, wide // steps), lambda j: (0, j))
    return pl.pallas_call(
        functools.partial(fold_core_kernel, extra),
        grid=(steps,),
        out_shape=[shape((out, wide), f32 if extra else bf16)]
        + [shape((out, wide // parts), bf16)] * parts,
        in_specs=[column(rows)] * 2,
        out_specs=[column(out)]
        + [pl.BlockSpec((out, wide // steps // parts), lambda j: (0, j))] * parts,
        compiler_params=params("arbitrary"),
        cost_estimate=cost(rows * wide, 7 * rows * wide),
        name="fold_core",
    )(keep, recv)


def fold_y_kernel(n, extra, parts, ids, mine, *refs):
    recvs, own, sends, stage = refs[:parts], refs[parts], refs[parts + 1 : -1], refs[-1]
    z = ids[2]
    rows = mine.shape[0] - extra
    size = rows // n
    recv = jnp.concatenate([ref[...] for ref in recvs], axis=1)
    stage[...] = mine[...].astype(f32) + recv.astype(f32)
    for d in range(n):
        block = stage[pl.ds(pl.multiple_of((z ^ d) * size, size), size), :]
        if d:
            sends[d - 1][0:size, :] = block.astype(bf16)
            if extra:
                sends[d - 1][size:, :] = stage[rows:, :].astype(bf16)
        else:
            own[0:size, :] = block
            if extra:
                own[size:, :] = stage[rows:, :].astype(bf16).astype(f32)


def fold_y(ids, mine, recvs, n, extra):
    rows, wide = mine.shape
    out = (rows - extra) // n + extra
    steps = 1 if extra else 3
    parts = len(recvs)
    column = lambda size: pl.BlockSpec((size, wide // steps), lambda j: (0, j))
    return pl.pallas_call(
        functools.partial(fold_y_kernel, n, extra, parts),
        grid=(steps,),
        out_shape=[shape((out, wide), f32)] + [shape((out, wide), bf16)] * (n - 1),
        in_specs=[SMEM, column(rows)]
        + [pl.BlockSpec((rows, wide // steps // parts), lambda j: (0, j))] * parts,
        out_specs=[column(out)] * n,
        scratch_shapes=[pltpu.VMEM((rows, wide // steps), f32)],
        compiler_params=params("arbitrary"),
        cost_estimate=cost(rows * wide, 9 * rows * wide),
        name="fold_y",
    )(ids, mine, *recvs)


def fold_z(own, got):
    return (own + got[0].astype(f32)) + (got[1].astype(f32) + got[2].astype(f32))


def fits(tokens, b_qv, w_qkv, w_gu):
    n = lax.axis_size("ctx")
    heads = b_qv.shape[1] // HD
    return (
        n == 4
        and lax.axis_size("shard") == 4
        and lax.axis_size("tp") == 2
        and (tokens.shape[0] * heads) % n == 0
        and w_qkv.shape[0] % 16 == 0
        and tokens.shape[1] % 256 == 0
        and b_qv.shape[1] == WIDTH
        and w_gu.shape[2] % BLOCK == 0
        and w_gu.shape[2] % WIDTH == 0
    )


def on_device(tokens, lengths, w_qkv, b_qv, w_out, w_gu, w_down, vectors, cotangent):
    if not fits(tokens, b_qv, w_qkv, w_gu):
        return by_gather(tokens, lengths, w_qkv, b_qv, w_out, w_gu, w_down, vectors, cotangent)
    n = lax.axis_size("ctx")
    seqs, slots, model = tokens.shape
    width = b_qv.shape[1]
    heads = width // HD
    per = seqs * heads // n
    units = w_gu.shape[2]
    rows = w_qkv.shape[0]
    count = seqs * slots
    shard = lax.axis_index("shard")
    ids = jnp.stack(
        [shard // 2, shard % 2, lax.axis_index("ctx"), lax.axis_index("tp")]
    ).astype(jnp.int32)
    slopes = jnp.asarray(slope_table())
    tok = tokens.reshape(count, model)
    cot = cotangent.reshape(count, model)

    first = [w_qkv.astype(bf16).reshape(rows, 3 * width)]
    first += [swap(first[0], "ctx", d) for d in range(1, n)]
    first += [swap(piece, "shard", 2) for piece in first]
    by_core = [swap(piece, "shard", 1) for piece in first]
    pieces = first[:n] + by_core[:n] + first[n:] + by_core[n:]
    front = jnp.concatenate([w_gu.reshape(rows, 2 * units), w_out.T], axis=1).astype(bf16)
    back = w_down.T.astype(bf16)
    (front,) = after([front], *pieces[1:n])
    front = [front] + [swap(front, "ctx", d) for d in range(1, n)]

    bias = jnp.concatenate([b_qv[0], jnp.zeros_like(b_qv[0]), b_qv[1]])[None, :]
    *sends, whole = project(ids, tok, bias, pieces, n, seqs, heads)
    blocks = [sends[0]] + [swap(sends[d], "ctx", d) for d in range(1, n)]
    front = jnp.concatenate(after(front, whole), axis=0)
    front_y = swap(front, "shard", 2)
    (back,) = after([back], *blocks)
    back = [back] + [swap(back, "ctx", d) for d in range(1, n)]
    *outs, att, den = attend(ids, lengths, slopes, blocks, n, heads, per)
    front, front_y = after([front, front_y], outs[0])
    front = [front, swap(front, "shard", 1), front_y, swap(front_y, "shard", 1)]
    back = jnp.concatenate(after(back, outs[0]), axis=0)
    back_y = swap(back, "shard", 2)
    outs = [outs[0]] + [swap(outs[d], "ctx", d) for d in range(1, n)]
    front = assemble(ids, front, n)
    *part, mixed = mix(ids, front, outs, n, seqs, heads)
    part_other = [swap(value, "tp", 1) for value in part]
    back, back_y = after([back, back_y], part[0])
    back = [back, swap(back, "shard", 1), back_y, swap(back_y, "shard", 1)]
    back = assemble(ids, back, n)
    hidden, low, act, gel, slope, ffn = zip(
        *(
            unit(s, tok, part[s], part_other[s], vectors, front, back)
            for s in range(seqs)
        )
    )
    ffn_other = [swap(value, "tp", 1) for value in ffn]
    output, dz2, dffn, dgate, dup, dlow, sums_two = zip(
        *(
            unit_back(
                s, ids, lengths, hidden[s], ffn[s], ffn_other[s], cot, vectors, front, back,
                gel[s], slope[s], n,
            )
            for s in range(seqs)
        )
    )
    dlow_other = [swap(value, "tp", 1) for value in dlow]
    far, near = weight_grads(ids, low, dffn, dgate, dup, act)
    *dlow_other, far = lax.optimization_barrier((*dlow_other, far))
    got = swap(far, "shard", 1)
    *sends, dz1, last_far, last_near, sums_one = mix_back(
        ids, tok, vectors, front, mixed, part, part_other, dz2, dlow, dlow_other, n, heads
    )
    sums_two = sum(sums_two)
    grads = [sends[0]] + [swap(sends[d], "ctx", d) for d in range(1, n)]
    got, sends[0] = lax.optimization_barrier((got, sends[0]))
    mine, far = fold_core(near, got, 0)
    *grads, far = lax.optimization_barrier((*grads, far))
    got = swap(far, "shard", 2)
    outs = attend_back(ids, lengths, slopes, blocks, grads, att, den, n, heads, per)
    outs = [outs[0]] + [swap(outs[d], "ctx", d) for d in range(1, n)]
    rest_own, *rest_sends = fold_y(ids, mine, [got], n, 0)
    *outs, rest_own = lax.optimization_barrier((*outs, rest_own))
    small = jnp.concatenate(
        [sums_one[0:2], sums_two[0:2], sums_one[2:3], sums_two[2:3], jnp.zeros_like(sums_one[:2])]
    )
    dx, far, near = project_back(
        ids, tok, whole, small, (last_far, last_near), outs, n, seqs, heads
    )
    got = swap(far, "shard", 1)
    mine, *far = fold_core(near, got, EXTRA)
    got = [swap(half, "shard", 2) for half in far]
    dx_other = swap(dx, "tp", 1)
    rest_got = [swap(block, "ctx", d + 1) for d, block in enumerate(rest_sends)]
    rest_got[0], got[0] = lax.optimization_barrier((rest_got[0], got[0]))
    own, *sends = fold_y(ids, mine, got, n, EXTRA)
    got = [swap(block, "ctx", d + 1) for d, block in enumerate(sends)]
    rest = fold_z(rest_own, rest_got)
    last = fold_z(own, got)
    input_grad = dz1 + (dx.astype(f32) + dx_other.astype(f32))
    small = last[rows : rows + 8, : 2 * width]
    return (
        jnp.stack(output),
        input_grad.reshape(tokens.shape),
        last[:rows, : 3 * width].reshape(w_qkv.shape),
        small[6].reshape(2, width),
        last[:rows, 3 * width :].T,
        rest[:, : 2 * units].reshape(w_gu.shape),
        rest[:, 2 * units :].T,
        small[:6],
    )


def alibi_slopes(first_head, head_count):
    power = 2 ** (H.bit_length() - 1)
    heads_index = first_head + jnp.arange(head_count, dtype=jnp.int32)
    early = -8.0 * (heads_index + 1).astype(jnp.float32) / power
    later = -4.0 * (2 * (heads_index - power) + 1).astype(jnp.float32) / power
    return jnp.exp2(jnp.where(heads_index < power, early, later))


def layer_norm(values, gain, shift):
    centred = values - jnp.mean(values, axis=-1, keepdims=True)
    spread = jnp.mean(centred * centred, axis=-1, keepdims=True)
    return centred * lax.rsqrt(spread + epsilon) * gain + shift


def gated_unit(gate_input, upper):
    return jax.nn.gelu(gate_input, approximate=False) * upper


def score_block(query_heads, key_heads, query_place, key_place, slopes, lengths):
    scores = (
        jnp.einsum("sqhe,skhe->shqk", query_heads, key_heads, preferred_element_type=jnp.float32)
        * 0.125
    )
    distance = jnp.abs(query_place[:, None] - key_place[None, :]).astype(jnp.float32)
    scores = scores - slopes[None, :, None, None] * distance[None, None]
    usable = key_place[None, :] < lengths[:, None]
    return jnp.where(usable[:, None, None, :], jnp.exp(scores), 0.0)


def backward_scores(
    query_heads,
    numer_heads,
    correction,
    key_heads,
    value_heads,
    query_place,
    key_place,
    slopes,
    lengths,
):
    weights = score_block(query_heads, key_heads, query_place, key_place, slopes, lengths)
    value_dots = jnp.einsum(
        "sqhe,skhe->shqk", numer_heads, value_heads, preferred_element_type=jnp.float32
    )
    grad_scores = (weights * (value_dots - correction[..., None])).astype(jnp.bfloat16)
    return (weights.astype(jnp.bfloat16), grad_scores)


def split_blocks(shard_piece, slot_count, ctx_count):
    piece_rows = shard_piece.shape[1]
    block_rows = math.gcd(piece_rows, 128)
    block_count = piece_rows // block_rows
    shaped = shard_piece.reshape(
        (shard_piece.shape[0], block_count, block_rows) + shard_piece.shape[2:]
    )
    blocks = jnp.moveaxis(shaped, 1, 0)
    row_ids = jnp.arange(piece_rows, dtype=jnp.int32)
    places = (row_ids % slot_count * ctx_count + row_ids // slot_count).reshape(
        block_count, block_rows
    )
    offsets = block_rows * jnp.arange(block_count, dtype=jnp.int32)
    return (blocks, places, offsets)


def by_gather(tokens, lengths, w_qkv, b_qv, w_out, w_gu, w_down, vectors, cotangent):
    ctx_count = lax.axis_size("ctx")
    ctx_rank = lax.axis_index("ctx")
    seq_count, slot_count, model_width = tokens.shape
    local_width = b_qv.shape[1]
    head_count = local_width // HD
    slopes = alibi_slopes(lax.axis_index("tp") * head_count, head_count)
    slot_ids = jnp.arange(slot_count, dtype=jnp.int32)
    query_place = slot_ids * ctx_count + ctx_rank
    query_live = (query_place[None, :] < lengths[:, None]).astype(jnp.float32)
    live_rows = query_live[:, :, None]
    head_shape = (seq_count, slot_count, head_count, HD)
    whole_qkv, whole_out, whole_gu, whole_down = (
        lax.all_gather(w_qkv.astype(jnp.bfloat16), ("shard", "ctx"), axis=0, tiled=True),
        lax.all_gather(w_out.astype(jnp.bfloat16), ("shard", "ctx"), axis=1, tiled=True),
        lax.all_gather(w_gu.astype(jnp.bfloat16), ("shard", "ctx"), axis=0, tiled=True),
        lax.all_gather(w_down.astype(jnp.bfloat16), ("shard", "ctx"), axis=1, tiled=True),
    )
    inputs = tokens.astype(jnp.float32)
    projected = jnp.einsum("std,dcm->stcm", tokens, whole_qkv, preferred_element_type=jnp.float32)
    query_rows = (projected[:, :, 0] + b_qv[0]).astype(jnp.bfloat16)
    key_rows = projected[:, :, 1].astype(jnp.bfloat16)
    value_rows = (projected[:, :, 2] + b_qv[1]).astype(jnp.bfloat16)
    query_heads = query_rows.reshape(head_shape)
    pairs = jnp.stack([key_rows, value_rows], axis=2)
    start_numer = jnp.zeros((seq_count, head_count, slot_count, HD), jnp.float32)
    start_denom = jnp.zeros((seq_count, head_count, slot_count), jnp.float32)
    blocks, places, offsets = split_blocks(
        lax.all_gather(pairs, "ctx", axis=1, tiled=True), slot_count, ctx_count
    )

    def forward_advance(inner_state, block_item):
        key_block, key_place, row_offset = block_item
        numerator, denominator = inner_state
        key_heads = key_block[:, :, 0].reshape(seq_count, -1, head_count, HD)
        value_heads = key_block[:, :, 1].reshape(seq_count, -1, head_count, HD)
        weights = score_block(query_heads, key_heads, query_place, key_place, slopes, lengths)
        numerator = numerator + jnp.einsum(
            "shqk,skhe->shqe",
            weights.astype(jnp.bfloat16),
            value_heads,
            preferred_element_type=jnp.float32,
        )
        return ((numerator, denominator + jnp.sum(weights, axis=-1)), None)

    result_state, unused = lax.scan(
        forward_advance, (start_numer, start_denom), (blocks, places, offsets)
    )
    numerator, denominator = result_state
    denominator = denominator + (1.0 - query_live)[:, None, :]
    attention_q = jnp.transpose(numerator / denominator[..., None], (0, 2, 1, 3))
    denom_q = jnp.transpose(denominator, (0, 2, 1))
    mixed = attention_q.reshape(seq_count, slot_count, local_width).astype(jnp.bfloat16)
    attn_part = jnp.einsum("stm,mn->stn", mixed, whole_out, preferred_element_type=jnp.float32)
    attn_branch = lax.psum(attn_part, "tp") + vectors[4]
    hidden, first_pull = jax.vjp(layer_norm, inputs + attn_branch, vectors[0], vectors[1])
    hidden_low = hidden.astype(jnp.bfloat16)
    gated = jnp.einsum("std,dcf->stcf", hidden_low, whole_gu, preferred_element_type=jnp.float32)
    activated, unit_pull = jax.vjp(gated_unit, gated[:, :, 0], gated[:, :, 1])
    act_low = activated.astype(jnp.bfloat16)
    ffn_part = jnp.einsum("stf,fn->stn", act_low, whole_down, preferred_element_type=jnp.float32)
    ffn_branch = lax.psum(ffn_part, "tp") + vectors[5]
    normed, second_pull = jax.vjp(layer_norm, hidden + ffn_branch, vectors[2], vectors[3])
    output = (normed * live_rows).astype(jnp.bfloat16)
    upstream = cotangent.astype(jnp.float32) * live_rows
    grad_second, grad_gain_two, grad_shift_two = second_pull(upstream)
    grad_ffn = grad_second.astype(jnp.bfloat16)
    grad_down = jnp.einsum("stf,stn->fn", act_low, grad_ffn, preferred_element_type=jnp.float32)
    grad_ffn_bias = jnp.sum(grad_ffn.astype(jnp.float32), axis=(0, 1))
    grad_act = jnp.einsum("stn,fn->stf", grad_ffn, whole_down, preferred_element_type=jnp.float32)
    grad_gate, grad_upper = unit_pull(grad_act)
    grad_gated = jnp.stack([grad_gate, grad_upper], axis=2).astype(jnp.bfloat16)
    grad_gu = jnp.einsum(
        "std,stcf->dcf", hidden_low, grad_gated, preferred_element_type=jnp.float32
    )
    hidden_part = jnp.einsum(
        "stcf,dcf->std", grad_gated, whole_gu, preferred_element_type=jnp.float32
    )
    grad_hidden = grad_second + lax.psum(hidden_part, "tp")
    grad_first, grad_gain_one, grad_shift_one = first_pull(grad_hidden)
    grad_attn = grad_first.astype(jnp.bfloat16)
    grad_out = jnp.einsum("stm,stn->mn", mixed, grad_attn, preferred_element_type=jnp.float32)
    grad_out_bias = jnp.sum(grad_attn.astype(jnp.float32), axis=(0, 1))
    grad_mixed = jnp.einsum(
        "stn,mn->stm", grad_attn, whole_out, preferred_element_type=jnp.float32
    ).astype(jnp.bfloat16)
    grad_mixed_heads = grad_mixed.reshape(head_shape).astype(jnp.float32)
    correction = jnp.transpose(
        jnp.sum(grad_mixed_heads * attention_q, axis=-1) / denom_q, (0, 2, 1)
    )
    numer_heads = (grad_mixed_heads / denom_q[..., None]).astype(jnp.bfloat16)
    start_query = jnp.zeros(head_shape, jnp.float32)
    start_state = (
        start_query,
        jnp.zeros((seq_count, slot_count * ctx_count, 2, local_width), jnp.float32),
    )
    blocks, places, offsets = split_blocks(
        lax.all_gather(pairs, "ctx", axis=1, tiled=True), slot_count, ctx_count
    )

    def backward_advance(current_state, block_item):
        key_block, key_place, row_offset = block_item
        key_heads = key_block[:, :, 0].reshape(seq_count, -1, head_count, HD)
        value_heads = key_block[:, :, 1].reshape(seq_count, -1, head_count, HD)
        weights_low, grad_scores = backward_scores(
            query_heads,
            numer_heads,
            correction,
            key_heads,
            value_heads,
            query_place,
            key_place,
            slopes,
            lengths,
        )
        grad_query = current_state[0] + jnp.einsum(
            "shqk,skhe->sqhe", grad_scores, key_heads, preferred_element_type=jnp.float32
        )
        grad_key = (
            jnp.einsum(
                "shqk,sqhe->skhe", grad_scores, query_heads, preferred_element_type=jnp.float32
            )
            * 0.125
        )
        grad_value = jnp.einsum(
            "shqk,sqhe->skhe", weights_low, numer_heads, preferred_element_type=jnp.float32
        )
        stacked = jnp.stack(
            [
                grad_key.reshape(seq_count, -1, local_width),
                grad_value.reshape(seq_count, -1, local_width),
            ],
            axis=2,
        )
        buffer = lax.dynamic_update_slice_in_dim(current_state[1], stacked, row_offset, axis=1)
        return ((grad_query, buffer), None)

    result_state, unused = lax.scan(backward_advance, start_state, (blocks, places, offsets))
    grad_pairs = lax.psum_scatter(
        result_state[1].astype(jnp.bfloat16), "ctx", scatter_dimension=1, tiled=True
    )
    grad_query_low = (
        (result_state[0] * 0.125).astype(jnp.bfloat16).reshape(seq_count, slot_count, local_width)
    )
    grad_proj = jnp.concatenate([grad_query_low[:, :, None], grad_pairs], axis=2)
    grad_qkv = jnp.einsum("std,stcm->dcm", tokens, grad_proj, preferred_element_type=jnp.float32)
    bias_terms = jnp.stack(
        [
            jnp.sum(grad_query_low.astype(jnp.float32), axis=(0, 1)),
            jnp.sum(grad_pairs[:, :, 1].astype(jnp.float32), axis=(0, 1)),
        ]
    )
    input_part = jnp.einsum(
        "stcm,dcm->std", grad_proj, whole_qkv, preferred_element_type=jnp.float32
    )
    input_grad = grad_first + lax.psum(input_part.astype(jnp.bfloat16), "tp").astype(jnp.float32)
    grad_weights = (
        lax.psum_scatter(grad_qkv, ("shard", "ctx"), scatter_dimension=0, tiled=True),
        lax.psum_scatter(grad_out, ("shard", "ctx"), scatter_dimension=1, tiled=True),
        lax.psum_scatter(grad_gu, ("shard", "ctx"), scatter_dimension=0, tiled=True),
        lax.psum_scatter(grad_down, ("shard", "ctx"), scatter_dimension=1, tiled=True),
    )
    vector_terms = jnp.stack(
        [grad_gain_one, grad_shift_one, grad_gain_two, grad_shift_two, grad_out_bias, grad_ffn_bias]
    )
    grad_bqv, grad_vectors = lax.psum((bias_terms, vector_terms), ("shard", "ctx"))
    return (
        output,
        input_grad,
        grad_weights[0],
        grad_bqv,
        grad_weights[1],
        grad_weights[2],
        grad_weights[3],
        grad_vectors,
    )


def solution(mesh):
    placed = (
        P("shard", "ctx", None),
        P("shard"),
        P(("shard", "ctx"), None, "tp"),
        P(None, "tp"),
        P("tp", ("shard", "ctx")),
        P(("shard", "ctx"), None, "tp"),
        P("tp", ("shard", "ctx")),
        P(),
        P("shard", "ctx", None),
    )
    return jax.shard_map(
        on_device,
        mesh=mesh,
        in_specs=placed,
        out_specs=(
            P("shard", "ctx", None),
            P("shard", "ctx", None),
            P(("shard", "ctx"), None, "tp"),
            P(None, "tp"),
            P("tp", ("shard", "ctx")),
            P(("shard", "ctx"), None, "tp"),
            P("tp", ("shard", "ctx")),
            P(),
        ),
        check_vma=False,
    )
```
